32 devices in a mesh: rows: 8 (over z, y), seq: 4 (over x, core).
Axes of the slice: x: 2, y: 2, z: 4, core: 2. Of those that a mesh axis runs over, the one named last changes fastest.
Arguments:
- tokens: bfloat16 [64, 512, 768], P('rows', 'seq'), may hold values from -6 to 6
- segments: int32 [64, 512], P('rows', 'seq'), may hold values from 0 to 3, never falling along the last dimension, each value on 1 to 256 neighbouring positions
- mix: bfloat16 [12, 512, 512], P(None, None, 'seq'), may hold values from -8 to 8
- w_value: bfloat16 [768, 768], P('rows'), may hold values from -0.21875 to 0.21875
- w_out: bfloat16 [768, 768], P('rows'), may hold values from -0.875 to 0.875
- w_in: bfloat16 [768, 3072], P(None, 'rows'), may hold values from -0.21875 to 0.21875
- w_back: bfloat16 [3072, 768], P('rows'), may hold values from -0.109375 to 0.109375
- gain_one: bfloat16 [768], P('rows'), may hold values from 0.5 to 1.5
- gain_two: bfloat16 [768], P('rows'), may hold values from 0.5 to 1.5
- out_grad: bfloat16 [64, 512, 768], P('rows', 'seq'), may hold values from -6 to 6
Outputs:
- result: bfloat16 [64, 512, 768], P('rows', 'seq')
- tokens_grad: float32 [64, 512, 768], P('rows', 'seq')
- mix_grad: float32 [12, 512, 512], P(None, None, 'seq')
- w_value_grad: float32 [768, 768], P('rows')
- w_out_grad: float32 [768, 768], P('rows')
- w_in_grad: float32 [768, 3072], P(None, 'rows')
- w_back_grad: float32 [3072, 768], P('rows')
- gain_one_grad: float32 [768], P('rows')
- gain_two_grad: float32 [768], P('rows')
- rms_residual: float32 [64, 512], P('rows', 'seq')
- rms_sublayer: float32 [64, 512], P('rows', 'seq')
The draws below stay inside these ranges and needn't reach their ends.
Inputs may be any that keep to these rules, and one draw needn't show every extreme that they name: `segments`: along each row the ids never fall; a document holds at most 256 tokens, and some document in each row holds exactly that many.
All inputs are finite; a program needn't handle non-finite values.
Results may differ from the reference program's by a relative error of at most 0.0085.
Values may be sent and summed in bfloat16 or wider, within the bound.
A program may use at most 128 MiB of HBM per device.

```python
import math
import jax
import jax.numpy as jnp
import numpy as np
from jax import lax

D = 768
HEADS = 12
HD = 64
FF = 3072
LEN = 512
SEQS = 8
SEQUENCES = 64


def block_scale(own_key, dims, cuts, low, high):
    factor_of, own = 1.0, jax.random.fold_in(own_key, 6)
    for position, parts in cuts:
        draws = jnp.exp(jax.random.uniform(jax.random.fold_in(own, position), (parts,), jnp.float32, low / len(cuts), high / len(cuts)))
        factor_of = factor_of * jnp.repeat(draws, dims[position] // parts).reshape([-1 if axis == position else 1 for axis in range(len(dims))])
    return factor_of


def length_profile(count, total, limit, slope):
    loads = [(1 << 20) // math.isqrt(rank ** slope) + 1 for rank in range(2, count + 1)]
    rest, counts = total - limit - (count - 1), [1] * (count - 1)
    while rest > 0:
        free = [i for i in range(count - 1) if counts[i] < limit]
        whole, budget = sum([loads[i] for i in free]), rest
        for i in free:
            addition = min(limit - counts[i], max(1, budget * loads[i] // whole), rest)
            counts[i] = counts[i] + addition
            rest = rest - addition
    return np.array([limit] + counts)


def ragged_sizes(stream_key, number_of, total, limit, skew):
    if number_of == 2:
        one = jax.random.randint(stream_key, (), max(1, total - limit), min(limit, total - 1) + 1)
        return jnp.stack([one, total - one])
    sizes = jnp.asarray(length_profile(number_of, total, limit, skew), jnp.int32)
    pairs = (number_of - 1) // 2
    donor, receiver = sizes[1:1 + 2 * pairs:2], sizes[2:2 + 2 * pairs:2]
    room = jnp.minimum(donor - 1, limit - receiver)
    moved = jax.random.randint(jax.random.fold_in(stream_key, 1), (pairs,), 0, 1 << 20) % (room + 1)
    sizes = sizes.at[1:1 + 2 * pairs:2].set(donor - moved).at[2:2 + 2 * pairs:2].set(receiver + moved)
    return sizes[jax.random.permutation(jax.random.fold_in(stream_key, 2), number_of)]


def centred(rng, dims, scale, most, shards=(), held_as=jnp.bfloat16):
    array = scale * jax.random.normal(rng, dims, jnp.float32)
    if shards:
        array = array * block_scale(rng, dims, shards, -0.22, 0.18)
    return jnp.clip(array, -most, most).astype(held_as)


def setup_inputs(seed: int = 0) -> dict:
    seeds = jax.random.split(jax.random.key(seed), 11)
    tokens = centred(seeds[0], (SEQUENCES, LEN, D), 1.0, 6.0, ((0, 8), (1, 4)))
    segments = jax.vmap(lambda own: jnp.searchsorted(jnp.cumsum(ragged_sizes(own, 4, LEN, LEN // 2, 2)), jnp.arange(LEN), side="right"))(jax.random.split(seeds[1], SEQUENCES)).reshape((SEQUENCES, LEN)).astype(jnp.int32)
    mix = centred(seeds[2], (HEADS, LEN, LEN), 1.5, 8.0, ((2, 4),))
    w_value = centred(seeds[3], (D, D), D ** -0.5, 0.21875, ((0, 8),))
    w_out = centred(seeds[4], (D, D), (D // 16) ** -0.5, 0.875, ((0, 8),))
    w_in = centred(seeds[5], (D, FF), D ** -0.5, 0.21875, ((1, 8),))
    w_back = centred(seeds[6], (FF, D), FF ** -0.5, 0.109375, ((0, 8),))
    gain_one = jnp.clip(1.0 + 0.1 * jax.random.normal(seeds[7], (D,), jnp.float32), 0.5, 1.5).astype(jnp.bfloat16)
    gain_two = jnp.clip(1.0 + 0.1 * jax.random.normal(seeds[8], (D,), jnp.float32), 0.5, 1.5).astype(jnp.bfloat16)
    out_grad = centred(seeds[9], (SEQUENCES, LEN, D), 1.0, 6.0, ((0, 8), (1, 4)))
    return {"tokens": tokens, "segments": segments, "mix": mix, "w_value": w_value, "w_out": w_out, "w_in": w_in, "w_back": w_back, "gain_one": gain_one, "gain_two": gain_two, "out_grad": out_grad}


NEG = -1e+30
EPS = 1e-06
HIGH = lax.Precision.HIGHEST

@jax.custom_vjp
def low(v):
    return lax.optimization_barrier(v.astype(jnp.bfloat16)).astype(jnp.float32)

@jax.custom_vjp
def low_back(v):
    return v

def low_keep(v):
    return (low(v), None)

def low_pass(kept, grad):
    return (grad,)

def back_keep(v):
    return (v, None)

def back_low(kept, grad):
    return (low(grad),)
low.defvjp(low_keep, low_pass)
low_back.defvjp(back_keep, back_low)

def rms_scaled(inputs, gain):
    scale = lax.rsqrt(lax.optimization_barrier(jnp.mean(inputs * inputs, axis=-1, keepdims=True)) + EPS)
    return inputs * scale * gain

def matmul_hi(left, right):
    return jnp.dot(left, right, precision=HIGH)

def group_forward(params, group_tokens, group_segs):
    w_value, w_out, w_in, w_back, mix, gain_first, gain_second = params
    resid_in = group_tokens.reshape(-1, D)
    entry_one = low(rms_scaled(resid_in, gain_first))
    values = low(low_back(matmul_hi(entry_one, w_value))).reshape(-1, LEN, HEADS, HD)
    same_doc = group_segs[:, :, None] == group_segs[:, None, :]
    scores = jnp.where(same_doc[:, None], mix[None], NEG)
    shifted = scores - lax.optimization_barrier(jnp.max(scores, axis=-1, keepdims=True))
    raised = jnp.exp(shifted)
    soft_probs = low(raised / lax.optimization_barrier(jnp.sum(raised, axis=-1, keepdims=True)))
    mixed = jnp.einsum('ghij,gjhd->gihd', soft_probs, values, precision=HIGH).reshape(-1, D)
    mixed_low = low(low_back(mixed))
    hidden_one = resid_in + low_back(matmul_hi(mixed_low, w_out))
    entry_two = low(rms_scaled(hidden_one, gain_second))
    pre_act = low_back(matmul_hi(entry_two, w_in))
    activ = low(jax.nn.gelu(pre_act, approximate=True))
    branch = matmul_hi(activ, w_back)
    rms_res = jnp.sqrt(lax.optimization_barrier(jnp.mean(hidden_one * hidden_one, axis=-1))).reshape(group_segs.shape)
    rms_sub = jnp.sqrt(lax.optimization_barrier(jnp.mean(branch * branch, axis=-1))).reshape(group_segs.shape)
    return ((hidden_one + branch).reshape(group_tokens.shape), (rms_res, rms_sub))

def reference(tokens, segments, mix, w_value, w_out, w_in, w_back, gain_one, gain_two, out_grad):
    params = tuple((weight_arr.astype(jnp.float32) for weight_arr in (w_value, w_out, w_in, w_back, mix, gain_one, gain_two)))
    groups = tokens.astype(jnp.float32).reshape(-1, SEQS, LEN, D)
    seg_groups = segments.reshape(-1, SEQS, LEN)
    step_fn = jax.checkpoint(group_forward)

    def whole_layer(layer_params, layer_groups):
        return lax.map(lambda group_pair: step_fn(layer_params, group_pair[0], group_pair[1]), (layer_groups, seg_groups))
    result, pullback, extras = jax.vjp(whole_layer, params, groups, has_aux=True)
    grads, grad_groups = pullback(out_grad.astype(jnp.float32).reshape(result.shape))
    grad_value, grad_out, grad_in, grad_back, grad_mix, grad_gain_one, grad_gain_two = grads
    rms_res, rms_sub = extras
    return (result.reshape(tokens.shape).astype(jnp.bfloat16), grad_groups.reshape(tokens.shape), grad_mix, grad_value, grad_out, grad_in, grad_back, grad_gain_one, grad_gain_two, rms_res.reshape(segments.shape), rms_sub.reshape(segments.shape))
```

```python
import functools
from functools import partial

import jax
import jax.numpy as jnp
from jax import lax
from jax.experimental import pallas as pl
from jax.experimental.pallas import tpu as pltpu
from jax.sharding import PartitionSpec as P

NEG = -1e30
EPS = 1e-06


def joined(part, axis, combine):
    gathered = jax.tree.map(lambda a: lax.all_gather(a, axis), part)

    def take(source):
        return jax.tree.map(lambda a: lax.dynamic_index_in_dim(a, source, 0, False), gathered)

    return lax.fori_loop(
        1, lax.axis_size(axis), lambda source, state: combine(state, take(source)), take(0)
    )


def normalize(inputs, gain):
    scale = lax.rsqrt(jnp.mean(inputs * inputs, axis=-1, keepdims=True) + EPS)
    normed = inputs * scale
    return (normed, scale, (normed * gain).astype(jnp.bfloat16))


def norm_back(upstream, normed, scale, gain):
    scaled = upstream * gain
    back = scale * (scaled - normed * jnp.mean(scaled * normed, axis=-1, keepdims=True))
    return (back, jnp.sum(upstream * normed, axis=0))


def combine_stats(first, second):
    max_first, sum_first = first
    max_second, sum_second = second
    row_max = jnp.maximum(max_first, max_second)
    return (
        row_max,
        sum_first * jnp.exp(max_first - row_max) + sum_second * jnp.exp(max_second - row_max),
    )


def local_stats(mix_cols, row_segs, own_segs):
    same_doc = (row_segs[:, None] == own_segs[None, :])[None]
    masked = jnp.where(same_doc, mix_cols, NEG)
    row_max = jnp.max(masked, axis=-1)
    row_sum = jnp.sum(jnp.where(same_doc, jnp.exp(masked - row_max[..., None]), 0.0), axis=-1)
    return (row_max, row_sum)


def make_probs(mix_cols, row_segs, own_segs, row_max, row_sum):
    same_doc = (row_segs[:, None] == own_segs[None, :])[None]
    masked = jnp.where(same_doc, mix_cols, NEG)
    raised = jnp.where(same_doc, jnp.exp(masked - row_max[..., None]), 0.0)
    return raised / row_sum[..., None]


def generic_body(tokens, segments, mix, w_value, w_out, w_in, w_back, gain_one, gain_two, out_grad):
    seq_count, col_count, model_width = tokens.shape
    head_count = mix.shape[0]
    head_dim = model_width // head_count
    f32 = jnp.float32
    bf16 = jnp.bfloat16
    gathered = (
        lax.all_gather(w_value, "rows", axis=0, tiled=True),
        lax.all_gather(w_out, "rows", axis=0, tiled=True),
        lax.all_gather(w_in, "rows", axis=1, tiled=True),
        lax.all_gather(w_back, "rows", axis=0, tiled=True),
        lax.all_gather(gain_one, "rows", axis=0, tiled=True),
        lax.all_gather(gain_two, "rows", axis=0, tiled=True),
    )
    wv_full, wo_full, wi_full, wb_full, gain_first, gain_second = gathered
    gain_first = gain_first.astype(f32)
    gain_second = gain_second.astype(f32)
    resid_in = tokens.astype(f32).reshape(seq_count * col_count, model_width)
    normed_one, scale_one, entry_one = normalize(resid_in, gain_first)
    values = jnp.dot(entry_one, wv_full, preferred_element_type=f32).astype(bf16)
    value_heads = values.reshape(seq_count, col_count, head_count, head_dim)
    row_segs = lax.all_gather(segments, "seq", axis=1, tiled=True)
    mix_cols = mix.astype(f32)
    local_max, local_sum = lax.map(
        lambda fields: local_stats(mix_cols, fields[0], fields[1]), (row_segs, segments)
    )
    row_max, row_sum = joined((local_max, local_sum), "seq", combine_stats)
    probs_low = lax.map(
        lambda fields: make_probs(mix_cols, fields[0], fields[1], fields[2], fields[3]).astype(
            bf16
        ),
        (row_segs, segments, row_max, row_sum),
    )
    products = jnp.einsum("shic,schd->ishd", probs_low, value_heads, preferred_element_type=f32)
    mixed = lax.psum_scatter(
        products.reshape(col_count * lax.axis_size("seq"), seq_count, model_width),
        "seq",
        scatter_dimension=0,
        tiled=True,
    )
    mixed = mixed.transpose(1, 0, 2).reshape(seq_count * col_count, model_width)
    mixed_low = mixed.astype(bf16)
    hidden_one = resid_in + jnp.dot(mixed_low, wo_full, preferred_element_type=f32)
    normed_two, scale_two, entry_two = normalize(hidden_one, gain_second)
    pre_act = jnp.dot(entry_two, wi_full, preferred_element_type=f32)
    activ, activ_back = jax.vjp(partial(jax.nn.gelu, approximate=True), pre_act)
    activ_low = activ.astype(bf16)
    branch = jnp.dot(activ_low, wb_full, preferred_element_type=f32)
    result = (hidden_one + branch).astype(bf16).reshape(tokens.shape)
    rms_residual = jnp.sqrt(jnp.mean(hidden_one * hidden_one, axis=-1)).reshape(
        seq_count, col_count
    )
    rms_sublayer = jnp.sqrt(jnp.mean(branch * branch, axis=-1)).reshape(seq_count, col_count)
    wv_back, wo_back, wi_back, wb_back = (
        lax.all_gather(w_value, "rows", axis=0, tiled=True),
        lax.all_gather(w_out, "rows", axis=0, tiled=True),
        lax.all_gather(w_in, "rows", axis=1, tiled=True),
        lax.all_gather(w_back, "rows", axis=0, tiled=True),
    )
    grad_out = out_grad.reshape(seq_count * col_count, model_width)
    grad_back = jnp.dot(activ_low.T, grad_out, preferred_element_type=f32)
    grad_activ = jnp.dot(grad_out, wb_back.T, preferred_element_type=f32)
    grad_pre = activ_back(grad_activ)[0].astype(bf16)
    grad_in = jnp.dot(entry_two.T, grad_pre, preferred_element_type=f32)
    grad_entry_two = jnp.dot(grad_pre, wi_back.T, preferred_element_type=f32)
    back_two, grad_gain_two = norm_back(grad_entry_two, normed_two, scale_two, gain_second)
    grad_hidden = grad_out.astype(f32) + back_two
    grad_hidden_low = grad_hidden.astype(bf16)
    grad_wo = jnp.dot(mixed_low.T, grad_hidden_low, preferred_element_type=f32)
    grad_mixed = jnp.dot(grad_hidden_low, wo_back.T, preferred_element_type=f32).astype(bf16)
    grad_rows = lax.all_gather(
        grad_mixed.reshape(seq_count, col_count, model_width), "seq", axis=1, tiled=True
    )
    grad_heads = grad_rows.reshape(seq_count, -1, head_count, head_dim)

    def delta_part(fields):
        seg_row, seg_own, max_row, sum_row, grad_row, value_row = fields
        soft_probs = make_probs(mix_cols, seg_row, seg_own, max_row, sum_row)
        grad_probs = jnp.einsum("ihd,chd->hic", grad_row, value_row, preferred_element_type=f32)
        return jnp.sum(soft_probs * grad_probs, axis=-1)

    partial_delta = lax.map(
        delta_part, (row_segs, segments, row_max, row_sum, grad_heads, value_heads)
    )
    delta = lax.psum(partial_delta, "seq")

    def seq_back(running, fields):
        seg_row, seg_own, max_row, sum_row, grad_row, value_row, delta_row = fields
        soft_probs = make_probs(mix_cols, seg_row, seg_own, max_row, sum_row)
        grad_probs = jnp.einsum("ihd,chd->hic", grad_row, value_row, preferred_element_type=f32)
        running = running + soft_probs * (grad_probs - delta_row[..., None])
        grad_value_row = jnp.einsum(
            "hic,ihd->chd", soft_probs.astype(bf16), grad_row, preferred_element_type=f32
        )
        return (running, grad_value_row)

    local_mix_grad, grad_values = lax.scan(
        seq_back,
        jnp.zeros(mix_cols.shape, f32),
        (row_segs, segments, row_max, row_sum, grad_heads, value_heads, delta),
    )
    mix_grad = lax.psum(local_mix_grad, "rows")
    grad_values = grad_values.reshape(seq_count * col_count, model_width).astype(bf16)
    grad_wv = jnp.dot(entry_one.T, grad_values, preferred_element_type=f32)
    grad_entry_one = jnp.dot(grad_values, wv_back.T, preferred_element_type=f32)
    back_one, grad_gain_one = norm_back(grad_entry_one, normed_one, scale_one, gain_first)
    tokens_grad = (grad_hidden + back_one).reshape(tokens.shape)
    owned = (
        lax.psum_scatter(grad_wv, "rows", scatter_dimension=0, tiled=True),
        lax.psum_scatter(grad_wo, "rows", scatter_dimension=0, tiled=True),
        lax.psum_scatter(grad_in, "rows", scatter_dimension=1, tiled=True),
        lax.psum_scatter(grad_back, "rows", scatter_dimension=0, tiled=True),
        lax.psum_scatter(grad_gain_one, "rows", scatter_dimension=0, tiled=True),
        lax.psum_scatter(grad_gain_two, "rows", scatter_dimension=0, tiled=True),
    )
    summed = lax.psum((owned[0], owned[1], owned[2], owned[3], owned[4], owned[5]), "seq")
    return (
        result,
        tokens_grad,
        mix_grad,
        summed[0],
        summed[1],
        summed[2],
        summed[3],
        summed[4],
        summed[5],
        rms_residual,
        rms_sublayer,
    )


F32 = jnp.float32
BF16 = jnp.bfloat16
MESH = pl.DeviceIdType.MESH
NT = (((1,), (1,)), ((), ()))
TN = (((0,), (0,)), ((), ()))
ANY = pl.BlockSpec(memory_space=pl.ANY)
RATE = 0.0925
VMEM_LIMIT = 60 * 2**20
ROW_LINK = {1: ("y", 1.0), 2: ("z", 1.0), 4: ("z", 2.0)}
SEQ_LINK = {1: ("core", 0.12), 2: ("x", 1.0), 3: ("x", 1.0)}


class Copy:
    def __init__(self, copy, remote):
        self.copy, self.remote, self.done = copy, remote, False

    def recv(self):
        if not self.done:
            self.done = True
            if self.remote:
                self.copy.wait_recv()
            else:
                self.copy.wait()


class Net:
    def __init__(self, send, recv, local):
        self.send, self.recv, self.local = send, recv, local
        self.remote, self.near = [], []

    def go(self, src, dst, dev):
        i = len(self.remote)
        copy = pltpu.make_async_remote_copy(
            src_ref=src, dst_ref=dst, send_sem=self.send.at[i], recv_sem=self.recv.at[i],
            device_id=dev, device_id_type=MESH)
        copy.start()
        self.remote.append(Copy(copy, True))
        return self.remote[-1]

    def cp(self, src, dst):
        copy = pltpu.make_async_copy(src, dst, self.local.at[len(self.near)])
        copy.start()
        self.near.append(Copy(copy, False))
        return self.near[-1]

    def finish(self):
        for copy in self.near + self.remote:
            copy.recv()
        for copy in self.remote:
            copy.copy.wait_send()


class Plan:
    def __init__(self, net, r, s):
        self.net, self.r, self.s = net, r, s
        self.tasks, self.copies = [], {}

    def comm(self, name, axis, bit, mb, deps, prio, src, dst):
        link, factor = (ROW_LINK if axis == "rows" else SEQ_LINK)[bit]
        dev = {axis: (self.r if axis == "rows" else self.s) ^ bit}

        def emit():
            self.wait(deps)
            self.copies[name] = self.net.go(src(), dst(), dev)

        self.tasks.append((name, link, factor * 2 * mb / RATE, deps, prio, emit))
        return name

    def near(self, name, mb, deps, prio, src, dst):
        def emit():
            self.wait(deps)
            self.copies[name] = self.net.cp(src(), dst())

        self.tasks.append((name, "hbm", mb / 2.0, deps, prio, emit))
        return name

    def work(self, name, us, deps, prio, run):
        def emit():
            self.wait(deps)
            run()

        self.tasks.append((name, "tc", us, deps, prio, emit))
        return name

    def wait(self, deps):
        for dep in deps:
            if dep in self.copies:
                self.copies[dep].recv()

    def solve(self):
        end, start, free, now = {}, {}, {}, 0.0
        left = list(self.tasks)
        while left:
            ready = [
                (max([free.get(t[1], 0.0)] + [end[d] for d in t[3]]), t[4], i)
                for i, t in enumerate(left) if all(d in end for d in t[3])
            ]
            first = min(ready)
            begin, _, pick = min(
                (b, p, i) for b, p, i in ready if b <= first[0] + 1e-9)
            name, link, cost, _, prio, _ = left.pop(pick)
            start[name] = (begin, link == "tc", prio)
            free[link] = begin + cost
            end[name] = begin + cost + (0.0 if link == "tc" else 2.0)
        self.start, self.end = start, end
        return sorted(self.tasks, key=lambda t: start[t[0]])

    def run(self):
        for task in self.solve():
            task[5]()
        self.net.finish()


def greet(r, s):
    barrier = pltpu.get_barrier_semaphore()
    for bit in (1, 2, 4):
        pl.semaphore_signal(barrier, inc=1, device_id={"rows": r ^ bit}, device_id_type=MESH)
    for bit in (1, 2, 3):
        pl.semaphore_signal(barrier, inc=1, device_id={"seq": s ^ bit}, device_id_type=MESH)
    pl.semaphore_wait(barrier, 6)


def cut(ref, start, size):
    return ref.at[pl.ds(pl.multiple_of(start, 16), size)]


def add_gather(plan, name, src, dst, order, ways, prio, mb):
    r, s = plan.r, plan.s
    core, x = s % 2, s // 2
    n = src.shape[0] // ways
    off = {1: 0, 2: core, 4: 2 * core + x}[ways] * n
    far = (2 * core + 1 - x) * n
    part = lambda q, o: cut(src if q == 0 else dst.at[r ^ q], o, n)
    home = lambda q, o: cut(dst.at[r ^ q], o, n)
    got = {0: None}
    for stage, bit in enumerate(order):
        new = {}
        for q, dep in got.items():
            new[q ^ bit] = plan.comm(
                f"{name}{q ^ bit}", "rows", bit, mb / ways, [dep] if dep else [], prio + 0.1 * stage,
                lambda q=q: part(q, off), lambda q=q: home(q, off))
        got.update(new)
    for q, dep in got.items():
        if q == 0 or ways == 1:
            continue
        args = lambda o: (lambda: part(q, o), lambda: home(q, o))
        plan.comm(f"{name}c{q}", "seq", 1, mb / ways, [dep], prio + 1,
                  lambda q=q: part(q, off), lambda q=q: home(q, off))
        if ways == 4:
            plan.comm(f"{name}x{q}", "seq", 2, mb / ways, [dep], prio + 1,
                      lambda q=q: part(q, off), lambda q=q: home(q, off))
            plan.comm(f"{name}f{q}", "seq", 1, mb / ways, [f"{name}x{q}"], prio + 1,
                      lambda q=q: part(q, far), lambda q=q: home(q, far))


def gather_kernel(tok, grd, seg, mix, wv, wo, wi, wb, gn,
                  Xg, Gg, Sg, Mg, wvg, wog, wig, wbg, gng, send, recv, local,
                  b0, b1, b2, b3, b4, b5, b6, b7, b8):
    r, s = lax.axis_index("rows"), lax.axis_index("seq")
    greet(r, s)
    y, zb = r % 2, (r // 2) % 2
    net = Net(send, recv, local)
    plan = Plan(net, r, s)
    for k in (2, 3, 1):
        plan.comm(f"seg{k}", "seq", k, 0.001, [], 0, lambda k=k: seg.at[s ^ k], lambda: Sg.at[s])
        plan.comm(f"tok{k}", "seq", k, 0.393, [], 5, lambda k=k: tok.at[pl.ds(2 * (s ^ k), 2)],
                  lambda: Xg.at[:, pl.ds(s * 128, 128)])
        plan.comm(f"grd{k}", "seq", k, 0.393, [], 50, lambda k=k: grd.at[pl.ds(2 * (s ^ k), 2)],
                  lambda: Gg.at[:, pl.ds(s * 128, 128)])
    quarter = lambda ref, a, b: ref.at[:, pl.ds((2 * a + b) * 128, 128)]
    plan.comm("mixc", "seq", 1, 1.57, [], 3, lambda: mix, lambda: Mg.at[s])
    plan.comm("mixx", "seq", 2, 0.393, [], 1, lambda: quarter(mix, y, zb), lambda: quarter(Mg.at[s], y, zb))
    other = lambda a, b: (lambda: quarter(Mg.at[s ^ 2], a, b))
    for name, axis, bit, dep, prio, a, b in (
            ("mixz", "rows", 2, "mixx", 2, y, zb), ("mixy", "rows", 1, "mixx", 2, y, zb),
            ("mixw", "rows", 1, "mixz", 2, y, 1 - zb), ("mixc0", "seq", 1, "mixx", 3, y, zb),
            ("mixc1", "seq", 1, "mixz", 3, y, 1 - zb), ("mixc2", "seq", 1, "mixy", 3, 1 - y, zb),
            ("mixc3", "seq", 1, "mixw", 3, 1 - y, 1 - zb)):
        plan.comm(name, axis, bit, 0.393, [dep], prio, other(a, b), other(a, b))
    add_gather(plan, "gn", gn, gng, [4, 2, 1], 1, 0, 0.024)
    add_gather(plan, "wv", wv, wvg, [4, 2, 1], 2, 1, 0.147)
    add_gather(plan, "wo", wo, wog, [4, 2, 1], 2, 10, 0.147)
    add_gather(plan, "wi", wi, wig, [4, 2, 1], 4, 20, 0.59)
    add_gather(plan, "wb", wb, wbg, [4, 2, 1], 4, 30, 0.59)
    for i, (src, buf, dst) in enumerate((
            (tok.at[pl.ds(2 * s, 2)], b0, Xg.at[:, pl.ds(s * 128, 128)]), (wv, b1, wvg.at[r]),
            (gn, b2, gng.at[r]), (mix, b3, Mg.at[s]), (wo, b4, wog.at[r]), (wi, b5, wig.at[r]),
            (wb, b6, wbg.at[r]), (grd.at[pl.ds(2 * s, 2)], b7, Gg.at[:, pl.ds(s * 128, 128)]),
            (seg.at[s], b8, Sg.at[s]))):
        plan.near(f"in{i}", 0.5, [], i, lambda src=src: src, lambda buf=buf: buf)
        plan.near(f"out{i}", 0.5, [f"in{i}"], i, lambda buf=buf: buf, lambda dst=dst: dst)
    plan.run()


def gather_all(tok, grd, seg, mix, wv, wo, wi, wb, gn):
    sd = jax.ShapeDtypeStruct
    outs = [sd((2, 512, 768), BF16), sd((2, 512, 768), BF16), sd((4, 2, 128), jnp.int32),
            sd((4, 12, 512, 128), BF16), sd((8, 96, 768), BF16), sd((8, 96, 768), BF16),
            sd((8, 768, 384), BF16), sd((8, 384, 768), BF16), sd((8, 16, 768), BF16)]
    dma = pltpu.SemaphoreType.DMA
    bufs = [pltpu.VMEM(a, BF16) for a in ((2, 128, 768), (96, 768), (16, 768), (12, 512, 128), (96, 768),
                                          (768, 384), (384, 768), (2, 128, 768))]
    return pl.pallas_call(
        gather_kernel, out_shape=outs, in_specs=[ANY] * 9, out_specs=[ANY] * 9,
        scratch_shapes=[dma((128,)), dma((128,)), dma((18,))] + bufs + [pltpu.VMEM((2, 128), jnp.int32)],
        compiler_params=pltpu.CompilerParams(collective_id=0, has_side_effects=True, vmem_limit_bytes=VMEM_LIMIT),
    )(tok, grd, seg, mix, wv, wo, wi, wb, gn)


def exp_mix(m_ref, hh):
    return jnp.concatenate([jnp.exp(m_ref[k, hh].astype(F32)) for k in range(4)], axis=1)


def mix_forward_kernel(m_ref, v_ref, sc_ref, sr_ref, o_ref, iz_ref):
    lane = lax.broadcasted_iota(jnp.int32, (1, 128), 1)
    raised = [exp_mix(m_ref, hh).astype(BF16) for hh in range(2)]
    for q in range(2):
        same = sc_ref[q] == sr_ref[q]
        rhs = jnp.concatenate([v_ref[q], jnp.ones((512, 128), BF16)], axis=1)
        both = [jnp.dot(jnp.where(same, e, jnp.zeros_like(e)), rhs, preferred_element_type=F32) for e in raised]
        total = jnp.where(lane < 64, both[0][:, :128], both[1][:, :128])
        inverse = 1.0 / jnp.where(lane < 64, both[0][:, 128:], both[1][:, 128:])
        o_ref[q] = (total * inverse).astype(BF16)
        iz_ref[q] = inverse


PAIR = pl.BlockSpec((2, 512, 128), lambda p: (0, 0, p))
MIX_PAIR = pl.BlockSpec((4, 2, 512, 128), lambda p: (0, p, 0, 0))
SEG_COL = pl.BlockSpec((2, 512, 1), lambda p: (0, 0, 0))
SEG_ROW = pl.BlockSpec((2, 1, 512), lambda p: (0, 0, 0))


def mix_forward(mix, values, seg_col, seg_row):
    return pl.pallas_call(
        mix_forward_kernel, grid=(6,), in_specs=[MIX_PAIR, PAIR, SEG_COL, SEG_ROW], out_specs=[PAIR, PAIR],
        out_shape=[jax.ShapeDtypeStruct((2, 512, 768), BF16), jax.ShapeDtypeStruct((2, 512, 768), F32)],
        compiler_params=pltpu.CompilerParams(vmem_limit_bytes=VMEM_LIMIT))(mix, values, seg_col, seg_row)


def mix_backward_kernel(m_ref, v_ref, dm_ref, mx_ref, iz_ref, sc_ref, sr_ref, mg_ref, gv_ref):
    lane = lax.broadcasted_iota(jnp.int32, (1, 128), 1)
    raised = [exp_mix(m_ref, hh) for hh in range(2)]
    low = [e.astype(BF16) for e in raised]
    acc = [None, None]
    for q in range(2):
        same = sc_ref[q] == sr_ref[q]
        scaled = dm_ref[q].astype(F32) * iz_ref[q]
        inner = scaled * mx_ref[q].astype(F32)
        grads = []
        for hh in range(2):
            mine = (lane < 64) if hh == 0 else (lane >= 64)
            delta = jnp.sum(jnp.where(mine, inner, 0.0), axis=1, keepdims=True)
            lhs = jnp.where(mine, scaled, 0.0).astype(BF16)
            back = lax.dot_general(lhs, v_ref[q], NT, preferred_element_type=F32)
            term = jnp.where(same, back - delta, 0.0)
            acc[hh] = term if q == 0 else acc[hh] + term
            masked = jnp.where(same, low[hh], jnp.zeros_like(low[hh]))
            grads.append(lax.dot_general(masked, scaled.astype(BF16), TN, preferred_element_type=F32))
        gv_ref[q] = jnp.where(lane < 64, grads[0], grads[1]).astype(BF16)
    for hh in range(2):
        out = (acc[hh] * raised[hh]).astype(BF16)
        for k in range(4):
            mg_ref[k, hh] = out[:, k * 128:(k + 1) * 128]


def mix_backward(mix, values, mixed_grad, mixed, inverse, seg_col, seg_row):
    return pl.pallas_call(
        mix_backward_kernel, grid=(6,), in_specs=[MIX_PAIR, PAIR, PAIR, PAIR, PAIR, SEG_COL, SEG_ROW],
        out_specs=[MIX_PAIR, PAIR],
        out_shape=[jax.ShapeDtypeStruct((4, 12, 512, 128), BF16), jax.ShapeDtypeStruct((2, 512, 768), BF16)],
        compiler_params=pltpu.CompilerParams(vmem_limit_bytes=VMEM_LIMIT),
    )(mix, values, mixed_grad, mixed, inverse, seg_col, seg_row)


def feed_kernel(e_ref, et_ref, g_ref, gt_ref, wi_ref, wb_ref, br_ref, e2_ref, gi_ref, gb_ref, act_s, pg_s):
    k = pl.program_id(0)
    tokens, step = e_ref.shape[0], 512
    pairs, model, cols = wi_ref.shape
    wi = jnp.concatenate([wi_ref[q] for q in range(pairs)], axis=1)
    wb = wb_ref[...].reshape(pairs * cols, model)
    c0, c1 = 0.7978845608028654, 0.044715
    for t in range(tokens // step):
        sl = pl.ds(t * step, step)
        pre = jnp.dot(e_ref[sl, :], wi, preferred_element_type=F32)
        up = lax.dot_general(g_ref[sl, :], wb, NT, preferred_element_type=F32)
        square = pre * pre
        th = jnp.tanh(pre * (c0 + (c0 * c1) * square))
        half = 0.5 + 0.5 * th
        act = (pre * half).astype(BF16)
        slope = half + pre * (1.0 - th * th) * ((0.5 * c0) + (1.5 * c0 * c1) * square)
        pg = (up * slope).astype(BF16)
        act_s[sl, :] = act
        pg_s[sl, :] = pg
        branch = jnp.dot(act, wb, preferred_element_type=F32)
        e2 = lax.dot_general(pg, wi, NT, preferred_element_type=F32)

        @pl.when(k == 0)
        def _():
            br_ref[sl, :] = branch
            e2_ref[sl, :] = e2

        @pl.when(k > 0)
        def _():
            br_ref[sl, :] += branch
            e2_ref[sl, :] += e2

    gi = jnp.dot(et_ref[...], pg_s[...], preferred_element_type=F32).astype(BF16)
    gb = jnp.dot(gt_ref[...], act_s[...], preferred_element_type=F32).astype(BF16)
    for q in range(pairs):
        gi_ref[q] = gi[:, q * cols:(q + 1) * cols]
        gb_ref[q] = gb[:, q * cols:(q + 1) * cols]


def feed(e, et, g, gt, wi, wb):
    n, model, cols = wi.shape
    tokens = e.shape[0]
    whole = lambda a: pl.BlockSpec(a.shape, lambda k: (0,) * a.ndim, pipeline_mode=pl.Buffered(1))
    sd = jax.ShapeDtypeStruct
    acc = pl.BlockSpec((tokens, model), lambda k: (0, 0))
    wide = pl.BlockSpec((2, model, cols), lambda k: (k, 0, 0))
    return pl.pallas_call(
        feed_kernel, grid=(n // 2,),
        in_specs=[whole(e), whole(et), whole(g), whole(gt), wide, pl.BlockSpec((2, cols, model), lambda k: (k, 0, 0))],
        out_specs=[acc, acc, wide, wide],
        out_shape=[sd((tokens, model), F32), sd((tokens, model), F32), sd((n, model, cols), BF16), sd((n, model, cols), BF16)],
        scratch_shapes=[pltpu.VMEM((tokens, 2 * cols), BF16), pltpu.VMEM((tokens, 2 * cols), BF16)],
        compiler_params=pltpu.CompilerParams(vmem_limit_bytes=VMEM_LIMIT),
    )(e, et, g, gt, wi, wb)


def add_reduce(plan, name, src, own, lands, outs, order, prio, mb, axis0):
    r, s = plan.r, plan.s
    core = s % 2
    near, rows, across, final = lands
    n = src.shape[1] // 2
    half = mb / 2
    for q in range(8):
        plan.near(f"{name}l{q}", half, [], prio, lambda q=q: cut(src.at[r ^ q], core * n, n), lambda q=q: own.at[q])
        plan.comm(f"{name}c{q}", "seq", 1, half, [], prio, lambda q=q: cut(src.at[r ^ q], (1 - core) * n, n),
                  lambda q=q: near.at[q])

        def add(q=q):
            own[q] = (own[q].astype(F32) + near[q].astype(F32)).astype(BF16)

        plan.work(f"{name}a{q}", 0.4, [f"{name}l{q}", f"{name}c{q}"], prio, add)
    last = {q: f"{name}a{q}" for q in range(8)}
    keep, slot = list(range(8)), 0
    for stage, bit in enumerate(order):
        for q in [q for q in keep if q & bit]:
            plan.comm(f"{name}r{q}", "rows", bit, half, [last[q]], prio + 0.1 * stage,
                      lambda q=q: own.at[q], lambda slot=slot: rows.at[slot])

            def add(q=q ^ bit, slot=slot):
                own[q] = (own[q].astype(F32) + rows[slot].astype(F32)).astype(BF16)

            last[q ^ bit] = plan.work(f"{name}b{stage}{q}", 0.4, [f"{name}r{q}", last[q ^ bit]], prio, add)
            slot += 1
        keep = [q for q in keep if not q & bit]
    plan.comm(f"{name}x", "seq", 2, half, [last[0]], prio + 0.5, lambda: own.at[0], lambda: across)

    def total():
        final[...] = own[0].astype(F32) + across[...].astype(F32)

    plan.work(f"{name}t", 0.5, [f"{name}x", last[0]], prio, total)
    plan.near(f"{name}o", mb, [f"{name}t"], prio, lambda: final, lambda: cut(outs, core * n, n))
    plan.comm(f"{name}k", "seq", 1, mb, [f"{name}t"], prio, lambda: final, lambda: cut(outs, core * n, n))


def reduce_kernel(res, tgr, gi, gb, go, gv, gn, mg,
                  res_o, tgr_o, gi_o, gb_o, go_o, gv_o, gn_o, mg_o, send, recv, local,
                  ia, ib, ic, idd, ie, ba, bb, bc, bd, be, oa, ob, oc, od, oe, va, vb, vc, vd, ve,
                  n0, n1, m0, m1, m2, m3, m4, t0, t1):
    r, s = lax.axis_index("rows"), lax.axis_index("seq")
    greet(r, s)
    core, x = s % 2, s // 2
    net = Net(send, recv, local)
    plan = Plan(net, r, s)
    for k in (2, 3, 1):
        plan.comm(f"tgr{k}", "seq", k, 0.393, [], 40, lambda k=k: tgr.at[:, pl.ds((s ^ k) * 128, 128)],
                  lambda: tgr_o.at[pl.ds(2 * s, 2)])
        plan.comm(f"res{k}", "seq", k, 0.393, [], 41, lambda k=k: res.at[:, pl.ds((s ^ k) * 128, 128)],
                  lambda: res_o.at[pl.ds(2 * s, 2)])
    for name, src, buf, dst in (("res", res, t0, res_o), ("tgr", tgr, t1, tgr_o)):
        plan.near(f"{name}i", 0.4, [], 9, lambda src=src: src.at[:, pl.ds(s * 128, 128)], lambda buf=buf: buf)
        plan.near(f"{name}o", 0.4, [f"{name}i"], 9, lambda buf=buf: buf, lambda dst=dst: dst.at[pl.ds(2 * s, 2)])
    for h in range(2):
        block = 2 * (x ^ h) + core
        plan.near(f"mgl{h}", 1.57, [], 1 - h, lambda block=block: mg.at[block], lambda h=h: m0.at[h])
        plan.comm(f"mgc{h}", "seq", 1, 1.57, [], 1 - h, lambda h=h: mg.at[2 * (x ^ h) + 1 - core],
                  lambda h=h: m1.at[h])

        def add(h=h):
            for a in range(12):
                m0[h, a] = (m0[h, a].astype(F32) + m1[h, a].astype(F32)).astype(BF16)

        plan.work(f"mga{h}", 1.5, [f"mgl{h}", f"mgc{h}"], 1 - h, add)
    piece = lambda ref, q: ref.at[:, pl.ds((r ^ q) * 64, 64)]
    for q in (1, 3, 5, 7, 2, 6, 4, 0):
        plan.comm(f"mgx{q}", "seq", 2, 0.197, ["mga1"], 1, lambda q=q: piece(m0.at[1], q), lambda q=q: piece(m2, q))

        def add(q=q):
            rows = pl.ds(pl.multiple_of((r ^ q) * 64, 64), 64)
            m0[0, :, rows] = (m0[0, :, rows].astype(F32) + m2[:, rows].astype(F32)).astype(BF16)

        plan.work(f"mgb{q}", 0.3, [f"mgx{q}", "mga0"], 1, add)
    last = {q: f"mgb{q}" for q in range(8)}
    slot, keep = 0, list(range(8))
    for bit in (1, 2, 4):
        for q in [q for q in keep if q & bit]:
            plan.comm(f"mgr{q}", "rows", bit, 0.197, [last[q]], 0, lambda q=q: piece(m0.at[0], q),
                      lambda slot=slot: m3.at[slot])

            def add(q=q ^ bit, slot=slot):
                rows = pl.ds(pl.multiple_of((r ^ q) * 64, 64), 64)
                m0[0, :, rows] = (m0[0, :, rows].astype(F32) + m3[slot].astype(F32)).astype(BF16)

            last[q ^ bit] = plan.work(f"mgd{q}", 0.3, [f"mgr{q}", last[q ^ bit]], 0, add)
            slot += 1
        keep = [q for q in keep if not q & bit]

    def final():
        rows = pl.ds(pl.multiple_of(r * 64, 64), 64)
        m4[:, rows] = m0[0, :, rows]

    done = plan.work("mgf", 0.2, [last[0]], 0, final)
    got = {0: done}
    for bit in (4, 2, 1):
        new = {}
        for q, dep in got.items():
            new[q ^ bit] = plan.comm(f"mgg{q ^ bit}", "rows", bit, 0.197, [dep], 0, lambda q=q: piece(m4, q),
                                     lambda q=q: piece(m4, q))
        got.update(new)
    plan.near("mgo", 1.57, list(got.values()), 0, lambda: m4, lambda: mg_o)
    for name, src, own, lands, out, mb, prio in (
            ("gi", gi, ia, (ba, oa, va, idd), gi_o, 0.59, 10), ("gb", gb, ib, (bb, ob, vb, ie), gb_o, 0.59, 10),
            ("go", go, ic, (bc, oc, vc, vd), go_o, 0.147, 12), ("gv", gv, be, (bd, od, oe, ve), gv_o, 0.147, 12)):
        add_reduce(plan, name, src, own, lands, out, [1, 2, 4], prio, mb, 0)
    plan.near("gnl", 0.02, [], 0, lambda: gn, lambda: n0.at[0])
    last = "gnl"
    for i, (axis, bit) in enumerate((("seq", 1), ("seq", 2), ("rows", 1), ("rows", 2), ("rows", 4))):
        plan.comm(f"gn{i}", axis, bit, 0.024, [last], 0, lambda i=i: n0.at[i], lambda i=i: n1.at[i])

        def add(i=i):
            n0[i + 1] = n0[i] + n1[i]

        last = plan.work(f"gna{i}", 0.1, [f"gn{i}"], 0, add)
    plan.near("gno", 0.02, [last], 0, lambda: n0.at[5], lambda: gn_o)
    plan.run()


def reduce_all(res, tgr, gi, gb, go, gv, gn, mg):
    sd = jax.ShapeDtypeStruct
    outs = [sd((8, 128, 768), BF16), sd((8, 128, 768), BF16), sd((768, 384), F32), sd((768, 384), F32),
            sd((96, 768), F32), sd((96, 768), F32), sd((8, 768), F32), sd((12, 512, 128), BF16)]
    dma = pltpu.SemaphoreType.DMA
    v = lambda *a: pltpu.VMEM(a, BF16)
    f = lambda *a: pltpu.VMEM(a, F32)
    big, small = (384, 384), (48, 768)
    scratch = [v(8, *big), v(8, *big), v(8, *small), f(*big), f(*big),
               v(8, *big), v(8, *big), v(8, *small), v(8, *small), v(8, *small),
               v(7, *big), v(7, *big), v(7, *small), v(7, *small), v(*small),
               v(*big), v(*big), v(*small), f(*small), f(*small),
               f(6, 8, 768), f(5, 8, 768), v(2, 12, 512, 128), v(2, 12, 512, 128), v(12, 512, 128),
               v(7, 12, 64, 128), v(12, 512, 128), v(2, 128, 768), v(2, 128, 768)]
    return pl.pallas_call(
        reduce_kernel, out_shape=outs, in_specs=[ANY] * 8, out_specs=[ANY] * 8,
        scratch_shapes=[dma((128,)), dma((128,)), dma((64,))] + scratch,
        compiler_params=pltpu.CompilerParams(collective_id=1, has_side_effects=True, vmem_limit_bytes=VMEM_LIMIT),
    )(res, tgr, gi, gb, go, gv, gn, mg)


def own_columns(r, gain):
    return lax.dynamic_update_slice(jnp.zeros((1, 768), BF16), gain[None], (0, r * 96))


def fast_body(tokens, segments, mix, w_value, w_out, w_in, w_back, gain_one, gain_two, out_grad):
    r, s = lax.axis_index("rows"), lax.axis_index("seq")
    gains = jnp.concatenate(
        [own_columns(r, gain_one), own_columns(r, gain_two), jnp.zeros((14, 768), BF16)], axis=0)
    x_low, grad_rows, seg_all, mix_all, wv, wo, wi, wb, gains_all = gather_all(
        tokens, out_grad, segments.reshape(4, 2, 128), mix, w_value, w_out, w_in, w_back, gains)
    gain_sum = jnp.sum(gains_all.astype(F32), axis=0)
    gain_first, gain_second = gain_sum[0], gain_sum[1]
    seg_rows = seg_all.transpose(1, 0, 2).reshape(2, 512)
    seg_col, seg_row = seg_rows[:, :, None], seg_rows[:, None, :]
    wv, wo = wv.reshape(768, 768), wo.reshape(768, 768)
    resid_in = x_low.reshape(1024, 768).astype(F32)
    normed_one, scale_one, entry_one = normalize(resid_in, gain_first)
    values = jnp.dot(entry_one, wv, preferred_element_type=F32).astype(BF16).reshape(2, 512, 768)
    mixed, inverse = mix_forward(mix_all, values, seg_col, seg_row)
    mixed_low = mixed.reshape(1024, 768)
    hidden_one = resid_in + jnp.dot(mixed_low, wo, preferred_element_type=F32)
    normed_two, scale_two, entry_two = normalize(hidden_one, gain_second)
    grad_low = grad_rows.reshape(1024, 768)
    branch, grad_entry_two, grad_in, grad_back = feed(entry_two, entry_two.T, grad_low, grad_low.T, wi, wb)
    result = (hidden_one + branch).astype(BF16)
    rms_residual = jnp.sqrt(jnp.mean(hidden_one * hidden_one, axis=-1))
    rms_sublayer = jnp.sqrt(jnp.mean(branch * branch, axis=-1))
    back_two, grad_gain_two = norm_back(grad_entry_two, normed_two, scale_two, gain_second)
    grad_hidden = grad_low.astype(F32) + back_two
    grad_hidden_low = grad_hidden.astype(BF16)
    grad_wo = jnp.dot(mixed_low.T, grad_hidden_low, preferred_element_type=F32).astype(BF16)
    grad_mixed = jnp.dot(grad_hidden_low, wo.T, preferred_element_type=F32).astype(BF16)
    grad_mix, grad_values = mix_backward(
        mix_all, values, grad_mixed.reshape(2, 512, 768), mixed, inverse, seg_col, seg_row)
    grad_values = grad_values.reshape(1024, 768)
    grad_wv = jnp.dot(entry_one.T, grad_values, preferred_element_type=F32).astype(BF16)
    grad_entry_one = jnp.dot(grad_values, wv.T, preferred_element_type=F32)
    back_one, grad_gain_one = norm_back(grad_entry_one, normed_one, scale_one, gain_first)
    tokens_grad = (grad_hidden + back_one).astype(BF16)
    gains_grad = jnp.concatenate([grad_gain_one[None], grad_gain_two[None], jnp.zeros((6, 768), F32)], axis=0)
    res, tgr, gi, gb, go, gv, gn, mg = reduce_all(
        result.reshape(2, 512, 768), tokens_grad.reshape(2, 512, 768), grad_in, grad_back,
        grad_wo.reshape(8, 96, 768), grad_wv.reshape(8, 96, 768), gains_grad, grad_mix)
    own = lax.dynamic_slice(gn, (0, r * 96), (2, 96))
    rms = jnp.stack([rms_residual, rms_sublayer]).reshape(2, 2, 4, 128)
    rms = lax.all_to_all(rms, "seq", 2, 1, tiled=False)
    rms = rms.reshape(2, 8, 128)
    return (res, tgr.astype(F32), mg.astype(F32), gv, go, gi, gb.T, own[0], own[1], rms[0], rms[1])


def solution(mesh):
    in_specs = (
        P("rows", "seq", None),
        P("rows", "seq"),
        P(None, None, "seq"),
        P("rows", None),
        P("rows", None),
        P(None, "rows"),
        P("rows", None),
        P("rows"),
        P("rows"),
        P("rows", "seq", None),
    )
    out_specs = (
        P("rows", "seq", None),
        P("rows", "seq", None),
        P(None, None, "seq"),
        P("rows", None),
        P("rows", None),
        P(None, "rows"),
        P("rows", None),
        P("rows"),
        P("rows"),
        P("rows", "seq"),
        P("rows", "seq"),
    )
    shape = dict(mesh.shape)
    body = fast_body if shape["rows"] == 8 and shape["seq"] == 4 else generic_body
    return jax.shard_map(body, mesh=mesh, in_specs=in_specs, out_specs=out_specs, check_vma=False)
```

```python
import functools
from functools import partial

import jax
import jax.numpy as jnp
from jax import lax
from jax.experimental import pallas as pl
from jax.experimental.pallas import tpu as pltpu
from jax.sharding import PartitionSpec as P

NEG = -1e30
EPS = 1e-06


def joined(part, axis, combine):
    gathered = jax.tree.map(lambda a: lax.all_gather(a, axis), part)

    def take(source):
        return jax.tree.map(lambda a: lax.dynamic_index_in_dim(a, source, 0, False), gathered)

    return lax.fori_loop(
        1, lax.axis_size(axis), lambda source, state: combine(state, take(source)), take(0)
    )


def normalize(inputs, gain):
    scale = lax.rsqrt(jnp.mean(inputs * inputs, axis=-1, keepdims=True) + EPS)
    normed = inputs * scale
    return (normed, scale, (normed * gain).astype(jnp.bfloat16))


def norm_back(upstream, normed, scale, gain):
    scaled = upstream * gain
    back = scale * (scaled - normed * jnp.mean(scaled * normed, axis=-1, keepdims=True))
    return (back, jnp.sum(upstream * normed, axis=0))


def combine_stats(first, second):
    max_first, sum_first = first
    max_second, sum_second = second
    row_max = jnp.maximum(max_first, max_second)
    return (
        row_max,
        sum_first * jnp.exp(max_first - row_max) + sum_second * jnp.exp(max_second - row_max),
    )


def local_stats(mix_cols, row_segs, own_segs):
    same_doc = (row_segs[:, None] == own_segs[None, :])[None]
    masked = jnp.where(same_doc, mix_cols, NEG)
    row_max = jnp.max(masked, axis=-1)
    row_sum = jnp.sum(jnp.where(same_doc, jnp.exp(masked - row_max[..., None]), 0.0), axis=-1)
    return (row_max, row_sum)


def make_probs(mix_cols, row_segs, own_segs, row_max, row_sum):
    same_doc = (row_segs[:, None] == own_segs[None, :])[None]
    masked = jnp.where(same_doc, mix_cols, NEG)
    raised = jnp.where(same_doc, jnp.exp(masked - row_max[..., None]), 0.0)
    return raised / row_sum[..., None]


def generic_body(tokens, segments, mix, w_value, w_out, w_in, w_back, gain_one, gain_two, out_grad):
    seq_count, col_count, model_width = tokens.shape
    head_count = mix.shape[0]
    head_dim = model_width // head_count
    f32 = jnp.float32
    bf16 = jnp.bfloat16
    gathered = (
        lax.all_gather(w_value, "rows", axis=0, tiled=True),
        lax.all_gather(w_out, "rows", axis=0, tiled=True),
        lax.all_gather(w_in, "rows", axis=1, tiled=True),
        lax.all_gather(w_back, "rows", axis=0, tiled=True),
        lax.all_gather(gain_one, "rows", axis=0, tiled=True),
        lax.all_gather(gain_two, "rows", axis=0, tiled=True),
    )
    wv_full, wo_full, wi_full, wb_full, gain_first, gain_second = gathered
    gain_first = gain_first.astype(f32)
    gain_second = gain_second.astype(f32)
    resid_in = tokens.astype(f32).reshape(seq_count * col_count, model_width)
    normed_one, scale_one, entry_one = normalize(resid_in, gain_first)
    values = jnp.dot(entry_one, wv_full, preferred_element_type=f32).astype(bf16)
    value_heads = values.reshape(seq_count, col_count, head_count, head_dim)
    row_segs = lax.all_gather(segments, "seq", axis=1, tiled=True)
    mix_cols = mix.astype(f32)
    local_max, local_sum = lax.map(
        lambda fields: local_stats(mix_cols, fields[0], fields[1]), (row_segs, segments)
    )
    row_max, row_sum = joined((local_max, local_sum), "seq", combine_stats)
    probs_low = lax.map(
        lambda fields: make_probs(mix_cols, fields[0], fields[1], fields[2], fields[3]).astype(
            bf16
        ),
        (row_segs, segments, row_max, row_sum),
    )
    products = jnp.einsum("shic,schd->ishd", probs_low, value_heads, preferred_element_type=f32)
    mixed = lax.psum_scatter(
        products.reshape(col_count * lax.axis_size("seq"), seq_count, model_width),
        "seq",
        scatter_dimension=0,
        tiled=True,
    )
    mixed = mixed.transpose(1, 0, 2).reshape(seq_count * col_count, model_width)
    mixed_low = mixed.astype(bf16)
    hidden_one = resid_in + jnp.dot(mixed_low, wo_full, preferred_element_type=f32)
    normed_two, scale_two, entry_two = normalize(hidden_one, gain_second)
    pre_act = jnp.dot(entry_two, wi_full, preferred_element_type=f32)
    activ, activ_back = jax.vjp(partial(jax.nn.gelu, approximate=True), pre_act)
    activ_low = activ.astype(bf16)
    branch = jnp.dot(activ_low, wb_full, preferred_element_type=f32)
    result = (hidden_one + branch).astype(bf16).reshape(tokens.shape)
    rms_residual = jnp.sqrt(jnp.mean(hidden_one * hidden_one, axis=-1)).reshape(
        seq_count, col_count
    )
    rms_sublayer = jnp.sqrt(jnp.mean(branch * branch, axis=-1)).reshape(seq_count, col_count)
    wv_back, wo_back, wi_back, wb_back = (
        lax.all_gather(w_value, "rows", axis=0, tiled=True),
        lax.all_gather(w_out, "rows", axis=0, tiled=True),
        lax.all_gather(w_in, "rows", axis=1, tiled=True),
        lax.all_gather(w_back, "rows", axis=0, tiled=True),
    )
    grad_out = out_grad.reshape(seq_count * col_count, model_width)
    grad_back = jnp.dot(activ_low.T, grad_out, preferred_element_type=f32)
    grad_activ = jnp.dot(grad_out, wb_back.T, preferred_element_type=f32)
    grad_pre = activ_back(grad_activ)[0].astype(bf16)
    grad_in = jnp.dot(entry_two.T, grad_pre, preferred_element_type=f32)
    grad_entry_two = jnp.dot(grad_pre, wi_back.T, preferred_element_type=f32)
    back_two, grad_gain_two = norm_back(grad_entry_two, normed_two, scale_two, gain_second)
    grad_hidden = grad_out.astype(f32) + back_two
    grad_hidden_low = grad_hidden.astype(bf16)
    grad_wo = jnp.dot(mixed_low.T, grad_hidden_low, preferred_element_type=f32)
    grad_mixed = jnp.dot(grad_hidden_low, wo_back.T, preferred_element_type=f32).astype(bf16)
    grad_rows = lax.all_gather(
        grad_mixed.reshape(seq_count, col_count, model_width), "seq", axis=1, tiled=True
    )
    grad_heads = grad_rows.reshape(seq_count, -1, head_count, head_dim)

    def delta_part(fields):
        seg_row, seg_own, max_row, sum_row, grad_row, value_row = fields
        soft_probs = make_probs(mix_cols, seg_row, seg_own, max_row, sum_row)
        grad_probs = jnp.einsum("ihd,chd->hic", grad_row, value_row, preferred_element_type=f32)
        return jnp.sum(soft_probs * grad_probs, axis=-1)

    partial_delta = lax.map(
        delta_part, (row_segs, segments, row_max, row_sum, grad_heads, value_heads)
    )
    delta = lax.psum(partial_delta, "seq")

    def seq_back(running, fields):
        seg_row, seg_own, max_row, sum_row, grad_row, value_row, delta_row = fields
        soft_probs = make_probs(mix_cols, seg_row, seg_own, max_row, sum_row)
        grad_probs = jnp.einsum("ihd,chd->hic", grad_row, value_row, preferred_element_type=f32)
        running = running + soft_probs * (grad_probs - delta_row[..., None])
        grad_value_row = jnp.einsum(
            "hic,ihd->chd", soft_probs.astype(bf16), grad_row, preferred_element_type=f32
        )
        return (running, grad_value_row)

    local_mix_grad, grad_values = lax.scan(
        seq_back,
        jnp.zeros(mix_cols.shape, f32),
        (row_segs, segments, row_max, row_sum, grad_heads, value_heads, delta),
    )
    mix_grad = lax.psum(local_mix_grad, "rows")
    grad_values = grad_values.reshape(seq_count * col_count, model_width).astype(bf16)
    grad_wv = jnp.dot(entry_one.T, grad_values, preferred_element_type=f32)
    grad_entry_one = jnp.dot(grad_values, wv_back.T, preferred_element_type=f32)
    back_one, grad_gain_one = norm_back(grad_entry_one, normed_one, scale_one, gain_first)
    tokens_grad = (grad_hidden + back_one).reshape(tokens.shape)
    owned = (
        lax.psum_scatter(grad_wv, "rows", scatter_dimension=0, tiled=True),
        lax.psum_scatter(grad_wo, "rows", scatter_dimension=0, tiled=True),
        lax.psum_scatter(grad_in, "rows", scatter_dimension=1, tiled=True),
        lax.psum_scatter(grad_back, "rows", scatter_dimension=0, tiled=True),
        lax.psum_scatter(grad_gain_one, "rows", scatter_dimension=0, tiled=True),
        lax.psum_scatter(grad_gain_two, "rows", scatter_dimension=0, tiled=True),
    )
    summed = lax.psum((owned[0], owned[1], owned[2], owned[3], owned[4], owned[5]), "seq")
    return (
        result,
        tokens_grad,
        mix_grad,
        summed[0],
        summed[1],
        summed[2],
        summed[3],
        summed[4],
        summed[5],
        rms_residual,
        rms_sublayer,
    )


F32 = jnp.float32
BF16 = jnp.bfloat16
MESH = pl.DeviceIdType.MESH
NT = (((1,), (1,)), ((), ()))
TN = (((0,), (0,)), ((), ()))
ANY = pl.BlockSpec(memory_space=pl.ANY)
RATE = 0.0925
VMEM_LIMIT = 60 * 2**20
ROW_LINK = {1: ("y", 1.0), 2: ("z", 1.0), 4: ("z", 2.0)}
SEQ_LINK = {1: ("core", 0.12), 2: ("x", 1.0), 3: ("x", 1.0)}


class Copy:
    def __init__(self, copy, remote):
        self.copy, self.remote, self.done = copy, remote, False

    def recv(self):
        if not self.done:
            self.done = True
            if self.remote:
                self.copy.wait_recv()
            else:
                self.copy.wait()


class Net:
    def __init__(self, send, recv, local):
        self.send, self.recv, self.local = send, recv, local
        self.remote, self.near = [], []

    def go(self, src, dst, dev):
        i = len(self.remote)
        copy = pltpu.make_async_remote_copy(
            src_ref=src, dst_ref=dst, send_sem=self.send.at[i], recv_sem=self.recv.at[i],
            device_id=dev, device_id_type=MESH)
        copy.start()
        self.remote.append(Copy(copy, True))
        return self.remote[-1]

    def cp(self, src, dst):
        copy = pltpu.make_async_copy(src, dst, self.local.at[len(self.near)])
        copy.start()
        self.near.append(Copy(copy, False))
        return self.near[-1]

    def finish(self):
        for copy in self.near + self.remote:
            copy.recv()
        for copy in self.remote:
            copy.copy.wait_send()


class Plan:
    def __init__(self, net, r, s):
        self.net, self.r, self.s = net, r, s
        self.tasks, self.copies = [], {}

    def comm(self, name, axis, bit, mb, deps, prio, src, dst):
        link, factor = (ROW_LINK if axis == "rows" else SEQ_LINK)[bit]
        dev = {axis: (self.r if axis == "rows" else self.s) ^ bit}

        def emit():
            self.wait(deps)
            self.copies[name] = self.net.go(src(), dst(), dev)

        self.tasks.append((name, link, factor * 2 * mb / RATE, deps, prio, emit))
        return name

    def near(self, name, mb, deps, prio, src, dst):
        def emit():
            self.wait(deps)
            self.copies[name] = self.net.cp(src(), dst())

        self.tasks.append((name, "hbm", mb / 2.0, deps, prio, emit))
        return name

    def work(self, name, us, deps, prio, run):
        def emit():
            self.wait(deps)
            run()

        self.tasks.append((name, "tc", us, deps, prio, emit))
        return name

    def wait(self, deps):
        for dep in deps:
            if dep in self.copies:
                self.copies[dep].recv()

    def solve(self):
        end, start, free, now = {}, {}, {}, 0.0
        left = list(self.tasks)
        while left:
            ready = [
                (max([free.get(t[1], 0.0)] + [end[d] for d in t[3]]), t[4], i)
                for i, t in enumerate(left) if all(d in end for d in t[3])
            ]
            first = min(ready)
            begin, _, pick = min(
                (b, p, i) for b, p, i in ready if b <= first[0] + 1e-9)
            name, link, cost, _, prio, _ = left.pop(pick)
            start[name] = (begin, link == "tc", prio)
            free[link] = begin + cost
            end[name] = begin + cost + (0.0 if link == "tc" else 2.0)
        self.start, self.end = start, end
        return sorted(self.tasks, key=lambda t: start[t[0]])

    def run(self):
        for task in self.solve():
            task[5]()
        self.net.finish()


def greet(r, s):
    barrier = pltpu.get_barrier_semaphore()
    for bit in (1, 2, 4):
        pl.semaphore_signal(barrier, inc=1, device_id={"rows": r ^ bit}, device_id_type=MESH)
    for bit in (1, 2, 3):
        pl.semaphore_signal(barrier, inc=1, device_id={"seq": s ^ bit}, device_id_type=MESH)
    pl.semaphore_wait(barrier, 6)


def cut(ref, start, size):
    return ref.at[pl.ds(pl.multiple_of(start, 16), size)]


def add_gather(plan, name, src, dst, order, ways, prio, mb):
    r, s = plan.r, plan.s
    core, x = s % 2, s // 2
    n = src.shape[0] // ways
    off = {1: 0, 2: core, 4: 2 * core + x}[ways] * n
    far = (2 * core + 1 - x) * n
    part = lambda q, o: cut(src if q == 0 else dst.at[r ^ q], o, n)
    home = lambda q, o: cut(dst.at[r ^ q], o, n)
    got = {0: None}
    for stage, bit in enumerate(order):
        new = {}
        for q, dep in got.items():
            new[q ^ bit] = plan.comm(
                f"{name}{q ^ bit}", "rows", bit, mb / ways, [dep] if dep else [], prio + 0.1 * stage,
                lambda q=q: part(q, off), lambda q=q: home(q, off))
        got.update(new)
    need = {q: [dep or f"{name}0"] for q, dep in got.items()}
    for q, dep in got.items():
        if q == 0 or ways == 1:
            continue
        need[q].append(plan.comm(f"{name}c{q}", "seq", 1, mb / ways, [dep], prio + 1,
                                 lambda q=q: part(q, off), lambda q=q: home(q, off)))
        if ways == 4:
            need[q].append(plan.comm(f"{name}x{q}", "seq", 2, mb / ways, [dep], prio + 1,
                                     lambda q=q: part(q, off), lambda q=q: home(q, off)))
            need[q].append(plan.comm(f"{name}f{q}", "seq", 1, mb / ways, [f"{name}x{q}"], prio + 1,
                                     lambda q=q: part(q, far), lambda q=q: home(q, far)))
    return need


def column(row):
    return jnp.broadcast_to(row, (128, 128)).T[:, :1]


def as_row(col):
    return jnp.broadcast_to(col, (128, 128)).T[:1]


def segment_layouts(seg, col, row):
    for q in range(2):
        for k in range(4):
            ids = seg[k, q:q + 1].astype(F32)
            row[q, :, k * 128:(k + 1) * 128] = ids
            col[q, k * 128:(k + 1) * 128] = column(ids)


def gain_row(gains, i):
    total = gains[0, i:i + 1].astype(F32)
    for k in range(1, 8):
        total = total + gains[k, i:i + 1].astype(F32)
    return total


def forward_kernel(tok, grd, seg, mix, wv, wo, wi, wb, gn,
                   x_o, g_o, seg_o, m_o, wv_o, wo_o, gn_o, val_o, mxd_o, iz_o, h_o, e2_o, res_o, rms_o, gi_o, gb_o,
                   send, recv, local,
                   x_v, g_v, seg_v, m_v, wv_v, wo_v, wi_v, wb_v, gn_v, val_v, mxd_v, h_v, e_v, et_v, gt_v,
                   br_v, e2_v, act_v, pg_v, gi_v, gb_v, rms_v, sc_v, sr_v):
    r, s = lax.axis_index("rows"), lax.axis_index("seq")
    greet(r, s)
    y, zb = r % 2, (r // 2) % 2
    net = Net(send, recv, local)
    plan = Plan(net, r, s)
    block = lambda k: pl.ds(pl.multiple_of((s ^ k) * 128, 128), 128)
    for k in (2, 3, 1):
        plan.comm(f"seg{k}", "seq", k, 0.001, [], 0, lambda k=k: seg.at[s ^ k], lambda: seg_v.at[s])
        plan.comm(f"tok{k}", "seq", k, 0.393, [], 5, lambda k=k: tok.at[pl.ds(2 * (s ^ k), 2)],
                  lambda: x_v.at[:, block(0)])
        plan.comm(f"grd{k}", "seq", k, 0.393, [], 15, lambda k=k: grd.at[pl.ds(2 * (s ^ k), 2)],
                  lambda: g_v.at[:, block(0)])
    quarter = lambda ref, a, b: ref.at[:, pl.ds((2 * a + b) * 128, 128)]
    plan.comm("mixc", "seq", 1, 1.57, [], 3, lambda: mix, lambda: m_v.at[s])
    plan.comm("mixx", "seq", 2, 0.393, [], 1, lambda: quarter(mix, y, zb), lambda: quarter(m_v.at[s], y, zb))
    other = lambda a, b: (lambda: quarter(m_v.at[s ^ 2], a, b))
    for name, axis, bit, dep, prio, a, b in (
            ("mixz", "rows", 2, "mixx", 2, y, zb), ("mixy", "rows", 1, "mixx", 2, y, zb),
            ("mixw", "rows", 1, "mixz", 2, y, 1 - zb), ("mixc0", "seq", 1, "mixx", 3, y, zb),
            ("mixc1", "seq", 1, "mixz", 3, y, 1 - zb), ("mixc2", "seq", 1, "mixy", 3, 1 - y, zb),
            ("mixc3", "seq", 1, "mixw", 3, 1 - y, 1 - zb)):
        plan.comm(name, axis, bit, 0.393, [dep], prio, other(a, b), other(a, b))
    flat = lambda got, *qs: [d for q in qs for d in got[q]]
    every = range(8)
    gn_d = add_gather(plan, "gn", gn, gn_v, [4, 2, 1], 1, 0, 0.024)
    wv_d = add_gather(plan, "wv", wv, wv_v, [4, 2, 1], 2, 1, 0.147)
    wo_d = add_gather(plan, "wo", wo, wo_v, [4, 2, 1], 2, 10, 0.147)
    wi_d = add_gather(plan, "wi", wi, wi_v, [4, 2, 1], 4, 20, 0.59)
    wb_d = add_gather(plan, "wb", wb, wb_v, [4, 2, 1], 2, 21, 0.59)
    for name, mb, src, dst in (
            ("tok0", 0.4, lambda: tok.at[pl.ds(2 * s, 2)], lambda: x_v.at[:, block(0)]),
            ("gn0", 0.02, lambda: gn, lambda: gn_v.at[r]), ("wv0", 0.15, lambda: wv, lambda: wv_v.at[r]),
            ("seg0", 0.01, lambda: seg.at[s], lambda: seg_v.at[s]), ("mix0", 1.5, lambda: mix, lambda: m_v.at[s]),
            ("wo0", 0.15, lambda: wo, lambda: wo_v.at[r]), ("wi0", 0.6, lambda: wi, lambda: wi_v.at[r]),
            ("wb0", 0.6, lambda: wb, lambda: wb_v.at[r]),
            ("grd0", 0.4, lambda: grd.at[pl.ds(2 * s, 2)], lambda: g_v.at[:, block(0)])):
        plan.near(name, mb, [], 0, src, dst)

    def put(name, mb, deps, src, dst):
        plan.near(name, mb, deps, 90, lambda: src, lambda: dst)

    for k in range(4):
        def values(k=k):
            x = x_v[:, block(k)].reshape(256, 768).astype(F32)
            scale = lax.rsqrt(jnp.mean(x * x, axis=-1, keepdims=True) + EPS)
            entry = (x * scale * gain_row(gn_v, 0)).astype(BF16)
            out = jnp.dot(entry, wv_v[...].reshape(768, 768), preferred_element_type=F32)
            val_v[:, block(k)] = out.astype(BF16).reshape(2, 128, 768)

        plan.work(f"val{k}", 1.2, [f"tok{k}"] + flat(wv_d, *every) + flat(gn_d, *every), 1, values)
    plan.work("segs", 1.0, [f"seg{k}" for k in range(4)], 0, lambda: segment_layouts(seg_v, sc_v, sr_v))
    for k in range(4):
        def turn(k=k):
            for q in range(2):
                at = pl.ds(pl.multiple_of(q * 512 + (s ^ k) * 128, 128), 128)
                gt_v[:, at] = g_v[q, block(k)].T

        plan.work(f"gt{k}", 0.6, [f"grd{k}"], 9, turn)
    lane = lax.broadcasted_iota(jnp.int32, (1, 128), 1)
    last = ["segs"] + [f"val{k}" for k in range(4)]
    mixes = ["mix0", "mixc", "mixx", "mixz", "mixy", "mixw", "mixc0", "mixc1", "mixc2", "mixc3"]
    groups = 3
    for g in range(groups):
        def mixing(g=g):
            @pl.loop(g * (6 // groups), (g + 1) * (6 // groups))
            def _(p):
                lanes = pl.ds(pl.multiple_of(p * 128, 128), 128)
                raised = [exp_mix(m_v, 2 * p + hh).astype(BF16) for hh in range(2)]
                for q in range(2):
                    same = sc_v[q] == sr_v[q]
                    rhs = jnp.concatenate([val_v[q, :, lanes], jnp.ones((512, 128), BF16)], axis=1)
                    both = [jnp.dot(jnp.where(same, e, jnp.zeros_like(e)), rhs, preferred_element_type=F32)
                            for e in raised]
                    total = jnp.where(lane < 64, both[0][:, :128], both[1][:, :128])
                    inverse = 1.0 / jnp.where(lane < 64, both[0][:, 128:], both[1][:, 128:])
                    mxd_v[q, :, lanes] = (total * inverse).astype(BF16)
                    br_v[q * 512:(q + 1) * 512, lanes] = inverse

        last = [plan.work(f"mf{g}", 10.0 / groups, last + mixes, 1, mixing)]
    put("iz_out", 1.5, last, br_v, iz_o)
    for q in range(2):
        def project(q=q):
            @pl.loop(0, 4)
            def _(k):
                inside = pl.ds(pl.multiple_of(k * 128, 128), 128)
                at = pl.ds(pl.multiple_of(q * 512 + k * 128, 128), 128)
                h = x_v[q, inside].astype(F32) + jnp.dot(
                    mxd_v[q, inside], wo_v[...].reshape(768, 768), preferred_element_type=F32)
                square = jnp.mean(h * h, axis=-1, keepdims=True)
                h_v[at] = h
                entry = (h * lax.rsqrt(square + EPS) * gain_row(gn_v, 1)).astype(BF16)
                e_v[at] = entry
                et_v[:, at] = entry.T
                rms_v[k, q:q + 1] = as_row(jnp.sqrt(square))

        last = [plan.work(f"out{q}", 2.5, last + flat(wo_d, *every), 1, project)]
    put("h_out", 1.5, last, h_v, h_o)
    c0, c1 = 0.7978845608028654, 0.044715
    step = 256
    for i, (a, b) in enumerate(((0, 4), (1, 5), (2, 6), (3, 7))):
        for half in range(2):
            def feed(a=a, b=b, i=i, half=half):
                weights = jnp.concatenate([wi_v[r ^ a], wi_v[r ^ b]], axis=1)
                back = jnp.concatenate([wb_v[r ^ a], wb_v[r ^ b]], axis=0)

                @pl.loop(2 * half, 2 * half + 2)
                def _(t):
                    at = pl.ds(pl.multiple_of(t * step, step), step)
                    inner = pl.ds(pl.multiple_of((t % 2) * step, step), step)
                    pre = jnp.dot(e_v[at], weights, preferred_element_type=F32)
                    up = lax.dot_general(g_v[half, inner], back, NT, preferred_element_type=F32)
                    square = pre * pre
                    th = jnp.tanh(pre * (c0 + (c0 * c1) * square))
                    gate = 0.5 + 0.5 * th
                    act = (pre * gate).astype(BF16)
                    slope = gate + pre * (1.0 - th * th) * ((0.5 * c0) + (1.5 * c0 * c1) * square)
                    pg = (up * slope).astype(BF16)
                    act_v[at] = act
                    pg_v[at] = pg
                    branch = jnp.dot(act, back, preferred_element_type=F32)
                    e2 = lax.dot_general(pg, weights, NT, preferred_element_type=F32)
                    if i == 0:
                        br_v[at] = branch
                        e2_v[at] = e2
                    else:
                        br_v[at] += branch
                        e2_v[at] += e2

            need = flat(wi_d, a, b) + flat(wb_d, a, b) + [f"grd{k}" for k in range(4)] + ["iz_out"]
            last = [plan.work(f"ff{i}{half}", 3.5, last + need, 1, feed)]

        def weight_grads(i=i):
            slot = i % 2

            @pl.loop(0, 3)
            def _(t):
                at = pl.ds(pl.multiple_of(t * 256, 256), 256)
                gi = jnp.dot(et_v[at], pg_v[...], preferred_element_type=F32).astype(BF16)
                gb = jnp.dot(gt_v[at], act_v[...], preferred_element_type=F32).astype(BF16)
                for q in range(2):
                    gi_v[slot, q, at] = gi[:, q * 384:(q + 1) * 384]
                    gb_v[slot, q, at] = gb[:, q * 384:(q + 1) * 384]

        free = [f"g{n}_out{i - 2}{q}" for n in "ib" for q in range(2)] if i >= 2 else []
        last = [plan.work(f"fg{i}", 3.5, last + free + [f"gt{k}" for k in range(4)], 1, weight_grads)]
        for q, owner in enumerate((a, b)):
            put(f"gi_out{i}{q}", 0.3, last, gi_v.at[i % 2, q], gi_o.at[r ^ owner])
            put(f"gb_out{i}{q}", 0.3, last, gb_v.at[i % 2, q], gb_o.at[r ^ owner])

    def finish():
        @pl.loop(0, 8)
        def _(t):
            at = pl.ds(pl.multiple_of(t * 128, 128), 128)
            q, k = t // 4, t % 4
            branch = br_v[at]
            e_v[at] = (h_v[at] + branch).astype(BF16)
            rms_v[k, pl.ds(2 + q, 1)] = as_row(jnp.sqrt(jnp.mean(branch * branch, axis=-1, keepdims=True)))

    last = [plan.work("fin", 2.0, last, 1, finish)]
    put("e2_out", 1.5, last, e2_v, e2_o)
    put("res_out", 0.8, last, e_v, res_o)
    put("rms_out", 0.1, last, rms_v, rms_o)
    toks, grds = [f"tok{k}" for k in range(4)], [f"grd{k}" for k in range(4)]
    put("x_out", 0.8, toks, x_v, x_o)
    put("g_out", 0.8, grds, g_v, g_o)
    put("seg_out", 0.1, ["segs"], seg_v, seg_o)
    put("m_out", 3.0, mixes, m_v, m_o)
    put("wv_out", 0.6, flat(wv_d, *every), wv_v, wv_o)
    put("wo_out", 0.6, flat(wo_d, *every), wo_v, wo_o)
    put("gn_out", 0.1, flat(gn_d, *every), gn_v, gn_o)
    put("val_out", 0.8, [f"val{k}" for k in range(4)], val_v, val_o)
    put("mxd_out", 0.8, [f"mf{groups - 1}"], mxd_v, mxd_o)
    plan.run()


def forward_all(tok, grd, seg, mix, wv, wo, wi, wb, gn):
    sd = jax.ShapeDtypeStruct
    rows, flat, big = (2, 512, 768), (1024, 768), (8, 768, 384)
    mixes, square, gains = (4, 12, 512, 128), (8, 96, 768), (8, 16, 768)
    outs = [sd(rows, BF16), sd(rows, BF16), sd((4, 2, 128), jnp.int32), sd(mixes, BF16), sd(square, BF16),
            sd(square, BF16), sd(gains, BF16), sd(rows, BF16), sd(rows, BF16), sd(flat, F32), sd(flat, F32),
            sd(flat, F32), sd(flat, BF16), sd((4, 8, 128), F32), sd(big, BF16), sd(big, BF16)]
    dma = pltpu.SemaphoreType.DMA
    v = lambda *a: pltpu.VMEM(a, BF16)
    f = lambda *a: pltpu.VMEM(a, F32)
    turned = (768, 1024)
    scratch = [v(*rows), v(*rows), pltpu.VMEM((4, 2, 128), jnp.int32), v(*mixes), v(*square), v(*square), v(*big),
               v(8, 384, 768), v(*gains), v(*rows), v(*rows), f(*flat), v(*flat), v(*turned), v(*turned),
               f(*flat), f(*flat), v(*flat), v(*flat), v(2, 2, 768, 384), v(2, 2, 768, 384), f(4, 8, 128),
               f(2, 512, 1), f(2, 1, 512)]
    return pl.pallas_call(
        forward_kernel, out_shape=outs, in_specs=[ANY] * 9, out_specs=[ANY] * len(outs),
        scratch_shapes=[dma((128,)), dma((128,)), dma((48,))] + scratch,
        compiler_params=pltpu.CompilerParams(collective_id=0, has_side_effects=True, vmem_limit_bytes=VMEM_LIMIT),
    )(tok, grd, seg, mix, wv, wo, wi, wb, gn)


def exp_mix(m_ref, hh):
    return jnp.concatenate([jnp.exp(m_ref[k, hh].astype(F32)) for k in range(4)], axis=1)


PAIR = pl.BlockSpec((2, 512, 128), lambda p: (0, 0, p))
MIX_PAIR = pl.BlockSpec((4, 2, 512, 128), lambda p: (0, p, 0, 0))
SEG_COL = pl.BlockSpec((2, 512, 1), lambda p: (0, 0, 0))
SEG_ROW = pl.BlockSpec((2, 1, 512), lambda p: (0, 0, 0))


def mix_backward_kernel(m_ref, v_ref, dm_ref, mx_ref, iz_ref, sc_ref, sr_ref, mg_ref, gv_ref):
    lane = lax.broadcasted_iota(jnp.int32, (1, 128), 1)
    raised = [exp_mix(m_ref, hh) for hh in range(2)]
    low = [e.astype(BF16) for e in raised]
    acc = [None, None]
    for q in range(2):
        same = sc_ref[q] == sr_ref[q]
        scaled = dm_ref[q].astype(F32) * iz_ref[q]
        inner = scaled * mx_ref[q].astype(F32)
        grads = []
        for hh in range(2):
            mine = (lane < 64) if hh == 0 else (lane >= 64)
            delta = jnp.sum(jnp.where(mine, inner, 0.0), axis=1, keepdims=True)
            lhs = jnp.where(mine, scaled, 0.0).astype(BF16)
            back = lax.dot_general(lhs, v_ref[q], NT, preferred_element_type=F32)
            term = jnp.where(same, back - delta, 0.0)
            acc[hh] = term if q == 0 else acc[hh] + term
            masked = jnp.where(same, low[hh], jnp.zeros_like(low[hh]))
            grads.append(lax.dot_general(masked, scaled.astype(BF16), TN, preferred_element_type=F32))
        gv_ref[q] = jnp.where(lane < 64, grads[0], grads[1]).astype(BF16)
    for hh in range(2):
        out = (acc[hh] * raised[hh]).astype(BF16)
        for k in range(4):
            mg_ref[k, hh] = out[:, k * 128:(k + 1) * 128]


def mix_backward(mix, values, mixed_grad, mixed, inverse, seg_col, seg_row):
    return pl.pallas_call(
        mix_backward_kernel, grid=(6,), in_specs=[MIX_PAIR, PAIR, PAIR, PAIR, PAIR, SEG_COL, SEG_ROW],
        out_specs=[MIX_PAIR, PAIR],
        out_shape=[jax.ShapeDtypeStruct((4, 12, 512, 128), BF16), jax.ShapeDtypeStruct((2, 512, 768), BF16)],
        compiler_params=pltpu.CompilerParams(vmem_limit_bytes=VMEM_LIMIT),
    )(mix, values, mixed_grad, mixed, inverse, seg_col, seg_row)


def add_reduce(plan, name, src, own, lands, outs, order, prio, mb, axis0):
    r, s = plan.r, plan.s
    core = s % 2
    near, rows, across, final = lands
    n = src.shape[1] // 2
    half = mb / 2
    for q in range(8):
        plan.near(f"{name}l{q}", half, [], prio, lambda q=q: cut(src.at[r ^ q], core * n, n), lambda q=q: own.at[q])
        plan.comm(f"{name}c{q}", "seq", 1, half, [], prio, lambda q=q: cut(src.at[r ^ q], (1 - core) * n, n),
                  lambda q=q: near.at[q])

        def add(q=q):
            own[q] = (own[q].astype(F32) + near[q].astype(F32)).astype(BF16)

        plan.work(f"{name}a{q}", 0.4, [f"{name}l{q}", f"{name}c{q}"], prio, add)
    last = {q: f"{name}a{q}" for q in range(8)}
    keep, slot = list(range(8)), 0
    for stage, bit in enumerate(order):
        for q in [q for q in keep if q & bit]:
            plan.comm(f"{name}r{q}", "rows", bit, half, [last[q]], prio + 0.1 * stage,
                      lambda q=q: own.at[q], lambda slot=slot: rows.at[slot])

            def add(q=q ^ bit, slot=slot):
                own[q] = (own[q].astype(F32) + rows[slot].astype(F32)).astype(BF16)

            last[q ^ bit] = plan.work(f"{name}b{stage}{q}", 0.4, [f"{name}r{q}", last[q ^ bit]], prio, add)
            slot += 1
        keep = [q for q in keep if not q & bit]
    plan.comm(f"{name}x", "seq", 2, half, [last[0]], prio + 0.5, lambda: own.at[0], lambda: across)

    def total():
        final[...] = own[0].astype(F32) + across[...].astype(F32)

    plan.work(f"{name}t", 0.5, [f"{name}x", last[0]], prio, total)
    plan.near(f"{name}o", mb, [f"{name}t"], prio, lambda: final, lambda: cut(outs, core * n, n))
    plan.comm(f"{name}k", "seq", 1, mb, [f"{name}t"], prio, lambda: final, lambda: cut(outs, core * n, n))


def reduce_kernel(res, tgr, gi, gb, go, gv, gn, mg,
                  res_o, tgr_o, gi_o, gb_o, go_o, gv_o, gn_o, mg_o, send, recv, local,
                  ia, ib, ic, idd, ie, ba, bb, bc, bd, be, oa, ob, oc, od, oe, va, vb, vc, vd, ve,
                  n0, n1, m0, m1, m2, m3, m4, t0, t1):
    r, s = lax.axis_index("rows"), lax.axis_index("seq")
    greet(r, s)
    core, x = s % 2, s // 2
    net = Net(send, recv, local)
    plan = Plan(net, r, s)
    for k in (2, 3, 1):
        plan.comm(f"tgr{k}", "seq", k, 0.393, [], 40, lambda k=k: tgr.at[:, pl.ds((s ^ k) * 128, 128)],
                  lambda: tgr_o.at[pl.ds(2 * s, 2)])
        plan.comm(f"res{k}", "seq", k, 0.393, [], 41, lambda k=k: res.at[:, pl.ds((s ^ k) * 128, 128)],
                  lambda: res_o.at[pl.ds(2 * s, 2)])
    for name, src, buf, dst in (("res", res, t0, res_o), ("tgr", tgr, t1, tgr_o)):
        plan.near(f"{name}i", 0.4, [], 9, lambda src=src: src.at[:, pl.ds(s * 128, 128)], lambda buf=buf: buf)
        plan.near(f"{name}o", 0.4, [f"{name}i"], 9, lambda buf=buf: buf, lambda dst=dst: dst.at[pl.ds(2 * s, 2)])
    for h in range(2):
        block = 2 * (x ^ h) + core
        plan.near(f"mgl{h}", 1.57, [], 1 - h, lambda block=block: mg.at[block], lambda h=h: m0.at[h])
        plan.comm(f"mgc{h}", "seq", 1, 1.57, [], 1 - h, lambda h=h: mg.at[2 * (x ^ h) + 1 - core],
                  lambda h=h: m1.at[h])

        def add(h=h):
            for a in range(12):
                m0[h, a] = (m0[h, a].astype(F32) + m1[h, a].astype(F32)).astype(BF16)

        plan.work(f"mga{h}", 1.5, [f"mgl{h}", f"mgc{h}"], 1 - h, add)
    piece = lambda ref, q: ref.at[:, pl.ds((r ^ q) * 64, 64)]
    for q in (1, 3, 5, 7, 2, 6, 4, 0):
        plan.comm(f"mgx{q}", "seq", 2, 0.197, ["mga1"], 1, lambda q=q: piece(m0.at[1], q), lambda q=q: piece(m2, q))

        def add(q=q):
            rows = pl.ds(pl.multiple_of((r ^ q) * 64, 64), 64)
            m0[0, :, rows] = (m0[0, :, rows].astype(F32) + m2[:, rows].astype(F32)).astype(BF16)

        plan.work(f"mgb{q}", 0.3, [f"mgx{q}", "mga0"], 1, add)
    last = {q: f"mgb{q}" for q in range(8)}
    slot, keep = 0, list(range(8))
    for bit in (1, 2, 4):
        for q in [q for q in keep if q & bit]:
            plan.comm(f"mgr{q}", "rows", bit, 0.197, [last[q]], 0, lambda q=q: piece(m0.at[0], q),
                      lambda slot=slot: m3.at[slot])

            def add(q=q ^ bit, slot=slot):
                rows = pl.ds(pl.multiple_of((r ^ q) * 64, 64), 64)
                m0[0, :, rows] = (m0[0, :, rows].astype(F32) + m3[slot].astype(F32)).astype(BF16)

            last[q ^ bit] = plan.work(f"mgd{q}", 0.3, [f"mgr{q}", last[q ^ bit]], 0, add)
            slot += 1
        keep = [q for q in keep if not q & bit]

    def final():
        rows = pl.ds(pl.multiple_of(r * 64, 64), 64)
        m4[:, rows] = m0[0, :, rows]

    done = plan.work("mgf", 0.2, [last[0]], 0, final)
    got = {0: done}
    for bit in (4, 2, 1):
        new = {}
        for q, dep in got.items():
            new[q ^ bit] = plan.comm(f"mgg{q ^ bit}", "rows", bit, 0.197, [dep], 0, lambda q=q: piece(m4, q),
                                     lambda q=q: piece(m4, q))
        got.update(new)
    plan.near("mgo", 1.57, list(got.values()), 0, lambda: m4, lambda: mg_o)
    for name, src, own, lands, out, mb, prio in (
            ("gi", gi, ia, (ba, oa, va, idd), gi_o, 0.59, 10), ("gb", gb, ib, (bb, ob, vb, ie), gb_o, 0.59, 10),
            ("go", go, ic, (bc, oc, vc, vd), go_o, 0.147, 12), ("gv", gv, be, (bd, od, oe, ve), gv_o, 0.147, 12)):
        add_reduce(plan, name, src, own, lands, out, [1, 2, 4], prio, mb, 0)
    plan.near("gnl", 0.02, [], 0, lambda: gn, lambda: n0.at[0])
    last = "gnl"
    for i, (axis, bit) in enumerate((("seq", 1), ("seq", 2), ("rows", 1), ("rows", 2), ("rows", 4))):
        plan.comm(f"gn{i}", axis, bit, 0.024, [last], 0, lambda i=i: n0.at[i], lambda i=i: n1.at[i])

        def add(i=i):
            n0[i + 1] = n0[i] + n1[i]

        last = plan.work(f"gna{i}", 0.1, [f"gn{i}"], 0, add)
    plan.near("gno", 0.02, [last], 0, lambda: n0.at[5], lambda: gn_o)
    plan.run()


def reduce_all(res, tgr, gi, gb, go, gv, gn, mg):
    sd = jax.ShapeDtypeStruct
    outs = [sd((8, 128, 768), BF16), sd((8, 128, 768), BF16), sd((768, 384), F32), sd((768, 384), F32),
            sd((96, 768), F32), sd((96, 768), F32), sd((8, 768), F32), sd((12, 512, 128), BF16)]
    dma = pltpu.SemaphoreType.DMA
    v = lambda *a: pltpu.VMEM(a, BF16)
    f = lambda *a: pltpu.VMEM(a, F32)
    big, small = (384, 384), (48, 768)
    scratch = [v(8, *big), v(8, *big), v(8, *small), f(*big), f(*big),
               v(8, *big), v(8, *big), v(8, *small), v(8, *small), v(8, *small),
               v(7, *big), v(7, *big), v(7, *small), v(7, *small), v(*small),
               v(*big), v(*big), v(*small), f(*small), f(*small),
               f(6, 8, 768), f(5, 8, 768), v(2, 12, 512, 128), v(2, 12, 512, 128), v(12, 512, 128),
               v(7, 12, 64, 128), v(12, 512, 128), v(2, 128, 768), v(2, 128, 768)]
    return pl.pallas_call(
        reduce_kernel, out_shape=outs, in_specs=[ANY] * 8, out_specs=[ANY] * 8,
        scratch_shapes=[dma((128,)), dma((128,)), dma((64,))] + scratch,
        compiler_params=pltpu.CompilerParams(collective_id=1, has_side_effects=True, vmem_limit_bytes=VMEM_LIMIT),
    )(res, tgr, gi, gb, go, gv, gn, mg)


def own_columns(r, gain):
    return lax.dynamic_update_slice(jnp.zeros((1, 768), BF16), gain[None], (0, r * 96))


def fast_body(tokens, segments, mix, w_value, w_out, w_in, w_back, gain_one, gain_two, out_grad):
    r, s = lax.axis_index("rows"), lax.axis_index("seq")
    gains = jnp.concatenate(
        [own_columns(r, gain_one), own_columns(r, gain_two), jnp.zeros((14, 768), BF16)], axis=0)
    (x_rows, grad_rows, seg_all, mix_all, wv, wo, gains_all, values, mixed, inverse, hidden_one, grad_entry_two,
     result, rms, grad_in, grad_back) = forward_all(
        tokens, out_grad, segments.reshape(4, 2, 128), mix, w_value, w_out, w_in, w_back, gains)
    gain_sum = jnp.sum(gains_all.astype(F32), axis=0)
    gain_first, gain_second = gain_sum[0], gain_sum[1]
    seg_rows = seg_all.transpose(1, 0, 2).reshape(2, 512)
    seg_col, seg_row = seg_rows[:, :, None], seg_rows[:, None, :]
    wv, wo = wv.reshape(768, 768), wo.reshape(768, 768)
    resid_in = x_rows.reshape(1024, 768).astype(F32)
    normed_one, scale_one, entry_one = normalize(resid_in, gain_first)
    mixed_low = mixed.reshape(1024, 768)
    normed_two, scale_two, _ = normalize(hidden_one, gain_second)
    grad_low = grad_rows.reshape(1024, 768)
    back_two, grad_gain_two = norm_back(grad_entry_two, normed_two, scale_two, gain_second)
    grad_hidden = grad_low.astype(F32) + back_two
    grad_hidden_low = grad_hidden.astype(BF16)
    grad_wo = jnp.dot(mixed_low.T, grad_hidden_low, preferred_element_type=F32).astype(BF16)
    grad_mixed = jnp.dot(grad_hidden_low, wo.T, preferred_element_type=F32).astype(BF16)
    grad_mix, grad_values = mix_backward(
        mix_all, values, grad_mixed.reshape(2, 512, 768), mixed, inverse.reshape(2, 512, 768), seg_col, seg_row)
    grad_values = grad_values.reshape(1024, 768)
    grad_wv = jnp.dot(entry_one.T, grad_values, preferred_element_type=F32).astype(BF16)
    grad_entry_one = jnp.dot(grad_values, wv.T, preferred_element_type=F32)
    back_one, grad_gain_one = norm_back(grad_entry_one, normed_one, scale_one, gain_first)
    tokens_grad = (grad_hidden + back_one).astype(BF16)
    gains_grad = jnp.concatenate([grad_gain_one[None], grad_gain_two[None], jnp.zeros((6, 768), F32)], axis=0)
    res, tgr, gi, gb, go, gv, gn, mg = reduce_all(
        result.reshape(2, 512, 768), tokens_grad.reshape(2, 512, 768), grad_in, grad_back,
        grad_wo.reshape(8, 96, 768), grad_wv.reshape(8, 96, 768), gains_grad, grad_mix)
    own = lax.dynamic_slice(gn, (0, r * 96), (2, 96))
    rms = lax.all_to_all(rms, "seq", 0, 0, tiled=False)[:, :4].reshape(4, 2, 2, 128)
    rms = rms.transpose(1, 0, 2, 3).reshape(2, 8, 128)
    return (res, tgr.astype(F32), mg.astype(F32), gv, go, gi, gb.T, own[0], own[1], rms[0], rms[1])


def solution(mesh):
    in_specs = (
        P("rows", "seq", None),
        P("rows", "seq"),
        P(None, None, "seq"),
        P("rows", None),
        P("rows", None),
        P(None, "rows"),
        P("rows", None),
        P("rows"),
        P("rows"),
        P("rows", "seq", None),
    )
    out_specs = (
        P("rows", "seq", None),
        P("rows", "seq", None),
        P(None, None, "seq"),
        P("rows", None),
        P("rows", None),
        P(None, "rows"),
        P("rows", None),
        P("rows"),
        P("rows"),
        P("rows", "seq"),
        P("rows", "seq"),
    )
    shape = dict(mesh.shape)
    body = fast_body if shape["rows"] == 8 and shape["seq"] == 4 else generic_body
    return jax.shard_map(body, mesh=mesh, in_specs=in_specs, out_specs=out_specs, check_vma=False)
```

```python
import functools
from functools import partial

import jax
import jax.numpy as jnp
from jax import lax
from jax.experimental import pallas as pl
from jax.experimental.pallas import tpu as pltpu
from jax.sharding import PartitionSpec as P

NEG = -1e30
EPS = 1e-06


def joined(part, axis, combine):
    gathered = jax.tree.map(lambda a: lax.all_gather(a, axis), part)

    def take(source):
        return jax.tree.map(lambda a: lax.dynamic_index_in_dim(a, source, 0, False), gathered)

    return lax.fori_loop(
        1, lax.axis_size(axis), lambda source, state: combine(state, take(source)), take(0)
    )


def normalize(inputs, gain):
    scale = lax.rsqrt(jnp.mean(inputs * inputs, axis=-1, keepdims=True) + EPS)
    normed = inputs * scale
    return (normed, scale, (normed * gain).astype(jnp.bfloat16))


def norm_back(upstream, normed, scale, gain):
    scaled = upstream * gain
    back = scale * (scaled - normed * jnp.mean(scaled * normed, axis=-1, keepdims=True))
    return (back, jnp.sum(upstream * normed, axis=0))


def combine_stats(first, second):
    max_first, sum_first = first
    max_second, sum_second = second
    row_max = jnp.maximum(max_first, max_second)
    return (
        row_max,
        sum_first * jnp.exp(max_first - row_max) + sum_second * jnp.exp(max_second - row_max),
    )


def local_stats(mix_cols, row_segs, own_segs):
    same_doc = (row_segs[:, None] == own_segs[None, :])[None]
    masked = jnp.where(same_doc, mix_cols, NEG)
    row_max = jnp.max(masked, axis=-1)
    row_sum = jnp.sum(jnp.where(same_doc, jnp.exp(masked - row_max[..., None]), 0.0), axis=-1)
    return (row_max, row_sum)


def make_probs(mix_cols, row_segs, own_segs, row_max, row_sum):
    same_doc = (row_segs[:, None] == own_segs[None, :])[None]
    masked = jnp.where(same_doc, mix_cols, NEG)
    raised = jnp.where(same_doc, jnp.exp(masked - row_max[..., None]), 0.0)
    return raised / row_sum[..., None]


def generic_body(tokens, segments, mix, w_value, w_out, w_in, w_back, gain_one, gain_two, out_grad):
    seq_count, col_count, model_width = tokens.shape
    head_count = mix.shape[0]
    head_dim = model_width // head_count
    f32 = jnp.float32
    bf16 = jnp.bfloat16
    gathered = (
        lax.all_gather(w_value, "rows", axis=0, tiled=True),
        lax.all_gather(w_out, "rows", axis=0, tiled=True),
        lax.all_gather(w_in, "rows", axis=1, tiled=True),
        lax.all_gather(w_back, "rows", axis=0, tiled=True),
        lax.all_gather(gain_one, "rows", axis=0, tiled=True),
        lax.all_gather(gain_two, "rows", axis=0, tiled=True),
    )
    wv_full, wo_full, wi_full, wb_full, gain_first, gain_second = gathered
    gain_first = gain_first.astype(f32)
    gain_second = gain_second.astype(f32)
    resid_in = tokens.astype(f32).reshape(seq_count * col_count, model_width)
    normed_one, scale_one, entry_one = normalize(resid_in, gain_first)
    values = jnp.dot(entry_one, wv_full, preferred_element_type=f32).astype(bf16)
    value_heads = values.reshape(seq_count, col_count, head_count, head_dim)
    row_segs = lax.all_gather(segments, "seq", axis=1, tiled=True)
    mix_cols = mix.astype(f32)
    local_max, local_sum = lax.map(
        lambda fields: local_stats(mix_cols, fields[0], fields[1]), (row_segs, segments)
    )
    row_max, row_sum = joined((local_max, local_sum), "seq", combine_stats)
    probs_low = lax.map(
        lambda fields: make_probs(mix_cols, fields[0], fields[1], fields[2], fields[3]).astype(
            bf16
        ),
        (row_segs, segments, row_max, row_sum),
    )
    products = jnp.einsum("shic,schd->ishd", probs_low, value_heads, preferred_element_type=f32)
    mixed = lax.psum_scatter(
        products.reshape(col_count * lax.axis_size("seq"), seq_count, model_width),
        "seq",
        scatter_dimension=0,
        tiled=True,
    )
    mixed = mixed.transpose(1, 0, 2).reshape(seq_count * col_count, model_width)
    mixed_low = mixed.astype(bf16)
    hidden_one = resid_in + jnp.dot(mixed_low, wo_full, preferred_element_type=f32)
    normed_two, scale_two, entry_two = normalize(hidden_one, gain_second)
    pre_act = jnp.dot(entry_two, wi_full, preferred_element_type=f32)
    activ, activ_back = jax.vjp(partial(jax.nn.gelu, approximate=True), pre_act)
    activ_low = activ.astype(bf16)
    branch = jnp.dot(activ_low, wb_full, preferred_element_type=f32)
    result = (hidden_one + branch).astype(bf16).reshape(tokens.shape)
    rms_residual = jnp.sqrt(jnp.mean(hidden_one * hidden_one, axis=-1)).reshape(
        seq_count, col_count
    )
    rms_sublayer = jnp.sqrt(jnp.mean(branch * branch, axis=-1)).reshape(seq_count, col_count)
    wv_back, wo_back, wi_back, wb_back = (
        lax.all_gather(w_value, "rows", axis=0, tiled=True),
        lax.all_gather(w_out, "rows", axis=0, tiled=True),
        lax.all_gather(w_in, "rows", axis=1, tiled=True),
        lax.all_gather(w_back, "rows", axis=0, tiled=True),
    )
    grad_out = out_grad.reshape(seq_count * col_count, model_width)
    grad_back = jnp.dot(activ_low.T, grad_out, preferred_element_type=f32)
    grad_activ = jnp.dot(grad_out, wb_back.T, preferred_element_type=f32)
    grad_pre = activ_back(grad_activ)[0].astype(bf16)
    grad_in = jnp.dot(entry_two.T, grad_pre, preferred_element_type=f32)
    grad_entry_two = jnp.dot(grad_pre, wi_back.T, preferred_element_type=f32)
    back_two, grad_gain_two = norm_back(grad_entry_two, normed_two, scale_two, gain_second)
    grad_hidden = grad_out.astype(f32) + back_two
    grad_hidden_low = grad_hidden.astype(bf16)
    grad_wo = jnp.dot(mixed_low.T, grad_hidden_low, preferred_element_type=f32)
    grad_mixed = jnp.dot(grad_hidden_low, wo_back.T, preferred_element_type=f32).astype(bf16)
    grad_rows = lax.all_gather(
        grad_mixed.reshape(seq_count, col_count, model_width), "seq", axis=1, tiled=True
    )
    grad_heads = grad_rows.reshape(seq_count, -1, head_count, head_dim)

    def delta_part(fields):
        seg_row, seg_own, max_row, sum_row, grad_row, value_row = fields
        soft_probs = make_probs(mix_cols, seg_row, seg_own, max_row, sum_row)
        grad_probs = jnp.einsum("ihd,chd->hic", grad_row, value_row, preferred_element_type=f32)
        return jnp.sum(soft_probs * grad_probs, axis=-1)

    partial_delta = lax.map(
        delta_part, (row_segs, segments, row_max, row_sum, grad_heads, value_heads)
    )
    delta = lax.psum(partial_delta, "seq")

    def seq_back(running, fields):
        seg_row, seg_own, max_row, sum_row, grad_row, value_row, delta_row = fields
        soft_probs = make_probs(mix_cols, seg_row, seg_own, max_row, sum_row)
        grad_probs = jnp.einsum("ihd,chd->hic", grad_row, value_row, preferred_element_type=f32)
        running = running + soft_probs * (grad_probs - delta_row[..., None])
        grad_value_row = jnp.einsum(
            "hic,ihd->chd", soft_probs.astype(bf16), grad_row, preferred_element_type=f32
        )
        return (running, grad_value_row)

    local_mix_grad, grad_values = lax.scan(
        seq_back,
        jnp.zeros(mix_cols.shape, f32),
        (row_segs, segments, row_max, row_sum, grad_heads, value_heads, delta),
    )
    mix_grad = lax.psum(local_mix_grad, "rows")
    grad_values = grad_values.reshape(seq_count * col_count, model_width).astype(bf16)
    grad_wv = jnp.dot(entry_one.T, grad_values, preferred_element_type=f32)
    grad_entry_one = jnp.dot(grad_values, wv_back.T, preferred_element_type=f32)
    back_one, grad_gain_one = norm_back(grad_entry_one, normed_one, scale_one, gain_first)
    tokens_grad = (grad_hidden + back_one).reshape(tokens.shape)
    owned = (
        lax.psum_scatter(grad_wv, "rows", scatter_dimension=0, tiled=True),
        lax.psum_scatter(grad_wo, "rows", scatter_dimension=0, tiled=True),
        lax.psum_scatter(grad_in, "rows", scatter_dimension=1, tiled=True),
        lax.psum_scatter(grad_back, "rows", scatter_dimension=0, tiled=True),
        lax.psum_scatter(grad_gain_one, "rows", scatter_dimension=0, tiled=True),
        lax.psum_scatter(grad_gain_two, "rows", scatter_dimension=0, tiled=True),
    )
    summed = lax.psum((owned[0], owned[1], owned[2], owned[3], owned[4], owned[5]), "seq")
    return (
        result,
        tokens_grad,
        mix_grad,
        summed[0],
        summed[1],
        summed[2],
        summed[3],
        summed[4],
        summed[5],
        rms_residual,
        rms_sublayer,
    )


F32 = jnp.float32
BF16 = jnp.bfloat16
MESH = pl.DeviceIdType.MESH
NT = (((1,), (1,)), ((), ()))
TN = (((0,), (0,)), ((), ()))
ANY = pl.BlockSpec(memory_space=pl.ANY)
RATE = 0.0925
VMEM_LIMIT = 60 * 2**20
ROW_LINK = {1: ("y", 1.0), 2: ("z", 1.0), 4: ("z", 2.0)}
SEQ_LINK = {1: ("core", 0.12), 2: ("x", 1.0), 3: ("x", 1.0)}


class Copy:
    def __init__(self, copy, remote):
        self.copy, self.remote, self.done = copy, remote, False

    def recv(self):
        if not self.done:
            self.done = True
            if self.remote:
                self.copy.wait_recv()
            else:
                self.copy.wait()


class Net:
    def __init__(self, send, recv, local):
        self.send, self.recv, self.local = send, recv, local
        self.remote, self.near = [], []

    def go(self, src, dst, dev):
        i = len(self.remote)
        copy = pltpu.make_async_remote_copy(
            src_ref=src, dst_ref=dst, send_sem=self.send.at[i], recv_sem=self.recv.at[i],
            device_id=dev, device_id_type=MESH)
        copy.start()
        self.remote.append(Copy(copy, True))
        return self.remote[-1]

    def cp(self, src, dst):
        copy = pltpu.make_async_copy(src, dst, self.local.at[len(self.near)])
        copy.start()
        self.near.append(Copy(copy, False))
        return self.near[-1]

    def finish(self):
        for copy in self.near + self.remote:
            copy.recv()
        for copy in self.remote:
            copy.copy.wait_send()


class Plan:
    def __init__(self, net, r, s):
        self.net, self.r, self.s = net, r, s
        self.tasks, self.copies = [], {}

    def comm(self, name, axis, bit, mb, deps, prio, src, dst):
        link, factor = (ROW_LINK if axis == "rows" else SEQ_LINK)[bit]
        dev = {axis: (self.r if axis == "rows" else self.s) ^ bit}

        def emit():
            self.wait(deps)
            self.copies[name] = self.net.go(src(), dst(), dev)

        self.tasks.append((name, link, factor * 2 * mb / RATE, deps, prio, emit))
        return name

    def near(self, name, mb, deps, prio, src, dst):
        def emit():
            self.wait(deps)
            self.copies[name] = self.net.cp(src(), dst())

        self.tasks.append((name, "hbm", mb / 2.0, deps, prio, emit))
        return name

    def work(self, name, us, deps, prio, run):
        def emit():
            self.wait(deps)
            run()

        self.tasks.append((name, "tc", us, deps, prio, emit))
        return name

    def add(self, name, deps, to, other, us=0.12):
        def run():
            target, term = to(), other()
            target[...] = target[...] + term[...]

        return self.work(name, us, deps, -5, run)

    def wait(self, deps):
        for dep in deps:
            if dep in self.copies:
                self.copies[dep].recv()

    def solve(self):
        end, start, free, now = {}, {}, {}, 0.0
        left = list(self.tasks)
        while left:
            ready = [
                (max([free.get(t[1], 0.0)] + [end[d] for d in t[3]]), t[4], i)
                for i, t in enumerate(left) if all(d in end for d in t[3])
            ]
            first = min(ready)
            begin, _, pick = min(
                (b, p, i) for b, p, i in ready if b <= first[0] + 1e-9)
            name, link, cost, _, prio, _ = left.pop(pick)
            start[name] = (begin, link == "tc", prio)
            free[link] = begin + cost
            end[name] = begin + cost + (0.0 if link == "tc" else 2.0)
        self.start, self.end = start, end
        return sorted(self.tasks, key=lambda t: start[t[0]])

    def run(self):
        for task in self.solve():
            task[5]()
        self.net.finish()


def greet(r, s):
    barrier = pltpu.get_barrier_semaphore()
    for bit in (1, 2, 4):
        pl.semaphore_signal(barrier, inc=1, device_id={"rows": r ^ bit}, device_id_type=MESH)
    for bit in (1, 2, 3):
        pl.semaphore_signal(barrier, inc=1, device_id={"seq": s ^ bit}, device_id_type=MESH)
    pl.semaphore_wait(barrier, 6)


def cut(ref, start, size):
    return ref.at[pl.ds(pl.multiple_of(start, 16), size)]


def add_gather(plan, name, src, dst, order, ways, prio, mb):
    r, s = plan.r, plan.s
    core, x = s % 2, s // 2
    n = src.shape[0] // ways
    off = {1: 0, 2: core, 4: 2 * core + x}[ways] * n
    far = (2 * core + 1 - x) * n
    part = lambda q, o: cut(src if q == 0 else dst.at[r ^ q], o, n)
    home = lambda q, o: cut(dst.at[r ^ q], o, n)
    got = {0: None}
    for stage, bit in enumerate(order):
        new = {}
        for q, dep in got.items():
            new[q ^ bit] = plan.comm(
                f"{name}{q ^ bit}", "rows", bit, mb / ways, [dep] if dep else [], prio + 0.1 * stage,
                lambda q=q: part(q, off), lambda q=q: home(q, off))
        got.update(new)
    need = {q: [dep or f"{name}0"] for q, dep in got.items()}
    for q, dep in got.items():
        if q == 0 or ways == 1:
            continue
        need[q].append(plan.comm(f"{name}c{q}", "seq", 1, mb / ways, [dep], prio + 1,
                                 lambda q=q: part(q, off), lambda q=q: home(q, off)))
        if ways == 4:
            need[q].append(plan.comm(f"{name}x{q}", "seq", 2, mb / ways, [dep], prio + 1,
                                     lambda q=q: part(q, off), lambda q=q: home(q, off)))
            need[q].append(plan.comm(f"{name}f{q}", "seq", 1, mb / ways, [f"{name}x{q}"], prio + 1,
                                     lambda q=q: part(q, far), lambda q=q: home(q, far)))
    return need


HALVES = 1


def column(row):
    return jnp.broadcast_to(row, (128, 128)).T[:, :1]


def as_row(col):
    return jnp.broadcast_to(col, (128, 128)).T[:1]


def segment_layouts(seg, col, row):
    for q in range(2):
        for k in range(4):
            ids = seg[k, q:q + 1].astype(F32)
            row[q, :, k * 128:(k + 1) * 128] = ids
            col[q, k * 128:(k + 1) * 128] = column(ids)


def gain_row(gains, i):
    total = gains[0, i:i + 1].astype(F32)
    for k in range(1, 8):
        total = total + gains[k, i:i + 1].astype(F32)
    return total


def forward_kernel(tok, grd, seg, mix, wv, wo, wi, wb, gn,
                   x_o, g_o, seg_o, m_o, wv_o, wo_o, gn_o, val_o, mxd_o, iz_o, h_o, e2_o, res_o, rms_o, gi_o, gb_o,
                   send, recv, local,
                   x_v, g_v, seg_v, m_v, wv_v, wo_v, wi_v, wb_v, gn_v, val_v, mxd_v, h_v, e_v, et_v, gt_v,
                   br_v, e2_v, act_v, pg_v, gi_v, gb_v, rms_v, sc_v, sr_v):
    r, s = lax.axis_index("rows"), lax.axis_index("seq")
    greet(r, s)
    y, zb = r % 2, (r // 2) % 2
    net = Net(send, recv, local)
    plan = Plan(net, r, s)
    block = lambda k: pl.ds(pl.multiple_of((s ^ k) * 128, 128), 128)
    for k in (2, 3, 1):
        plan.comm(f"seg{k}", "seq", k, 0.001, [], 0, lambda k=k: seg.at[s ^ k], lambda: seg_v.at[s])
        plan.comm(f"tok{k}", "seq", k, 0.393, [], 5, lambda k=k: tok.at[pl.ds(2 * (s ^ k), 2)],
                  lambda: x_v.at[:, block(0)])
        plan.comm(f"grd{k}", "seq", k, 0.393, [], 15, lambda k=k: grd.at[pl.ds(2 * (s ^ k), 2)],
                  lambda: g_v.at[:, block(0)])
    quarter = lambda ref, a, b: ref.at[:, pl.ds((2 * a + b) * 128, 128)]
    plan.comm("mixc", "seq", 1, 1.57, [], 3, lambda: mix, lambda: m_v.at[s])
    plan.comm("mixx", "seq", 2, 0.393, [], 1, lambda: quarter(mix, y, zb), lambda: quarter(m_v.at[s], y, zb))
    other = lambda a, b: (lambda: quarter(m_v.at[s ^ 2], a, b))
    for name, axis, bit, dep, prio, a, b in (
            ("mixz", "rows", 2, "mixx", 2, y, zb), ("mixy", "rows", 1, "mixx", 2, y, zb),
            ("mixw", "rows", 1, "mixz", 2, y, 1 - zb), ("mixc0", "seq", 1, "mixx", 3, y, zb),
            ("mixc1", "seq", 1, "mixz", 3, y, 1 - zb), ("mixc2", "seq", 1, "mixy", 3, 1 - y, zb),
            ("mixc3", "seq", 1, "mixw", 3, 1 - y, 1 - zb)):
        plan.comm(name, axis, bit, 0.393, [dep], prio, other(a, b), other(a, b))
    flat = lambda got, *qs: [d for q in qs for d in got[q]]
    every = range(8)
    gn_d = add_gather(plan, "gn", gn, gn_v, [4, 2, 1], 1, 0, 0.024)
    wv_d = add_gather(plan, "wv", wv, wv_v, [4, 2, 1], 2, 1, 0.147)
    wo_d = add_gather(plan, "wo", wo, wo_v, [4, 2, 1], 2, 10, 0.147)
    wi_d = add_gather(plan, "wi", wi, wi_v, [4, 2, 1], 4, 20, 0.59)
    wb_d = add_gather(plan, "wb", wb, wb_v, [4, 2, 1], 2, 21, 0.59)
    for name, mb, src, dst in (
            ("tok0", 0.4, lambda: tok.at[pl.ds(2 * s, 2)], lambda: x_v.at[:, block(0)]),
            ("gn0", 0.02, lambda: gn, lambda: gn_v.at[r]), ("wv0", 0.15, lambda: wv, lambda: wv_v.at[r]),
            ("seg0", 0.01, lambda: seg.at[s], lambda: seg_v.at[s]), ("mix0", 1.5, lambda: mix, lambda: m_v.at[s]),
            ("wo0", 0.15, lambda: wo, lambda: wo_v.at[r]), ("wi0", 0.6, lambda: wi, lambda: wi_v.at[r]),
            ("wb0", 0.6, lambda: wb, lambda: wb_v.at[r]),
            ("grd0", 0.4, lambda: grd.at[pl.ds(2 * s, 2)], lambda: g_v.at[:, block(0)])):
        plan.near(name, mb, [], 0, src, dst)

    def put(name, mb, deps, src, dst):
        plan.near(name, mb, deps, 90, lambda: src, lambda: dst)

    for k in range(4):
        def values(k=k):
            x = x_v[:, block(k)].reshape(256, 768).astype(F32)
            scale = lax.rsqrt(jnp.mean(x * x, axis=-1, keepdims=True) + EPS)
            entry = (x * scale * gain_row(gn_v, 0)).astype(BF16)
            out = jnp.dot(entry, wv_v[...].reshape(768, 768), preferred_element_type=F32)
            val_v[:, block(k)] = out.astype(BF16).reshape(2, 128, 768)

        plan.work(f"val{k}", 1.2, [f"tok{k}"] + flat(wv_d, *every) + flat(gn_d, *every), 1, values)
    plan.work("segs", 1.0, [f"seg{k}" for k in range(4)], 0, lambda: segment_layouts(seg_v, sc_v, sr_v))
    for k in range(4):
        def turn(k=k):
            for q in range(2):
                at = pl.ds(pl.multiple_of(q * 512 + (s ^ k) * 128, 128), 128)
                gt_v[:, at] = g_v[q, block(k)].T

        plan.work(f"gt{k}", 0.6, [f"grd{k}"], 9, turn)
    lane = lax.broadcasted_iota(jnp.int32, (1, 128), 1)
    last = ["segs"] + [f"val{k}" for k in range(4)]
    mixes = ["mix0", "mixc", "mixx", "mixz", "mixy", "mixw", "mixc0", "mixc1", "mixc2", "mixc3"]
    groups = 3
    for g in range(groups):
        def mixing(g=g):
            @pl.loop(g * (6 // groups), (g + 1) * (6 // groups))
            def _(p):
                lanes = pl.ds(pl.multiple_of(p * 128, 128), 128)
                raised = [exp_mix(m_v, 2 * p + hh).astype(BF16) for hh in range(2)]
                for q in range(2):
                    same = sc_v[q] == sr_v[q]
                    rhs = jnp.concatenate([val_v[q, :, lanes], jnp.ones((512, 128), BF16)], axis=1)
                    both = [jnp.dot(jnp.where(same, e, jnp.zeros_like(e)), rhs, preferred_element_type=F32)
                            for e in raised]
                    total = jnp.where(lane < 64, both[0][:, :128], both[1][:, :128])
                    inverse = 1.0 / jnp.where(lane < 64, both[0][:, 128:], both[1][:, 128:])
                    mxd_v[q, :, lanes] = (total * inverse).astype(BF16)
                    br_v[q * 512:(q + 1) * 512, lanes] = inverse

        last = [plan.work(f"mf{g}", 10.0 / groups, last + mixes, 1, mixing)]
    put("iz_out", 1.5, last, br_v, iz_o)
    for q in range(2):
        def project(q=q):
            @pl.loop(0, 4)
            def _(k):
                inside = pl.ds(pl.multiple_of(k * 128, 128), 128)
                at = pl.ds(pl.multiple_of(q * 512 + k * 128, 128), 128)
                h = x_v[q, inside].astype(F32) + jnp.dot(
                    mxd_v[q, inside], wo_v[...].reshape(768, 768), preferred_element_type=F32)
                square = jnp.mean(h * h, axis=-1, keepdims=True)
                h_v[at] = h
                entry = (h * lax.rsqrt(square + EPS) * gain_row(gn_v, 1)).astype(BF16)
                e_v[at] = entry
                et_v[:, at] = entry.T
                rms_v[k, q:q + 1] = as_row(jnp.sqrt(square))

        last = [plan.work(f"out{q}", 2.5, last + flat(wo_d, *every), 1, project)]
    put("h_out", 1.5, last, h_v, h_o)
    c0, c1 = 0.7978845608028654, 0.044715
    step = 256
    for i, (a, b) in enumerate(((0, 4), (1, 5), (2, 6), (3, 7))):
        for half in range(HALVES):
            def feed(a=a, b=b, i=i, half=half):
                weights = jnp.concatenate([wi_v[r ^ a], wi_v[r ^ b]], axis=1)
                back = jnp.concatenate([wb_v[r ^ a], wb_v[r ^ b]], axis=0)

                @pl.loop(half * 4 // HALVES, (half + 1) * 4 // HALVES)
                def _(t):
                    at = pl.ds(pl.multiple_of(t * step, step), step)
                    inner = pl.ds(pl.multiple_of((t % 2) * step, step), step)
                    pre = jnp.dot(e_v[at], weights, preferred_element_type=F32)
                    up = lax.dot_general(g_v[t // 2, inner], back, NT, preferred_element_type=F32)
                    square = pre * pre
                    th = jnp.tanh(pre * (c0 + (c0 * c1) * square))
                    gate = 0.5 + 0.5 * th
                    act = (pre * gate).astype(BF16)
                    slope = gate + pre * (1.0 - th * th) * ((0.5 * c0) + (1.5 * c0 * c1) * square)
                    pg = (up * slope).astype(BF16)
                    act_v[at] = act
                    pg_v[at] = pg
                    branch = jnp.dot(act, back, preferred_element_type=F32)
                    e2 = lax.dot_general(pg, weights, NT, preferred_element_type=F32)
                    if i == 0:
                        br_v[at] = branch
                        e2_v[at] = e2
                    else:
                        br_v[at] += branch
                        e2_v[at] += e2

            need = flat(wi_d, a, b) + flat(wb_d, a, b) + [f"grd{k}" for k in range(4)] + ["iz_out"]
            last = [plan.work(f"ff{i}{half}", 7.0 / HALVES, last + need, 1, feed)]

        def weight_grads(i=i):
            slot = i % 2

            @pl.loop(0, 3)
            def _(t):
                at = pl.ds(pl.multiple_of(t * 256, 256), 256)
                gi = jnp.dot(et_v[at], pg_v[...], preferred_element_type=F32).astype(BF16)
                gb = jnp.dot(gt_v[at], act_v[...], preferred_element_type=F32).astype(BF16)
                for q in range(2):
                    gi_v[slot, q, at] = gi[:, q * 384:(q + 1) * 384]
                    gb_v[slot, q, at] = gb[:, q * 384:(q + 1) * 384]

        free = [f"g{n}_out{i - 2}{q}" for n in "ib" for q in range(2)] if i >= 2 else []
        last = [plan.work(f"fg{i}", 3.5, last + free + [f"gt{k}" for k in range(4)], 1, weight_grads)]
        for q, owner in enumerate((a, b)):
            put(f"gi_out{i}{q}", 0.3, last, gi_v.at[i % 2, q], gi_o.at[r ^ owner])
            put(f"gb_out{i}{q}", 0.3, last, gb_v.at[i % 2, q], gb_o.at[r ^ owner])

    def finish():
        @pl.loop(0, 8)
        def _(t):
            at = pl.ds(pl.multiple_of(t * 128, 128), 128)
            q, k = t // 4, t % 4
            branch = br_v[at]
            e_v[at] = (h_v[at] + branch).astype(BF16)
            rms_v[k, pl.ds(2 + q, 1)] = as_row(jnp.sqrt(jnp.mean(branch * branch, axis=-1, keepdims=True)))

    last = [plan.work("fin", 2.0, last, 1, finish)]
    put("e2_out", 1.5, last, e2_v, e2_o)
    put("res_out", 0.8, last, e_v, res_o)
    put("rms_out", 0.1, last, rms_v, rms_o)
    toks, grds = [f"tok{k}" for k in range(4)], [f"grd{k}" for k in range(4)]
    put("x_out", 0.8, toks, x_v, x_o)
    put("g_out", 0.8, grds, g_v, g_o)
    put("seg_out", 0.1, ["segs"], seg_v, seg_o)
    put("m_out", 3.0, mixes, m_v, m_o)
    put("wv_out", 0.6, flat(wv_d, *every), wv_v, wv_o)
    put("wo_out", 0.6, flat(wo_d, *every), wo_v, wo_o)
    put("gn_out", 0.1, flat(gn_d, *every), gn_v, gn_o)
    put("val_out", 0.8, [f"val{k}" for k in range(4)], val_v, val_o)
    put("mxd_out", 0.8, [f"mf{groups - 1}"], mxd_v, mxd_o)
    plan.run()


def forward_all(tok, grd, seg, mix, wv, wo, wi, wb, gn):
    sd = jax.ShapeDtypeStruct
    rows, flat, big = (2, 512, 768), (1024, 768), (8, 768, 384)
    mixes, square, gains = (4, 12, 512, 128), (8, 96, 768), (8, 16, 768)
    outs = [sd(rows, BF16), sd(rows, BF16), sd((4, 2, 128), jnp.int32), sd(mixes, BF16), sd(square, BF16),
            sd(square, BF16), sd(gains, BF16), sd(rows, BF16), sd(rows, BF16), sd(flat, F32), sd(flat, F32),
            sd(flat, F32), sd(flat, BF16), sd((4, 8, 128), F32), sd(big, BF16), sd(big, BF16)]
    dma = pltpu.SemaphoreType.DMA
    v = lambda *a: pltpu.VMEM(a, BF16)
    f = lambda *a: pltpu.VMEM(a, F32)
    turned = (768, 1024)
    scratch = [v(*rows), v(*rows), pltpu.VMEM((4, 2, 128), jnp.int32), v(*mixes), v(*square), v(*square), v(*big),
               v(8, 384, 768), v(*gains), v(*rows), v(*rows), f(*flat), v(*flat), v(*turned), v(*turned),
               f(*flat), f(*flat), v(*flat), v(*flat), v(2, 2, 768, 384), v(2, 2, 768, 384), f(4, 8, 128),
               f(2, 512, 1), f(2, 1, 512)]
    return pl.pallas_call(
        forward_kernel, out_shape=outs, in_specs=[ANY] * 9, out_specs=[ANY] * len(outs),
        scratch_shapes=[dma((128,)), dma((128,)), dma((48,))] + scratch,
        compiler_params=pltpu.CompilerParams(collective_id=0, has_side_effects=True, vmem_limit_bytes=VMEM_LIMIT),
    )(tok, grd, seg, mix, wv, wo, wi, wb, gn)


def exp_mix(m_ref, hh):
    return jnp.concatenate([jnp.exp(m_ref[k, hh].astype(F32)) for k in range(4)], axis=1)


class Reduce:
    def __init__(self, plan, name, src, made, local, bufs, out, order, first, prio, mb):
        self.plan, self.name, self.src, self.local, self.bufs = plan, name, src, local, bufs
        r, s = plan.r, plan.s
        self.core, self.x = s % 2, s // 2
        self.n = src.shape[1] // 2
        half = mb / 2
        own, near, across, rows, final = bufs
        last = {}
        for q in range(8):
            deps = made[q]
            if not local:
                plan.near(f"{name}l{q}", half, deps, prio, lambda q=q: self.half(src.at[r ^ q], self.core),
                          lambda q=q: own.at[q])
            plan.comm(f"{name}c{q}", "seq", 1, half, deps, prio, lambda q=q: self.half(src.at[r ^ q], 1 - self.core),
                      lambda q=q: near.at[q])
            last[q] = plan.add(f"{name}a{q}", [f"{name}c{q}"] + (deps if local else [f"{name}l{q}"]),
                               lambda q=q: self.mine(q), lambda q=q: near.at[q])
        if first:
            half = half / 2
            for q in range(8):
                plan.comm(f"{name}X{q}", "seq", 2, half, [last[q]], prio,
                          lambda q=q: self.quarter(self.mine(q), 1 - self.x), lambda q=q: across.at[q])
                last[q] = plan.add(f"{name}A{q}", [f"{name}X{q}", last[q]],
                                   lambda q=q: self.quarter(self.mine(q), self.x), lambda q=q: across.at[q])
        item = (lambda q: self.quarter(self.mine(q), self.x)) if first else self.mine
        keep, slot = list(range(8)), 0
        for stage, bit in enumerate(order):
            for q in [q for q in keep if q & bit]:
                plan.comm(f"{name}r{q}", "rows", bit, half, [last[q]], prio + 0.1 * stage,
                          lambda q=q: item(q), lambda slot=slot: rows.at[slot])
                last[q ^ bit] = plan.add(f"{name}b{q}", [f"{name}r{q}", last[q ^ bit]],
                                         lambda q=q ^ bit: item(q), lambda slot=slot: rows.at[slot])
                slot += 1
            keep = [q for q in keep if not q & bit]
        if first:
            def widen():
                self.quarter(final, self.x)[...] = item(0)[...].astype(F32)

            plan.work(f"{name}t", 0.2, [last[0]], -5, widen)
            plan.comm(f"{name}x", "seq", 2, 2 * half, [f"{name}t"], prio + 0.5,
                      lambda: self.quarter(final, self.x), lambda: self.quarter(final, self.x))
            for name2, dep, which in (("m", "t", 0), ("o", "x", 1)):
                side = (lambda which=which: self.quarter(final, self.x if which == 0 else 1 - self.x))
                place = (lambda which=which: self.quarter(self.half(out, self.core),
                                                          self.x if which == 0 else 1 - self.x))
                plan.near(f"{name}{name2}", mb / 2, [f"{name}{dep}"], prio, side, place)
                plan.comm(f"{name}{name2}k", "seq", 1, mb / 2, [f"{name}{dep}"], prio, side, place)
        else:
            plan.comm(f"{name}x", "seq", 2, half, [last[0]], prio + 0.5, lambda: item(0), lambda: across)

            def total():
                final[...] = item(0)[...].astype(F32) + across[...].astype(F32)

            plan.work(f"{name}t", 0.2, [f"{name}x", last[0]], -5, total)
            plan.near(f"{name}o", mb, [f"{name}t"], prio, lambda: final, lambda: self.half(out, self.core))
            plan.comm(f"{name}k", "seq", 1, mb, [f"{name}t"], prio, lambda: final, lambda: self.half(out, self.core))

    def half(self, ref, which):
        return cut(ref, which * self.n, self.n)

    def quarter(self, ref, which):
        return cut(ref, which * (self.n // 2), self.n // 2)

    def mine(self, q):
        return self.half(self.src.at[self.plan.r ^ q], self.core) if self.local else self.bufs[0].at[q]


def backward_kernel(x_i, g_i, seg_i, m_i, wv_i, wo_i, gn_i, val_i, mxd_i, iz_i, h_i, e2_i, res_i, rms_i, gi, gb,
                    res_o, tgr_o, gi_o, gb_o, go_o, gv_o, gn_o, mg_o, rms_o, send, recv, local,
                    x_v, g_v, seg_v, m_v, wv_v, wo_v, gn_v, val_v, mxd_v, iz_v, h_v, q_v, hl_v, en_v, go_v, gv_v,
                    sc_v, sr_v, n0, n1, m1, m3, m4, t0, t1,
                    i0, i1, i2, i3, i4, b0, b1, b2, b3, b4, o0, o1, o2, o3, o4, v0, v1, v2, v3, v4):
    r, s = lax.axis_index("rows"), lax.axis_index("seq")
    greet(r, s)
    core, x = s % 2, s // 2
    net = Net(send, recv, local)
    plan = Plan(net, r, s)
    place = lambda k: pl.ds(pl.multiple_of((s ^ k) * 128, 128), 128)
    for name, mb, prio, src, dst in (
            ("h", 3.1, 0, h_i, h_v), ("e2", 3.1, 1, e2_i, q_v), ("g", 1.6, 2, g_i, g_v), ("gn", 0.1, 0, gn_i, gn_v),
            ("wo", 1.2, 3, wo_i, wo_v), ("seg", 0.1, 3, seg_i, seg_v), ("mxd", 1.6, 4, mxd_i, mxd_v),
            ("val", 1.6, 4, val_i, val_v), ("iz", 3.1, 4, iz_i, iz_v), ("m", 6.3, 5, m_i, m_v),
            ("x", 1.6, 6, x_i, x_v), ("wv", 1.2, 6, wv_i, wv_v)):
        plan.near(f"in_{name}", mb, [], prio, lambda src=src: src, lambda dst=dst: dst)
    for k in (2, 3, 1):
        plan.comm(f"res{k}", "seq", k, 0.393, [], 60, lambda k=k: res_i.at[:, place(k)], lambda: res_o.at[pl.ds(2 * s, 2)])
        plan.comm(f"rms{k}", "seq", k, 0.004, [], 61, lambda k=k: rms_i.at[s ^ k], lambda: rms_o.at[s])
    for name, src, buf, dst in (("res", res_i.at[:, place(0)], t0, res_o.at[pl.ds(2 * s, 2)]),
                                ("rms", rms_i.at[s], t1, rms_o.at[s])):
        plan.near(f"{name}i", 0.4, [], 9, lambda src=src: src, lambda buf=buf: buf)
        plan.near(f"{name}o", 0.4, [f"{name}i"], 9, lambda buf=buf: buf, lambda dst=dst: dst)

    def start():
        n0[...] = jnp.zeros_like(n0)
        segment_layouts(seg_v, sc_v, sr_v)

    plan.work("segs", 1.0, ["in_seg"], -2, start)
    last = ["segs"] + [f"in_{n}" for n in ("h", "e2", "g", "gn", "wo")]
    for part in range(2):
        def post(part=part):
            @pl.loop(0, 4)
            def _(k):
                at = pl.ds(pl.multiple_of(part * 512 + k * 128, 128), 128)
                inside = pl.ds(pl.multiple_of(k * 128, 128), 128)
                h = h_v[at]
                scale = lax.rsqrt(jnp.mean(h * h, axis=-1, keepdims=True) + EPS)
                normed = h * scale
                up = q_v[at]
                n0[0, 1:2] += jnp.sum(up * normed, axis=0, keepdims=True)
                scaled = up * gain_row(gn_v, 1)
                back = scale * (scaled - normed * jnp.mean(scaled * normed, axis=-1, keepdims=True))
                grad = g_v[part, inside].astype(F32) + back
                q_v[at] = grad
                grad_low = grad.astype(BF16)
                hl_v[at] = grad_low
                g_v[part, inside] = lax.dot_general(
                    grad_low, wo_v[...].reshape(768, 768), NT, preferred_element_type=F32).astype(BF16)

        last = [plan.work(f"post{part}", 3.0, last, -1, post)]

    def out_grad():
        @pl.loop(0, 2)
        def _(t):
            lanes = pl.ds(pl.multiple_of(t * 384, 128), 384)
            grad = lax.dot_general(mxd_v[...].reshape(1024, 768), hl_v[:, lanes], TN, preferred_element_type=F32)
            go_v[:, :, lanes] = grad.astype(BF16).reshape(8, 96, 384)

    last = [plan.work("go", 2.5, last + ["in_mxd"], -1, out_grad)]
    go_made = last
    lane = lax.broadcasted_iota(jnp.int32, (1, 128), 1)
    orders = MIX_ORDERS
    groups = len(orders)
    heads = 12 // groups
    for g, order in enumerate(orders):
        def mixing(g=g):
            @pl.loop(g * heads // 2, (g + 1) * heads // 2)
            def _(p):
                lanes = pl.ds(pl.multiple_of(p * 128, 128), 128)
                raised = [exp_mix(m_v, 2 * p + hh) for hh in range(2)]
                low = [e.astype(BF16) for e in raised]
                acc = [None, None]
                for q in range(2):
                    same = sc_v[q] == sr_v[q]
                    scaled = g_v[q, :, lanes].astype(F32) * iz_v[q * 512:(q + 1) * 512, lanes]
                    inner = scaled * mxd_v[q, :, lanes].astype(F32)
                    grads = []
                    for hh in range(2):
                        mine = (lane < 64) if hh == 0 else (lane >= 64)
                        delta = jnp.sum(jnp.where(mine, inner, 0.0), axis=1, keepdims=True)
                        lhs = jnp.where(mine, scaled, 0.0).astype(BF16)
                        back = lax.dot_general(lhs, val_v[q, :, lanes], NT, preferred_element_type=F32)
                        term = jnp.where(same, back - delta, 0.0)
                        acc[hh] = term if q == 0 else acc[hh] + term
                        masked = jnp.where(same, low[hh], jnp.zeros_like(low[hh]))
                        grads.append(lax.dot_general(masked, scaled.astype(BF16), TN, preferred_element_type=F32))
                    mxd_v[q, :, lanes] = jnp.where(lane < 64, grads[0], grads[1]).astype(BF16)
                for hh in range(2):
                    out = (acc[hh] * raised[hh]).astype(BF16)
                    for k in range(4):
                        m_v[k, 2 * p + hh] = out[:, k * 128:(k + 1) * 128]

        last = [plan.work(f"mb{g}", 2.7 * heads / 2, last + ["in_m", "in_val", "in_iz"], -1, mixing)]
        mine = pl.ds(g * heads, heads)
        mb = 0.01638 * heads
        prio = 5 + 0.01 * g
        done = {}
        block = lambda h, side, mine=mine: m_v.at[2 * (x ^ h) + (core if side == 0 else 1 - core), mine]
        for h in range(2):
            plan.comm(f"mg{g}c{h}", "seq", 1, 8 * mb, last, prio, lambda h=h, block=block: block(h, 1),
                      lambda h=h, mine=mine: m1.at[h, mine])
            made = plan.add(f"mg{g}a{h}", [f"mg{g}c{h}"] + last, lambda h=h, block=block: block(h, 0),
                            lambda h=h, mine=mine: m1.at[h, mine], 0.3)
            for q in range(8):
                done[h, q] = made
        rows = lambda q: pl.ds(pl.multiple_of((r ^ q) * 64, 64), 64)
        item = lambda h, q, mine=mine: m_v.at[2 * (x ^ h) + core, mine, rows(q)]
        keep, slot = [(h, q) for h in range(2) for q in range(8)], 0
        for bit in order:
            hit = (lambda h, q: h) if bit == 0 else (lambda h, q, bit=bit: q & bit)
            for h, q in [k for k in keep if hit(*k)]:
                to = (0, q) if bit == 0 else (h, q ^ bit)
                name = f"mg{g}r{h}{q}"
                plan.comm(name, "rows" if bit else "seq", bit or 2, mb, [done[h, q]], prio,
                          lambda h=h, q=q, item=item: item(h, q), lambda slot=slot, mine=mine: m3.at[slot, mine])
                done[to] = plan.add(name + "d", [name, done[to]], lambda to=to, item=item: item(*to),
                                    lambda slot=slot, mine=mine: m3.at[slot, mine])
                slot += 1
            keep = [k for k in keep if not hit(*k)]

        def final(mine=mine, item=item):
            m4[mine, rows(0)] = item(0, 0)[...]

        got = {0: plan.work(f"mg{g}f", 0.1, [done[0, 0]], -5, final)}
        for bit in [b for b in reversed(order) if b]:
            new = {}
            for q, dep in got.items():
                part = lambda q=q, mine=mine: m4.at[mine, rows(q)]
                new[q ^ bit] = plan.comm(f"mg{g}g{q ^ bit}", "rows", bit, mb, [dep], prio, part, part)
            got.update(new)
        plan.near(f"mg{g}o", 0.4, list(got.values()), 0, lambda mine=mine: m4.at[mine], lambda mine=mine: mg_o.at[mine])
    for k in (2, 3, 1, 0):
        def tokens(k=k):
            for q in range(2):
                at = pl.ds(pl.multiple_of(q * 512 + (s ^ k) * 128, 128), 128)
                up = lax.dot_general(mxd_v[q, place(k)], wv_v[...].reshape(768, 768), NT, preferred_element_type=F32)
                xs = x_v[q, place(k)].astype(F32)
                scale = lax.rsqrt(jnp.mean(xs * xs, axis=-1, keepdims=True) + EPS)
                normed = xs * scale
                gain = gain_row(gn_v, 0)
                en_v[at] = (normed * gain).astype(BF16)
                n0[0, 0:1] += jnp.sum(up * normed, axis=0, keepdims=True)
                scaled = up * gain
                back = scale * (scaled - normed * jnp.mean(scaled * normed, axis=-1, keepdims=True))
                x_v[q, place(k)] = (q_v[at] + back).astype(BF16)

        last = [plan.work(f"tok{k}", 1.2, last + ["in_x", "in_wv"], -1, tokens)]
        if k:
            plan.comm(f"tgr{k}", "seq", k, 0.393, last, 30, lambda k=k: x_v.at[:, place(k)],
                      lambda: tgr_o.at[pl.ds(2 * s, 2)])
        else:
            plan.near("tgro", 0.4, last, 9, lambda: x_v.at[:, place(0)], lambda: tgr_o.at[pl.ds(2 * s, 2)])
    tok_done = last

    def value_grad():
        @pl.loop(0, 2)
        def _(t):
            lanes = pl.ds(pl.multiple_of(t * 384, 128), 384)
            grad = lax.dot_general(en_v[...], mxd_v[:, :, lanes].reshape(1024, 384), TN, preferred_element_type=F32)
            gv_v[:, :, lanes] = grad.astype(BF16).reshape(8, 96, 384)

    gv_made = [plan.work("gv", 2.5, last, -1, value_grad)]
    every = range(8)
    Reduce(plan, "gi", gi, {q: [] for q in every}, False, (i0, i1, i2, i3, i4), gi_o, [1, 2, 4], True, 10, 0.59)
    Reduce(plan, "gb", gb, {q: [] for q in every}, False, (b0, b1, b2, b3, b4), gb_o, [1, 2, 4], True, 11, 0.59)
    Reduce(plan, "go", go_v, {q: go_made for q in every}, True, (o0, o1, o2, o3, o4), go_o, [2, 1, 4], False, 12, 0.147)
    Reduce(plan, "gv", gv_v, {q: gv_made for q in every}, True, (v0, v1, v2, v3, v4), gv_o, [1, 2, 4], False, 4, 0.147)
    last = tok_done
    for i, (axis, bit) in enumerate((("seq", 1), ("seq", 2), ("rows", 1), ("rows", 2), ("rows", 4))):
        plan.comm(f"gn{i}", axis, bit, 0.024, last, 0, lambda i=i: n0.at[i], lambda i=i: n1.at[i])

        def add(i=i):
            n0[i + 1] = n0[i] + n1[i]

        last = [plan.work(f"gna{i}", 0.1, [f"gn{i}"] + last, -5, add)]
    plan.near("gno", 0.02, last, 0, lambda: n0.at[5], lambda: gn_o)
    plan.run()


MIX_ORDERS = ((1, 0, 2, 4), (0, 1, 2, 4), (2, 0, 1, 4))


def backward_all(*args):
    sd = jax.ShapeDtypeStruct
    outs = [sd((8, 128, 768), BF16), sd((8, 128, 768), BF16), sd((768, 384), F32), sd((768, 384), F32),
            sd((96, 768), F32), sd((96, 768), F32), sd((8, 768), F32), sd((12, 512, 128), BF16), sd((4, 8, 128), F32)]
    dma = pltpu.SemaphoreType.DMA
    v = lambda *a: pltpu.VMEM(a, BF16)
    f = lambda *a: pltpu.VMEM(a, F32)
    big, piece, small = (384, 384), (192, 384), (48, 768)
    rows, flat = (2, 512, 768), (1024, 768)
    scratch = [v(*rows), v(*rows), pltpu.VMEM((4, 2, 128), jnp.int32), v(4, 12, 512, 128), v(8, 96, 768), v(8, 96, 768),
               v(8, 16, 768), v(*rows), v(*rows), f(*flat), f(*flat), f(*flat), v(*flat), v(*flat), v(8, 96, 768),
               v(8, 96, 768), f(2, 512, 1), f(2, 1, 512), f(6, 8, 768), f(5, 8, 768),
               v(2, 12, 512, 128), v(15, 12, 64, 128), v(12, 512, 128), v(2, 128, 768), f(8, 128)]
    for _ in range(2):
        scratch += [v(8, *big), v(8, *big), v(8, *piece), v(7, *piece), f(*big)]
    for _ in range(2):
        scratch += [v(16, 128), v(8, *small), v(*small), v(7, *small), f(*small)]
    return pl.pallas_call(
        backward_kernel, out_shape=outs, in_specs=[ANY] * len(args), out_specs=[ANY] * len(outs),
        scratch_shapes=[dma((200,)), dma((200,)), dma((64,))] + scratch,
        compiler_params=pltpu.CompilerParams(collective_id=1, has_side_effects=True, vmem_limit_bytes=67043328),
    )(*args)


def own_columns(r, gain):
    return lax.dynamic_update_slice(jnp.zeros((1, 768), BF16), gain[None], (0, r * 96))


def fast_body(tokens, segments, mix, w_value, w_out, w_in, w_back, gain_one, gain_two, out_grad):
    r, s = lax.axis_index("rows"), lax.axis_index("seq")
    gains = jnp.concatenate(
        [own_columns(r, gain_one), own_columns(r, gain_two), jnp.zeros((14, 768), BF16)], axis=0)
    (x_rows, grad_rows, seg_all, mix_all, wv, wo, gains_all, values, mixed, inverse, hidden_one, grad_entry_two,
     result, rms, grad_in, grad_back) = forward_all(
        tokens, out_grad, segments.reshape(4, 2, 128), mix, w_value, w_out, w_in, w_back, gains)
    res, tgr, gi, gb, go, gv, gn, mg, rms = backward_all(
        x_rows, grad_rows, seg_all, mix_all, wv, wo, gains_all, values, mixed, inverse, hidden_one, grad_entry_two,
        result.reshape(2, 512, 768), rms, grad_in, grad_back)
    own = lax.dynamic_slice(gn, (0, r * 96), (2, 96))
    rms = rms[:, :4].reshape(4, 2, 2, 128)
    rms = rms.transpose(1, 0, 2, 3).reshape(2, 8, 128)
    return (res, tgr.astype(F32), mg.astype(F32), gv, go, gi, gb.T, own[0], own[1], rms[0], rms[1])


def solution(mesh):
    in_specs = (
        P("rows", "seq", None),
        P("rows", "seq"),
        P(None, None, "seq"),
        P("rows", None),
        P("rows", None),
        P(None, "rows"),
        P("rows", None),
        P("rows"),
        P("rows"),
        P("rows", "seq", None),
    )
    out_specs = (
        P("rows", "seq", None),
        P("rows", "seq", None),
        P(None, None, "seq"),
        P("rows", None),
        P("rows", None),
        P(None, "rows"),
        P("rows", None),
        P("rows"),
        P("rows"),
        P("rows", "seq"),
        P("rows", "seq"),
    )
    shape = dict(mesh.shape)
    body = fast_body if shape["rows"] == 8 and shape["seq"] == 4 else generic_body
    return jax.shard_map(body, mesh=mesh, in_specs=in_specs, out_specs=out_specs, check_vma=False)
```

```python
import functools
from functools import partial

import jax
import jax.numpy as jnp
from jax import lax
from jax.experimental import pallas as pl
from jax.experimental.pallas import tpu as pltpu
from jax.sharding import PartitionSpec as P

ROWS, SEQ = "rows", "seq"
NEG = -1e30
EPS = 1e-06


def joined(part, axis, combine):
    gathered = jax.tree.map(lambda a: lax.all_gather(a, axis), part)

    def take(source):
        return jax.tree.map(lambda a: lax.dynamic_index_in_dim(a, source, 0, False), gathered)

    return lax.fori_loop(
        1, lax.axis_size(axis), lambda source, state: combine(state, take(source)), take(0)
    )


def normalize(inputs, gain):
    scale = lax.rsqrt(jnp.mean(inputs * inputs, axis=-1, keepdims=True) + EPS)
    normed = inputs * scale
    return (normed, scale, (normed * gain).astype(jnp.bfloat16))


def norm_back(upstream, normed, scale, gain):
    scaled = upstream * gain
    back = scale * (scaled - normed * jnp.mean(scaled * normed, axis=-1, keepdims=True))
    return (back, jnp.sum(upstream * normed, axis=0))


def combine_stats(first, second):
    max_first, sum_first = first
    max_second, sum_second = second
    row_max = jnp.maximum(max_first, max_second)
    return (
        row_max,
        sum_first * jnp.exp(max_first - row_max) + sum_second * jnp.exp(max_second - row_max),
    )


def local_stats(mix_cols, row_segs, own_segs):
    same_doc = (row_segs[:, None] == own_segs[None, :])[None]
    masked = jnp.where(same_doc, mix_cols, NEG)
    row_max = jnp.max(masked, axis=-1)
    row_sum = jnp.sum(jnp.where(same_doc, jnp.exp(masked - row_max[..., None]), 0.0), axis=-1)
    return (row_max, row_sum)


def make_probs(mix_cols, row_segs, own_segs, row_max, row_sum):
    same_doc = (row_segs[:, None] == own_segs[None, :])[None]
    masked = jnp.where(same_doc, mix_cols, NEG)
    raised = jnp.where(same_doc, jnp.exp(masked - row_max[..., None]), 0.0)
    return raised / row_sum[..., None]


def generic_body(tokens, segments, mix, w_value, w_out, w_in, w_back, gain_one, gain_two, out_grad):
    seq_count, col_count, model_width = tokens.shape
    head_count = mix.shape[0]
    head_dim = model_width // head_count
    f32 = jnp.float32
    bf16 = jnp.bfloat16
    gathered = (
        lax.all_gather(w_value, ROWS, axis=0, tiled=True),
        lax.all_gather(w_out, ROWS, axis=0, tiled=True),
        lax.all_gather(w_in, ROWS, axis=1, tiled=True),
        lax.all_gather(w_back, ROWS, axis=0, tiled=True),
        lax.all_gather(gain_one, ROWS, axis=0, tiled=True),
        lax.all_gather(gain_two, ROWS, axis=0, tiled=True),
    )
    wv_full, wo_full, wi_full, wb_full, gain_first, gain_second = gathered
    gain_first = gain_first.astype(f32)
    gain_second = gain_second.astype(f32)
    resid_in = tokens.astype(f32).reshape(seq_count * col_count, model_width)
    normed_one, scale_one, entry_one = normalize(resid_in, gain_first)
    values = jnp.dot(entry_one, wv_full, preferred_element_type=f32).astype(bf16)
    value_heads = values.reshape(seq_count, col_count, head_count, head_dim)
    row_segs = lax.all_gather(segments, SEQ, axis=1, tiled=True)
    mix_cols = mix.astype(f32)
    local_max, local_sum = lax.map(
        lambda fields: local_stats(mix_cols, fields[0], fields[1]), (row_segs, segments)
    )
    row_max, row_sum = joined((local_max, local_sum), SEQ, combine_stats)
    probs_low = lax.map(
        lambda fields: make_probs(mix_cols, fields[0], fields[1], fields[2], fields[3]).astype(
            bf16
        ),
        (row_segs, segments, row_max, row_sum),
    )
    products = jnp.einsum("shic,schd->ishd", probs_low, value_heads, preferred_element_type=f32)
    mixed = lax.psum_scatter(
        products.reshape(col_count * lax.axis_size(SEQ), seq_count, model_width),
        SEQ,
        scatter_dimension=0,
        tiled=True,
    )
    mixed = mixed.transpose(1, 0, 2).reshape(seq_count * col_count, model_width)
    mixed_low = mixed.astype(bf16)
    hidden_one = resid_in + jnp.dot(mixed_low, wo_full, preferred_element_type=f32)
    normed_two, scale_two, entry_two = normalize(hidden_one, gain_second)
    pre_act = jnp.dot(entry_two, wi_full, preferred_element_type=f32)
    activ, activ_back = jax.vjp(partial(jax.nn.gelu, approximate=True), pre_act)
    activ_low = activ.astype(bf16)
    branch = jnp.dot(activ_low, wb_full, preferred_element_type=f32)
    result = (hidden_one + branch).astype(bf16).reshape(tokens.shape)
    rms_residual = jnp.sqrt(jnp.mean(hidden_one * hidden_one, axis=-1)).reshape(
        seq_count, col_count
    )
    rms_sublayer = jnp.sqrt(jnp.mean(branch * branch, axis=-1)).reshape(seq_count, col_count)
    wv_back, wo_back, wi_back, wb_back = (
        lax.all_gather(w_value, ROWS, axis=0, tiled=True),
        lax.all_gather(w_out, ROWS, axis=0, tiled=True),
        lax.all_gather(w_in, ROWS, axis=1, tiled=True),
        lax.all_gather(w_back, ROWS, axis=0, tiled=True),
    )
    grad_out = out_grad.reshape(seq_count * col_count, model_width)
    grad_back = jnp.dot(activ_low.T, grad_out, preferred_element_type=f32)
    grad_activ = jnp.dot(grad_out, wb_back.T, preferred_element_type=f32)
    grad_pre = activ_back(grad_activ)[0].astype(bf16)
    grad_in = jnp.dot(entry_two.T, grad_pre, preferred_element_type=f32)
    grad_entry_two = jnp.dot(grad_pre, wi_back.T, preferred_element_type=f32)
    back_two, grad_gain_two = norm_back(grad_entry_two, normed_two, scale_two, gain_second)
    grad_hidden = grad_out.astype(f32) + back_two
    grad_hidden_low = grad_hidden.astype(bf16)
    grad_wo = jnp.dot(mixed_low.T, grad_hidden_low, preferred_element_type=f32)
    grad_mixed = jnp.dot(grad_hidden_low, wo_back.T, preferred_element_type=f32).astype(bf16)
    grad_rows = lax.all_gather(
        grad_mixed.reshape(seq_count, col_count, model_width), SEQ, axis=1, tiled=True
    )
    grad_heads = grad_rows.reshape(seq_count, -1, head_count, head_dim)

    def delta_part(fields):
        seg_row, seg_own, max_row, sum_row, grad_row, value_row = fields
        soft_probs = make_probs(mix_cols, seg_row, seg_own, max_row, sum_row)
        grad_probs = jnp.einsum("ihd,chd->hic", grad_row, value_row, preferred_element_type=f32)
        return jnp.sum(soft_probs * grad_probs, axis=-1)

    partial_delta = lax.map(
        delta_part, (row_segs, segments, row_max, row_sum, grad_heads, value_heads)
    )
    delta = lax.psum(partial_delta, SEQ)

    def seq_back(running, fields):
        seg_row, seg_own, max_row, sum_row, grad_row, value_row, delta_row = fields
        soft_probs = make_probs(mix_cols, seg_row, seg_own, max_row, sum_row)
        grad_probs = jnp.einsum("ihd,chd->hic", grad_row, value_row, preferred_element_type=f32)
        running = running + soft_probs * (grad_probs - delta_row[..., None])
        grad_value_row = jnp.einsum(
            "hic,ihd->chd", soft_probs.astype(bf16), grad_row, preferred_element_type=f32
        )
        return (running, grad_value_row)

    local_mix_grad, grad_values = lax.scan(
        seq_back,
        jnp.zeros(mix_cols.shape, f32),
        (row_segs, segments, row_max, row_sum, grad_heads, value_heads, delta),
    )
    mix_grad = lax.psum(local_mix_grad, ROWS)
    grad_values = grad_values.reshape(seq_count * col_count, model_width).astype(bf16)
    grad_wv = jnp.dot(entry_one.T, grad_values, preferred_element_type=f32)
    grad_entry_one = jnp.dot(grad_values, wv_back.T, preferred_element_type=f32)
    back_one, grad_gain_one = norm_back(grad_entry_one, normed_one, scale_one, gain_first)
    tokens_grad = (grad_hidden + back_one).reshape(tokens.shape)
    owned = (
        lax.psum_scatter(grad_wv, ROWS, scatter_dimension=0, tiled=True),
        lax.psum_scatter(grad_wo, ROWS, scatter_dimension=0, tiled=True),
        lax.psum_scatter(grad_in, ROWS, scatter_dimension=1, tiled=True),
        lax.psum_scatter(grad_back, ROWS, scatter_dimension=0, tiled=True),
        lax.psum_scatter(grad_gain_one, ROWS, scatter_dimension=0, tiled=True),
        lax.psum_scatter(grad_gain_two, ROWS, scatter_dimension=0, tiled=True),
    )
    summed = lax.psum((owned[0], owned[1], owned[2], owned[3], owned[4], owned[5]), SEQ)
    return (
        result,
        tokens_grad,
        mix_grad,
        summed[0],
        summed[1],
        summed[2],
        summed[3],
        summed[4],
        summed[5],
        rms_residual,
        rms_sublayer,
    )


F32 = jnp.float32
BF16 = jnp.bfloat16
MESH = pl.DeviceIdType.MESH
NT = (((1,), (1,)), ((), ()))
TN = (((0,), (0,)), ((), ()))
ANY = pl.BlockSpec(memory_space=pl.ANY)
RATE = 0.0925
VMEM_LIMIT = 60 * 2**20
ROW_LINK = {1: ("y", 1.0), 2: ("z", 1.0), 4: ("z", 2.0)}
SEQ_LINK = {1: ("core", 0.12), 2: ("x", 1.0), 3: ("x", 1.0)}


def tag(*parts):
    return "".join(map(str, parts))


class Copy:
    def __init__(self, copy, remote):
        self.copy, self.remote, self.done = copy, remote, False

    def recv(self):
        if not self.done:
            self.done = True
            if self.remote:
                self.copy.wait_recv()
            else:
                self.copy.wait()


class Net:
    def __init__(self, send, recv, local):
        self.send, self.recv, self.local = send, recv, local
        self.remote, self.near = [], []

    def go(self, src, dst, dev):
        i = len(self.remote)
        copy = pltpu.make_async_remote_copy(
            src_ref=src, dst_ref=dst, send_sem=self.send.at[i], recv_sem=self.recv.at[i],
            device_id=dev, device_id_type=MESH)
        copy.start()
        self.remote.append(Copy(copy, True))
        return self.remote[-1]

    def cp(self, src, dst):
        copy = pltpu.make_async_copy(src, dst, self.local.at[len(self.near)])
        copy.start()
        self.near.append(Copy(copy, False))
        return self.near[-1]

    def finish(self):
        for copy in self.near + self.remote:
            copy.recv()
        for copy in self.remote:
            copy.copy.wait_send()


class Plan:
    def __init__(self, net, r, s):
        self.net, self.r, self.s = net, r, s
        self.tasks, self.copies = [], {}

    def comm(self, name, axis, bit, mb, deps, prio, src, dst):
        link, factor = (ROW_LINK if axis == ROWS else SEQ_LINK)[bit]
        dev = {axis: (self.r if axis == ROWS else self.s) ^ bit}

        def emit():
            self.wait(deps)
            self.copies[name] = self.net.go(src(), dst(), dev)

        self.tasks.append((name, link, factor * 2 * mb / RATE, deps, prio, emit))
        return name

    def near(self, name, mb, deps, prio, src, dst):
        def emit():
            self.wait(deps)
            self.copies[name] = self.net.cp(src(), dst())

        self.tasks.append((name, "hbm", mb / 2.0, deps, prio, emit))
        return name

    def work(self, name, us, deps, prio, run):
        def emit():
            self.wait(deps)
            run()

        self.tasks.append((name, "tc", us, deps, prio, emit))
        return name

    def add(self, name, deps, to, other, us=0.12):
        def run():
            target, term = to(), other()
            target[...] = target[...] + term[...]

        return self.work(name, us, deps, -5, run)

    def wait(self, deps):
        for dep in deps:
            if dep in self.copies:
                self.copies[dep].recv()

    def solve(self):
        end, start, free, now = {}, {}, {}, 0.0
        left = list(self.tasks)
        while left:
            ready = [
                (max([free.get(t[1], 0.0)] + [end[d] for d in t[3]]), t[4], i)
                for i, t in enumerate(left) if all(d in end for d in t[3])
            ]
            first = min(ready)
            begin, _, pick = min(
                (b, p, i) for b, p, i in ready if b <= first[0] + 1e-9)
            name, link, cost, _, prio, _ = left.pop(pick)
            start[name] = (begin, link == "tc", prio)
            free[link] = begin + cost
            end[name] = begin + cost + (0.0 if link == "tc" else 2.0)
        self.start, self.end = start, end
        return sorted(self.tasks, key=lambda t: start[t[0]])

    def run(self):
        for task in self.solve():
            task[5]()
        self.net.finish()


def greet(r, s):
    barrier = pltpu.get_barrier_semaphore()
    for bit in (1, 2, 4):
        pl.semaphore_signal(barrier, inc=1, device_id={ROWS: r ^ bit}, device_id_type=MESH)
    for bit in (1, 2, 3):
        pl.semaphore_signal(barrier, inc=1, device_id={SEQ: s ^ bit}, device_id_type=MESH)
    pl.semaphore_wait(barrier, 6)


def cut(ref, start, size):
    return ref.at[pl.ds(pl.multiple_of(start, 16), size)]


def add_gather(plan, name, src, dst, order, ways, prio, mb):
    r, s = plan.r, plan.s
    core, x = s % 2, s // 2
    n = src.shape[0] // ways
    off = {1: 0, 2: core, 4: 2 * core + x}[ways] * n
    far = (2 * core + 1 - x) * n
    part = lambda q, o: cut(src if q == 0 else dst.at[r ^ q], o, n)
    home = lambda q, o: cut(dst.at[r ^ q], o, n)
    got = {0: None}
    for stage, bit in enumerate(order):
        new = {}
        for q, dep in got.items():
            new[q ^ bit] = plan.comm(
                tag(name, q ^ bit), ROWS, bit, mb / ways, [dep] if dep else [], prio + 0.1 * stage,
                lambda q=q: part(q, off), lambda q=q: home(q, off))
        got.update(new)
    need = {q: [dep or tag(name, "0")] for q, dep in got.items()}
    for q, dep in got.items():
        if q == 0 or ways == 1:
            continue
        need[q].append(plan.comm(tag(name, "c", q), SEQ, 1, mb / ways, [dep], prio + 1,
                                 lambda q=q: part(q, off), lambda q=q: home(q, off)))
        if ways == 4:
            need[q].append(plan.comm(tag(name, "x", q), SEQ, 2, mb / ways, [dep], prio + 1,
                                     lambda q=q: part(q, off), lambda q=q: home(q, off)))
            need[q].append(plan.comm(tag(name, "f", q), SEQ, 1, mb / ways, [tag(name, "x", q)], prio + 1,
                                     lambda q=q: part(q, far), lambda q=q: home(q, far)))
    return need


HALVES = 1


def column(row):
    return jnp.broadcast_to(row, (128, 128)).T[:, :1]


def as_row(col):
    return jnp.broadcast_to(col, (128, 128)).T[:1]


def segment_layouts(seg, col, row):
    for q in range(2):
        for k in range(4):
            ids = seg[k, q:q + 1].astype(F32)
            row[q, :, k * 128:(k + 1) * 128] = ids
            col[q, k * 128:(k + 1) * 128] = column(ids)


def gain_row(gains, i):
    total = gains[0, i:i + 1].astype(F32)
    for k in range(1, 8):
        total = total + gains[k, i:i + 1].astype(F32)
    return total


def forward_kernel(tok, grd, seg, mix, wv, wo, wi, wb, gn,
                   x_o, g_o, seg_o, m_o, wv_o, wo_o, gn_o, val_o, mxd_o, iz_o, h_o, e2_o, res_o, rms_o, gi_o, gb_o,
                   send, recv, local,
                   x_v, g_v, seg_v, m_v, wv_v, wo_v, wi_v, wb_v, gn_v, val_v, mxd_v, h_v, e_v, et_v, gt_v,
                   br_v, e2_v, act_v, pg_v, gi_v, gb_v, rms_v, sc_v, sr_v):
    r, s = lax.axis_index(ROWS), lax.axis_index(SEQ)
    greet(r, s)
    y, zb = r % 2, (r // 2) % 2
    net = Net(send, recv, local)
    plan = Plan(net, r, s)
    block = lambda k: pl.ds(pl.multiple_of((s ^ k) * 128, 128), 128)
    for k in (2, 3, 1):
        plan.comm(tag("seg", k), SEQ, k, 0.001, [], 0, lambda k=k: seg.at[s ^ k], lambda: seg_v.at[s])
        plan.comm(tag("tok", k), SEQ, k, 0.393, [], 5, lambda k=k: tok.at[pl.ds(2 * (s ^ k), 2)],
                  lambda: x_v.at[:, block(0)])
        plan.comm(tag("grd", k), SEQ, k, 0.393, [], 15, lambda k=k: grd.at[pl.ds(2 * (s ^ k), 2)],
                  lambda: g_v.at[:, block(0)])
    quarter = lambda ref, a, b: ref.at[:, pl.ds((2 * a + b) * 128, 128)]
    plan.comm("mixc", SEQ, 1, 1.57, [], 3, lambda: mix, lambda: m_v.at[s])
    plan.comm("mixx", SEQ, 2, 0.393, [], 1, lambda: quarter(mix, y, zb), lambda: quarter(m_v.at[s], y, zb))
    other = lambda a, b: (lambda: quarter(m_v.at[s ^ 2], a, b))
    for name, axis, bit, dep, prio, a, b in (
            ("mixz", ROWS, 2, "mixx", 2, y, zb), ("mixy", ROWS, 1, "mixx", 2, y, zb),
            ("mixw", ROWS, 1, "mixz", 2, y, 1 - zb), ("mixc0", SEQ, 1, "mixx", 3, y, zb),
            ("mixc1", SEQ, 1, "mixz", 3, y, 1 - zb), ("mixc2", SEQ, 1, "mixy", 3, 1 - y, zb),
            ("mixc3", SEQ, 1, "mixw", 3, 1 - y, 1 - zb)):
        plan.comm(name, axis, bit, 0.393, [dep], prio, other(a, b), other(a, b))
    flat = lambda got, *qs: [d for q in qs for d in got[q]]
    every = range(8)
    gn_d = add_gather(plan, "gn", gn, gn_v, [4, 2, 1], 1, 0, 0.024)
    wv_d = add_gather(plan, "wv", wv, wv_v, [4, 2, 1], 2, 1, 0.147)
    wo_d = add_gather(plan, "wo", wo, wo_v, [4, 2, 1], 2, 10, 0.147)
    wi_d = add_gather(plan, "wi", wi, wi_v, [4, 2, 1], 4, 20, 0.59)
    wb_d = add_gather(plan, "wb", wb, wb_v, [4, 2, 1], 2, 21, 0.59)
    for name, mb, src, dst in (
            ("tok0", 0.4, lambda: tok.at[pl.ds(2 * s, 2)], lambda: x_v.at[:, block(0)]),
            ("gn0", 0.02, lambda: gn, lambda: gn_v.at[r]), ("wv0", 0.15, lambda: wv, lambda: wv_v.at[r]),
            ("seg0", 0.01, lambda: seg.at[s], lambda: seg_v.at[s]), ("mix0", 1.5, lambda: mix, lambda: m_v.at[s]),
            ("wo0", 0.15, lambda: wo, lambda: wo_v.at[r]), ("wi0", 0.6, lambda: wi, lambda: wi_v.at[r]),
            ("wb0", 0.6, lambda: wb, lambda: wb_v.at[r]),
            ("grd0", 0.4, lambda: grd.at[pl.ds(2 * s, 2)], lambda: g_v.at[:, block(0)])):
        plan.near(name, mb, [], 0, src, dst)

    def put(name, mb, deps, src, dst):
        plan.near(name, mb, deps, 90, lambda: src, lambda: dst)

    for k in range(4):
        def values(k=k):
            x = x_v[:, block(k)].reshape(256, 768).astype(F32)
            scale = lax.rsqrt(jnp.mean(x * x, axis=-1, keepdims=True) + EPS)
            entry = (x * scale * gain_row(gn_v, 0)).astype(BF16)
            out = jnp.dot(entry, wv_v[...].reshape(768, 768), preferred_element_type=F32)
            val_v[:, block(k)] = out.astype(BF16).reshape(2, 128, 768)

        plan.work(tag("val", k), 1.2, [tag("tok", k)] + flat(wv_d, *every) + flat(gn_d, *every), 1, values)
    plan.work("segs", 1.0, [tag("seg", k) for k in range(4)], 0, lambda: segment_layouts(seg_v, sc_v, sr_v))
    for k in range(4):
        def turn(k=k):
            for q in range(2):
                at = pl.ds(pl.multiple_of(q * 512 + (s ^ k) * 128, 128), 128)
                gt_v[:, at] = g_v[q, block(k)].T

        plan.work(tag("gt", k), 0.6, [tag("grd", k)], 9, turn)
    lane = lax.broadcasted_iota(jnp.int32, (1, 128), 1)
    last = ["segs"] + [tag("val", k) for k in range(4)]
    mixes = ["mix0", "mixc", "mixx", "mixz", "mixy", "mixw", "mixc0", "mixc1", "mixc2", "mixc3"]
    groups = 3
    for g in range(groups):
        def mixing(g=g):
            @pl.loop(g * (6 // groups), (g + 1) * (6 // groups))
            def _(p):
                lanes = pl.ds(pl.multiple_of(p * 128, 128), 128)
                raised = [exp_mix(m_v, 2 * p + hh).astype(BF16) for hh in range(2)]
                for q in range(2):
                    same = sc_v[q] == sr_v[q]
                    rhs = jnp.concatenate([val_v[q, :, lanes], jnp.ones((512, 128), BF16)], axis=1)
                    both = [jnp.dot(jnp.where(same, e, jnp.zeros_like(e)), rhs, preferred_element_type=F32)
                            for e in raised]
                    total = jnp.where(lane < 64, both[0][:, :128], both[1][:, :128])
                    inverse = 1.0 / jnp.where(lane < 64, both[0][:, 128:], both[1][:, 128:])
                    mxd_v[q, :, lanes] = (total * inverse).astype(BF16)
                    br_v[q * 512:(q + 1) * 512, lanes] = inverse

        last = [plan.work(tag("mf", g), 10.0 / groups, last + mixes, 1, mixing)]
    put("iz_out", 1.5, last, br_v, iz_o)
    for q in range(2):
        def project(q=q):
            @pl.loop(0, 4)
            def _(k):
                inside = pl.ds(pl.multiple_of(k * 128, 128), 128)
                at = pl.ds(pl.multiple_of(q * 512 + k * 128, 128), 128)
                h = x_v[q, inside].astype(F32) + jnp.dot(
                    mxd_v[q, inside], wo_v[...].reshape(768, 768), preferred_element_type=F32)
                square = jnp.mean(h * h, axis=-1, keepdims=True)
                h_v[at] = h
                entry = (h * lax.rsqrt(square + EPS) * gain_row(gn_v, 1)).astype(BF16)
                e_v[at] = entry
                et_v[:, at] = entry.T
                rms_v[k, q:q + 1] = as_row(jnp.sqrt(square))

        last = [plan.work(tag("out", q), 2.5, last + flat(wo_d, *every), 1, project)]
    put("h_out", 1.5, last, h_v, h_o)
    c0, c1 = 0.7978845608028654, 0.044715
    step = 256
    for i, (a, b) in enumerate(((0, 4), (1, 5), (2, 6), (3, 7))):
        for half in range(HALVES):
            def feed(a=a, b=b, i=i, half=half):
                weights = jnp.concatenate([wi_v[r ^ a], wi_v[r ^ b]], axis=1)
                back = jnp.concatenate([wb_v[r ^ a], wb_v[r ^ b]], axis=0)

                @pl.loop(half * 4 // HALVES, (half + 1) * 4 // HALVES)
                def _(t):
                    at = pl.ds(pl.multiple_of(t * step, step), step)
                    inner = pl.ds(pl.multiple_of((t % 2) * step, step), step)
                    pre = jnp.dot(e_v[at], weights, preferred_element_type=F32)
                    up = lax.dot_general(g_v[t // 2, inner], back, NT, preferred_element_type=F32)
                    square = pre * pre
                    th = jnp.tanh(pre * (c0 + (c0 * c1) * square))
                    gate = 0.5 + 0.5 * th
                    act = (pre * gate).astype(BF16)
                    slope = gate + pre * (1.0 - th * th) * ((0.5 * c0) + (1.5 * c0 * c1) * square)
                    pg = (up * slope).astype(BF16)
                    act_v[at] = act
                    pg_v[at] = pg
                    branch = jnp.dot(act, back, preferred_element_type=F32)
                    e2 = lax.dot_general(pg, weights, NT, preferred_element_type=F32)
                    if i == 0:
                        br_v[at] = branch
                        e2_v[at] = e2
                    else:
                        br_v[at] += branch
                        e2_v[at] += e2

            need = flat(wi_d, a, b) + flat(wb_d, a, b) + [tag("grd", k) for k in range(4)] + ["iz_out"]
            last = [plan.work(tag("ff", i, half), 7.0 / HALVES, last + need, 1, feed)]

        def weight_grads(i=i):
            slot = i % 2

            @pl.loop(0, 3)
            def _(t):
                at = pl.ds(pl.multiple_of(t * 256, 256), 256)
                gi = jnp.dot(et_v[at], pg_v[...], preferred_element_type=F32).astype(BF16)
                gb = jnp.dot(gt_v[at], act_v[...], preferred_element_type=F32).astype(BF16)
                for q in range(2):
                    gi_v[slot, q, at] = gi[:, q * 384:(q + 1) * 384]
                    gb_v[slot, q, at] = gb[:, q * 384:(q + 1) * 384]

        free = [tag("g", n, "_out", i - 2, q) for n in "ib" for q in range(2)] if i >= 2 else []
        last = [plan.work(tag("fg", i), 3.5, last + free + [tag("gt", k) for k in range(4)], 1, weight_grads)]
        for q, owner in enumerate((a, b)):
            put(tag("gi_out", i, q), 0.3, last, gi_v.at[i % 2, q], gi_o.at[r ^ owner])
            put(tag("gb_out", i, q), 0.3, last, gb_v.at[i % 2, q], gb_o.at[r ^ owner])

    def finish():
        @pl.loop(0, 8)
        def _(t):
            at = pl.ds(pl.multiple_of(t * 128, 128), 128)
            q, k = t // 4, t % 4
            branch = br_v[at]
            e_v[at] = (h_v[at] + branch).astype(BF16)
            rms_v[k, pl.ds(2 + q, 1)] = as_row(jnp.sqrt(jnp.mean(branch * branch, axis=-1, keepdims=True)))

    last = [plan.work("fin", 2.0, last, 1, finish)]
    put("e2_out", 1.5, last, e2_v, e2_o)
    put("res_out", 0.8, last, e_v, res_o)
    put("rms_out", 0.1, last, rms_v, rms_o)
    toks, grds = [tag("tok", k) for k in range(4)], [tag("grd", k) for k in range(4)]
    put("x_out", 0.8, toks, x_v, x_o)
    put("g_out", 0.8, grds, g_v, g_o)
    put("seg_out", 0.1, ["segs"], seg_v, seg_o)
    put("m_out", 3.0, mixes, m_v, m_o)
    put("wv_out", 0.6, flat(wv_d, *every), wv_v, wv_o)
    put("wo_out", 0.6, flat(wo_d, *every), wo_v, wo_o)
    put("gn_out", 0.1, flat(gn_d, *every), gn_v, gn_o)
    put("val_out", 0.8, [tag("val", k) for k in range(4)], val_v, val_o)
    put("mxd_out", 0.8, [tag("mf", groups - 1)], mxd_v, mxd_o)
    plan.run()


def forward_all(tok, grd, seg, mix, wv, wo, wi, wb, gn):
    sd = jax.ShapeDtypeStruct
    rows, flat, big = (2, 512, 768), (1024, 768), (8, 768, 384)
    mixes, square, gains = (4, 12, 512, 128), (8, 96, 768), (8, 16, 768)
    outs = [sd(rows, BF16), sd(rows, BF16), sd((4, 2, 128), jnp.int32), sd(mixes, BF16), sd(square, BF16),
            sd(square, BF16), sd(gains, BF16), sd(rows, BF16), sd(rows, BF16), sd(flat, F32), sd(flat, F32),
            sd(flat, F32), sd(flat, BF16), sd((4, 8, 128), F32), sd(big, BF16), sd(big, BF16)]
    dma = pltpu.SemaphoreType.DMA
    v = lambda *a: pltpu.VMEM(a, BF16)
    f = lambda *a: pltpu.VMEM(a, F32)
    turned = (768, 1024)
    scratch = [v(*rows), v(*rows), pltpu.VMEM((4, 2, 128), jnp.int32), v(*mixes), v(*square), v(*square), v(*big),
               v(8, 384, 768), v(*gains), v(*rows), v(*rows), f(*flat), v(*flat), v(*turned), v(*turned),
               f(*flat), f(*flat), v(*flat), v(*flat), v(2, 2, 768, 384), v(2, 2, 768, 384), f(4, 8, 128),
               f(2, 512, 1), f(2, 1, 512)]
    return pl.pallas_call(
        forward_kernel, out_shape=outs, in_specs=[ANY] * 9, out_specs=[ANY] * len(outs),
        scratch_shapes=[dma((128,)), dma((128,)), dma((48,))] + scratch,
        compiler_params=pltpu.CompilerParams(collective_id=0, has_side_effects=True, vmem_limit_bytes=VMEM_LIMIT),
    )(tok, grd, seg, mix, wv, wo, wi, wb, gn)


def exp_mix(m_ref, hh):
    return jnp.concatenate([jnp.exp(m_ref[k, hh].astype(F32)) for k in range(4)], axis=1)


class Reduce:
    def __init__(self, plan, name, src, made, local, bufs, out, order, first, prio, mb, pieces):
        self.plan, self.name, self.src, self.local, self.bufs = plan, name, src, local, bufs
        r, s = plan.r, plan.s
        self.core, self.x = s % 2, s // 2
        self.n = src.shape[1] // 2
        half = mb / 2
        own, near, across, rows, final = bufs
        last = {}
        for q in pieces:
            deps = made[q]
            if not local:
                plan.near(tag(name, "l", q), half, deps, prio, lambda q=q: self.half(src.at[r ^ q], self.core),
                          lambda q=q: own.at[q])
            plan.comm(tag(name, "c", q), SEQ, 1, half, deps, prio, lambda q=q: self.half(src.at[r ^ q], 1 - self.core),
                      lambda q=q: near.at[q])
            last[q] = plan.add(tag(name, "a", q), [tag(name, "c", q)] + (deps if local else [tag(name, "l", q)]),
                               lambda q=q: self.mine(q), lambda q=q: near.at[q])
        if first:
            half = half / 2
            for q in pieces:
                plan.comm(tag(name, "X", q), SEQ, 2, half, [last[q]], prio,
                          lambda q=q: self.quarter(self.mine(q), 1 - self.x), lambda q=q: across.at[q])
                last[q] = plan.add(tag(name, "A", q), [tag(name, "X", q), last[q]],
                                   lambda q=q: self.quarter(self.mine(q), self.x), lambda q=q: across.at[q])
        item = (lambda q: self.quarter(self.mine(q), self.x)) if first else self.mine
        keep, slot = list(range(8)), 0
        for stage, bit in enumerate(order):
            for q in [q for q in pieces if q in keep and q & bit]:
                plan.comm(tag(name, "r", q), ROWS, bit, half, [last[q]], prio + 0.1 * stage,
                          lambda q=q: item(q), lambda slot=slot: rows.at[slot])
                last[q ^ bit] = plan.add(tag(name, "b", q), [tag(name, "r", q), last[q ^ bit]],
                                         lambda q=q ^ bit: item(q), lambda slot=slot: rows.at[slot])
                slot += 1
            keep = [q for q in keep if not q & bit]
        if first:
            def widen():
                self.quarter(final, self.x)[...] = item(0)[...].astype(F32)

            plan.work(tag(name, "t"), 0.2, [last[0]], -5, widen)
            plan.comm(tag(name, "x"), SEQ, 2, 2 * half, [tag(name, "t")], prio + 0.5,
                      lambda: self.quarter(final, self.x), lambda: self.quarter(final, self.x))
            for name2, dep, which in (("m", "t", 0), ("o", "x", 1)):
                side = (lambda which=which: self.quarter(final, self.x if which == 0 else 1 - self.x))
                place = (lambda which=which: self.quarter(self.half(out, self.core),
                                                          self.x if which == 0 else 1 - self.x))
                plan.near(tag(name, name2), mb / 2, [tag(name, dep)], prio, side, place)
                plan.comm(tag(name, name2, "k"), SEQ, 1, mb / 2, [tag(name, dep)], prio, side, place)
        else:
            plan.comm(tag(name, "x"), SEQ, 2, half, [last[0]], prio + 0.5, lambda: item(0), lambda: across)

            def total():
                final[...] = item(0)[...].astype(F32) + across[...].astype(F32)

            plan.work(tag(name, "t"), 0.2, [tag(name, "x"), last[0]], -5, total)
            plan.near(tag(name, "o"), mb, [tag(name, "t")], prio, lambda: final, lambda: self.half(out, self.core))
            plan.comm(tag(name, "k"), SEQ, 1, mb, [tag(name, "t")], prio, lambda: final, lambda: self.half(out, self.core))

    def half(self, ref, which):
        return cut(ref, which * self.n, self.n)

    def quarter(self, ref, which):
        return cut(ref, which * (self.n // 2), self.n // 2)

    def mine(self, q):
        return self.half(self.src.at[self.plan.r ^ q], self.core) if self.local else self.bufs[0].at[q]


def backward_kernel(x_i, g_i, seg_i, m_i, wv_i, wo_i, gn_i, val_i, mxd_i, iz_i, h_i, e2_i, res_i, rms_i, gi, gb,
                    res_o, tgr_o, gi_o, gb_o, go_o, gv_o, gn_o, mg_o, rms_o, send, recv, local,
                    x_v, g_v, seg_v, m_v, wv_v, wo_v, gn_v, val_v, mxd_v, iz_v, h_v, q_v, hl_v, go_v, gv_v,
                    sc_v, sr_v, n0, n1, m1, m3, m4, t0, t1,
                    i0, i1, i2, i3, i4, b0, b1, b2, b3, b4, o0, o1, o2, o3, o4, v0, v1, v2, v3, v4):
    r, s = lax.axis_index(ROWS), lax.axis_index(SEQ)
    greet(r, s)
    core, x = s % 2, s // 2
    net = Net(send, recv, local)
    plan = Plan(net, r, s)
    place = lambda k: pl.ds(pl.multiple_of((s ^ k) * 128, 128), 128)
    for name, mb, prio, src, dst in (
            ("h", 3.1, 0, h_i, h_v), ("e2", 3.1, 1, e2_i, q_v), ("g", 1.6, 2, g_i, g_v), ("gn", 0.1, 0, gn_i, gn_v),
            ("wo", 1.2, 3, wo_i, wo_v), ("seg", 0.1, 3, seg_i, seg_v), ("mxd", 1.6, 4, mxd_i, mxd_v),
            ("val", 1.6, 4, val_i, val_v), ("iz", 3.1, 4, iz_i, iz_v), ("m", 6.3, 5, m_i, m_v),
            ("x", 1.6, 6, x_i, x_v), ("wv", 1.2, 6, wv_i, wv_v)):
        plan.near(tag("in_", name), mb, [], prio, lambda src=src: src, lambda dst=dst: dst)
    for k in (2, 3, 1):
        plan.comm(tag("res", k), SEQ, k, 0.393, [], 2, lambda k=k: res_i.at[:, place(k)], lambda: res_o.at[pl.ds(2 * s, 2)])
        plan.comm(tag("rms", k), SEQ, k, 0.004, [], 3, lambda k=k: rms_i.at[s ^ k], lambda: rms_o.at[s])
    for name, src, buf, dst in (("res", res_i.at[:, place(0)], t0, res_o.at[pl.ds(2 * s, 2)]),
                                ("rms", rms_i.at[s], t1, rms_o.at[s])):
        plan.near(tag(name, "i"), 0.4, [], 9, lambda src=src: src, lambda buf=buf: buf)
        plan.near(tag(name, "o"), 0.4, [tag(name, "i")], 9, lambda buf=buf: buf, lambda dst=dst: dst)

    def start():
        n0[...] = jnp.zeros_like(n0)
        segment_layouts(seg_v, sc_v, sr_v)

    plan.work("segs", 1.0, ["in_seg"], -2, start)
    last = ["segs"] + [tag("in_", n) for n in ("h", "e2", "g", "gn", "wo")]
    for part in range(2):
        def post(part=part):
            @pl.loop(0, 4)
            def _(k):
                at = pl.ds(pl.multiple_of(part * 512 + k * 128, 128), 128)
                inside = pl.ds(pl.multiple_of(k * 128, 128), 128)
                h = h_v[at]
                scale = lax.rsqrt(jnp.mean(h * h, axis=-1, keepdims=True) + EPS)
                normed = h * scale
                up = q_v[at]
                n0[0, 1:2] += jnp.sum(up * normed, axis=0, keepdims=True)
                scaled = up * gain_row(gn_v, 1)
                back = scale * (scaled - normed * jnp.mean(scaled * normed, axis=-1, keepdims=True))
                grad = g_v[part, inside].astype(F32) + back
                q_v[at] = grad
                grad_low = grad.astype(BF16)
                hl_v[at] = grad_low
                g_v[part, inside] = lax.dot_general(
                    grad_low, wo_v[...].reshape(768, 768), NT, preferred_element_type=F32).astype(BF16)

        last = [plan.work(tag("post", part), 3.0, last, -1, post)]

    def out_grad():
        @pl.loop(0, 2)
        def _(t):
            lanes = pl.ds(pl.multiple_of(t * 384, 128), 384)
            grad = lax.dot_general(mxd_v[...].reshape(1024, 768), hl_v[:, lanes], TN, preferred_element_type=F32)
            go_v[:, :, lanes] = grad.astype(BF16).reshape(8, 96, 384)

    last = [plan.work("go", 2.5, last + ["in_mxd"], -1, out_grad)]
    go_made = last
    lane = lax.broadcasted_iota(jnp.int32, (1, 128), 1)
    orders = MIX_ORDERS
    groups = len(orders)
    heads = 12 // groups
    for g, order in enumerate(orders):
        def mixing(g=g):
            @pl.loop(g * heads // 2, (g + 1) * heads // 2)
            def _(p):
                lanes = pl.ds(pl.multiple_of(p * 128, 128), 128)
                raised = [exp_mix(m_v, 2 * p + hh) for hh in range(2)]
                low = [e.astype(BF16) for e in raised]
                acc = [None, None]
                for q in range(2):
                    same = sc_v[q] == sr_v[q]
                    scaled = g_v[q, :, lanes].astype(F32) * iz_v[q * 512:(q + 1) * 512, lanes]
                    inner = scaled * mxd_v[q, :, lanes].astype(F32)
                    grads = []
                    for hh in range(2):
                        mine = (lane < 64) if hh == 0 else (lane >= 64)
                        delta = jnp.sum(jnp.where(mine, inner, 0.0), axis=1, keepdims=True)
                        lhs = jnp.where(mine, scaled, 0.0).astype(BF16)
                        back = lax.dot_general(lhs, val_v[q, :, lanes], NT, preferred_element_type=F32)
                        term = jnp.where(same, back - delta, 0.0)
                        acc[hh] = term if q == 0 else acc[hh] + term
                        masked = jnp.where(same, low[hh], jnp.zeros_like(low[hh]))
                        grads.append(lax.dot_general(masked, scaled.astype(BF16), TN, preferred_element_type=F32))
                    mxd_v[q, :, lanes] = jnp.where(lane < 64, grads[0], grads[1]).astype(BF16)
                for hh in range(2):
                    out = (acc[hh] * raised[hh]).astype(BF16)
                    for k in range(4):
                        m_v[k, 2 * p + hh] = out[:, k * 128:(k + 1) * 128]

        last = [plan.work(tag("mb", g), 2.7 * heads / 2, last + ["in_m", "in_val", "in_iz"], -1, mixing)]
        mine = pl.ds(g * heads, heads)
        mb = 0.01638 * heads
        prio = MIX_URGENCY[g]
        done = {}
        block = lambda h, side, mine=mine: m_v.at[2 * (x ^ h) + (core if side == 0 else 1 - core), mine]
        for h in range(2):
            plan.comm(tag("mg", g, "c", h), SEQ, 1, 8 * mb, last, prio, lambda h=h, block=block: block(h, 1),
                      lambda h=h, mine=mine: m1.at[h, mine])
            made = plan.add(tag("mg", g, "a", h), [tag("mg", g, "c", h)] + last, lambda h=h, block=block: block(h, 0),
                            lambda h=h, mine=mine: m1.at[h, mine], 0.3)
            for q in range(8):
                done[h, q] = made
        rows = lambda q: pl.ds(pl.multiple_of((r ^ q) * 64, 64), 64)
        item = lambda h, q, mine=mine: m_v.at[2 * (x ^ h) + core, mine, rows(q)]
        keep, slot = [(h, q) for h in range(2) for q in range(8)], 0
        for bit in order:
            hit = (lambda h, q: h) if bit == 0 else (lambda h, q, bit=bit: q & bit)
            for h, q in [k for k in keep if hit(*k)]:
                to = (0, q) if bit == 0 else (h, q ^ bit)
                name = tag("mg", g, "r", h, q)
                plan.comm(name, ROWS if bit else SEQ, bit or 2, mb, [done[h, q]], prio,
                          lambda h=h, q=q, item=item: item(h, q), lambda slot=slot, mine=mine: m3.at[slot, mine])
                done[to] = plan.add(name + "d", [name, done[to]], lambda to=to, item=item: item(*to),
                                    lambda slot=slot, mine=mine: m3.at[slot, mine])
                slot += 1
            keep = [k for k in keep if not hit(*k)]

        def final(mine=mine, item=item):
            m4[mine, rows(0)] = item(0, 0)[...]

        got = {0: plan.work(tag("mg", g, "f"), 0.1, [done[0, 0]], -5, final)}
        for bit in [b for b in reversed(order) if b]:
            new = {}
            for q, dep in got.items():
                part = lambda q=q, mine=mine: m4.at[mine, rows(q)]
                new[q ^ bit] = plan.comm(tag("mg", g, "g", q ^ bit), ROWS, bit, mb, [dep], prio, part, part)
            got.update(new)
        plan.near(tag("mg", g, "o"), 0.4, list(got.values()), 0, lambda mine=mine: m4.at[mine], lambda mine=mine: mg_o.at[mine])
    for k in (2, 3, 1, 0):
        def tokens(k=k):
            for q in range(2):
                at = pl.ds(pl.multiple_of(q * 512 + (s ^ k) * 128, 128), 128)
                up = lax.dot_general(mxd_v[q, place(k)], wv_v[...].reshape(768, 768), NT, preferred_element_type=F32)
                xs = x_v[q, place(k)].astype(F32)
                scale = lax.rsqrt(jnp.mean(xs * xs, axis=-1, keepdims=True) + EPS)
                normed = xs * scale
                gain = gain_row(gn_v, 0)
                hl_v[at] = (normed * gain).astype(BF16)
                n0[0, 0:1] += jnp.sum(up * normed, axis=0, keepdims=True)
                scaled = up * gain
                back = scale * (scaled - normed * jnp.mean(scaled * normed, axis=-1, keepdims=True))
                x_v[q, place(k)] = (q_v[at] + back).astype(BF16)

        last = [plan.work(tag("tok", k), 1.2, last + ["in_x", "in_wv"], -1, tokens)]
        if k:
            plan.comm(tag("tgr", k), SEQ, k, 0.393, last, 30, lambda k=k: x_v.at[:, place(k)],
                      lambda: tgr_o.at[pl.ds(2 * s, 2)])
        else:
            plan.near("tgro", 0.4, last, 9, lambda: x_v.at[:, place(0)], lambda: tgr_o.at[pl.ds(2 * s, 2)])
    tok_done = last

    def value_grad():
        @pl.loop(0, 2)
        def _(t):
            lanes = pl.ds(pl.multiple_of(t * 384, 128), 384)
            grad = lax.dot_general(hl_v[...], mxd_v[:, :, lanes].reshape(1024, 384), TN, preferred_element_type=F32)
            gv_v[:, :, lanes] = grad.astype(BF16).reshape(8, 96, 384)

    gv_made = [plan.work("gv", 2.5, last, -1, value_grad)]
    every = range(8)
    Reduce(plan, "gi", gi, {q: [] for q in every}, False, (i0, i1, i2, i3, i4), gi_o, [1, 2, 4], True, 10, 0.59, ODD)
    Reduce(plan, "gb", gb, {q: [] for q in every}, False, (b0, b1, b2, b3, b4), gb_o, [2, 1, 4], False, 4, 0.59, HIGH)
    Reduce(plan, "go", go_v, {q: go_made for q in every}, True, (o0, o1, o2, o3, o4), go_o, [1, 2, 4], False, 2, 0.147, ODD)
    Reduce(plan, "gv", gv_v, {q: gv_made for q in every}, True, (v0, v1, v2, v3, v4), gv_o, [1, 2, 4], False, 6, 0.147, HIGH)
    last = tok_done
    for i, (axis, bit) in enumerate(((SEQ, 1), (SEQ, 2), (ROWS, 1), (ROWS, 2), (ROWS, 4))):
        plan.comm(tag("gn", i), axis, bit, 0.024, last, 0, lambda i=i: n0.at[i], lambda i=i: n1.at[i])

        def add(i=i):
            n0[i + 1] = n0[i] + n1[i]

        last = [plan.work(tag("gna", i), 0.1, [tag("gn", i)] + last, -5, add)]
    plan.near("gno", 0.02, last, 0, lambda: n0.at[5], lambda: gn_o)
    plan.run()


MIX_ORDERS = ((1, 0, 2, 4), (0, 1, 2, 4), (0, 1, 2, 4))
MIX_URGENCY = (12.0, 12.01, 5.02)
ODD, HIGH = (3, 7, 1, 5, 2, 6, 4, 0), (6, 7, 2, 3, 4, 5, 0, 1)


def backward_all(*args):
    sd = jax.ShapeDtypeStruct
    outs = [sd((8, 128, 768), BF16), sd((8, 128, 768), BF16), sd((768, 384), F32), sd((768, 384), F32),
            sd((96, 768), F32), sd((96, 768), F32), sd((8, 768), F32), sd((12, 512, 128), BF16), sd((4, 8, 128), F32)]
    dma = pltpu.SemaphoreType.DMA
    v = lambda *a: pltpu.VMEM(a, BF16)
    f = lambda *a: pltpu.VMEM(a, F32)
    big, piece, small = (384, 384), (192, 384), (48, 768)
    rows, flat = (2, 512, 768), (1024, 768)
    scratch = [v(*rows), v(*rows), pltpu.VMEM((4, 2, 128), jnp.int32), v(4, 12, 512, 128), v(8, 96, 768), v(8, 96, 768),
               v(8, 16, 768), v(*rows), v(*rows), f(*flat), f(*flat), f(*flat), v(*flat), v(8, 96, 768),
               v(8, 96, 768), f(2, 512, 1), f(2, 1, 512), f(6, 8, 768), f(5, 8, 768),
               v(2, 12, 512, 128), v(15, 12, 64, 128), v(12, 512, 128), v(2, 128, 768), f(8, 128)]
    scratch += [v(8, *big), v(8, *big), v(8, *piece), v(7, *piece), f(*big)]
    scratch += [v(8, *big), v(8, *big), v(*big), v(7, *big), f(*big)]
    for _ in range(2):
        scratch += [v(16, 128), v(8, *small), v(*small), v(7, *small), f(*small)]
    return pl.pallas_call(
        backward_kernel, out_shape=outs, in_specs=[ANY] * len(args), out_specs=[ANY] * len(outs),
        scratch_shapes=[dma((200,)), dma((200,)), dma((64,))] + scratch,
        compiler_params=pltpu.CompilerParams(collective_id=1, has_side_effects=True, vmem_limit_bytes=67043328),
    )(*args)


def own_columns(r, gain):
    return lax.dynamic_update_slice(jnp.zeros((1, 768), BF16), gain[None], (0, r * 96))


def fast_body(tokens, segments, mix, w_value, w_out, w_in, w_back, gain_one, gain_two, out_grad):
    r, s = lax.axis_index(ROWS), lax.axis_index(SEQ)
    gains = jnp.concatenate(
        [own_columns(r, gain_one), own_columns(r, gain_two), jnp.zeros((14, 768), BF16)], axis=0)
    (x_rows, grad_rows, seg_all, mix_all, wv, wo, gains_all, values, mixed, inverse, hidden_one, grad_entry_two,
     result, rms, grad_in, grad_back) = forward_all(
        tokens, out_grad, segments.reshape(4, 2, 128), mix, w_value, w_out, w_in, w_back, gains)
    res, tgr, gi, gb, go, gv, gn, mg, rms = backward_all(
        x_rows, grad_rows, seg_all, mix_all, wv, wo, gains_all, values, mixed, inverse, hidden_one, grad_entry_two,
        result.reshape(2, 512, 768), rms, grad_in, grad_back)
    own = lax.dynamic_slice(gn, (0, r * 96), (2, 96))
    rms = rms[:, :4].reshape(4, 2, 2, 128)
    rms = rms.transpose(1, 0, 2, 3).reshape(2, 8, 128)
    return (res, tgr.astype(F32), mg.astype(F32), gv, go, gi, gb.T, own[0], own[1], rms[0], rms[1])


def solution(mesh):
    in_specs = (
        P(ROWS, SEQ, None),
        P(ROWS, SEQ),
        P(None, None, SEQ),
        P(ROWS, None),
        P(ROWS, None),
        P(None, ROWS),
        P(ROWS, None),
        P(ROWS),
        P(ROWS),
        P(ROWS, SEQ, None),
    )
    out_specs = (
        P(ROWS, SEQ, None),
        P(ROWS, SEQ, None),
        P(None, None, SEQ),
        P(ROWS, None),
        P(ROWS, None),
        P(None, ROWS),
        P(ROWS, None),
        P(ROWS),
        P(ROWS),
        P(ROWS, SEQ),
        P(ROWS, SEQ),
    )
    shape = dict(mesh.shape)
    body = fast_body if shape[ROWS] == 8 and shape[SEQ] == 4 else generic_body
    return jax.shard_map(body, mesh=mesh, in_specs=in_specs, out_specs=out_specs, check_vma=False)
```

```python
import functools
from functools import partial

import jax
import jax.numpy as jnp
from jax import lax
from jax.experimental import pallas as pl
from jax.experimental.pallas import tpu as pltpu
from jax.sharding import PartitionSpec as P

ROWS, SEQ = "rows", "seq"
NEG = -1e30
EPS = 1e-06


def joined(part, axis, combine):
    gathered = jax.tree.map(lambda a: lax.all_gather(a, axis), part)

    def take(source):
        return jax.tree.map(lambda a: lax.dynamic_index_in_dim(a, source, 0, False), gathered)

    return lax.fori_loop(
        1, lax.axis_size(axis), lambda source, state: combine(state, take(source)), take(0)
    )


def normalize(inputs, gain):
    scale = lax.rsqrt(jnp.mean(inputs * inputs, axis=-1, keepdims=True) + EPS)
    normed = inputs * scale
    return (normed, scale, (normed * gain).astype(jnp.bfloat16))


def norm_back(upstream, normed, scale, gain):
    scaled = upstream * gain
    back = scale * (scaled - normed * jnp.mean(scaled * normed, axis=-1, keepdims=True))
    return (back, jnp.sum(upstream * normed, axis=0))


def combine_stats(first, second):
    max_first, sum_first = first
    max_second, sum_second = second
    row_max = jnp.maximum(max_first, max_second)
    return (
        row_max,
        sum_first * jnp.exp(max_first - row_max) + sum_second * jnp.exp(max_second - row_max),
    )


def local_stats(mix_cols, row_segs, own_segs):
    same_doc = (row_segs[:, None] == own_segs[None, :])[None]
    masked = jnp.where(same_doc, mix_cols, NEG)
    row_max = jnp.max(masked, axis=-1)
    row_sum = jnp.sum(jnp.where(same_doc, jnp.exp(masked - row_max[..., None]), 0.0), axis=-1)
    return (row_max, row_sum)


def make_probs(mix_cols, row_segs, own_segs, row_max, row_sum):
    same_doc = (row_segs[:, None] == own_segs[None, :])[None]
    masked = jnp.where(same_doc, mix_cols, NEG)
    raised = jnp.where(same_doc, jnp.exp(masked - row_max[..., None]), 0.0)
    return raised / row_sum[..., None]


def generic_body(tokens, segments, mix, w_value, w_out, w_in, w_back, gain_one, gain_two, out_grad):
    seq_count, col_count, model_width = tokens.shape
    head_count = mix.shape[0]
    head_dim = model_width // head_count
    f32 = jnp.float32
    bf16 = jnp.bfloat16
    gathered = (
        lax.all_gather(w_value, ROWS, axis=0, tiled=True),
        lax.all_gather(w_out, ROWS, axis=0, tiled=True),
        lax.all_gather(w_in, ROWS, axis=1, tiled=True),
        lax.all_gather(w_back, ROWS, axis=0, tiled=True),
        lax.all_gather(gain_one, ROWS, axis=0, tiled=True),
        lax.all_gather(gain_two, ROWS, axis=0, tiled=True),
    )
    wv_full, wo_full, wi_full, wb_full, gain_first, gain_second = gathered
    gain_first = gain_first.astype(f32)
    gain_second = gain_second.astype(f32)
    resid_in = tokens.astype(f32).reshape(seq_count * col_count, model_width)
    normed_one, scale_one, entry_one = normalize(resid_in, gain_first)
    values = jnp.dot(entry_one, wv_full, preferred_element_type=f32).astype(bf16)
    value_heads = values.reshape(seq_count, col_count, head_count, head_dim)
    row_segs = lax.all_gather(segments, SEQ, axis=1, tiled=True)
    mix_cols = mix.astype(f32)
    local_max, local_sum = lax.map(
        lambda fields: local_stats(mix_cols, fields[0], fields[1]), (row_segs, segments)
    )
    row_max, row_sum = joined((local_max, local_sum), SEQ, combine_stats)
    probs_low = lax.map(
        lambda fields: make_probs(mix_cols, fields[0], fields[1], fields[2], fields[3]).astype(
            bf16
        ),
        (row_segs, segments, row_max, row_sum),
    )
    products = jnp.einsum("shic,schd->ishd", probs_low, value_heads, preferred_element_type=f32)
    mixed = lax.psum_scatter(
        products.reshape(col_count * lax.axis_size(SEQ), seq_count, model_width),
        SEQ,
        scatter_dimension=0,
        tiled=True,
    )
    mixed = mixed.transpose(1, 0, 2).reshape(seq_count * col_count, model_width)
    mixed_low = mixed.astype(bf16)
    hidden_one = resid_in + jnp.dot(mixed_low, wo_full, preferred_element_type=f32)
    normed_two, scale_two, entry_two = normalize(hidden_one, gain_second)
    pre_act = jnp.dot(entry_two, wi_full, preferred_element_type=f32)
    activ, activ_back = jax.vjp(partial(jax.nn.gelu, approximate=True), pre_act)
    activ_low = activ.astype(bf16)
    branch = jnp.dot(activ_low, wb_full, preferred_element_type=f32)
    result = (hidden_one + branch).astype(bf16).reshape(tokens.shape)
    rms_residual = jnp.sqrt(jnp.mean(hidden_one * hidden_one, axis=-1)).reshape(
        seq_count, col_count
    )
    rms_sublayer = jnp.sqrt(jnp.mean(branch * branch, axis=-1)).reshape(seq_count, col_count)
    wv_back, wo_back, wi_back, wb_back = (
        lax.all_gather(w_value, ROWS, axis=0, tiled=True),
        lax.all_gather(w_out, ROWS, axis=0, tiled=True),
        lax.all_gather(w_in, ROWS, axis=1, tiled=True),
        lax.all_gather(w_back, ROWS, axis=0, tiled=True),
    )
    grad_out = out_grad.reshape(seq_count * col_count, model_width)
    grad_back = jnp.dot(activ_low.T, grad_out, preferred_element_type=f32)
    grad_activ = jnp.dot(grad_out, wb_back.T, preferred_element_type=f32)
    grad_pre = activ_back(grad_activ)[0].astype(bf16)
    grad_in = jnp.dot(entry_two.T, grad_pre, preferred_element_type=f32)
    grad_entry_two = jnp.dot(grad_pre, wi_back.T, preferred_element_type=f32)
    back_two, grad_gain_two = norm_back(grad_entry_two, normed_two, scale_two, gain_second)
    grad_hidden = grad_out.astype(f32) + back_two
    grad_hidden_low = grad_hidden.astype(bf16)
    grad_wo = jnp.dot(mixed_low.T, grad_hidden_low, preferred_element_type=f32)
    grad_mixed = jnp.dot(grad_hidden_low, wo_back.T, preferred_element_type=f32).astype(bf16)
    grad_rows = lax.all_gather(
        grad_mixed.reshape(seq_count, col_count, model_width), SEQ, axis=1, tiled=True
    )
    grad_heads = grad_rows.reshape(seq_count, -1, head_count, head_dim)

    def delta_part(fields):
        seg_row, seg_own, max_row, sum_row, grad_row, value_row = fields
        soft_probs = make_probs(mix_cols, seg_row, seg_own, max_row, sum_row)
        grad_probs = jnp.einsum("ihd,chd->hic", grad_row, value_row, preferred_element_type=f32)
        return jnp.sum(soft_probs * grad_probs, axis=-1)

    partial_delta = lax.map(
        delta_part, (row_segs, segments, row_max, row_sum, grad_heads, value_heads)
    )
    delta = lax.psum(partial_delta, SEQ)

    def seq_back(running, fields):
        seg_row, seg_own, max_row, sum_row, grad_row, value_row, delta_row = fields
        soft_probs = make_probs(mix_cols, seg_row, seg_own, max_row, sum_row)
        grad_probs = jnp.einsum("ihd,chd->hic", grad_row, value_row, preferred_element_type=f32)
        running = running + soft_probs * (grad_probs - delta_row[..., None])
        grad_value_row = jnp.einsum(
            "hic,ihd->chd", soft_probs.astype(bf16), grad_row, preferred_element_type=f32
        )
        return (running, grad_value_row)

    local_mix_grad, grad_values = lax.scan(
        seq_back,
        jnp.zeros(mix_cols.shape, f32),
        (row_segs, segments, row_max, row_sum, grad_heads, value_heads, delta),
    )
    mix_grad = lax.psum(local_mix_grad, ROWS)
    grad_values = grad_values.reshape(seq_count * col_count, model_width).astype(bf16)
    grad_wv = jnp.dot(entry_one.T, grad_values, preferred_element_type=f32)
    grad_entry_one = jnp.dot(grad_values, wv_back.T, preferred_element_type=f32)
    back_one, grad_gain_one = norm_back(grad_entry_one, normed_one, scale_one, gain_first)
    tokens_grad = (grad_hidden + back_one).reshape(tokens.shape)
    owned = (
        lax.psum_scatter(grad_wv, ROWS, scatter_dimension=0, tiled=True),
        lax.psum_scatter(grad_wo, ROWS, scatter_dimension=0, tiled=True),
        lax.psum_scatter(grad_in, ROWS, scatter_dimension=1, tiled=True),
        lax.psum_scatter(grad_back, ROWS, scatter_dimension=0, tiled=True),
        lax.psum_scatter(grad_gain_one, ROWS, scatter_dimension=0, tiled=True),
        lax.psum_scatter(grad_gain_two, ROWS, scatter_dimension=0, tiled=True),
    )
    summed = lax.psum((owned[0], owned[1], owned[2], owned[3], owned[4], owned[5]), SEQ)
    return (
        result,
        tokens_grad,
        mix_grad,
        summed[0],
        summed[1],
        summed[2],
        summed[3],
        summed[4],
        summed[5],
        rms_residual,
        rms_sublayer,
    )


F32 = jnp.float32
BF16 = jnp.bfloat16
MESH = pl.DeviceIdType.MESH
NT = (((1,), (1,)), ((), ()))
TN = (((0,), (0,)), ((), ()))
ANY = pl.BlockSpec(memory_space=pl.ANY)
RATE = 0.0925
VMEM_LIMIT = 60 * 2**20
ROW_LINK = {1: ("y", 1.0), 2: ("z", 1.0), 4: ("z", 2.0)}
SEQ_LINK = {1: ("core", 0.12), 2: ("x", 1.0), 3: ("x", 1.0)}


def tag(*parts):
    return "".join(map(str, parts))


class Copy:
    def __init__(self, copy, remote):
        self.copy, self.remote, self.done = copy, remote, False

    def recv(self):
        if not self.done:
            self.done = True
            if self.remote:
                self.copy.wait_recv()
            else:
                self.copy.wait()


class Net:
    def __init__(self, send, recv, local):
        self.send, self.recv, self.local = send, recv, local
        self.remote, self.near = [], []

    def go(self, src, dst, dev):
        i = len(self.remote)
        copy = pltpu.make_async_remote_copy(
            src_ref=src, dst_ref=dst, send_sem=self.send.at[i], recv_sem=self.recv.at[i],
            device_id=dev, device_id_type=MESH)
        copy.start()
        self.remote.append(Copy(copy, True))
        return self.remote[-1]

    def cp(self, src, dst):
        copy = pltpu.make_async_copy(src, dst, self.local.at[len(self.near)])
        copy.start()
        self.near.append(Copy(copy, False))
        return self.near[-1]

    def finish(self):
        for copy in self.near + self.remote:
            copy.recv()
        for copy in self.remote:
            copy.copy.wait_send()


class Plan:
    def __init__(self, net, r, s):
        self.net, self.r, self.s = net, r, s
        self.tasks, self.copies = [], {}

    def comm(self, name, axis, bit, mb, deps, prio, src, dst):
        link, factor = (ROW_LINK if axis == ROWS else SEQ_LINK)[bit]
        dev = {axis: (self.r if axis == ROWS else self.s) ^ bit}

        def emit():
            self.wait(deps)
            self.copies[name] = self.net.go(src(), dst(), dev)

        self.tasks.append((name, link, factor * 2 * mb / RATE, deps, prio, emit))
        return name

    def near(self, name, mb, deps, prio, src, dst):
        def emit():
            self.wait(deps)
            self.copies[name] = self.net.cp(src(), dst())

        self.tasks.append((name, "hbm", mb / 2.0, deps, prio, emit))
        return name

    def work(self, name, us, deps, prio, run):
        def emit():
            self.wait(deps)
            run()

        self.tasks.append((name, "tc", us, deps, prio, emit))
        return name

    def add(self, name, deps, to, other, us=0.12):
        def run():
            target, term = to(), other()
            target[...] = target[...] + term[...]

        return self.work(name, us, deps, -5, run)

    def wait(self, deps):
        for dep in deps:
            if dep in self.copies:
                self.copies[dep].recv()

    def solve(self):
        end, start, free, now = {}, {}, {}, 0.0
        left = list(self.tasks)
        while left:
            ready = [
                (max([free.get(t[1], 0.0)] + [end[d] for d in t[3]]), t[4], i)
                for i, t in enumerate(left) if all(d in end for d in t[3])
            ]
            first = min(ready)
            begin, _, pick = min(
                (b, p, i) for b, p, i in ready if b <= first[0] + 1e-9)
            name, link, cost, _, prio, _ = left.pop(pick)
            start[name] = (begin, link == "tc", prio)
            free[link] = begin + cost
            end[name] = begin + cost + (0.0 if link == "tc" else 2.0)
        self.start, self.end = start, end
        return sorted(self.tasks, key=lambda t: start[t[0]])

    def run(self):
        order = self.solve()
        early = [task for task in order if task[1] == "hbm" and not task[3]]
        for task in early:
            task[5]()
        greet(self.r, self.s)
        for task in order:
            if task not in early:
                task[5]()
        self.net.finish()


def greet(r, s):
    barrier = pltpu.get_barrier_semaphore()
    for bit in (1, 2, 4):
        pl.semaphore_signal(barrier, inc=1, device_id={ROWS: r ^ bit}, device_id_type=MESH)
    for bit in (1, 2, 3):
        pl.semaphore_signal(barrier, inc=1, device_id={SEQ: s ^ bit}, device_id_type=MESH)
    pl.semaphore_wait(barrier, 6)


def cut(ref, start, size):
    return ref.at[pl.ds(pl.multiple_of(start, 16), size)]


def add_gather(plan, name, src, dst, order, ways, prio, mb):
    r, s = plan.r, plan.s
    core, x = s % 2, s // 2
    n = src.shape[0] // ways
    off = {1: 0, 2: core, 4: 2 * core + x}[ways] * n
    far = (2 * core + 1 - x) * n
    part = lambda q, o: cut(src if q == 0 else dst.at[r ^ q], o, n)
    home = lambda q, o: cut(dst.at[r ^ q], o, n)
    got = {0: None}
    for stage, bit in enumerate(order):
        new = {}
        for q, dep in got.items():
            new[q ^ bit] = plan.comm(
                tag(name, q ^ bit), ROWS, bit, mb / ways, [dep] if dep else [], prio + 0.1 * stage,
                lambda q=q: part(q, off), lambda q=q: home(q, off))
        got.update(new)
    need = {q: [dep or tag(name, "0")] for q, dep in got.items()}
    for q, dep in got.items():
        if q == 0 or ways == 1:
            continue
        need[q].append(plan.comm(tag(name, "c", q), SEQ, 1, mb / ways, [dep], prio + 1,
                                 lambda q=q: part(q, off), lambda q=q: home(q, off)))
        if ways == 4:
            need[q].append(plan.comm(tag(name, "x", q), SEQ, 2, mb / ways, [dep], prio + 1,
                                     lambda q=q: part(q, off), lambda q=q: home(q, off)))
            need[q].append(plan.comm(tag(name, "f", q), SEQ, 1, mb / ways, [tag(name, "x", q)], prio + 1,
                                     lambda q=q: part(q, far), lambda q=q: home(q, far)))
    return need


HALVES = 1


def column(row):
    return jnp.broadcast_to(row, (128, 128)).T[:, :1]


def as_row(col):
    return jnp.broadcast_to(col, (128, 128)).T[:1]


def segment_layouts(seg, col, row):
    for q in range(2):
        for k in range(4):
            ids = seg[k, q:q + 1].astype(F32)
            row[q, :, k * 128:(k + 1) * 128] = ids
            col[q, k * 128:(k + 1) * 128] = column(ids)


def gain_row(gains, i):
    total = gains[0, i:i + 1].astype(F32)
    for k in range(1, 8):
        total = total + gains[k, i:i + 1].astype(F32)
    return total


def forward_kernel(tok, grd, seg, mix, wv, wo, wi, wb, gn,
                   x_o, g_o, seg_o, m_o, wv_o, wo_o, gn_o, val_o, mxd_o, iz_o, h_o, e2_o, res_o, rms_o, gi_o, gb_o,
                   send, recv, local,
                   x_v, g_v, seg_v, m_v, wv_v, wo_v, wi_v, wb_v, gn_v, val_v, mxd_v, h_v, e_v, et_v, gt_v,
                   br_v, e2_v, act_v, pg_v, gi_v, gb_v, rms_v, sc_v, sr_v):
    r, s = lax.axis_index(ROWS), lax.axis_index(SEQ)
    y, zb = r % 2, (r // 2) % 2
    net = Net(send, recv, local)
    plan = Plan(net, r, s)
    block = lambda k: pl.ds(pl.multiple_of((s ^ k) * 128, 128), 128)
    for k in (2, 3, 1):
        plan.comm(tag("seg", k), SEQ, k, 0.001, [], 0, lambda k=k: seg.at[s ^ k], lambda: seg_v.at[s])
        plan.comm(tag("tok", k), SEQ, k, 0.393, [], 5, lambda k=k: tok.at[pl.ds(2 * (s ^ k), 2)],
                  lambda: x_v.at[:, block(0)])
        plan.comm(tag("grd", k), SEQ, k, 0.393, [], 15, lambda k=k: grd.at[pl.ds(2 * (s ^ k), 2)],
                  lambda: g_v.at[:, block(0)])
    groups = 3
    mixes = []
    for g, urgent in enumerate((1.0, 4.01, 1.02)):
        heads = pl.ds(12 // groups * g, 12 // groups)
        quarter = lambda ref, a, b, heads=heads: ref.at[heads, pl.ds((2 * a + b) * 128, 128)]
        other = lambda a, b, quarter=quarter: (lambda: quarter(m_v.at[s ^ 2], a, b))
        size = 0.393 / groups
        plan.comm(tag("mixc", g), SEQ, 1, 4 * size, [], 3 + 0.01 * g, lambda heads=heads: mix.at[heads],
                  lambda heads=heads: m_v.at[s, heads])
        plan.comm(tag("mixx", g), SEQ, 2, size, [], urgent, lambda quarter=quarter: quarter(mix, y, zb),
                  lambda quarter=quarter: quarter(m_v.at[s], y, zb))
        names = ["mix0", tag("mixc", g), tag("mixx", g)]
        for name, axis, bit, dep, prio, a, b in (
                ("mixz", ROWS, 2, "mixx", 2, y, zb), ("mixy", ROWS, 1, "mixx", 2, y, zb),
                ("mixw", ROWS, 1, "mixz", 2, y, 1 - zb), ("mixp", SEQ, 1, "mixx", 3, y, zb),
                ("mixq", SEQ, 1, "mixz", 3, y, 1 - zb), ("mixr", SEQ, 1, "mixy", 3, 1 - y, zb),
                ("mixs", SEQ, 1, "mixw", 3, 1 - y, 1 - zb)):
            names.append(plan.comm(tag(name, g), axis, bit, size, [tag(dep, g)], prio + 0.01 * g, other(a, b), other(a, b)))
        mixes.append(names)
    flat = lambda got, *qs: [d for q in qs for d in got[q]]
    every = range(8)
    gn_d = add_gather(plan, "gn", gn, gn_v, [4, 2, 1], 1, 0, 0.024)
    wv_d = add_gather(plan, "wv", wv, wv_v, [4, 2, 1], 2, 1, 0.147)
    wo_d = add_gather(plan, "wo", wo, wo_v, [4, 2, 1], 2, 10, 0.147)
    wi_d = add_gather(plan, "wi", wi, wi_v, [4, 1, 2], 4, 20, 0.59)
    wb_d = add_gather(plan, "wb", wb, wb_v, [4, 2, 1], 2, 20.05, 0.59)
    for name, mb, src, dst in (
            ("tok0", 0.4, lambda: tok.at[pl.ds(2 * s, 2)], lambda: x_v.at[:, block(0)]),
            ("gn0", 0.02, lambda: gn, lambda: gn_v.at[r]), ("wv0", 0.15, lambda: wv, lambda: wv_v.at[r]),
            ("seg0", 0.01, lambda: seg.at[s], lambda: seg_v.at[s]), ("mix0", 1.5, lambda: mix, lambda: m_v.at[s]),
            ("wo0", 0.15, lambda: wo, lambda: wo_v.at[r]), ("wi0", 0.6, lambda: wi, lambda: wi_v.at[r]),
            ("wb0", 0.6, lambda: wb, lambda: wb_v.at[r]),
            ("grd0", 0.4, lambda: grd.at[pl.ds(2 * s, 2)], lambda: g_v.at[:, block(0)])):
        plan.near(name, mb, [], 0, src, dst)

    def put(name, mb, deps, src, dst):
        plan.near(name, mb, deps, 90, lambda: src, lambda: dst)

    for k in range(4):
        def values(k=k):
            x = x_v[:, block(k)].reshape(256, 768).astype(F32)
            scale = lax.rsqrt(jnp.mean(x * x, axis=-1, keepdims=True) + EPS)
            entry = (x * scale * gain_row(gn_v, 0)).astype(BF16)
            out = jnp.dot(entry, wv_v[...].reshape(768, 768), preferred_element_type=F32)
            val_v[:, block(k)] = out.astype(BF16).reshape(2, 128, 768)

        plan.work(tag("val", k), 1.2, [tag("tok", k)] + flat(wv_d, *every) + flat(gn_d, *every), 1, values)
    plan.work("segs", 1.0, [tag("seg", k) for k in range(4)], 0, lambda: segment_layouts(seg_v, sc_v, sr_v))
    for k in range(4):
        def turn(k=k):
            for q in range(2):
                at = pl.ds(pl.multiple_of(q * 512 + (s ^ k) * 128, 128), 128)
                gt_v[:, at] = g_v[q, block(k)].T

        plan.work(tag("gt", k), 0.6, [tag("grd", k)], 9, turn)
    lane = lax.broadcasted_iota(jnp.int32, (1, 128), 1)
    last = ["segs"] + [tag("val", k) for k in range(4)]
    for g in range(groups):
        def mixing(g=g):
            @pl.loop(g * (6 // groups), (g + 1) * (6 // groups))
            def _(p):
                lanes = pl.ds(pl.multiple_of(p * 128, 128), 128)
                raised = [exp_mix(m_v, 2 * p + hh).astype(BF16) for hh in range(2)]
                for q in range(2):
                    same = sc_v[q] == sr_v[q]
                    rhs = jnp.concatenate([val_v[q, :, lanes], jnp.ones((512, 128), BF16)], axis=1)
                    both = [jnp.dot(jnp.where(same, e, jnp.zeros_like(e)), rhs, preferred_element_type=F32)
                            for e in raised]
                    total = jnp.where(lane < 64, both[0][:, :128], both[1][:, :128])
                    inverse = 1.0 / jnp.where(lane < 64, both[0][:, 128:], both[1][:, 128:])
                    mxd_v[q, :, lanes] = (total * inverse).astype(BF16)
                    br_v[q * 512:(q + 1) * 512, lanes] = inverse

        last = [plan.work(tag("mf", g), 10.0 / groups, last + mixes[g], 1, mixing)]
    put("iz_out", 1.5, last, br_v, iz_o)
    for q in range(2):
        def project(q=q):
            @pl.loop(0, 4)
            def _(k):
                inside = pl.ds(pl.multiple_of(k * 128, 128), 128)
                at = pl.ds(pl.multiple_of(q * 512 + k * 128, 128), 128)
                h = x_v[q, inside].astype(F32) + jnp.dot(
                    mxd_v[q, inside], wo_v[...].reshape(768, 768), preferred_element_type=F32)
                square = jnp.mean(h * h, axis=-1, keepdims=True)
                h_v[at] = h
                entry = (h * lax.rsqrt(square + EPS) * gain_row(gn_v, 1)).astype(BF16)
                e_v[at] = entry
                et_v[:, at] = entry.T
                rms_v[k, q:q + 1] = as_row(jnp.sqrt(square))

        last = [plan.work(tag("out", q), 2.5, last + flat(wo_d, *every), 1, project)]
    put("h_out", 1.5, last, h_v, h_o)
    c0, c1 = 0.7978845608028654, 0.044715
    step = 256
    for i, (a, b) in enumerate(((0, 4), (1, 5), (2, 6), (3, 7))):
        for half in range(HALVES):
            def feed(a=a, b=b, i=i, half=half):
                weights = jnp.concatenate([wi_v[r ^ a], wi_v[r ^ b]], axis=1)
                back = jnp.concatenate([wb_v[r ^ a], wb_v[r ^ b]], axis=0)

                @pl.loop(half * 4 // HALVES, (half + 1) * 4 // HALVES)
                def _(t):
                    at = pl.ds(pl.multiple_of(t * step, step), step)
                    inner = pl.ds(pl.multiple_of((t % 2) * step, step), step)
                    pre = jnp.dot(e_v[at], weights, preferred_element_type=F32)
                    up = lax.dot_general(g_v[t // 2, inner], back, NT, preferred_element_type=F32)
                    square = pre * pre
                    th = jnp.tanh(pre * (c0 + (c0 * c1) * square))
                    gate = 0.5 + 0.5 * th
                    act = (pre * gate).astype(BF16)
                    slope = gate + pre * (1.0 - th * th) * ((0.5 * c0) + (1.5 * c0 * c1) * square)
                    pg = (up * slope).astype(BF16)
                    act_v[at] = act
                    pg_v[at] = pg
                    branch = jnp.dot(act, back, preferred_element_type=F32)
                    e2 = lax.dot_general(pg, weights, NT, preferred_element_type=F32)
                    if i == 0:
                        br_v[at] = branch
                        e2_v[at] = e2
                    else:
                        br_v[at] += branch
                        e2_v[at] += e2

            need = flat(wi_d, a, b) + flat(wb_d, a, b) + [tag("grd", k) for k in range(4)] + ["iz_out"]
            last = [plan.work(tag("ff", i, half), 7.0 / HALVES, last + need, 1, feed)]

        def weight_grads(i=i):
            slot = i % 2

            @pl.loop(0, 3)
            def _(t):
                at = pl.ds(pl.multiple_of(t * 256, 256), 256)
                gi = jnp.dot(et_v[at], pg_v[...], preferred_element_type=F32).astype(BF16)
                gb = jnp.dot(gt_v[at], act_v[...], preferred_element_type=F32).astype(BF16)
                for q in range(2):
                    gi_v[slot, q, at] = gi[:, q * 384:(q + 1) * 384]
                    gb_v[slot, q, at] = gb[:, q * 384:(q + 1) * 384]

        free = [tag("g", n, "_out", i - 2, q) for n in "ib" for q in range(2)] if i >= 2 else []
        last = [plan.work(tag("fg", i), 3.5, last + free + [tag("gt", k) for k in range(4)], 1, weight_grads)]
        for q, owner in enumerate((a, b)):
            put(tag("gi_out", i, q), 0.3, last, gi_v.at[i % 2, q], gi_o.at[r ^ owner])
            put(tag("gb_out", i, q), 0.3, last, gb_v.at[i % 2, q], gb_o.at[r ^ owner])

    def finish():
        @pl.loop(0, 8)
        def _(t):
            at = pl.ds(pl.multiple_of(t * 128, 128), 128)
            q, k = t // 4, t % 4
            branch = br_v[at]
            e_v[at] = (h_v[at] + branch).astype(BF16)
            rms_v[k, pl.ds(2 + q, 1)] = as_row(jnp.sqrt(jnp.mean(branch * branch, axis=-1, keepdims=True)))

    last = [plan.work("fin", 2.0, last, 1, finish)]
    put("e2_out", 1.5, last, e2_v, e2_o)
    put("res_out", 0.8, last, e_v, res_o)
    put("rms_out", 0.1, last, rms_v, rms_o)
    toks, grds = [tag("tok", k) for k in range(4)], [tag("grd", k) for k in range(4)]
    put("x_out", 0.8, toks, x_v, x_o)
    put("g_out", 0.8, grds, g_v, g_o)
    put("seg_out", 0.1, ["segs"], seg_v, seg_o)
    put("m_out", 3.0, sum(mixes, []), m_v, m_o)
    put("wv_out", 0.6, flat(wv_d, *every), wv_v, wv_o)
    put("wo_out", 0.6, flat(wo_d, *every), wo_v, wo_o)
    put("gn_out", 0.1, flat(gn_d, *every), gn_v, gn_o)
    put("val_out", 0.8, [tag("val", k) for k in range(4)], val_v, val_o)
    put("mxd_out", 0.8, [tag("mf", groups - 1)], mxd_v, mxd_o)
    plan.run()


def forward_all(tok, grd, seg, mix, wv, wo, wi, wb, gn):
    sd = jax.ShapeDtypeStruct
    rows, flat, big = (2, 512, 768), (1024, 768), (8, 768, 384)
    mixes, square, gains = (4, 12, 512, 128), (8, 96, 768), (8, 16, 768)
    outs = [sd(rows, BF16), sd(rows, BF16), sd((4, 2, 128), jnp.int32), sd(mixes, BF16), sd(square, BF16),
            sd(square, BF16), sd(gains, BF16), sd(rows, BF16), sd(rows, BF16), sd(flat, F32), sd(flat, F32),
            sd(flat, F32), sd(flat, BF16), sd((4, 8, 128), F32), sd(big, BF16), sd(big, BF16)]
    dma = pltpu.SemaphoreType.DMA
    v = lambda *a: pltpu.VMEM(a, BF16)
    f = lambda *a: pltpu.VMEM(a, F32)
    turned = (768, 1024)
    scratch = [v(*rows), v(*rows), pltpu.VMEM((4, 2, 128), jnp.int32), v(*mixes), v(*square), v(*square), v(*big),
               v(8, 384, 768), v(*gains), v(*rows), v(*rows), f(*flat), v(*flat), v(*turned), v(*turned),
               f(*flat), f(*flat), v(*flat), v(*flat), v(2, 2, 768, 384), v(2, 2, 768, 384), f(4, 8, 128),
               f(2, 512, 1), f(2, 1, 512)]
    return pl.pallas_call(
        forward_kernel, out_shape=outs, in_specs=[ANY] * 9, out_specs=[ANY] * len(outs),
        scratch_shapes=[dma((128,)), dma((128,)), dma((48,))] + scratch,
        compiler_params=pltpu.CompilerParams(collective_id=0, has_side_effects=True, vmem_limit_bytes=VMEM_LIMIT),
    )(tok, grd, seg, mix, wv, wo, wi, wb, gn)


def exp_mix(m_ref, hh):
    return jnp.concatenate([jnp.exp(m_ref[k, hh].astype(F32)) for k in range(4)], axis=1)


class Reduce:
    def __init__(self, plan, name, src, made, local, bufs, out, order, first, prio, mb, pieces):
        self.plan, self.name, self.src, self.local, self.bufs = plan, name, src, local, bufs
        r, s = plan.r, plan.s
        self.core, self.x = s % 2, s // 2
        self.n = src.shape[1] // 2
        half = mb / 2
        own, near, across, rows, final = bufs
        last = {}
        for q in pieces:
            deps = made[q]
            if not local:
                plan.near(tag(name, "l", q), half, deps, prio, lambda q=q: self.half(src.at[r ^ q], self.core),
                          lambda q=q: own.at[q])
            plan.comm(tag(name, "c", q), SEQ, 1, half, deps, prio, lambda q=q: self.half(src.at[r ^ q], 1 - self.core),
                      lambda q=q: near.at[q])
            last[q] = plan.add(tag(name, "a", q), [tag(name, "c", q)] + (deps if local else [tag(name, "l", q)]),
                               lambda q=q: self.mine(q), lambda q=q: near.at[q])
        if first:
            half = half / 2
            for q in pieces:
                plan.comm(tag(name, "X", q), SEQ, 2, half, [last[q]], prio,
                          lambda q=q: self.quarter(self.mine(q), 1 - self.x), lambda q=q: across.at[q])
                last[q] = plan.add(tag(name, "A", q), [tag(name, "X", q), last[q]],
                                   lambda q=q: self.quarter(self.mine(q), self.x), lambda q=q: across.at[q])
        item = (lambda q: self.quarter(self.mine(q), self.x)) if first else self.mine
        keep, slot = list(range(8)), 0
        for stage, bit in enumerate(order):
            for q in [q for q in pieces if q in keep and q & bit]:
                plan.comm(tag(name, "r", q), ROWS, bit, half, [last[q]], prio + 0.1 * stage,
                          lambda q=q: item(q), lambda slot=slot: rows.at[slot])
                last[q ^ bit] = plan.add(tag(name, "b", q), [tag(name, "r", q), last[q ^ bit]],
                                         lambda q=q ^ bit: item(q), lambda slot=slot: rows.at[slot])
                slot += 1
            keep = [q for q in keep if not q & bit]
        if first:
            def widen():
                self.quarter(final, self.x)[...] = item(0)[...].astype(F32)

            plan.work(tag(name, "t"), 0.2, [last[0]], -5, widen)
            plan.comm(tag(name, "x"), SEQ, 2, 2 * half, [tag(name, "t")], prio + 0.5,
                      lambda: self.quarter(final, self.x), lambda: self.quarter(final, self.x))
            for name2, dep, which in (("m", "t", 0), ("o", "x", 1)):
                side = (lambda which=which: self.quarter(final, self.x if which == 0 else 1 - self.x))
                place = (lambda which=which: self.quarter(self.half(out, self.core),
                                                          self.x if which == 0 else 1 - self.x))
                plan.near(tag(name, name2), mb / 2, [tag(name, dep)], prio, side, place)
                plan.comm(tag(name, name2, "k"), SEQ, 1, mb / 2, [tag(name, dep)], prio, side, place)
        else:
            plan.comm(tag(name, "x"), SEQ, 2, half, [last[0]], prio + 0.5, lambda: item(0), lambda: across)

            def total():
                final[...] = item(0)[...].astype(F32) + across[...].astype(F32)

            plan.work(tag(name, "t"), 0.2, [tag(name, "x"), last[0]], -5, total)
            plan.near(tag(name, "o"), mb, [tag(name, "t")], prio, lambda: final, lambda: self.half(out, self.core))
            plan.comm(tag(name, "k"), SEQ, 1, mb, [tag(name, "t")], prio, lambda: final, lambda: self.half(out, self.core))

    def half(self, ref, which):
        return cut(ref, which * self.n, self.n)

    def quarter(self, ref, which):
        return cut(ref, which * (self.n // 2), self.n // 2)

    def mine(self, q):
        return self.half(self.src.at[self.plan.r ^ q], self.core) if self.local else self.bufs[0].at[q]


def backward_kernel(x_i, g_i, seg_i, m_i, wv_i, wo_i, gn_i, val_i, mxd_i, iz_i, h_i, e2_i, res_i, rms_i, gi, gb,
                    res_o, tgr_o, gi_o, gb_o, go_o, gv_o, gn_o, mg_o, rms_o, send, recv, local,
                    x_v, g_v, seg_v, m_v, wv_v, wo_v, gn_v, val_v, mxd_v, iz_v, h_v, q_v, hl_v, go_v, gv_v,
                    sc_v, sr_v, n0, n1, m1, m3, m4, t0, t1,
                    i0, i1, i2, i3, i4, b0, b1, b2, b3, b4, o0, o1, o2, o3, o4, v0, v1, v2, v3, v4):
    r, s = lax.axis_index(ROWS), lax.axis_index(SEQ)
    core, x = s % 2, s // 2
    net = Net(send, recv, local)
    plan = Plan(net, r, s)
    place = lambda k: pl.ds(pl.multiple_of((s ^ k) * 128, 128), 128)
    for name, mb, prio, src, dst in (
            ("h", 3.1, 0, h_i, h_v), ("e2", 3.1, 1, e2_i, q_v), ("g", 1.6, 2, g_i, g_v), ("gn", 0.1, 0, gn_i, gn_v),
            ("wo", 1.2, 3, wo_i, wo_v), ("seg", 0.1, 3, seg_i, seg_v), ("mxd", 1.6, 4, mxd_i, mxd_v),
            ("val", 1.6, 4, val_i, val_v), ("iz", 3.1, 4, iz_i, iz_v), ("m", 6.3, 5, m_i, m_v),
            ("x", 1.6, 6, x_i, x_v), ("wv", 1.2, 6, wv_i, wv_v)):
        plan.near(tag("in_", name), mb, [], prio, lambda src=src: src, lambda dst=dst: dst)
    for k in (2, 3, 1):
        plan.comm(tag("res", k), SEQ, k, 0.393, [], 2, lambda k=k: res_i.at[:, place(k)], lambda: res_o.at[pl.ds(2 * s, 2)])
        plan.comm(tag("rms", k), SEQ, k, 0.004, [], 3, lambda k=k: rms_i.at[s ^ k], lambda: rms_o.at[s])
    for name, src, buf, dst in (("res", res_i.at[:, place(0)], t0, res_o.at[pl.ds(2 * s, 2)]),
                                ("rms", rms_i.at[s], t1, rms_o.at[s])):
        plan.near(tag(name, "i"), 0.4, [], 9, lambda src=src: src, lambda buf=buf: buf)
        plan.near(tag(name, "o"), 0.4, [tag(name, "i")], 9, lambda buf=buf: buf, lambda dst=dst: dst)

    def start():
        n0[...] = jnp.zeros_like(n0)
        segment_layouts(seg_v, sc_v, sr_v)

    plan.work("segs", 1.0, ["in_seg"], -2, start)
    last = ["segs"] + [tag("in_", n) for n in ("h", "e2", "g", "gn", "wo")]
    for part in range(2):
        def post(part=part):
            @pl.loop(0, 4)
            def _(k):
                at = pl.ds(pl.multiple_of(part * 512 + k * 128, 128), 128)
                inside = pl.ds(pl.multiple_of(k * 128, 128), 128)
                h = h_v[at]
                scale = lax.rsqrt(jnp.mean(h * h, axis=-1, keepdims=True) + EPS)
                normed = h * scale
                up = q_v[at]
                n0[0, 1:2] += jnp.sum(up * normed, axis=0, keepdims=True)
                scaled = up * gain_row(gn_v, 1)
                back = scale * (scaled - normed * jnp.mean(scaled * normed, axis=-1, keepdims=True))
                grad = g_v[part, inside].astype(F32) + back
                q_v[at] = grad
                grad_low = grad.astype(BF16)
                hl_v[at] = grad_low
                g_v[part, inside] = lax.dot_general(
                    grad_low, wo_v[...].reshape(768, 768), NT, preferred_element_type=F32).astype(BF16)

        last = [plan.work(tag("post", part), 3.0, last, -1, post)]

    lane = lax.broadcasted_iota(jnp.int32, (1, 128), 1)
    orders = MIX_ORDERS
    groups = len(orders)
    heads = 12 // groups
    for g, order in enumerate(orders):
        def mixing(g=g):
            @pl.loop(g * heads // 2, (g + 1) * heads // 2)
            def _(p):
                lanes = pl.ds(pl.multiple_of(p * 128, 128), 128)
                raised = [exp_mix(m_v, 2 * p + hh) for hh in range(2)]
                low = [e.astype(BF16) for e in raised]
                acc = [None, None]
                for q in range(2):
                    same = sc_v[q] == sr_v[q]
                    scaled = g_v[q, :, lanes].astype(F32) * iz_v[q * 512:(q + 1) * 512, lanes]
                    inner = scaled * mxd_v[q, :, lanes].astype(F32)
                    grads = []
                    for hh in range(2):
                        mine = (lane < 64) if hh == 0 else (lane >= 64)
                        delta = jnp.sum(jnp.where(mine, inner, 0.0), axis=1, keepdims=True)
                        lhs = jnp.where(mine, scaled, 0.0).astype(BF16)
                        back = lax.dot_general(lhs, val_v[q, :, lanes], NT, preferred_element_type=F32)
                        term = jnp.where(same, back - delta, 0.0)
                        acc[hh] = term if q == 0 else acc[hh] + term
                        masked = jnp.where(same, low[hh], jnp.zeros_like(low[hh]))
                        grads.append(lax.dot_general(masked, scaled.astype(BF16), TN, preferred_element_type=F32))
                    val_v[q, :, lanes] = jnp.where(lane < 64, grads[0], grads[1]).astype(BF16)
                for hh in range(2):
                    out = (acc[hh] * raised[hh]).astype(BF16)
                    for k in range(4):
                        m_v[k, 2 * p + hh] = out[:, k * 128:(k + 1) * 128]

        last = [plan.work(tag("mb", g), 2.7 * heads / 2, last + ["in_m", "in_val", "in_iz", "in_mxd"], -1, mixing)]
        mine = pl.ds(g * heads, heads)
        mb = 0.01638 * heads
        prio = MIX_URGENCY[g]
        done = {}
        block = lambda h, side, mine=mine: m_v.at[2 * (x ^ h) + (core if side == 0 else 1 - core), mine]
        for h in range(2):
            plan.comm(tag("mg", g, "c", h), SEQ, 1, 8 * mb, last, prio, lambda h=h, block=block: block(h, 1),
                      lambda h=h, mine=mine: m1.at[h, mine])
            made = plan.add(tag("mg", g, "a", h), [tag("mg", g, "c", h)] + last, lambda h=h, block=block: block(h, 0),
                            lambda h=h, mine=mine: m1.at[h, mine], 0.3)
            for q in range(8):
                done[h, q] = made
        rows = lambda q: pl.ds(pl.multiple_of((r ^ q) * 64, 64), 64)
        item = lambda h, q, mine=mine: m_v.at[2 * (x ^ h) + core, mine, rows(q)]
        keep, slot = [(h, q) for h in range(2) for q in range(8)], 0
        for bit in order:
            hit = (lambda h, q: h) if bit == 0 else (lambda h, q, bit=bit: q & bit)
            for h, q in [k for k in keep if hit(*k)]:
                to = (0, q) if bit == 0 else (h, q ^ bit)
                name = tag("mg", g, "r", h, q)
                plan.comm(name, ROWS if bit else SEQ, bit or 2, mb, [done[h, q]], prio,
                          lambda h=h, q=q, item=item: item(h, q), lambda slot=slot, mine=mine: m3.at[slot, mine])
                done[to] = plan.add(name + "d", [name, done[to]], lambda to=to, item=item: item(*to),
                                    lambda slot=slot, mine=mine: m3.at[slot, mine])
                slot += 1
            keep = [k for k in keep if not hit(*k)]

        def final(mine=mine, item=item):
            m4[mine, rows(0)] = item(0, 0)[...]

        got = {0: plan.work(tag("mg", g, "f"), 0.1, [done[0, 0]], -5, final)}
        for bit in [b for b in reversed(order) if b]:
            new = {}
            for q, dep in got.items():
                part = lambda q=q, mine=mine: m4.at[mine, rows(q)]
                new[q ^ bit] = plan.comm(tag("mg", g, "g", q ^ bit), ROWS, bit, mb, [dep], prio, part, part)
            got.update(new)
        plan.near(tag("mg", g, "o"), 0.4, list(got.values()), 0, lambda mine=mine: m4.at[mine], lambda mine=mine: mg_o.at[mine])
    def out_grad():
        @pl.loop(0, 2)
        def _(t):
            lanes = pl.ds(pl.multiple_of(t * 384, 128), 384)
            grad = lax.dot_general(mxd_v[...].reshape(1024, 768), hl_v[:, lanes], TN, preferred_element_type=F32)
            go_v[:, :, lanes] = grad.astype(BF16).reshape(8, 96, 384)

    last = [plan.work("go", 2.5, last, -1, out_grad)]
    go_made = last
    for k in (2, 3, 1, 0):
        def tokens(k=k):
            for q in range(2):
                at = pl.ds(pl.multiple_of(q * 512 + (s ^ k) * 128, 128), 128)
                up = lax.dot_general(val_v[q, place(k)], wv_v[...].reshape(768, 768), NT, preferred_element_type=F32)
                xs = x_v[q, place(k)].astype(F32)
                scale = lax.rsqrt(jnp.mean(xs * xs, axis=-1, keepdims=True) + EPS)
                normed = xs * scale
                gain = gain_row(gn_v, 0)
                hl_v[at] = (normed * gain).astype(BF16)
                n0[0, 0:1] += jnp.sum(up * normed, axis=0, keepdims=True)
                scaled = up * gain
                back = scale * (scaled - normed * jnp.mean(scaled * normed, axis=-1, keepdims=True))
                x_v[q, place(k)] = (q_v[at] + back).astype(BF16)

        last = [plan.work(tag("tok", k), 1.2, last + ["in_x", "in_wv"], -1, tokens)]
        if k:
            plan.comm(tag("tgr", k), SEQ, k, 0.393, last, 30, lambda k=k: x_v.at[:, place(k)],
                      lambda: tgr_o.at[pl.ds(2 * s, 2)])
        else:
            plan.near("tgro", 0.4, last, 9, lambda: x_v.at[:, place(0)], lambda: tgr_o.at[pl.ds(2 * s, 2)])
    tok_done = last

    def value_grad():
        @pl.loop(0, 2)
        def _(t):
            lanes = pl.ds(pl.multiple_of(t * 384, 128), 384)
            grad = lax.dot_general(hl_v[...], val_v[:, :, lanes].reshape(1024, 384), TN, preferred_element_type=F32)
            gv_v[:, :, lanes] = grad.astype(BF16).reshape(8, 96, 384)

    gv_made = [plan.work("gv", 2.5, last, -1, value_grad)]
    every = range(8)
    Reduce(plan, "gi", gi, {q: [] for q in every}, False, (i0, i1, i2, i3, i4), gi_o, [1, 2, 4], True, 10, 0.59, HIGH)
    Reduce(plan, "gb", gb, {q: [] for q in every}, False, (b0, b1, b2, b3, b4), gb_o, [1, 2, 4], False, 4, 0.59, FAR)
    Reduce(plan, "go", go_v, {q: go_made for q in every}, True, (o0, o1, o2, o3, o4), go_o, [1, 2, 4], False, 2, 0.147, ODD)
    Reduce(plan, "gv", gv_v, {q: gv_made for q in every}, True, (v0, v1, v2, v3, v4), gv_o, [1, 2, 4], False, 13, 0.147, HIGH)
    last = tok_done
    for i, (axis, bit) in enumerate(((SEQ, 1), (SEQ, 2), (ROWS, 1), (ROWS, 2), (ROWS, 4))):
        plan.comm(tag("gn", i), axis, bit, 0.024, last, 0, lambda i=i: n0.at[i], lambda i=i: n1.at[i])

        def add(i=i):
            n0[i + 1] = n0[i] + n1[i]

        last = [plan.work(tag("gna", i), 0.1, [tag("gn", i)] + last, -5, add)]
    plan.near("gno", 0.02, last, 0, lambda: n0.at[5], lambda: gn_o)
    plan.run()


MIX_ORDERS = ((1, 0, 2, 4), (0, 1, 2, 4), (0, 1, 2, 4))
MIX_URGENCY = (0.0, 5.01, 12.02)
ODD, HIGH, FAR = (3, 7, 1, 5, 2, 6, 4, 0), (6, 7, 2, 3, 4, 5, 0, 1), (7, 3, 5, 1, 6, 2, 4, 0)


def backward_all(*args):
    sd = jax.ShapeDtypeStruct
    outs = [sd((8, 128, 768), BF16), sd((8, 128, 768), BF16), sd((768, 384), F32), sd((768, 384), F32),
            sd((96, 768), F32), sd((96, 768), F32), sd((8, 768), F32), sd((12, 512, 128), BF16), sd((4, 8, 128), F32)]
    dma = pltpu.SemaphoreType.DMA
    v = lambda *a: pltpu.VMEM(a, BF16)
    f = lambda *a: pltpu.VMEM(a, F32)
    big, piece, small = (384, 384), (192, 384), (48, 768)
    rows, flat = (2, 512, 768), (1024, 768)
    scratch = [v(*rows), v(*rows), pltpu.VMEM((4, 2, 128), jnp.int32), v(4, 12, 512, 128), v(8, 96, 768), v(8, 96, 768),
               v(8, 16, 768), v(*rows), v(*rows), f(*flat), f(*flat), f(*flat), v(*flat), v(8, 96, 768),
               v(8, 96, 768), f(2, 512, 1), f(2, 1, 512), f(6, 8, 768), f(5, 8, 768),
               v(2, 12, 512, 128), v(15, 12, 64, 128), v(12, 512, 128), v(2, 128, 768), f(8, 128)]
    scratch += [v(8, *big), v(8, *big), v(8, *piece), v(7, *piece), f(*big)]
    scratch += [v(8, *big), v(8, *big), v(*big), v(7, *big), f(*big)]
    for _ in range(2):
        scratch += [v(16, 128), v(8, *small), v(*small), v(7, *small), f(*small)]
    return pl.pallas_call(
        backward_kernel, out_shape=outs, in_specs=[ANY] * len(args), out_specs=[ANY] * len(outs),
        scratch_shapes=[dma((200,)), dma((200,)), dma((64,))] + scratch,
        compiler_params=pltpu.CompilerParams(collective_id=1, has_side_effects=True, vmem_limit_bytes=67043328),
    )(*args)


def own_gains(r, first, second):
    row = lax.broadcasted_iota(jnp.int32, (16, 8, 96), 0)
    owner = lax.broadcasted_iota(jnp.int32, (16, 8, 96), 1)
    both = jnp.where(row == 0, first, jnp.where(row == 1, second, jnp.zeros_like(second)))
    return jnp.where(owner == r, both, jnp.zeros_like(both)).reshape(16, 768)


def final_kernel(res, tgr, mg, gv, go, gi, gb, res_o, tgr_o, mg_o, gv_o, go_o, gi_o, gb_o):
    for src, dst in ((res, res_o), (gv, gv_o), (go, go_o), (gi, gi_o)):
        dst[...] = src[...]
    tgr_o[...] = tgr[...].astype(F32)
    mg_o[...] = mg[...].astype(F32)
    gb_o[...] = gb[...].T


def final_types(*args):
    sd = jax.ShapeDtypeStruct
    plain = lambda *b: pl.BlockSpec(b, lambda i: (i,) + (0,) * (len(b) - 1))
    tok, mix, small, wide = plain(2, 128, 768), plain(3, 512, 128), plain(24, 768), plain(192, 384)
    side = pl.BlockSpec((768, 128), lambda i: (0, jnp.minimum(i, 2)))
    turned = pl.BlockSpec((128, 768), lambda i: (jnp.minimum(i, 2), 0))
    return pl.pallas_call(
        final_kernel, grid=(4,), in_specs=[tok, tok, mix, small, small, wide, side],
        out_specs=[tok, tok, mix, small, small, wide, turned],
        out_shape=[sd((8, 128, 768), BF16), sd((8, 128, 768), F32), sd((12, 512, 128), F32), sd((96, 768), F32),
                   sd((96, 768), F32), sd((768, 384), F32), sd((384, 768), F32)],
        compiler_params=pltpu.CompilerParams(vmem_limit_bytes=VMEM_LIMIT))(*args)


def fast_body(tokens, segments, mix, w_value, w_out, w_in, w_back, gain_one, gain_two, out_grad):
    r, s = lax.axis_index(ROWS), lax.axis_index(SEQ)
    gains = own_gains(r, gain_one, gain_two)
    (x_rows, grad_rows, seg_all, mix_all, wv, wo, gains_all, values, mixed, inverse, hidden_one, grad_entry_two,
     result, rms, grad_in, grad_back) = forward_all(
        tokens, out_grad, segments.reshape(4, 2, 128), mix, w_value, w_out, w_in, w_back, gains)
    res, tgr, gi, gb, go, gv, gn, mg, rms = backward_all(
        x_rows, grad_rows, seg_all, mix_all, wv, wo, gains_all, values, mixed, inverse, hidden_one, grad_entry_two,
        result.reshape(2, 512, 768), rms, grad_in, grad_back)
    own = lax.dynamic_slice(gn, (0, r * 96), (2, 96))
    rms = rms[:, :4].reshape(4, 2, 2, 128)
    rms = rms.transpose(1, 0, 2, 3).reshape(2, 8, 128)
    res, tgr, mg, gv, go, gi, gb = final_types(res, tgr, mg, gv, go, gi, gb)
    return (res, tgr, mg, gv, go, gi, gb, own[0], own[1], rms[0], rms[1])


def solution(mesh):
    in_specs = (
        P(ROWS, SEQ, None),
        P(ROWS, SEQ),
        P(None, None, SEQ),
        P(ROWS, None),
        P(ROWS, None),
        P(None, ROWS),
        P(ROWS, None),
        P(ROWS),
        P(ROWS),
        P(ROWS, SEQ, None),
    )
    out_specs = (
        P(ROWS, SEQ, None),
        P(ROWS, SEQ, None),
        P(None, None, SEQ),
        P(ROWS, None),
        P(ROWS, None),
        P(None, ROWS),
        P(ROWS, None),
        P(ROWS),
        P(ROWS),
        P(ROWS, SEQ),
        P(ROWS, SEQ),
    )
    shape = dict(mesh.shape)
    body = fast_body if shape[ROWS] == 8 and shape[SEQ] == 4 else generic_body
    return jax.shard_map(body, mesh=mesh, in_specs=in_specs, out_specs=out_specs, check_vma=False)
```

```python
import functools
from functools import partial

import jax
import jax.numpy as jnp
from jax import lax
from jax.experimental import pallas as pl
from jax.experimental.pallas import tpu as pltpu
from jax.sharding import PartitionSpec as P

ROWS, SEQ = "rows", "seq"
NEG = -1e30
EPS = 1e-06


def joined(part, axis, combine):
    gathered = jax.tree.map(lambda a: lax.all_gather(a, axis), part)

    def take(source):
        return jax.tree.map(lambda a: lax.dynamic_index_in_dim(a, source, 0, False), gathered)

    return lax.fori_loop(
        1, lax.axis_size(axis), lambda source, state: combine(state, take(source)), take(0)
    )


def normalize(inputs, gain):
    scale = lax.rsqrt(jnp.mean(inputs * inputs, axis=-1, keepdims=True) + EPS)
    normed = inputs * scale
    return (normed, scale, (normed * gain).astype(jnp.bfloat16))


def norm_back(upstream, normed, scale, gain):
    scaled = upstream * gain
    back = scale * (scaled - normed * jnp.mean(scaled * normed, axis=-1, keepdims=True))
    return (back, jnp.sum(upstream * normed, axis=0))


def combine_stats(first, second):
    max_first, sum_first = first
    max_second, sum_second = second
    row_max = jnp.maximum(max_first, max_second)
    return (
        row_max,
        sum_first * jnp.exp(max_first - row_max) + sum_second * jnp.exp(max_second - row_max),
    )


def local_stats(mix_cols, row_segs, own_segs):
    same_doc = (row_segs[:, None] == own_segs[None, :])[None]
    masked = jnp.where(same_doc, mix_cols, NEG)
    row_max = jnp.max(masked, axis=-1)
    row_sum = jnp.sum(jnp.where(same_doc, jnp.exp(masked - row_max[..., None]), 0.0), axis=-1)
    return (row_max, row_sum)


def make_probs(mix_cols, row_segs, own_segs, row_max, row_sum):
    same_doc = (row_segs[:, None] == own_segs[None, :])[None]
    masked = jnp.where(same_doc, mix_cols, NEG)
    raised = jnp.where(same_doc, jnp.exp(masked - row_max[..., None]), 0.0)
    return raised / row_sum[..., None]


def generic_body(tokens, segments, mix, w_value, w_out, w_in, w_back, gain_one, gain_two, out_grad):
    seq_count, col_count, model_width = tokens.shape
    head_count = mix.shape[0]
    head_dim = model_width // head_count
    f32 = jnp.float32
    bf16 = jnp.bfloat16
    gathered = (
        lax.all_gather(w_value, ROWS, axis=0, tiled=True),
        lax.all_gather(w_out, ROWS, axis=0, tiled=True),
        lax.all_gather(w_in, ROWS, axis=1, tiled=True),
        lax.all_gather(w_back, ROWS, axis=0, tiled=True),
        lax.all_gather(gain_one, ROWS, axis=0, tiled=True),
        lax.all_gather(gain_two, ROWS, axis=0, tiled=True),
    )
    wv_full, wo_full, wi_full, wb_full, gain_first, gain_second = gathered
    gain_first = gain_first.astype(f32)
    gain_second = gain_second.astype(f32)
    resid_in = tokens.astype(f32).reshape(seq_count * col_count, model_width)
    normed_one, scale_one, entry_one = normalize(resid_in, gain_first)
    values = jnp.dot(entry_one, wv_full, preferred_element_type=f32).astype(bf16)
    value_heads = values.reshape(seq_count, col_count, head_count, head_dim)
    row_segs = lax.all_gather(segments, SEQ, axis=1, tiled=True)
    mix_cols = mix.astype(f32)
    local_max, local_sum = lax.map(
        lambda fields: local_stats(mix_cols, fields[0], fields[1]), (row_segs, segments)
    )
    row_max, row_sum = joined((local_max, local_sum), SEQ, combine_stats)
    probs_low = lax.map(
        lambda fields: make_probs(mix_cols, fields[0], fields[1], fields[2], fields[3]).astype(
            bf16
        ),
        (row_segs, segments, row_max, row_sum),
    )
    products = jnp.einsum("shic,schd->ishd", probs_low, value_heads, preferred_element_type=f32)
    mixed = lax.psum_scatter(
        products.reshape(col_count * lax.axis_size(SEQ), seq_count, model_width),
        SEQ,
        scatter_dimension=0,
        tiled=True,
    )
    mixed = mixed.transpose(1, 0, 2).reshape(seq_count * col_count, model_width)
    mixed_low = mixed.astype(bf16)
    hidden_one = resid_in + jnp.dot(mixed_low, wo_full, preferred_element_type=f32)
    normed_two, scale_two, entry_two = normalize(hidden_one, gain_second)
    pre_act = jnp.dot(entry_two, wi_full, preferred_element_type=f32)
    activ, activ_back = jax.vjp(partial(jax.nn.gelu, approximate=True), pre_act)
    activ_low = activ.astype(bf16)
    branch = jnp.dot(activ_low, wb_full, preferred_element_type=f32)
    result = (hidden_one + branch).astype(bf16).reshape(tokens.shape)
    rms_residual = jnp.sqrt(jnp.mean(hidden_one * hidden_one, axis=-1)).reshape(
        seq_count, col_count
    )
    rms_sublayer = jnp.sqrt(jnp.mean(branch * branch, axis=-1)).reshape(seq_count, col_count)
    wv_back, wo_back, wi_back, wb_back = (
        lax.all_gather(w_value, ROWS, axis=0, tiled=True),
        lax.all_gather(w_out, ROWS, axis=0, tiled=True),
        lax.all_gather(w_in, ROWS, axis=1, tiled=True),
        lax.all_gather(w_back, ROWS, axis=0, tiled=True),
    )
    grad_out = out_grad.reshape(seq_count * col_count, model_width)
    grad_back = jnp.dot(activ_low.T, grad_out, preferred_element_type=f32)
    grad_activ = jnp.dot(grad_out, wb_back.T, preferred_element_type=f32)
    grad_pre = activ_back(grad_activ)[0].astype(bf16)
    grad_in = jnp.dot(entry_two.T, grad_pre, preferred_element_type=f32)
    grad_entry_two = jnp.dot(grad_pre, wi_back.T, preferred_element_type=f32)
    back_two, grad_gain_two = norm_back(grad_entry_two, normed_two, scale_two, gain_second)
    grad_hidden = grad_out.astype(f32) + back_two
    grad_hidden_low = grad_hidden.astype(bf16)
    grad_wo = jnp.dot(mixed_low.T, grad_hidden_low, preferred_element_type=f32)
    grad_mixed = jnp.dot(grad_hidden_low, wo_back.T, preferred_element_type=f32).astype(bf16)
    grad_rows = lax.all_gather(
        grad_mixed.reshape(seq_count, col_count, model_width), SEQ, axis=1, tiled=True
    )
    grad_heads = grad_rows.reshape(seq_count, -1, head_count, head_dim)

    def delta_part(fields):
        seg_row, seg_own, max_row, sum_row, grad_row, value_row = fields
        soft_probs = make_probs(mix_cols, seg_row, seg_own, max_row, sum_row)
        grad_probs = jnp.einsum("ihd,chd->hic", grad_row, value_row, preferred_element_type=f32)
        return jnp.sum(soft_probs * grad_probs, axis=-1)

    partial_delta = lax.map(
        delta_part, (row_segs, segments, row_max, row_sum, grad_heads, value_heads)
    )
    delta = lax.psum(partial_delta, SEQ)

    def seq_back(running, fields):
        seg_row, seg_own, max_row, sum_row, grad_row, value_row, delta_row = fields
        soft_probs = make_probs(mix_cols, seg_row, seg_own, max_row, sum_row)
        grad_probs = jnp.einsum("ihd,chd->hic", grad_row, value_row, preferred_element_type=f32)
        running = running + soft_probs * (grad_probs - delta_row[..., None])
        grad_value_row = jnp.einsum(
            "hic,ihd->chd", soft_probs.astype(bf16), grad_row, preferred_element_type=f32
        )
        return (running, grad_value_row)

    local_mix_grad, grad_values = lax.scan(
        seq_back,
        jnp.zeros(mix_cols.shape, f32),
        (row_segs, segments, row_max, row_sum, grad_heads, value_heads, delta),
    )
    mix_grad = lax.psum(local_mix_grad, ROWS)
    grad_values = grad_values.reshape(seq_count * col_count, model_width).astype(bf16)
    grad_wv = jnp.dot(entry_one.T, grad_values, preferred_element_type=f32)
    grad_entry_one = jnp.dot(grad_values, wv_back.T, preferred_element_type=f32)
    back_one, grad_gain_one = norm_back(grad_entry_one, normed_one, scale_one, gain_first)
    tokens_grad = (grad_hidden + back_one).reshape(tokens.shape)
    owned = (
        lax.psum_scatter(grad_wv, ROWS, scatter_dimension=0, tiled=True),
        lax.psum_scatter(grad_wo, ROWS, scatter_dimension=0, tiled=True),
        lax.psum_scatter(grad_in, ROWS, scatter_dimension=1, tiled=True),
        lax.psum_scatter(grad_back, ROWS, scatter_dimension=0, tiled=True),
        lax.psum_scatter(grad_gain_one, ROWS, scatter_dimension=0, tiled=True),
        lax.psum_scatter(grad_gain_two, ROWS, scatter_dimension=0, tiled=True),
    )
    summed = lax.psum((owned[0], owned[1], owned[2], owned[3], owned[4], owned[5]), SEQ)
    return (
        result,
        tokens_grad,
        mix_grad,
        summed[0],
        summed[1],
        summed[2],
        summed[3],
        summed[4],
        summed[5],
        rms_residual,
        rms_sublayer,
    )


F32 = jnp.float32
BF16 = jnp.bfloat16
MESH = pl.DeviceIdType.MESH
NT = (((1,), (1,)), ((), ()))
TN = (((0,), (0,)), ((), ()))
ANY = pl.BlockSpec(memory_space=pl.ANY)
RATE = 0.0925
VMEM_LIMIT = 60 * 2**20
ROW_LINK = {1: ("y", 1.0), 2: ("z", 1.0), 4: ("z", 2.0)}
SEQ_LINK = {1: ("core", 0.12), 2: ("x", 1.0), 3: ("x", 1.0)}


def tag(*parts):
    return "".join(map(str, parts))


class Copy:
    def __init__(self, make, remote):
        self.make, self.remote, self.done = make, remote, False

    def recv(self):
        if not self.done:
            self.done = True
            if self.remote:
                self.make().wait_recv()
            else:
                self.make().wait()


class Net:
    def __init__(self, send, recv, local):
        self.send, self.recv, self.local = send, recv, local
        self.remote, self.near = [], []

    def go(self, src, dst, dev):
        i = len(self.remote)
        make = lambda: pltpu.make_async_remote_copy(
            src_ref=src(), dst_ref=dst(), send_sem=self.send.at[i], recv_sem=self.recv.at[i],
            device_id=dev, device_id_type=MESH)
        make().start()
        self.remote.append(Copy(make, True))
        return self.remote[-1]

    def cp(self, src, dst):
        i = len(self.near)
        make = lambda: pltpu.make_async_copy(src(), dst(), self.local.at[i])
        make().start()
        self.near.append(Copy(make, False))
        return self.near[-1]

    def finish(self):
        for copy in self.near + self.remote:
            copy.recv()
        for copy in self.remote:
            copy.make().wait_send()


class Plan:
    def __init__(self, net, r, s, inside):
        self.net, self.r, self.s, self.inside = net, r, s, inside
        self.tasks, self.copies, self.loops = [], {}, {}

    def comm(self, name, axis, bit, mb, deps, prio, src, dst):
        link, factor = (ROW_LINK if axis == ROWS else SEQ_LINK)[bit]
        dev = {axis: (self.r if axis == ROWS else self.s) ^ bit}

        def emit():
            self.wait(deps)
            self.copies[name] = self.net.go(src, dst, dev)

        self.tasks.append((name, link, factor * 2 * mb / RATE, deps, prio, emit))
        return name

    def near(self, name, mb, deps, prio, src, dst):
        def emit():
            self.wait(deps)
            self.copies[name] = self.net.cp(src, dst)

        self.tasks.append((name, "hbm", mb / 2.0, deps, prio, emit))
        return name

    def work(self, name, us, deps, prio, run):
        def emit():
            self.wait(deps)
            run()

        self.tasks.append((name, "tc", us, deps, prio, emit))
        return name

    def loop(self, name, count, us, deps, prio, body, setup=lambda: None):
        if not self.inside:
            def run():
                held = setup()

                @pl.loop(0, count)
                def _(t):
                    body(t, held)

            return self.work(name, us * count, deps, prio, run)
        for t in range(count):
            step = tag(name, "_", t)
            self.loops[step] = (name, t, count, body, setup, deps)
            self.tasks.append((step, "tc", us, deps if t == 0 else [tag(name, "_", t - 1)], prio, None))
        return tag(name, "_", count - 1)

    def emit_loop(self, inner):
        name, _, count, body, setup, deps = self.loops[inner[0][0]]
        slots = [[] for _ in range(count)]
        now = 0
        for task in inner:
            if task[0] in self.loops:
                assert self.loops[task[0]][0] == name
                now = self.loops[task[0]][1]
            else:
                slots[now].append(task)
        self.wait(deps)
        held = setup()

        @pl.loop(0, count)
        def _(t):
            body(t, held)
            for k, tasks in enumerate(slots):
                if tasks:
                    @pl.when(t == k)
                    def _(tasks=tasks):
                        for task in tasks:
                            task[5]()

    def add(self, name, deps, to, other, us=0.12):
        def run():
            target, term = to(), other()
            target[...] = target[...] + term[...]

        return self.work(name, us, deps, -5, run)

    def wait(self, deps):
        for dep in deps:
            if dep in self.copies:
                self.copies[dep].recv()

    def solve(self):
        end, start, free, now = {}, {}, {}, 0.0
        left = list(self.tasks)
        while left:
            ready = [
                (max([free.get(t[1], 0.0)] + [end[d] for d in t[3]]), t[4], i)
                for i, t in enumerate(left) if all(d in end for d in t[3])
            ]
            first = min(ready)
            begin, _, pick = min(
                (b, p, i) for b, p, i in ready if b <= first[0] + 1e-9)
            name, link, cost, _, prio, _ = left.pop(pick)
            start[name] = (begin, link == "tc", prio)
            free[link] = begin + cost
            end[name] = begin + cost + (0.0 if link == "tc" else 2.0)
        self.start, self.end = start, end
        return sorted(self.tasks, key=lambda t: start[t[0]])

    def run(self):
        order = self.solve()
        early = [task for task in order if task[1] == "hbm" and not task[3]]
        for task in early:
            task[5]()
        greet(self.r, self.s)
        rest = [task for task in order if task not in early]
        names = [task[0] for task in rest]
        i = 0
        while i < len(rest):
            if names[i] in self.loops:
                name, _, count = self.loops[names[i]][:3]
                end = names.index(tag(name, "_", count - 1))
                self.emit_loop(rest[i:end + 1])
                i = end
            else:
                rest[i][5]()
            i += 1
        self.net.finish()


def greet(r, s):
    barrier = pltpu.get_barrier_semaphore()
    for bit in (1, 2, 4):
        pl.semaphore_signal(barrier, inc=1, device_id={ROWS: r ^ bit}, device_id_type=MESH)
    for bit in (1, 2, 3):
        pl.semaphore_signal(barrier, inc=1, device_id={SEQ: s ^ bit}, device_id_type=MESH)
    pl.semaphore_wait(barrier, 6)


def cut(ref, start, size):
    return ref.at[pl.ds(pl.multiple_of(start, 16), size)]


def add_gather(plan, name, src, dst, order, ways, prio, mb):
    r, s = plan.r, plan.s
    core, x = s % 2, s // 2
    n = src.shape[0] // ways
    off = {1: 0, 2: core, 4: 2 * core + x}[ways] * n
    far = (2 * core + 1 - x) * n
    part = lambda q, o: cut(src if q == 0 else dst.at[r ^ q], o, n)
    home = lambda q, o: cut(dst.at[r ^ q], o, n)
    got = {0: None}
    for stage, bit in enumerate(order):
        new = {}
        for q, dep in got.items():
            new[q ^ bit] = plan.comm(
                tag(name, q ^ bit), ROWS, bit, mb / ways, [dep] if dep else [], prio + 0.1 * stage,
                lambda q=q: part(q, off), lambda q=q: home(q, off))
        got.update(new)
    need = {q: [dep or tag(name, "0")] for q, dep in got.items()}
    for q, dep in got.items():
        if q == 0 or ways == 1:
            continue
        need[q].append(plan.comm(tag(name, "c", q), SEQ, 1, mb / ways, [dep], prio + 1,
                                 lambda q=q: part(q, off), lambda q=q: home(q, off)))
        if ways == 4:
            need[q].append(plan.comm(tag(name, "x", q), SEQ, 2, mb / ways, [dep], prio + 1,
                                     lambda q=q: part(q, off), lambda q=q: home(q, off)))
            need[q].append(plan.comm(tag(name, "f", q), SEQ, 1, mb / ways, [tag(name, "x", q)], prio + 1,
                                     lambda q=q: part(q, far), lambda q=q: home(q, far)))
    return need


def column(row):
    return jnp.broadcast_to(row, (128, 128)).T[:, :1]


def as_row(col):
    return jnp.broadcast_to(col, (128, 128)).T[:1]


def segment_layouts(seg, col, row):
    for q in range(2):
        for k in range(4):
            ids = seg[k, q:q + 1].astype(F32)
            row[q, :, k * 128:(k + 1) * 128] = ids
            col[q, k * 128:(k + 1) * 128] = column(ids)


def gain_row(gains, i):
    total = gains[0, i:i + 1].astype(F32)
    for k in range(1, 8):
        total = total + gains[k, i:i + 1].astype(F32)
    return total


def forward_kernel(tok, grd, seg, mix, wv, wo, wi, wb, gn,
                   x_o, g_o, seg_o, m_o, wv_o, wo_o, gn_o, val_o, mxd_o, iz_o, h_o, e2_o, res_o, rms_o, gi_o, gb_o,
                   send, recv, local,
                   x_v, g_v, seg_v, m_v, wv_v, wo_v, wi_v, wb_v, gn_v, val_v, mxd_v, h_v, e_v, et_v, gt_v,
                   br_v, e2_v, act_v, pg_v, gi_v, gb_v, rms_v, sc_v, sr_v):
    r, s = lax.axis_index(ROWS), lax.axis_index(SEQ)
    y, zb = r % 2, (r // 2) % 2
    net = Net(send, recv, local)
    plan = Plan(net, r, s, True)
    block = lambda k: pl.ds(pl.multiple_of((s ^ k) * 128, 128), 128)
    for k in (2, 3, 1):
        plan.comm(tag("seg", k), SEQ, k, 0.001, [], 0, lambda k=k: seg.at[s ^ k], lambda: seg_v.at[s])
        plan.comm(tag("tok", k), SEQ, k, 0.393, [], 5, lambda k=k: tok.at[pl.ds(2 * (s ^ k), 2)],
                  lambda: x_v.at[:, block(0)])
        plan.comm(tag("grd", k), SEQ, k, 0.393, [], 15, lambda k=k: grd.at[pl.ds(2 * (s ^ k), 2)],
                  lambda: g_v.at[:, block(0)])
    groups = 3
    mixes = []
    for g, urgent in enumerate((1.0, 4.01, 1.02)):
        heads = pl.ds(12 // groups * g, 12 // groups)
        quarter = lambda ref, a, b, heads=heads: ref.at[heads, pl.ds((2 * a + b) * 128, 128)]
        other = lambda a, b, quarter=quarter: (lambda: quarter(m_v.at[s ^ 2], a, b))
        size = 0.393 / groups
        plan.comm(tag("mixc", g), SEQ, 1, 4 * size, [], 3 + 0.01 * g, lambda heads=heads: mix.at[heads],
                  lambda heads=heads: m_v.at[s, heads])
        plan.comm(tag("mixx", g), SEQ, 2, size, [], urgent, lambda quarter=quarter: quarter(mix, y, zb),
                  lambda quarter=quarter: quarter(m_v.at[s], y, zb))
        names = ["mix0", tag("mixc", g), tag("mixx", g)]
        for name, axis, bit, dep, prio, a, b in (
                ("mixz", ROWS, 2, "mixx", 2, y, zb), ("mixy", ROWS, 1, "mixx", 2, y, zb),
                ("mixw", ROWS, 1, "mixz", 2, y, 1 - zb), ("mixp", SEQ, 1, "mixx", 3, y, zb),
                ("mixq", SEQ, 1, "mixz", 3, y, 1 - zb), ("mixr", SEQ, 1, "mixy", 3, 1 - y, zb),
                ("mixs", SEQ, 1, "mixw", 3, 1 - y, 1 - zb)):
            names.append(plan.comm(tag(name, g), axis, bit, size, [tag(dep, g)], prio + 0.01 * g, other(a, b), other(a, b)))
        mixes.append(names)
    flat = lambda got, *qs: [d for q in qs for d in got[q]]
    every = range(8)
    gn_d = add_gather(plan, "gn", gn, gn_v, [4, 2, 1], 1, 0, 0.024)
    wv_d = add_gather(plan, "wv", wv, wv_v, [4, 2, 1], 2, 1, 0.147)
    wo_d = add_gather(plan, "wo", wo, wo_v, [4, 2, 1], 2, 10, 0.147)
    wi_d = add_gather(plan, "wi", wi, wi_v, [4, 1, 2], 4, 20, 0.59)
    wb_d = add_gather(plan, "wb", wb, wb_v, [4, 2, 1], 2, 20.05, 0.59)
    for name, mb, src, dst in (
            ("tok0", 0.4, lambda: tok.at[pl.ds(2 * s, 2)], lambda: x_v.at[:, block(0)]),
            ("gn0", 0.02, lambda: gn, lambda: gn_v.at[r]), ("wv0", 0.15, lambda: wv, lambda: wv_v.at[r]),
            ("seg0", 0.01, lambda: seg.at[s], lambda: seg_v.at[s]), ("mix0", 1.5, lambda: mix, lambda: m_v.at[s]),
            ("wo0", 0.15, lambda: wo, lambda: wo_v.at[r]), ("wi0", 0.6, lambda: wi, lambda: wi_v.at[r]),
            ("wb0", 0.6, lambda: wb, lambda: wb_v.at[r]),
            ("grd0", 0.4, lambda: grd.at[pl.ds(2 * s, 2)], lambda: g_v.at[:, block(0)])):
        plan.near(name, mb, [], 0, src, dst)

    def put(name, mb, deps, src, dst):
        plan.near(name, mb, deps, 90, lambda: src, lambda: dst)

    for k in range(4):
        def values(k=k):
            x = x_v[:, block(k)].reshape(256, 768).astype(F32)
            scale = lax.rsqrt(jnp.mean(x * x, axis=-1, keepdims=True) + EPS)
            entry = (x * scale * gain_row(gn_v, 0)).astype(BF16)
            out = jnp.dot(entry, wv_v[...].reshape(768, 768), preferred_element_type=F32)
            val_v[:, block(k)] = out.astype(BF16).reshape(2, 128, 768)

        plan.work(tag("val", k), 1.2, [tag("tok", k)] + flat(wv_d, *every) + flat(gn_d, *every), 1, values)
    plan.work("segs", 1.0, [tag("seg", k) for k in range(4)], 0, lambda: segment_layouts(seg_v, sc_v, sr_v))
    for k in range(4):
        def turn(k=k):
            for q in range(2):
                at = pl.ds(pl.multiple_of(q * 512 + (s ^ k) * 128, 128), 128)
                gt_v[:, at] = g_v[q, block(k)].T

        plan.work(tag("gt", k), 0.6, [tag("grd", k)], 9, turn)
    lane = lax.broadcasted_iota(jnp.int32, (1, 128), 1)
    last = ["segs"] + [tag("val", k) for k in range(4)]
    for g in range(groups):
        def mixing(t, _, g=g):
            p = g * (6 // groups) + t
            lanes = pl.ds(pl.multiple_of(p * 128, 128), 128)
            raised = [exp_mix(m_v, 2 * p + hh).astype(BF16) for hh in range(2)]
            for q in range(2):
                same = sc_v[q] == sr_v[q]
                rhs = jnp.concatenate([val_v[q, :, lanes], jnp.ones((512, 128), BF16)], axis=1)
                both = [jnp.dot(jnp.where(same, e, jnp.zeros_like(e)), rhs, preferred_element_type=F32)
                        for e in raised]
                total = jnp.where(lane < 64, both[0][:, :128], both[1][:, :128])
                inverse = 1.0 / jnp.where(lane < 64, both[0][:, 128:], both[1][:, 128:])
                mxd_v[q, :, lanes] = (total * inverse).astype(BF16)
                br_v[q * 512:(q + 1) * 512, lanes] = inverse

        last = [plan.loop(tag("mf", g), 6 // groups, 1.7, last + mixes[g], 1, mixing)]
    mixed_by = last
    put("iz_out", 1.5, last, br_v, iz_o)
    for q in range(2):
        def project(k, _, q=q):
            inside = pl.ds(pl.multiple_of(k * 128, 128), 128)
            at = pl.ds(pl.multiple_of(q * 512 + k * 128, 128), 128)
            h = x_v[q, inside].astype(F32) + jnp.dot(
                mxd_v[q, inside], wo_v[...].reshape(768, 768), preferred_element_type=F32)
            square = jnp.mean(h * h, axis=-1, keepdims=True)
            h_v[at] = h
            entry = (h * lax.rsqrt(square + EPS) * gain_row(gn_v, 1)).astype(BF16)
            e_v[at] = entry
            et_v[:, at] = entry.T
            rms_v[k, q:q + 1] = as_row(jnp.sqrt(square))

        last = [plan.loop(tag("out", q), 4, 0.6, last + flat(wo_d, *every), 1, project)]
    put("h_out", 1.5, last, h_v, h_o)
    c0, c1 = 0.7978845608028654, 0.044715
    step = 256
    for i, (a, b) in enumerate(((0, 4), (1, 5), (2, 6), (3, 7))):
        def load(a=a, b=b):
            weights = jnp.concatenate([wi_v[r ^ a], wi_v[r ^ b]], axis=1)
            return weights, jnp.concatenate([wb_v[r ^ a], wb_v[r ^ b]], axis=0)

        def feed(t, held, i=i):
            weights, back = held
            at = pl.ds(pl.multiple_of(t * step, step), step)
            inner = pl.ds(pl.multiple_of((t % 2) * step, step), step)
            pre = jnp.dot(e_v[at], weights, preferred_element_type=F32)
            up = lax.dot_general(g_v[t // 2, inner], back, NT, preferred_element_type=F32)
            square = pre * pre
            th = jnp.tanh(pre * (c0 + (c0 * c1) * square))
            gate = 0.5 + 0.5 * th
            act = (pre * gate).astype(BF16)
            slope = gate + pre * (1.0 - th * th) * ((0.5 * c0) + (1.5 * c0 * c1) * square)
            pg = (up * slope).astype(BF16)
            act_v[at] = act
            pg_v[at] = pg
            branch = jnp.dot(act, back, preferred_element_type=F32)
            e2 = lax.dot_general(pg, weights, NT, preferred_element_type=F32)
            if i == 0:
                br_v[at] = branch
                e2_v[at] = e2
            else:
                br_v[at] += branch
                e2_v[at] += e2

        need = flat(wi_d, a, b) + flat(wb_d, a, b) + [tag("grd", k) for k in range(4)] + ["iz_out"]
        last = [plan.loop(tag("ff", i), 4, 1.9, last + need, 1, feed, load)]

        def weight_grads(t, _, i=i):
            slot = i % 2
            at = pl.ds(pl.multiple_of(t * 256, 256), 256)
            gi = jnp.dot(et_v[at], pg_v[...], preferred_element_type=F32).astype(BF16)
            gb = jnp.dot(gt_v[at], act_v[...], preferred_element_type=F32).astype(BF16)
            for q in range(2):
                gi_v[slot, q, at] = gi[:, q * 384:(q + 1) * 384]
                gb_v[slot, q, at] = gb[:, q * 384:(q + 1) * 384]

        free = [tag("g", n, "_out", i - 2, q) for n in "ib" for q in range(2)] if i >= 2 else []
        last = [plan.loop(tag("fg", i), 3, 1.3, last + free + [tag("gt", k) for k in range(4)], 1, weight_grads)]
        for q, owner in enumerate((a, b)):
            put(tag("gi_out", i, q), 0.3, last, gi_v.at[i % 2, q], gi_o.at[r ^ owner])
            put(tag("gb_out", i, q), 0.3, last, gb_v.at[i % 2, q], gb_o.at[r ^ owner])

    def finish():
        @pl.loop(0, 8)
        def _(t):
            at = pl.ds(pl.multiple_of(t * 128, 128), 128)
            q, k = t // 4, t % 4
            branch = br_v[at]
            e_v[at] = (h_v[at] + branch).astype(BF16)
            rms_v[k, pl.ds(2 + q, 1)] = as_row(jnp.sqrt(jnp.mean(branch * branch, axis=-1, keepdims=True)))

    last = [plan.work("fin", 2.0, last, 1, finish)]
    put("e2_out", 1.5, last, e2_v, e2_o)
    put("res_out", 0.8, last, e_v, res_o)
    put("rms_out", 0.1, last, rms_v, rms_o)
    toks, grds = [tag("tok", k) for k in range(4)], [tag("grd", k) for k in range(4)]
    put("x_out", 0.8, toks, x_v, x_o)
    put("g_out", 0.8, grds, g_v, g_o)
    put("seg_out", 0.1, ["segs"], seg_v, seg_o)
    put("m_out", 3.0, sum(mixes, []), m_v, m_o)
    put("wv_out", 0.6, flat(wv_d, *every), wv_v, wv_o)
    put("wo_out", 0.6, flat(wo_d, *every), wo_v, wo_o)
    put("gn_out", 0.1, flat(gn_d, *every), gn_v, gn_o)
    put("val_out", 0.8, [tag("val", k) for k in range(4)], val_v, val_o)
    put("mxd_out", 0.8, mixed_by, mxd_v, mxd_o)
    plan.run()


def forward_all(tok, grd, seg, mix, wv, wo, wi, wb, gn):
    sd = jax.ShapeDtypeStruct
    rows, flat, big = (2, 512, 768), (1024, 768), (8, 768, 384)
    mixes, square, gains = (4, 12, 512, 128), (8, 96, 768), (8, 16, 768)
    outs = [sd(rows, BF16), sd(rows, BF16), sd((4, 2, 128), jnp.int32), sd(mixes, BF16), sd(square, BF16),
            sd(square, BF16), sd(gains, BF16), sd(rows, BF16), sd(rows, BF16), sd(flat, F32), sd(flat, F32),
            sd(flat, F32), sd(flat, BF16), sd((4, 8, 128), F32), sd(big, BF16), sd(big, BF16)]
    dma = pltpu.SemaphoreType.DMA
    v = lambda *a: pltpu.VMEM(a, BF16)
    f = lambda *a: pltpu.VMEM(a, F32)
    turned = (768, 1024)
    scratch = [v(*rows), v(*rows), pltpu.VMEM((4, 2, 128), jnp.int32), v(*mixes), v(*square), v(*square), v(*big),
               v(8, 384, 768), v(*gains), v(*rows), v(*rows), f(*flat), v(*flat), v(*turned), v(*turned),
               f(*flat), f(*flat), v(*flat), v(*flat), v(2, 2, 768, 384), v(2, 2, 768, 384), f(4, 8, 128),
               f(2, 512, 1), f(2, 1, 512)]
    return pl.pallas_call(
        forward_kernel, out_shape=outs, in_specs=[ANY] * 9, out_specs=[ANY] * len(outs),
        scratch_shapes=[dma((128,)), dma((128,)), dma((48,))] + scratch,
        compiler_params=pltpu.CompilerParams(collective_id=0, has_side_effects=True, vmem_limit_bytes=VMEM_LIMIT),
    )(tok, grd, seg, mix, wv, wo, wi, wb, gn)


def exp_mix(m_ref, hh):
    return jnp.concatenate([jnp.exp(m_ref[k, hh].astype(F32)) for k in range(4)], axis=1)


class Reduce:
    def __init__(self, plan, name, src, made, local, bufs, out, order, first, prio, mb, pieces):
        self.plan, self.name, self.src, self.local, self.bufs = plan, name, src, local, bufs
        r, s = plan.r, plan.s
        self.core, self.x = s % 2, s // 2
        self.n = src.shape[1] // 2
        half = mb / 2
        own, near, across, rows, final = bufs
        last = {}
        for q in pieces:
            deps = made[q]
            if not local:
                plan.near(tag(name, "l", q), half, deps, prio, lambda q=q: self.half(src.at[r ^ q], self.core),
                          lambda q=q: own.at[q])
            plan.comm(tag(name, "c", q), SEQ, 1, half, deps, prio, lambda q=q: self.half(src.at[r ^ q], 1 - self.core),
                      lambda q=q: near.at[q])
            last[q] = plan.add(tag(name, "a", q), [tag(name, "c", q)] + (deps if local else [tag(name, "l", q)]),
                               lambda q=q: self.mine(q), lambda q=q: near.at[q])
        if first:
            half = half / 2
            for q in pieces:
                plan.comm(tag(name, "X", q), SEQ, 2, half, [last[q]], prio,
                          lambda q=q: self.quarter(self.mine(q), 1 - self.x), lambda q=q: across.at[q])
                last[q] = plan.add(tag(name, "A", q), [tag(name, "X", q), last[q]],
                                   lambda q=q: self.quarter(self.mine(q), self.x), lambda q=q: across.at[q])
        item = (lambda q: self.quarter(self.mine(q), self.x)) if first else self.mine
        keep, slot = list(range(8)), 0
        for stage, bit in enumerate(order):
            for q in [q for q in pieces if q in keep and q & bit]:
                plan.comm(tag(name, "r", q), ROWS, bit, half, [last[q]], prio + 0.1 * stage,
                          lambda q=q: item(q), lambda slot=slot: rows.at[slot])
                last[q ^ bit] = plan.add(tag(name, "b", q), [tag(name, "r", q), last[q ^ bit]],
                                         lambda q=q ^ bit: item(q), lambda slot=slot: rows.at[slot])
                slot += 1
            keep = [q for q in keep if not q & bit]
        if first:
            def widen():
                self.quarter(final, self.x)[...] = item(0)[...].astype(F32)

            plan.work(tag(name, "t"), 0.2, [last[0]], -5, widen)
            plan.comm(tag(name, "x"), SEQ, 2, 2 * half, [tag(name, "t")], prio + 0.5,
                      lambda: self.quarter(final, self.x), lambda: self.quarter(final, self.x))
            for name2, dep, which in (("m", "t", 0), ("o", "x", 1)):
                side = (lambda which=which: self.quarter(final, self.x if which == 0 else 1 - self.x))
                place = (lambda which=which: self.quarter(self.half(out, self.core),
                                                          self.x if which == 0 else 1 - self.x))
                plan.near(tag(name, name2), mb / 2, [tag(name, dep)], prio, side, place)
                plan.comm(tag(name, name2, "k"), SEQ, 1, mb / 2, [tag(name, dep)], prio, side, place)
        else:
            plan.comm(tag(name, "x"), SEQ, 2, half, [last[0]], prio + 0.5, lambda: item(0), lambda: across)

            def total():
                final[...] = item(0)[...].astype(F32) + across[...].astype(F32)

            plan.work(tag(name, "t"), 0.2, [tag(name, "x"), last[0]], -5, total)
            plan.near(tag(name, "o"), mb, [tag(name, "t")], prio, lambda: final, lambda: self.half(out, self.core))
            plan.comm(tag(name, "k"), SEQ, 1, mb, [tag(name, "t")], prio, lambda: final, lambda: self.half(out, self.core))

    def half(self, ref, which):
        return cut(ref, which * self.n, self.n)

    def quarter(self, ref, which):
        return cut(ref, which * (self.n // 2), self.n // 2)

    def mine(self, q):
        return self.half(self.src.at[self.plan.r ^ q], self.core) if self.local else self.bufs[0].at[q]


def backward_kernel(x_i, g_i, seg_i, m_i, wv_i, wo_i, gn_i, val_i, mxd_i, iz_i, h_i, e2_i, res_i, rms_i, gi, gb,
                    res_o, tgr_o, gi_o, gb_o, go_o, gv_o, gn_o, mg_o, rms_o, send, recv, local,
                    x_v, g_v, seg_v, m_v, wv_v, wo_v, gn_v, val_v, mxd_v, iz_v, h_v, q_v, hl_v, go_v, gv_v,
                    sc_v, sr_v, n0, n1, m1, m3, m4, t0, t1,
                    i0, i1, i2, i3, i4, b0, b1, b2, b3, b4, o0, o1, o2, o3, o4, v0, v1, v2, v3, v4):
    r, s = lax.axis_index(ROWS), lax.axis_index(SEQ)
    core, x = s % 2, s // 2
    net = Net(send, recv, local)
    plan = Plan(net, r, s, False)
    place = lambda k: pl.ds(pl.multiple_of((s ^ k) * 128, 128), 128)
    for name, mb, prio, src, dst in (
            ("h", 3.1, 0, h_i, h_v), ("e2", 3.1, 1, e2_i, q_v), ("g", 1.6, 2, g_i, g_v), ("gn", 0.1, 0, gn_i, gn_v),
            ("wo", 1.2, 3, wo_i, wo_v), ("seg", 0.1, 3, seg_i, seg_v), ("mxd", 1.6, 4, mxd_i, mxd_v),
            ("val", 1.6, 4, val_i, val_v), ("iz", 3.1, 4, iz_i, iz_v), ("m", 6.3, 5, m_i, m_v),
            ("x", 1.6, 6, x_i, x_v), ("wv", 1.2, 6, wv_i, wv_v)):
        plan.near(tag("in_", name), mb, [], prio, lambda src=src: src, lambda dst=dst: dst)
    for k in (2, 3, 1):
        plan.comm(tag("res", k), SEQ, k, 0.393, [], 2, lambda k=k: res_i.at[:, place(k)], lambda: res_o.at[pl.ds(2 * s, 2)])
        plan.comm(tag("rms", k), SEQ, k, 0.004, [], 3, lambda k=k: rms_i.at[s ^ k], lambda: rms_o.at[s])
    for name, src, buf, dst in (("res", res_i.at[:, place(0)], t0, res_o.at[pl.ds(2 * s, 2)]),
                                ("rms", rms_i.at[s], t1, rms_o.at[s])):
        plan.near(tag(name, "i"), 0.4, [], 9, lambda src=src: src, lambda buf=buf: buf)
        plan.near(tag(name, "o"), 0.4, [tag(name, "i")], 9, lambda buf=buf: buf, lambda dst=dst: dst)

    def start():
        n0[...] = jnp.zeros_like(n0)
        segment_layouts(seg_v, sc_v, sr_v)

    plan.work("segs", 1.0, ["in_seg"], -2, start)
    last = ["segs"] + [tag("in_", n) for n in ("h", "e2", "g", "gn", "wo")]
    for part in range(2):
        def post(k, _, part=part):
            at = pl.ds(pl.multiple_of(part * 512 + k * 128, 128), 128)
            inside = pl.ds(pl.multiple_of(k * 128, 128), 128)
            h = h_v[at]
            scale = lax.rsqrt(jnp.mean(h * h, axis=-1, keepdims=True) + EPS)
            normed = h * scale
            up = q_v[at]
            n0[0, 1:2] += jnp.sum(up * normed, axis=0, keepdims=True)
            scaled = up * gain_row(gn_v, 1)
            back = scale * (scaled - normed * jnp.mean(scaled * normed, axis=-1, keepdims=True))
            grad = g_v[part, inside].astype(F32) + back
            q_v[at] = grad
            grad_low = grad.astype(BF16)
            hl_v[at] = grad_low
            g_v[part, inside] = lax.dot_general(
                grad_low, wo_v[...].reshape(768, 768), NT, preferred_element_type=F32).astype(BF16)

        last = [plan.loop(tag("post", part), 4, 0.75, last, -1, post)]

    lane = lax.broadcasted_iota(jnp.int32, (1, 128), 1)
    orders = MIX_ORDERS
    groups = len(orders)
    heads = 12 // groups
    for g, order in enumerate(orders):
        def mixing(t, _, g=g):
            p = g * (heads // 2) + t
            lanes = pl.ds(pl.multiple_of(p * 128, 128), 128)
            raised = [exp_mix(m_v, 2 * p + hh) for hh in range(2)]
            low = [e.astype(BF16) for e in raised]
            acc = [None, None]
            for q in range(2):
                same = sc_v[q] == sr_v[q]
                scaled = g_v[q, :, lanes].astype(F32) * iz_v[q * 512:(q + 1) * 512, lanes]
                inner = scaled * mxd_v[q, :, lanes].astype(F32)
                grads = []
                for hh in range(2):
                    mine = (lane < 64) if hh == 0 else (lane >= 64)
                    delta = jnp.sum(jnp.where(mine, inner, 0.0), axis=1, keepdims=True)
                    lhs = jnp.where(mine, scaled, 0.0).astype(BF16)
                    back = lax.dot_general(lhs, val_v[q, :, lanes], NT, preferred_element_type=F32)
                    term = jnp.where(same, back - delta, 0.0)
                    acc[hh] = term if q == 0 else acc[hh] + term
                    masked = jnp.where(same, low[hh], jnp.zeros_like(low[hh]))
                    grads.append(lax.dot_general(masked, scaled.astype(BF16), TN, preferred_element_type=F32))
                val_v[q, :, lanes] = jnp.where(lane < 64, grads[0], grads[1]).astype(BF16)
            for hh in range(2):
                out = (acc[hh] * raised[hh]).astype(BF16)
                for k in range(4):
                    m_v[k, 2 * p + hh] = out[:, k * 128:(k + 1) * 128]

        last = [plan.loop(tag("mb", g), heads // 2, 2.7, last + ["in_m", "in_val", "in_iz", "in_mxd"], -1, mixing)]
        mine = pl.ds(g * heads, heads)
        mb = 0.01638 * heads
        prio = MIX_URGENCY[g]
        done = {}
        block = lambda h, side, mine=mine: m_v.at[2 * (x ^ h) + (core if side == 0 else 1 - core), mine]
        for h in range(2):
            plan.comm(tag("mg", g, "c", h), SEQ, 1, 8 * mb, last, prio, lambda h=h, block=block: block(h, 1),
                      lambda h=h, mine=mine: m1.at[h, mine])
            made = plan.add(tag("mg", g, "a", h), [tag("mg", g, "c", h)] + last, lambda h=h, block=block: block(h, 0),
                            lambda h=h, mine=mine: m1.at[h, mine], 0.3)
            for q in range(8):
                done[h, q] = made
        rows = lambda q: pl.ds(pl.multiple_of((r ^ q) * 64, 64), 64)
        item = lambda h, q, mine=mine: m_v.at[2 * (x ^ h) + core, mine, rows(q)]
        keep, slot = [(h, q) for h in range(2) for q in range(8)], 0
        for bit in order:
            hit = (lambda h, q: h) if bit == 0 else (lambda h, q, bit=bit: q & bit)
            for h, q in [k for k in keep if hit(*k)]:
                to = (0, q) if bit == 0 else (h, q ^ bit)
                name = tag("mg", g, "r", h, q)
                plan.comm(name, ROWS if bit else SEQ, bit or 2, mb, [done[h, q]], prio,
                          lambda h=h, q=q, item=item: item(h, q), lambda slot=slot, mine=mine: m3.at[slot, mine])
                done[to] = plan.add(name + "d", [name, done[to]], lambda to=to, item=item: item(*to),
                                    lambda slot=slot, mine=mine: m3.at[slot, mine])
                slot += 1
            keep = [k for k in keep if not hit(*k)]

        def final(mine=mine, item=item):
            m4[mine, rows(0)] = item(0, 0)[...]

        got = {0: plan.work(tag("mg", g, "f"), 0.1, [done[0, 0]], -5, final)}
        for bit in [b for b in reversed(order) if b]:
            new = {}
            for q, dep in got.items():
                part = lambda q=q, mine=mine: m4.at[mine, rows(q)]
                new[q ^ bit] = plan.comm(tag("mg", g, "g", q ^ bit), ROWS, bit, mb, [dep], prio, part, part)
            got.update(new)
        plan.near(tag("mg", g, "o"), 0.4, list(got.values()), 0, lambda mine=mine: m4.at[mine], lambda mine=mine: mg_o.at[mine])
    def out_grad():
        @pl.loop(0, 2)
        def _(t):
            lanes = pl.ds(pl.multiple_of(t * 384, 128), 384)
            grad = lax.dot_general(mxd_v[...].reshape(1024, 768), hl_v[:, lanes], TN, preferred_element_type=F32)
            go_v[:, :, lanes] = grad.astype(BF16).reshape(8, 96, 384)

    last = [plan.work("go", 2.5, last, -1, out_grad)]
    go_made = last
    for k in (2, 3, 1, 0):
        def tokens(k=k):
            for q in range(2):
                at = pl.ds(pl.multiple_of(q * 512 + (s ^ k) * 128, 128), 128)
                up = lax.dot_general(val_v[q, place(k)], wv_v[...].reshape(768, 768), NT, preferred_element_type=F32)
                xs = x_v[q, place(k)].astype(F32)
                scale = lax.rsqrt(jnp.mean(xs * xs, axis=-1, keepdims=True) + EPS)
                normed = xs * scale
                gain = gain_row(gn_v, 0)
                hl_v[at] = (normed * gain).astype(BF16)
                n0[0, 0:1] += jnp.sum(up * normed, axis=0, keepdims=True)
                scaled = up * gain
                back = scale * (scaled - normed * jnp.mean(scaled * normed, axis=-1, keepdims=True))
                x_v[q, place(k)] = (q_v[at] + back).astype(BF16)

        last = [plan.work(tag("tok", k), 1.2, last + ["in_x", "in_wv"], -1, tokens)]
        if k:
            plan.comm(tag("tgr", k), SEQ, k, 0.393, last, 30, lambda k=k: x_v.at[:, place(k)],
                      lambda: tgr_o.at[pl.ds(2 * s, 2)])
        else:
            plan.near("tgro", 0.4, last, 9, lambda: x_v.at[:, place(0)], lambda: tgr_o.at[pl.ds(2 * s, 2)])
    tok_done = last

    def value_grad():
        @pl.loop(0, 2)
        def _(t):
            lanes = pl.ds(pl.multiple_of(t * 384, 128), 384)
            grad = lax.dot_general(hl_v[...], val_v[:, :, lanes].reshape(1024, 384), TN, preferred_element_type=F32)
            gv_v[:, :, lanes] = grad.astype(BF16).reshape(8, 96, 384)

    gv_made = [plan.work("gv", 2.5, last, -1, value_grad)]
    every = range(8)
    Reduce(plan, "gi", gi, {q: [] for q in every}, False, (i0, i1, i2, i3, i4), gi_o, [1, 2, 4], True, 10, 0.59, HIGH)
    Reduce(plan, "gb", gb, {q: [] for q in every}, False, (b0, b1, b2, b3, b4), gb_o, [1, 2, 4], False, 4, 0.59, FAR)
    Reduce(plan, "go", go_v, {q: go_made for q in every}, True, (o0, o1, o2, o3, o4), go_o, [1, 2, 4], False, 2, 0.147, ODD)
    Reduce(plan, "gv", gv_v, {q: gv_made for q in every}, True, (v0, v1, v2, v3, v4), gv_o, [1, 2, 4], False, 13, 0.147, HIGH)
    last = tok_done
    for i, (axis, bit) in enumerate(((SEQ, 1), (SEQ, 2), (ROWS, 1), (ROWS, 2), (ROWS, 4))):
        plan.comm(tag("gn", i), axis, bit, 0.024, last, 0, lambda i=i: n0.at[i], lambda i=i: n1.at[i])

        def add(i=i):
            n0[i + 1] = n0[i] + n1[i]

        last = [plan.work(tag("gna", i), 0.1, [tag("gn", i)] + last, -5, add)]
    plan.near("gno", 0.02, last, 0, lambda: n0.at[5], lambda: gn_o)
    plan.run()


MIX_ORDERS = ((1, 0, 2, 4), (0, 1, 2, 4), (0, 1, 2, 4))
MIX_URGENCY = (0.0, 5.01, 12.02)
ODD, HIGH, FAR = (3, 7, 1, 5, 2, 6, 4, 0), (6, 7, 2, 3, 4, 5, 0, 1), (7, 3, 5, 1, 6, 2, 4, 0)


def backward_all(*args):
    sd = jax.ShapeDtypeStruct
    outs = [sd((8, 128, 768), BF16), sd((8, 128, 768), BF16), sd((768, 384), F32), sd((768, 384), F32),
            sd((96, 768), F32), sd((96, 768), F32), sd((8, 768), F32), sd((12, 512, 128), BF16), sd((4, 8, 128), F32)]
    dma = pltpu.SemaphoreType.DMA
    v = lambda *a: pltpu.VMEM(a, BF16)
    f = lambda *a: pltpu.VMEM(a, F32)
    big, piece, small = (384, 384), (192, 384), (48, 768)
    rows, flat = (2, 512, 768), (1024, 768)
    scratch = [v(*rows), v(*rows), pltpu.VMEM((4, 2, 128), jnp.int32), v(4, 12, 512, 128), v(8, 96, 768), v(8, 96, 768),
               v(8, 16, 768), v(*rows), v(*rows), f(*flat), f(*flat), f(*flat), v(*flat), v(8, 96, 768),
               v(8, 96, 768), f(2, 512, 1), f(2, 1, 512), f(6, 8, 768), f(5, 8, 768),
               v(2, 12, 512, 128), v(15, 12, 64, 128), v(12, 512, 128), v(2, 128, 768), f(8, 128)]
    scratch += [v(8, *big), v(8, *big), v(8, *piece), v(7, *piece), f(*big)]
    scratch += [v(8, *big), v(8, *big), v(*big), v(7, *big), f(*big)]
    for _ in range(2):
        scratch += [v(16, 128), v(8, *small), v(*small), v(7, *small), f(*small)]
    return pl.pallas_call(
        backward_kernel, out_shape=outs, in_specs=[ANY] * len(args), out_specs=[ANY] * len(outs),
        scratch_shapes=[dma((200,)), dma((200,)), dma((64,))] + scratch,
        compiler_params=pltpu.CompilerParams(collective_id=1, has_side_effects=True, vmem_limit_bytes=67043328),
    )(*args)


def own_gains(r, first, second):
    row = lax.broadcasted_iota(jnp.int32, (16, 8, 96), 0)
    owner = lax.broadcasted_iota(jnp.int32, (16, 8, 96), 1)
    both = jnp.where(row == 0, first, jnp.where(row == 1, second, jnp.zeros_like(second)))
    return jnp.where(owner == r, both, jnp.zeros_like(both)).reshape(16, 768)


def final_kernel(res, tgr, mg, gv, go, gi, gb, res_o, tgr_o, mg_o, gv_o, go_o, gi_o, gb_o):
    for src, dst in ((res, res_o), (gv, gv_o), (go, go_o), (gi, gi_o)):
        dst[...] = src[...]
    tgr_o[...] = tgr[...].astype(F32)
    mg_o[...] = mg[...].astype(F32)
    gb_o[...] = gb[...].T


def final_types(*args):
    sd = jax.ShapeDtypeStruct
    plain = lambda *b: pl.BlockSpec(b, lambda i: (i,) + (0,) * (len(b) - 1))
    tok, mix, small, wide = plain(2, 128, 768), plain(3, 512, 128), plain(24, 768), plain(192, 384)
    side = pl.BlockSpec((768, 128), lambda i: (0, jnp.minimum(i, 2)))
    turned = pl.BlockSpec((128, 768), lambda i: (jnp.minimum(i, 2), 0))
    return pl.pallas_call(
        final_kernel, grid=(4,), in_specs=[tok, tok, mix, small, small, wide, side],
        out_specs=[tok, tok, mix, small, small, wide, turned],
        out_shape=[sd((8, 128, 768), BF16), sd((8, 128, 768), F32), sd((12, 512, 128), F32), sd((96, 768), F32),
                   sd((96, 768), F32), sd((768, 384), F32), sd((384, 768), F32)],
        compiler_params=pltpu.CompilerParams(vmem_limit_bytes=VMEM_LIMIT))(*args)


def fast_body(tokens, segments, mix, w_value, w_out, w_in, w_back, gain_one, gain_two, out_grad):
    r, s = lax.axis_index(ROWS), lax.axis_index(SEQ)
    gains = own_gains(r, gain_one, gain_two)
    (x_rows, grad_rows, seg_all, mix_all, wv, wo, gains_all, values, mixed, inverse, hidden_one, grad_entry_two,
     result, rms, grad_in, grad_back) = forward_all(
        tokens, out_grad, segments.reshape(4, 2, 128), mix, w_value, w_out, w_in, w_back, gains)
    res, tgr, gi, gb, go, gv, gn, mg, rms = backward_all(
        x_rows, grad_rows, seg_all, mix_all, wv, wo, gains_all, values, mixed, inverse, hidden_one, grad_entry_two,
        result.reshape(2, 512, 768), rms, grad_in, grad_back)
    own = lax.dynamic_slice(gn, (0, r * 96), (2, 96))
    rms = rms[:, :4].reshape(4, 2, 2, 128)
    rms = rms.transpose(1, 0, 2, 3).reshape(2, 8, 128)
    res, tgr, mg, gv, go, gi, gb = final_types(res, tgr, mg, gv, go, gi, gb)
    return (res, tgr, mg, gv, go, gi, gb, own[0], own[1], rms[0], rms[1])


def solution(mesh):
    in_specs = (
        P(ROWS, SEQ, None),
        P(ROWS, SEQ),
        P(None, None, SEQ),
        P(ROWS, None),
        P(ROWS, None),
        P(None, ROWS),
        P(ROWS, None),
        P(ROWS),
        P(ROWS),
        P(ROWS, SEQ, None),
    )
    out_specs = (
        P(ROWS, SEQ, None),
        P(ROWS, SEQ, None),
        P(None, None, SEQ),
        P(ROWS, None),
        P(ROWS, None),
        P(None, ROWS),
        P(ROWS, None),
        P(ROWS),
        P(ROWS),
        P(ROWS, SEQ),
        P(ROWS, SEQ),
    )
    shape = dict(mesh.shape)
    body = fast_body if shape[ROWS] == 8 and shape[SEQ] == 4 else generic_body
    return jax.shard_map(body, mesh=mesh, in_specs=in_specs, out_specs=out_specs, check_vma=False)
```

```python
import functools
from functools import partial

import jax
import jax.numpy as jnp
from jax import lax
from jax.experimental import pallas as pl
from jax.experimental.pallas import tpu as pltpu
from jax.sharding import PartitionSpec as P

ROWS, SEQ = "rows", "seq"
NEG = -1e30
EPS = 1e-06


def joined(part, axis, combine):
    gathered = jax.tree.map(lambda a: lax.all_gather(a, axis), part)

    def take(source):
        return jax.tree.map(lambda a: lax.dynamic_index_in_dim(a, source, 0, False), gathered)

    return lax.fori_loop(
        1, lax.axis_size(axis), lambda source, state: combine(state, take(source)), take(0)
    )


def normalize(inputs, gain):
    scale = lax.rsqrt(jnp.mean(inputs * inputs, axis=-1, keepdims=True) + EPS)
    normed = inputs * scale
    return (normed, scale, (normed * gain).astype(jnp.bfloat16))


def norm_back(upstream, normed, scale, gain):
    scaled = upstream * gain
    back = scale * (scaled - normed * jnp.mean(scaled * normed, axis=-1, keepdims=True))
    return (back, jnp.sum(upstream * normed, axis=0))


def combine_stats(first, second):
    max_first, sum_first = first
    max_second, sum_second = second
    row_max = jnp.maximum(max_first, max_second)
    return (
        row_max,
        sum_first * jnp.exp(max_first - row_max) + sum_second * jnp.exp(max_second - row_max),
    )


def local_stats(mix_cols, row_segs, own_segs):
    same_doc = (row_segs[:, None] == own_segs[None, :])[None]
    masked = jnp.where(same_doc, mix_cols, NEG)
    row_max = jnp.max(masked, axis=-1)
    row_sum = jnp.sum(jnp.where(same_doc, jnp.exp(masked - row_max[..., None]), 0.0), axis=-1)
    return (row_max, row_sum)


def make_probs(mix_cols, row_segs, own_segs, row_max, row_sum):
    same_doc = (row_segs[:, None] == own_segs[None, :])[None]
    masked = jnp.where(same_doc, mix_cols, NEG)
    raised = jnp.where(same_doc, jnp.exp(masked - row_max[..., None]), 0.0)
    return raised / row_sum[..., None]


def generic_body(tokens, segments, mix, w_value, w_out, w_in, w_back, gain_one, gain_two, out_grad):
    seq_count, col_count, model_width = tokens.shape
    head_count = mix.shape[0]
    head_dim = model_width // head_count
    f32 = jnp.float32
    bf16 = jnp.bfloat16
    gathered = (
        lax.all_gather(w_value, ROWS, axis=0, tiled=True),
        lax.all_gather(w_out, ROWS, axis=0, tiled=True),
        lax.all_gather(w_in, ROWS, axis=1, tiled=True),
        lax.all_gather(w_back, ROWS, axis=0, tiled=True),
        lax.all_gather(gain_one, ROWS, axis=0, tiled=True),
        lax.all_gather(gain_two, ROWS, axis=0, tiled=True),
    )
    wv_full, wo_full, wi_full, wb_full, gain_first, gain_second = gathered
    gain_first = gain_first.astype(f32)
    gain_second = gain_second.astype(f32)
    resid_in = tokens.astype(f32).reshape(seq_count * col_count, model_width)
    normed_one, scale_one, entry_one = normalize(resid_in, gain_first)
    values = jnp.dot(entry_one, wv_full, preferred_element_type=f32).astype(bf16)
    value_heads = values.reshape(seq_count, col_count, head_count, head_dim)
    row_segs = lax.all_gather(segments, SEQ, axis=1, tiled=True)
    mix_cols = mix.astype(f32)
    local_max, local_sum = lax.map(
        lambda fields: local_stats(mix_cols, fields[0], fields[1]), (row_segs, segments)
    )
    row_max, row_sum = joined((local_max, local_sum), SEQ, combine_stats)
    probs_low = lax.map(
        lambda fields: make_probs(mix_cols, fields[0], fields[1], fields[2], fields[3]).astype(
            bf16
        ),
        (row_segs, segments, row_max, row_sum),
    )
    products = jnp.einsum("shic,schd->ishd", probs_low, value_heads, preferred_element_type=f32)
    mixed = lax.psum_scatter(
        products.reshape(col_count * lax.axis_size(SEQ), seq_count, model_width),
        SEQ,
        scatter_dimension=0,
        tiled=True,
    )
    mixed = mixed.transpose(1, 0, 2).reshape(seq_count * col_count, model_width)
    mixed_low = mixed.astype(bf16)
    hidden_one = resid_in + jnp.dot(mixed_low, wo_full, preferred_element_type=f32)
    normed_two, scale_two, entry_two = normalize(hidden_one, gain_second)
    pre_act = jnp.dot(entry_two, wi_full, preferred_element_type=f32)
    activ, activ_back = jax.vjp(partial(jax.nn.gelu, approximate=True), pre_act)
    activ_low = activ.astype(bf16)
    branch = jnp.dot(activ_low, wb_full, preferred_element_type=f32)
    result = (hidden_one + branch).astype(bf16).reshape(tokens.shape)
    rms_residual = jnp.sqrt(jnp.mean(hidden_one * hidden_one, axis=-1)).reshape(
        seq_count, col_count
    )
    rms_sublayer = jnp.sqrt(jnp.mean(branch * branch, axis=-1)).reshape(seq_count, col_count)
    wv_back, wo_back, wi_back, wb_back = (
        lax.all_gather(w_value, ROWS, axis=0, tiled=True),
        lax.all_gather(w_out, ROWS, axis=0, tiled=True),
        lax.all_gather(w_in, ROWS, axis=1, tiled=True),
        lax.all_gather(w_back, ROWS, axis=0, tiled=True),
    )
    grad_out = out_grad.reshape(seq_count * col_count, model_width)
    grad_back = jnp.dot(activ_low.T, grad_out, preferred_element_type=f32)
    grad_activ = jnp.dot(grad_out, wb_back.T, preferred_element_type=f32)
    grad_pre = activ_back(grad_activ)[0].astype(bf16)
    grad_in = jnp.dot(entry_two.T, grad_pre, preferred_element_type=f32)
    grad_entry_two = jnp.dot(grad_pre, wi_back.T, preferred_element_type=f32)
    back_two, grad_gain_two = norm_back(grad_entry_two, normed_two, scale_two, gain_second)
    grad_hidden = grad_out.astype(f32) + back_two
    grad_hidden_low = grad_hidden.astype(bf16)
    grad_wo = jnp.dot(mixed_low.T, grad_hidden_low, preferred_element_type=f32)
    grad_mixed = jnp.dot(grad_hidden_low, wo_back.T, preferred_element_type=f32).astype(bf16)
    grad_rows = lax.all_gather(
        grad_mixed.reshape(seq_count, col_count, model_width), SEQ, axis=1, tiled=True
    )
    grad_heads = grad_rows.reshape(seq_count, -1, head_count, head_dim)

    def delta_part(fields):
        seg_row, seg_own, max_row, sum_row, grad_row, value_row = fields
        soft_probs = make_probs(mix_cols, seg_row, seg_own, max_row, sum_row)
        grad_probs = jnp.einsum("ihd,chd->hic", grad_row, value_row, preferred_element_type=f32)
        return jnp.sum(soft_probs * grad_probs, axis=-1)

    partial_delta = lax.map(
        delta_part, (row_segs, segments, row_max, row_sum, grad_heads, value_heads)
    )
    delta = lax.psum(partial_delta, SEQ)

    def seq_back(running, fields):
        seg_row, seg_own, max_row, sum_row, grad_row, value_row, delta_row = fields
        soft_probs = make_probs(mix_cols, seg_row, seg_own, max_row, sum_row)
        grad_probs = jnp.einsum("ihd,chd->hic", grad_row, value_row, preferred_element_type=f32)
        running = running + soft_probs * (grad_probs - delta_row[..., None])
        grad_value_row = jnp.einsum(
            "hic,ihd->chd", soft_probs.astype(bf16), grad_row, preferred_element_type=f32
        )
        return (running, grad_value_row)

    local_mix_grad, grad_values = lax.scan(
        seq_back,
        jnp.zeros(mix_cols.shape, f32),
        (row_segs, segments, row_max, row_sum, grad_heads, value_heads, delta),
    )
    mix_grad = lax.psum(local_mix_grad, ROWS)
    grad_values = grad_values.reshape(seq_count * col_count, model_width).astype(bf16)
    grad_wv = jnp.dot(entry_one.T, grad_values, preferred_element_type=f32)
    grad_entry_one = jnp.dot(grad_values, wv_back.T, preferred_element_type=f32)
    back_one, grad_gain_one = norm_back(grad_entry_one, normed_one, scale_one, gain_first)
    tokens_grad = (grad_hidden + back_one).reshape(tokens.shape)
    owned = (
        lax.psum_scatter(grad_wv, ROWS, scatter_dimension=0, tiled=True),
        lax.psum_scatter(grad_wo, ROWS, scatter_dimension=0, tiled=True),
        lax.psum_scatter(grad_in, ROWS, scatter_dimension=1, tiled=True),
        lax.psum_scatter(grad_back, ROWS, scatter_dimension=0, tiled=True),
        lax.psum_scatter(grad_gain_one, ROWS, scatter_dimension=0, tiled=True),
        lax.psum_scatter(grad_gain_two, ROWS, scatter_dimension=0, tiled=True),
    )
    summed = lax.psum((owned[0], owned[1], owned[2], owned[3], owned[4], owned[5]), SEQ)
    return (
        result,
        tokens_grad,
        mix_grad,
        summed[0],
        summed[1],
        summed[2],
        summed[3],
        summed[4],
        summed[5],
        rms_residual,
        rms_sublayer,
    )


F32 = jnp.float32
BF16 = jnp.bfloat16
MESH = pl.DeviceIdType.MESH
NT = (((1,), (1,)), ((), ()))
TN = (((0,), (0,)), ((), ()))
ANY = pl.BlockSpec(memory_space=pl.ANY)
RATE = 0.0925
VMEM_LIMIT = 60 * 2**20
ROW_LINK = {1: ("y", 1.0), 2: ("z", 1.0), 4: ("z", 2.0)}
SEQ_LINK = {1: ("core", 0.12), 2: ("x", 1.0), 3: ("x", 1.0)}


def tag(*parts):
    return "".join(map(str, parts))


class Copy:
    def __init__(self, make, remote):
        self.make, self.remote, self.done = make, remote, False

    def recv(self):
        if not self.done:
            self.done = True
            if self.remote:
                self.make().wait_recv()
            else:
                self.make().wait()


class Net:
    def __init__(self, send, recv, local):
        self.send, self.recv, self.local = send, recv, local
        self.remote, self.near = [], []

    def go(self, src, dst, dev):
        i = len(self.remote)
        make = lambda: pltpu.make_async_remote_copy(
            src_ref=src(), dst_ref=dst(), send_sem=self.send.at[i], recv_sem=self.recv.at[i],
            device_id=dev, device_id_type=MESH)
        make().start()
        self.remote.append(Copy(make, True))
        return self.remote[-1]

    def cp(self, src, dst):
        i = len(self.near)
        make = lambda: pltpu.make_async_copy(src(), dst(), self.local.at[i])
        make().start()
        self.near.append(Copy(make, False))
        return self.near[-1]

    def finish(self):
        for copy in self.near + self.remote:
            copy.recv()
        for copy in self.remote:
            copy.make().wait_send()


class Plan:
    def __init__(self, net, r, s, inside):
        self.net, self.r, self.s, self.inside = net, r, s, inside
        self.tasks, self.copies, self.loops = [], {}, {}

    def comm(self, name, axis, bit, mb, deps, prio, src, dst):
        link, factor = (ROW_LINK if axis == ROWS else SEQ_LINK)[bit]
        dev = {axis: (self.r if axis == ROWS else self.s) ^ bit}

        def emit():
            self.wait(deps)
            self.copies[name] = self.net.go(src, dst, dev)

        self.tasks.append((name, link, factor * 2 * mb / RATE, deps, prio, emit))
        return name

    def near(self, name, mb, deps, prio, src, dst):
        def emit():
            self.wait(deps)
            self.copies[name] = self.net.cp(src, dst)

        self.tasks.append((name, "hbm", mb / 2.0, deps, prio, emit))
        return name

    def work(self, name, us, deps, prio, run):
        def emit():
            self.wait(deps)
            run()

        self.tasks.append((name, "tc", us, deps, prio, emit))
        return name

    def loop(self, name, count, us, deps, prio, body, setup=lambda: None):
        if not self.inside:
            def run():
                held = setup()

                @pl.loop(0, count)
                def _(t):
                    body(t, held)

            return self.work(name, us * count, deps, prio, run)
        for t in range(count):
            step = tag(name, "_", t)
            self.loops[step] = (name, t, count, body, setup, deps)
            self.tasks.append((step, "tc", us, deps if t == 0 else [tag(name, "_", t - 1)], prio, None))
        return tag(name, "_", count - 1)

    def emit_loop(self, inner):
        name, _, count, body, setup, deps = self.loops[inner[0][0]]
        slots = [[] for _ in range(count)]
        now = 0
        for task in inner:
            if task[0] in self.loops:
                assert self.loops[task[0]][0] == name
                now = self.loops[task[0]][1]
            else:
                slots[now].append(task)
        self.wait(deps)
        held = setup()

        @pl.loop(0, count)
        def _(t):
            body(t, held)
            for k, tasks in enumerate(slots):
                if tasks:
                    @pl.when(t == k)
                    def _(tasks=tasks):
                        for task in tasks:
                            task[5]()

    def add(self, name, deps, to, other, us=0.12):
        def run():
            target, term = to(), other()
            target[...] = target[...] + term[...]

        return self.work(name, us, deps, -5, run)

    def wait(self, deps):
        for dep in deps:
            if dep in self.copies:
                self.copies[dep].recv()

    def solve(self):
        end, start, free, now = {}, {}, {}, 0.0
        left = list(self.tasks)
        while left:
            ready = [
                (max([free.get(t[1], 0.0)] + [end[d] for d in t[3]]), t[4], i)
                for i, t in enumerate(left) if all(d in end for d in t[3])
            ]
            first = min(ready)
            begin, _, pick = min(
                (b, p, i) for b, p, i in ready if b <= first[0] + 1e-9)
            name, link, cost, _, prio, _ = left.pop(pick)
            start[name] = (begin, link == "tc", prio)
            free[link] = begin + cost
            end[name] = begin + cost + (0.0 if link == "tc" else 2.0)
        self.start, self.end = start, end
        return sorted(self.tasks, key=lambda t: start[t[0]])

    def run(self):
        order = self.solve()
        early = [task for task in order if task[1] == "hbm" and not task[3]]
        for task in early:
            task[5]()
        greet(self.r, self.s)
        rest = [task for task in order if task not in early]
        names = [task[0] for task in rest]
        i = 0
        while i < len(rest):
            if names[i] in self.loops:
                name, _, count = self.loops[names[i]][:3]
                end = names.index(tag(name, "_", count - 1))
                self.emit_loop(rest[i:end + 1])
                i = end
            else:
                rest[i][5]()
            i += 1
        self.net.finish()


def greet(r, s):
    barrier = pltpu.get_barrier_semaphore()
    for bit in (1, 2, 4):
        pl.semaphore_signal(barrier, inc=1, device_id={ROWS: r ^ bit}, device_id_type=MESH)
    for bit in (1, 2, 3):
        pl.semaphore_signal(barrier, inc=1, device_id={SEQ: s ^ bit}, device_id_type=MESH)
    pl.semaphore_wait(barrier, 6)


def cut(ref, start, size):
    return ref.at[pl.ds(pl.multiple_of(start, 16), size)]


def add_gather(plan, name, src, dst, order, ways, prio, mb):
    r, s = plan.r, plan.s
    core, x = s % 2, s // 2
    n = src.shape[0] // ways
    off = {1: 0, 2: core, 4: 2 * core + x}[ways] * n
    far = (2 * core + 1 - x) * n
    part = lambda q, o: cut(src if q == 0 else dst.at[r ^ q], o, n)
    home = lambda q, o: cut(dst.at[r ^ q], o, n)
    got = {0: None}
    for stage, bit in enumerate(order):
        new = {}
        for q, dep in got.items():
            new[q ^ bit] = plan.comm(
                tag(name, q ^ bit), ROWS, bit, mb / ways, [dep] if dep else [], prio + 0.1 * stage,
                lambda q=q: part(q, off), lambda q=q: home(q, off))
        got.update(new)
    need = {q: [dep or tag(name, "0")] for q, dep in got.items()}
    for q, dep in got.items():
        if q == 0 or ways == 1:
            continue
        need[q].append(plan.comm(tag(name, "c", q), SEQ, 1, mb / ways, [dep], prio + 1,
                                 lambda q=q: part(q, off), lambda q=q: home(q, off)))
        if ways == 4:
            need[q].append(plan.comm(tag(name, "x", q), SEQ, 2, mb / ways, [dep], prio + 1,
                                     lambda q=q: part(q, off), lambda q=q: home(q, off)))
            need[q].append(plan.comm(tag(name, "f", q), SEQ, 1, mb / ways, [tag(name, "x", q)], prio + 1,
                                     lambda q=q: part(q, far), lambda q=q: home(q, far)))
    return need


def column(row):
    return jnp.broadcast_to(row, (128, 128)).T[:, :1]


def as_row(col):
    return jnp.broadcast_to(col, (128, 128)).T[:1]


def segment_layouts(seg, col, row):
    for q in range(2):
        for k in range(4):
            ids = seg[k, q:q + 1].astype(F32)
            row[q, :, k * 128:(k + 1) * 128] = ids
            col[q, k * 128:(k + 1) * 128] = column(ids)


def gain_row(gains, i):
    total = gains[0, i:i + 1].astype(F32)
    for k in range(1, 8):
        total = total + gains[k, i:i + 1].astype(F32)
    return total


def forward_kernel(tok, grd, seg, mix, wv, wo, wi, wb, gn,
                   x_o, g_o, seg_o, m_o, wv_o, wo_o, gn_o, val_o, mxd_o, iz_o, h_o, e2_o, res_o, rms_o, gi_o, gb_o,
                   send, recv, local,
                   x_v, g_v, seg_v, m_v, wv_v, wo_v, wi_v, wb_v, gn_v, val_v, mxd_v, h_v, e_v, et_v, gt_v,
                   br_v, e2_v, act_v, pg_v, gi_v, gb_v, rms_v, sc_v, sr_v):
    r, s = lax.axis_index(ROWS), lax.axis_index(SEQ)
    y, zb = r % 2, (r // 2) % 2
    net = Net(send, recv, local)
    plan = Plan(net, r, s, True)
    block = lambda k: pl.ds(pl.multiple_of((s ^ k) * 128, 128), 128)
    for k in (2, 3, 1):
        plan.comm(tag("seg", k), SEQ, k, 0.001, [], 0, lambda k=k: seg.at[s ^ k], lambda: seg_v.at[s])
        plan.comm(tag("tok", k), SEQ, k, 0.393, [], 5, lambda k=k: tok.at[pl.ds(2 * (s ^ k), 2)],
                  lambda: x_v.at[:, block(0)])
        plan.comm(tag("grd", k), SEQ, k, 0.393, [], 15, lambda k=k: grd.at[pl.ds(2 * (s ^ k), 2)],
                  lambda: g_v.at[:, block(0)])
    groups = 3
    mixes = []
    for g, urgent in enumerate((1.0, 4.01, 1.02)):
        heads = pl.ds(12 // groups * g, 12 // groups)
        quarter = lambda ref, a, b, heads=heads: ref.at[heads, pl.ds((2 * a + b) * 128, 128)]
        other = lambda a, b, quarter=quarter: (lambda: quarter(m_v.at[s ^ 2], a, b))
        size = 0.393 / groups
        plan.comm(tag("mixc", g), SEQ, 1, 4 * size, [], 3 + 0.01 * g, lambda heads=heads: mix.at[heads],
                  lambda heads=heads: m_v.at[s, heads])
        plan.comm(tag("mixx", g), SEQ, 2, size, [], urgent, lambda quarter=quarter: quarter(mix, y, zb),
                  lambda quarter=quarter: quarter(m_v.at[s], y, zb))
        names = ["mix0", tag("mixc", g), tag("mixx", g)]
        for name, axis, bit, dep, prio, a, b in (
                ("mixz", ROWS, 2, "mixx", 2, y, zb), ("mixy", ROWS, 1, "mixx", 2, y, zb),
                ("mixw", ROWS, 1, "mixz", 2, y, 1 - zb), ("mixp", SEQ, 1, "mixx", 3, y, zb),
                ("mixq", SEQ, 1, "mixz", 3, y, 1 - zb), ("mixr", SEQ, 1, "mixy", 3, 1 - y, zb),
                ("mixs", SEQ, 1, "mixw", 3, 1 - y, 1 - zb)):
            names.append(plan.comm(tag(name, g), axis, bit, size, [tag(dep, g)], prio + 0.01 * g, other(a, b), other(a, b)))
        mixes.append(names)
    flat = lambda got, *qs: [d for q in qs for d in got[q]]
    every = range(8)
    gn_d = add_gather(plan, "gn", gn, gn_v, [4, 2, 1], 1, 0, 0.024)
    wv_d = add_gather(plan, "wv", wv, wv_v, [4, 2, 1], 2, 1, 0.147)
    wo_d = add_gather(plan, "wo", wo, wo_v, [4, 2, 1], 2, 10, 0.147)
    wi_d = add_gather(plan, "wi", wi, wi_v, [4, 1, 2], 4, 20, 0.59)
    wb_d = add_gather(plan, "wb", wb, wb_v, [4, 2, 1], 2, 20.05, 0.59)
    for name, mb, src, dst in (
            ("tok0", 0.4, lambda: tok.at[pl.ds(2 * s, 2)], lambda: x_v.at[:, block(0)]),
            ("gn0", 0.02, lambda: gn, lambda: gn_v.at[r]), ("wv0", 0.15, lambda: wv, lambda: wv_v.at[r]),
            ("seg0", 0.01, lambda: seg.at[s], lambda: seg_v.at[s]), ("mix0", 1.5, lambda: mix, lambda: m_v.at[s]),
            ("wo0", 0.15, lambda: wo, lambda: wo_v.at[r]), ("wi0", 0.6, lambda: wi, lambda: wi_v.at[r]),
            ("wb0", 0.6, lambda: wb, lambda: wb_v.at[r]),
            ("grd0", 0.4, lambda: grd.at[pl.ds(2 * s, 2)], lambda: g_v.at[:, block(0)])):
        plan.near(name, mb, [], 0, src, dst)

    def put(name, mb, deps, src, dst):
        plan.near(name, mb, deps, 90, lambda: src, lambda: dst)

    for k in range(4):
        def values(k=k):
            x = x_v[:, block(k)].reshape(256, 768).astype(F32)
            scale = lax.rsqrt(jnp.mean(x * x, axis=-1, keepdims=True) + EPS)
            entry = (x * scale * gain_row(gn_v, 0)).astype(BF16)
            out = jnp.dot(entry, wv_v[...].reshape(768, 768), preferred_element_type=F32)
            val_v[:, block(k)] = out.astype(BF16).reshape(2, 128, 768)

        plan.work(tag("val", k), 1.2, [tag("tok", k)] + flat(wv_d, *every) + flat(gn_d, *every), 1, values)
    plan.work("segs", 1.0, [tag("seg", k) for k in range(4)], 0, lambda: segment_layouts(seg_v, sc_v, sr_v))
    for k in range(4):
        def turn(k=k):
            for q in range(2):
                at = pl.ds(pl.multiple_of(q * 512 + (s ^ k) * 128, 128), 128)
                gt_v[:, at] = g_v[q, block(k)].T

        plan.work(tag("gt", k), 0.6, [tag("grd", k)], 9, turn)
    lane = lax.broadcasted_iota(jnp.int32, (1, 128), 1)
    last = ["segs"] + [tag("val", k) for k in range(4)]
    for g in range(groups):
        def mixing(t, _, g=g):
            p = g * (6 // groups) + t
            lanes = pl.ds(pl.multiple_of(p * 128, 128), 128)
            raised = [exp_mix(m_v, 2 * p + hh).astype(BF16) for hh in range(2)]
            for q in range(2):
                same = sc_v[q] == sr_v[q]
                rhs = jnp.concatenate([val_v[q, :, lanes], jnp.ones((512, 128), BF16)], axis=1)
                both = [jnp.dot(jnp.where(same, e, jnp.zeros_like(e)), rhs, preferred_element_type=F32)
                        for e in raised]
                total = jnp.where(lane < 64, both[0][:, :128], both[1][:, :128])
                inverse = 1.0 / jnp.where(lane < 64, both[0][:, 128:], both[1][:, 128:])
                mxd_v[q, :, lanes] = (total * inverse).astype(BF16)
                br_v[q * 512:(q + 1) * 512, lanes] = inverse

        last = [plan.loop(tag("mf", g), 6 // groups, 1.7, last + mixes[g], 1, mixing)]
    mixed_by = last
    put("iz_out", 1.5, last, br_v, iz_o)
    for q in range(2):
        def project(k, _, q=q):
            inside = pl.ds(pl.multiple_of(k * 128, 128), 128)
            at = pl.ds(pl.multiple_of(q * 512 + k * 128, 128), 128)
            h = x_v[q, inside].astype(F32) + jnp.dot(
                mxd_v[q, inside], wo_v[...].reshape(768, 768), preferred_element_type=F32)
            square = jnp.mean(h * h, axis=-1, keepdims=True)
            h_v[at] = h
            entry = (h * lax.rsqrt(square + EPS) * gain_row(gn_v, 1)).astype(BF16)
            e_v[at] = entry
            et_v[:, at] = entry.T
            rms_v[k, q:q + 1] = as_row(jnp.sqrt(square))

        last = [plan.loop(tag("out", q), 4, 0.6, last + flat(wo_d, *every), 1, project)]
    put("h_out", 1.5, last, h_v, h_o)
    c0, c1 = 0.7978845608028654, 0.044715
    step = 256
    for i, (a, b) in enumerate(((0, 4), (1, 5), (2, 6), (3, 7))):
        def load(a=a, b=b):
            weights = jnp.concatenate([wi_v[r ^ a], wi_v[r ^ b]], axis=1)
            return weights, jnp.concatenate([wb_v[r ^ a], wb_v[r ^ b]], axis=0)

        def feed(t, held, i=i):
            weights, back = held
            at = pl.ds(pl.multiple_of(t * step, step), step)
            inner = pl.ds(pl.multiple_of((t % 2) * step, step), step)
            pre = jnp.dot(e_v[at], weights, preferred_element_type=F32)
            up = lax.dot_general(g_v[t // 2, inner], back, NT, preferred_element_type=F32)
            square = pre * pre
            th = jnp.tanh(pre * (c0 + (c0 * c1) * square))
            gate = 0.5 + 0.5 * th
            act = (pre * gate).astype(BF16)
            slope = gate + pre * (1.0 - th * th) * ((0.5 * c0) + (1.5 * c0 * c1) * square)
            pg = (up * slope).astype(BF16)
            act_v[at] = act
            pg_v[at] = pg
            branch = jnp.dot(act, back, preferred_element_type=F32)
            e2 = lax.dot_general(pg, weights, NT, preferred_element_type=F32)
            if i == 0:
                br_v[at] = branch
                e2_v[at] = e2
            else:
                br_v[at] += branch
                e2_v[at] += e2

        need = flat(wi_d, a, b) + flat(wb_d, a, b) + [tag("grd", k) for k in range(4)] + ["iz_out"]
        last = [plan.loop(tag("ff", i), 4, 1.9, last + need, 1, feed, load)]

        def weight_grads(t, _, i=i):
            slot = i % 2
            at = pl.ds(pl.multiple_of(t * 256, 256), 256)
            gi = jnp.dot(et_v[at], pg_v[...], preferred_element_type=F32).astype(BF16)
            gb = jnp.dot(gt_v[at], act_v[...], preferred_element_type=F32).astype(BF16)
            for q in range(2):
                gi_v[slot, q, at] = gi[:, q * 384:(q + 1) * 384]
                gb_v[slot, q, at] = gb[:, q * 384:(q + 1) * 384]

        free = [tag("g", n, "_out", i - 2, q) for n in "ib" for q in range(2)] if i >= 2 else []
        last = [plan.loop(tag("fg", i), 3, 1.3, last + free + [tag("gt", k) for k in range(4)], 1, weight_grads)]
        for q, owner in enumerate((a, b)):
            put(tag("gi_out", i, q), 0.3, last, gi_v.at[i % 2, q], gi_o.at[r ^ owner])
            put(tag("gb_out", i, q), 0.3, last, gb_v.at[i % 2, q], gb_o.at[r ^ owner])

    def finish():
        @pl.loop(0, 8)
        def _(t):
            at = pl.ds(pl.multiple_of(t * 128, 128), 128)
            q, k = t // 4, t % 4
            branch = br_v[at]
            e_v[at] = (h_v[at] + branch).astype(BF16)
            rms_v[k, pl.ds(2 + q, 1)] = as_row(jnp.sqrt(jnp.mean(branch * branch, axis=-1, keepdims=True)))

    last = [plan.work("fin", 2.0, last, 1, finish)]
    put("e2_out", 1.5, last, e2_v, e2_o)
    put("res_out", 0.8, last, e_v, res_o)
    put("rms_out", 0.1, last, rms_v, rms_o)
    toks, grds = [tag("tok", k) for k in range(4)], [tag("grd", k) for k in range(4)]
    put("x_out", 0.8, toks, x_v, x_o)
    put("g_out", 0.8, grds, g_v, g_o)
    put("seg_out", 0.1, ["segs"], seg_v, seg_o)
    put("m_out", 3.0, sum(mixes, []), m_v, m_o)
    put("wv_out", 0.6, flat(wv_d, *every), wv_v, wv_o)
    put("wo_out", 0.6, flat(wo_d, *every), wo_v, wo_o)
    put("gn_out", 0.1, flat(gn_d, *every), gn_v, gn_o)
    put("val_out", 0.8, [tag("val", k) for k in range(4)], val_v, val_o)
    put("mxd_out", 0.8, mixed_by, mxd_v, mxd_o)
    plan.run()


def forward_all(tok, grd, seg, mix, wv, wo, wi, wb, gn):
    sd = jax.ShapeDtypeStruct
    rows, flat, big = (2, 512, 768), (1024, 768), (8, 768, 384)
    mixes, square, gains = (4, 12, 512, 128), (8, 96, 768), (8, 16, 768)
    outs = [sd(rows, BF16), sd(rows, BF16), sd((4, 2, 128), jnp.int32), sd(mixes, BF16), sd(square, BF16),
            sd(square, BF16), sd(gains, BF16), sd(rows, BF16), sd(rows, BF16), sd(flat, F32), sd(flat, F32),
            sd(flat, F32), sd(flat, BF16), sd((4, 8, 128), F32), sd(big, BF16), sd(big, BF16)]
    dma = pltpu.SemaphoreType.DMA
    v = lambda *a: pltpu.VMEM(a, BF16)
    f = lambda *a: pltpu.VMEM(a, F32)
    turned = (768, 1024)
    scratch = [v(*rows), v(*rows), pltpu.VMEM((4, 2, 128), jnp.int32), v(*mixes), v(*square), v(*square), v(*big),
               v(8, 384, 768), v(*gains), v(*rows), v(*rows), f(*flat), v(*flat), v(*turned), v(*turned),
               f(*flat), f(*flat), v(*flat), v(*flat), v(2, 2, 768, 384), v(2, 2, 768, 384), f(4, 8, 128),
               f(2, 512, 1), f(2, 1, 512)]
    return pl.pallas_call(
        forward_kernel, out_shape=outs, in_specs=[ANY] * 9, out_specs=[ANY] * len(outs),
        scratch_shapes=[dma((128,)), dma((128,)), dma((48,))] + scratch,
        compiler_params=pltpu.CompilerParams(collective_id=0, has_side_effects=True, vmem_limit_bytes=VMEM_LIMIT),
    )(tok, grd, seg, mix, wv, wo, wi, wb, gn)


def exp_mix(m_ref, hh):
    return jnp.concatenate([jnp.exp(m_ref[k, hh].astype(F32)) for k in range(4)], axis=1)


class Reduce:
    def __init__(self, plan, name, src, made, local, bufs, out, order, first, prio, mb, pieces):
        self.plan, self.name, self.src, self.local, self.bufs = plan, name, src, local, bufs
        r, s = plan.r, plan.s
        self.core, self.x = s % 2, s // 2
        self.n = src.shape[1] // 2
        half = mb / 2
        own, near, across, rows, final = bufs
        last = {}
        for q in pieces:
            deps = made[q]
            if not local:
                plan.near(tag(name, "l", q), half, deps, prio, lambda q=q: self.half(src.at[r ^ q], self.core),
                          lambda q=q: own.at[q])
            plan.comm(tag(name, "c", q), SEQ, 1, half, deps, prio, lambda q=q: self.half(src.at[r ^ q], 1 - self.core),
                      lambda q=q: near.at[q])
            last[q] = plan.add(tag(name, "a", q), [tag(name, "c", q)] + (deps if local else [tag(name, "l", q)]),
                               lambda q=q: self.mine(q), lambda q=q: near.at[q])
        if first:
            half = half / 2
            for q in pieces:
                plan.comm(tag(name, "X", q), SEQ, 2, half, [last[q]], prio,
                          lambda q=q: self.quarter(self.mine(q), 1 - self.x), lambda q=q: across.at[q])
                last[q] = plan.add(tag(name, "A", q), [tag(name, "X", q), last[q]],
                                   lambda q=q: self.quarter(self.mine(q), self.x), lambda q=q: across.at[q])
        item = (lambda q: self.quarter(self.mine(q), self.x)) if first else self.mine
        keep, slot = list(range(8)), 0
        for stage, bit in enumerate(order):
            for q in [q for q in pieces if q in keep and q & bit]:
                plan.comm(tag(name, "r", q), ROWS, bit, half, [last[q]], prio + 0.1 * stage,
                          lambda q=q: item(q), lambda slot=slot: rows.at[slot])
                last[q ^ bit] = plan.add(tag(name, "b", q), [tag(name, "r", q), last[q ^ bit]],
                                         lambda q=q ^ bit: item(q), lambda slot=slot: rows.at[slot])
                slot += 1
            keep = [q for q in keep if not q & bit]
        if first:
            def widen():
                self.quarter(final, self.x)[...] = item(0)[...].astype(F32)

            plan.work(tag(name, "t"), 0.2, [last[0]], -5, widen)
            plan.comm(tag(name, "x"), SEQ, 2, 2 * half, [tag(name, "t")], prio + 0.5,
                      lambda: self.quarter(final, self.x), lambda: self.quarter(final, self.x))
            for name2, dep, which in (("m", "t", 0), ("o", "x", 1)):
                side = (lambda which=which: self.quarter(final, self.x if which == 0 else 1 - self.x))
                place = (lambda which=which: self.quarter(self.half(out, self.core),
                                                          self.x if which == 0 else 1 - self.x))
                plan.near(tag(name, name2), mb / 2, [tag(name, dep)], prio, side, place)
                plan.comm(tag(name, name2, "k"), SEQ, 1, mb / 2, [tag(name, dep)], prio, side, place)
        else:
            plan.comm(tag(name, "x"), SEQ, 2, half, [last[0]], prio + 0.5, lambda: item(0), lambda: across)

            def total():
                final[...] = item(0)[...].astype(F32) + across[...].astype(F32)

            plan.work(tag(name, "t"), 0.2, [tag(name, "x"), last[0]], -5, total)
            plan.near(tag(name, "o"), mb, [tag(name, "t")], prio, lambda: final, lambda: self.half(out, self.core))
            plan.comm(tag(name, "k"), SEQ, 1, mb, [tag(name, "t")], prio, lambda: final, lambda: self.half(out, self.core))

    def half(self, ref, which):
        return cut(ref, which * self.n, self.n)

    def quarter(self, ref, which):
        return cut(ref, which * (self.n // 2), self.n // 2)

    def mine(self, q):
        return self.half(self.src.at[self.plan.r ^ q], self.core) if self.local else self.bufs[0].at[q]


def backward_kernel(x_i, g_i, seg_i, m_i, wv_i, wo_i, gn_i, val_i, mxd_i, iz_i, h_i, e2_i, res_i, rms_i, gi, gb,
                    res_o, tgr_o, gi_o, gb_o, go_o, gv_o, gn_o, mg_o, rms_o, send, recv, local,
                    x_v, g_v, seg_v, m_v, wv_v, wo_v, gn_v, val_v, mxd_v, iz_v, h_v, q_v, hl_v, go_v, gv_v,
                    sc_v, sr_v, n0, n1, m1, m3, m4, t0, t1,
                    i0, i1, i2, i3, i4, b0, b1, b2, b3, b4, o0, o1, o2, o3, o4, v0, v1, v2, v3, v4):
    r, s = lax.axis_index(ROWS), lax.axis_index(SEQ)
    core, x = s % 2, s // 2
    net = Net(send, recv, local)
    plan = Plan(net, r, s, False)
    place = lambda k: pl.ds(pl.multiple_of((s ^ k) * 128, 128), 128)
    for name, mb, prio, src, dst in (
            ("h0", 1.6, 0, h_i.at[:512], h_v.at[:512]), ("e0", 1.6, 1, e2_i.at[:512], q_v.at[:512]),
            ("g0", 0.8, 1, g_i.at[0], g_v.at[0]), ("gn", 0.1, 0, gn_i, gn_v), ("wo", 1.2, 1, wo_i, wo_v),
            ("h1", 1.6, 2, h_i.at[512:], h_v.at[512:]), ("e1", 1.6, 2, e2_i.at[512:], q_v.at[512:]),
            ("g1", 0.8, 2, g_i.at[1], g_v.at[1]), ("seg", 0.1, 3, seg_i, seg_v), ("mxd", 1.6, 4, mxd_i, mxd_v),
            ("val", 1.6, 4, val_i, val_v), ("iz", 3.1, 4, iz_i, iz_v), ("m", 6.3, 5, m_i, m_v),
            ("x", 1.6, 6, x_i, x_v), ("wv", 1.2, 6, wv_i, wv_v)):
        plan.near(tag("in_", name), mb, [], prio, lambda src=src: src, lambda dst=dst: dst)
    for k in (2, 3, 1):
        plan.comm(tag("res", k), SEQ, k, 0.393, [], 0.008, lambda k=k: res_i.at[:, place(k)], lambda: res_o.at[pl.ds(2 * s, 2)])
        plan.comm(tag("rms", k), SEQ, k, 0.004, [], 3, lambda k=k: rms_i.at[s ^ k], lambda: rms_o.at[s])
    for name, src, buf, dst in (("res", res_i.at[:, place(0)], t0, res_o.at[pl.ds(2 * s, 2)]),
                                ("rms", rms_i.at[s], t1, rms_o.at[s])):
        plan.near(tag(name, "i"), 0.4, [], 9, lambda src=src: src, lambda buf=buf: buf)
        plan.near(tag(name, "o"), 0.4, [tag(name, "i")], 9, lambda buf=buf: buf, lambda dst=dst: dst)

    def clear():
        n0[...] = jnp.zeros_like(n0)

    plan.work("zero", 0.1, [], -2, clear)
    plan.work("segs", 1.0, ["in_seg"], -1, lambda: segment_layouts(seg_v, sc_v, sr_v))
    last = ["in_gn", "in_wo"]
    for part in range(2):
        def post(k, _, part=part):
            at = pl.ds(pl.multiple_of(part * 512 + k * 128, 128), 128)
            inside = pl.ds(pl.multiple_of(k * 128, 128), 128)
            h = h_v[at]
            scale = lax.rsqrt(jnp.mean(h * h, axis=-1, keepdims=True) + EPS)
            normed = h * scale
            up = q_v[at]
            n0[0, 1:2] += jnp.sum(up * normed, axis=0, keepdims=True)
            scaled = up * gain_row(gn_v, 1)
            back = scale * (scaled - normed * jnp.mean(scaled * normed, axis=-1, keepdims=True))
            grad = g_v[part, inside].astype(F32) + back
            q_v[at] = grad
            grad_low = grad.astype(BF16)
            hl_v[at] = grad_low
            g_v[part, inside] = lax.dot_general(
                grad_low, wo_v[...].reshape(768, 768), NT, preferred_element_type=F32).astype(BF16)

        last = [plan.loop(tag("post", part), 4, 0.75, last + ["zero"] + [tag("in_", n, part) for n in "heg"], -1, post)]

    lane = lax.broadcasted_iota(jnp.int32, (1, 128), 1)
    orders = MIX_ORDERS
    groups = len(orders)
    heads = 12 // groups
    for g, order in enumerate(orders):
        def mixing(t, _, g=g):
            p = g * (heads // 2) + t
            lanes = pl.ds(pl.multiple_of(p * 128, 128), 128)
            raised = [exp_mix(m_v, 2 * p + hh) for hh in range(2)]
            low = [e.astype(BF16) for e in raised]
            acc = [None, None]
            for q in range(2):
                same = sc_v[q] == sr_v[q]
                scaled = g_v[q, :, lanes].astype(F32) * iz_v[q * 512:(q + 1) * 512, lanes]
                inner = scaled * mxd_v[q, :, lanes].astype(F32)
                grads = []
                for hh in range(2):
                    mine = (lane < 64) if hh == 0 else (lane >= 64)
                    delta = jnp.sum(jnp.where(mine, inner, 0.0), axis=1, keepdims=True)
                    lhs = jnp.where(mine, scaled, 0.0).astype(BF16)
                    back = lax.dot_general(lhs, val_v[q, :, lanes], NT, preferred_element_type=F32)
                    term = jnp.where(same, back - delta, 0.0)
                    acc[hh] = term if q == 0 else acc[hh] + term
                    masked = jnp.where(same, low[hh], jnp.zeros_like(low[hh]))
                    grads.append(lax.dot_general(masked, scaled.astype(BF16), TN, preferred_element_type=F32))
                val_v[q, :, lanes] = jnp.where(lane < 64, grads[0], grads[1]).astype(BF16)
            for hh in range(2):
                out = (acc[hh] * raised[hh]).astype(BF16)
                for k in range(4):
                    m_v[k, 2 * p + hh] = out[:, k * 128:(k + 1) * 128]

        last = [plan.loop(tag("mb", g), heads // 2, 2.7, last + ["segs", "in_m", "in_val", "in_iz", "in_mxd"], -1, mixing)]
        mine = pl.ds(g * heads, heads)
        mb = 0.01638 * heads
        prio = MIX_URGENCY[g]
        done = {}
        block = lambda h, side, mine=mine: m_v.at[2 * (x ^ h) + (core if side == 0 else 1 - core), mine]
        for h in range(2):
            plan.comm(tag("mg", g, "c", h), SEQ, 1, 8 * mb, last, prio, lambda h=h, block=block: block(h, 1),
                      lambda h=h, mine=mine: m1.at[h, mine])
            made = plan.add(tag("mg", g, "a", h), [tag("mg", g, "c", h)] + last, lambda h=h, block=block: block(h, 0),
                            lambda h=h, mine=mine: m1.at[h, mine], 0.3)
            for q in range(8):
                done[h, q] = made
        rows = lambda q: pl.ds(pl.multiple_of((r ^ q) * 64, 64), 64)
        item = lambda h, q, mine=mine: m_v.at[2 * (x ^ h) + core, mine, rows(q)]
        keep, slot = [(h, q) for h in range(2) for q in range(8)], 0
        for bit in order:
            hit = (lambda h, q: h) if bit == 0 else (lambda h, q, bit=bit: q & bit)
            for h, q in [k for k in keep if hit(*k)]:
                to = (0, q) if bit == 0 else (h, q ^ bit)
                name = tag("mg", g, "r", h, q)
                plan.comm(name, ROWS if bit else SEQ, bit or 2, mb, [done[h, q]], prio,
                          lambda h=h, q=q, item=item: item(h, q), lambda slot=slot, mine=mine: m3.at[slot, mine])
                done[to] = plan.add(name + "d", [name, done[to]], lambda to=to, item=item: item(*to),
                                    lambda slot=slot, mine=mine: m3.at[slot, mine])
                slot += 1
            keep = [k for k in keep if not hit(*k)]

        def final(mine=mine, item=item):
            m4[mine, rows(0)] = item(0, 0)[...]

        got = {0: plan.work(tag("mg", g, "f"), 0.1, [done[0, 0]], -5, final)}
        for bit in [b for b in reversed(order) if b]:
            new = {}
            for q, dep in got.items():
                part = lambda q=q, mine=mine: m4.at[mine, rows(q)]
                new[q ^ bit] = plan.comm(tag("mg", g, "g", q ^ bit), ROWS, bit, mb, [dep], prio, part, part)
            got.update(new)
        plan.near(tag("mg", g, "o"), 0.4, list(got.values()), 0, lambda mine=mine: m4.at[mine], lambda mine=mine: mg_o.at[mine])
    def out_grad():
        @pl.loop(0, 2)
        def _(t):
            lanes = pl.ds(pl.multiple_of(t * 384, 128), 384)
            grad = lax.dot_general(mxd_v[...].reshape(1024, 768), hl_v[:, lanes], TN, preferred_element_type=F32)
            go_v[:, :, lanes] = grad.astype(BF16).reshape(8, 96, 384)

    last = [plan.work("go", 2.5, last, -1, out_grad)]
    go_made = last
    for k in (2, 3, 1, 0):
        def tokens(k=k):
            for q in range(2):
                at = pl.ds(pl.multiple_of(q * 512 + (s ^ k) * 128, 128), 128)
                up = lax.dot_general(val_v[q, place(k)], wv_v[...].reshape(768, 768), NT, preferred_element_type=F32)
                xs = x_v[q, place(k)].astype(F32)
                scale = lax.rsqrt(jnp.mean(xs * xs, axis=-1, keepdims=True) + EPS)
                normed = xs * scale
                gain = gain_row(gn_v, 0)
                hl_v[at] = (normed * gain).astype(BF16)
                n0[0, 0:1] += jnp.sum(up * normed, axis=0, keepdims=True)
                scaled = up * gain
                back = scale * (scaled - normed * jnp.mean(scaled * normed, axis=-1, keepdims=True))
                x_v[q, place(k)] = (q_v[at] + back).astype(BF16)

        last = [plan.work(tag("tok", k), 1.2, last + ["in_x", "in_wv"], -1, tokens)]
        if k:
            plan.comm(tag("tgr", k), SEQ, k, 0.393, last, 30, lambda k=k: x_v.at[:, place(k)],
                      lambda: tgr_o.at[pl.ds(2 * s, 2)])
        else:
            plan.near("tgro", 0.4, last, 9, lambda: x_v.at[:, place(0)], lambda: tgr_o.at[pl.ds(2 * s, 2)])
    tok_done = last

    def value_grad():
        @pl.loop(0, 2)
        def _(t):
            lanes = pl.ds(pl.multiple_of(t * 384, 128), 384)
            grad = lax.dot_general(hl_v[...], val_v[:, :, lanes].reshape(1024, 384), TN, preferred_element_type=F32)
            gv_v[:, :, lanes] = grad.astype(BF16).reshape(8, 96, 384)

    gv_made = [plan.work("gv", 2.5, last, -1, value_grad)]
    every = range(8)
    Reduce(plan, "gi", gi, {q: [] for q in every}, False, (i0, i1, i2, i3, i4), gi_o, [1, 2, 4], True, 15.005, 0.59, HIGH)
    Reduce(plan, "gb", gb, {q: [] for q in every}, False, (b0, b1, b2, b3, b4), gb_o, [1, 2, 4], False, 0.009, 0.59, FAR)
    Reduce(plan, "go", go_v, {q: go_made for q in every}, True, (o0, o1, o2, o3, o4), go_o, [1, 2, 4], False, 15.007, 0.147, ODD)
    Reduce(plan, "gv", gv_v, {q: gv_made for q in every}, True, (v0, v1, v2, v3, v4), gv_o, [1, 2, 4], False, 15.001, 0.147, HIGH)
    last = tok_done
    for i, (axis, bit) in enumerate(((SEQ, 1), (SEQ, 2), (ROWS, 1), (ROWS, 2), (ROWS, 4))):
        plan.comm(tag("gn", i), axis, bit, 0.024, last, 0, lambda i=i: n0.at[i], lambda i=i: n1.at[i])

        def add(i=i):
            n0[i + 1] = n0[i] + n1[i]

        last = [plan.work(tag("gna", i), 0.1, [tag("gn", i)] + last, -5, add)]
    plan.near("gno", 0.02, last, 0, lambda: n0.at[5], lambda: gn_o)
    plan.run()


MIX_ORDERS = ((1, 0, 2, 4), (0, 1, 2, 4), (0, 1, 2, 4))
MIX_URGENCY = (15.009, 15.011, 12.02)
ODD, HIGH, FAR = (3, 7, 1, 5, 2, 6, 4, 0), (6, 7, 2, 3, 4, 5, 0, 1), (7, 3, 5, 1, 6, 2, 4, 0)


def backward_all(*args):
    sd = jax.ShapeDtypeStruct
    outs = [sd((8, 128, 768), BF16), sd((8, 128, 768), BF16), sd((768, 384), F32), sd((768, 384), F32),
            sd((96, 768), F32), sd((96, 768), F32), sd((8, 768), F32), sd((12, 512, 128), BF16), sd((4, 8, 128), F32)]
    dma = pltpu.SemaphoreType.DMA
    v = lambda *a: pltpu.VMEM(a, BF16)
    f = lambda *a: pltpu.VMEM(a, F32)
    big, piece, small = (384, 384), (192, 384), (48, 768)
    rows, flat = (2, 512, 768), (1024, 768)
    scratch = [v(*rows), v(*rows), pltpu.VMEM((4, 2, 128), jnp.int32), v(4, 12, 512, 128), v(8, 96, 768), v(8, 96, 768),
               v(8, 16, 768), v(*rows), v(*rows), f(*flat), f(*flat), f(*flat), v(*flat), v(8, 96, 768),
               v(8, 96, 768), f(2, 512, 1), f(2, 1, 512), f(6, 8, 768), f(5, 8, 768),
               v(2, 12, 512, 128), v(15, 12, 64, 128), v(12, 512, 128), v(2, 128, 768), f(8, 128)]
    scratch += [v(8, *big), v(8, *big), v(8, *piece), v(7, *piece), f(*big)]
    scratch += [v(8, *big), v(8, *big), v(*big), v(7, *big), f(*big)]
    for _ in range(2):
        scratch += [v(16, 128), v(8, *small), v(*small), v(7, *small), f(*small)]
    return pl.pallas_call(
        backward_kernel, out_shape=outs, in_specs=[ANY] * len(args), out_specs=[ANY] * len(outs),
        scratch_shapes=[dma((200,)), dma((200,)), dma((64,))] + scratch,
        compiler_params=pltpu.CompilerParams(collective_id=1, has_side_effects=True, vmem_limit_bytes=67043328),
    )(*args)


def own_gains(r, first, second):
    row = lax.broadcasted_iota(jnp.int32, (16, 8, 96), 0)
    owner = lax.broadcasted_iota(jnp.int32, (16, 8, 96), 1)
    both = jnp.where(row == 0, first, jnp.where(row == 1, second, jnp.zeros_like(second)))
    return jnp.where(owner == r, both, jnp.zeros_like(both)).reshape(16, 768)


def final_kernel(res, tgr, mg, gv, go, gi, gb, rms, res_o, tgr_o, mg_o, gv_o, go_o, gi_o, gb_o, first_o, second_o):
    for src, dst in ((res, res_o), (gv, gv_o), (go, go_o), (gi, gi_o)):
        dst[...] = src[...]
    tgr_o[...] = tgr[...].astype(F32)
    mg_o[...] = mg[...].astype(F32)
    gb_o[...] = gb[...].T
    for k in range(4):
        first_o[2 * k:2 * k + 2] = rms[k, :2]
        second_o[2 * k:2 * k + 2] = rms[k, 2:4]


def final_types(*args):
    sd = jax.ShapeDtypeStruct
    plain = lambda *b: pl.BlockSpec(b, lambda i: (i,) + (0,) * (len(b) - 1))
    tok, mix, small, wide = plain(2, 128, 768), plain(3, 512, 128), plain(24, 768), plain(192, 384)
    side = pl.BlockSpec((768, 128), lambda i: (0, jnp.minimum(i, 2)))
    turned = pl.BlockSpec((128, 768), lambda i: (jnp.minimum(i, 2), 0))
    means = pl.BlockSpec((4, 8, 128), lambda i: (0, 0, 0))
    mean = pl.BlockSpec((8, 128), lambda i: (0, 0))
    return pl.pallas_call(
        final_kernel, grid=(4,), in_specs=[tok, tok, mix, small, small, wide, side, means],
        out_specs=[tok, tok, mix, small, small, wide, turned, mean, mean],
        out_shape=[sd((8, 128, 768), BF16), sd((8, 128, 768), F32), sd((12, 512, 128), F32), sd((96, 768), F32),
                   sd((96, 768), F32), sd((768, 384), F32), sd((384, 768), F32), sd((8, 128), F32), sd((8, 128), F32)],
        compiler_params=pltpu.CompilerParams(vmem_limit_bytes=VMEM_LIMIT))(*args)


def fast_body(tokens, segments, mix, w_value, w_out, w_in, w_back, gain_one, gain_two, out_grad):
    r, s = lax.axis_index(ROWS), lax.axis_index(SEQ)
    gains = own_gains(r, gain_one, gain_two)
    (x_rows, grad_rows, seg_all, mix_all, wv, wo, gains_all, values, mixed, inverse, hidden_one, grad_entry_two,
     result, rms, grad_in, grad_back) = forward_all(
        tokens, out_grad, segments.reshape(4, 2, 128), mix, w_value, w_out, w_in, w_back, gains)
    res, tgr, gi, gb, go, gv, gn, mg, rms = backward_all(
        x_rows, grad_rows, seg_all, mix_all, wv, wo, gains_all, values, mixed, inverse, hidden_one, grad_entry_two,
        result.reshape(2, 512, 768), rms, grad_in, grad_back)
    own = lax.dynamic_slice(gn, (0, r * 96), (2, 96))
    res, tgr, mg, gv, go, gi, gb, first, second = final_types(res, tgr, mg, gv, go, gi, gb, rms)
    return (res, tgr, mg, gv, go, gi, gb, own[0], own[1], first, second)


def solution(mesh):
    in_specs = (
        P(ROWS, SEQ, None),
        P(ROWS, SEQ),
        P(None, None, SEQ),
        P(ROWS, None),
        P(ROWS, None),
        P(None, ROWS),
        P(ROWS, None),
        P(ROWS),
        P(ROWS),
        P(ROWS, SEQ, None),
    )
    out_specs = (
        P(ROWS, SEQ, None),
        P(ROWS, SEQ, None),
        P(None, None, SEQ),
        P(ROWS, None),
        P(ROWS, None),
        P(None, ROWS),
        P(ROWS, None),
        P(ROWS),
        P(ROWS),
        P(ROWS, SEQ),
        P(ROWS, SEQ),
    )
    shape = dict(mesh.shape)
    body = fast_body if shape[ROWS] == 8 and shape[SEQ] == 4 else generic_body
    return jax.shard_map(body, mesh=mesh, in_specs=in_specs, out_specs=out_specs, check_vma=False)
```

```python
import functools
from functools import partial

import jax
import jax.numpy as jnp
from jax import lax
from jax.experimental import pallas as pl
from jax.experimental.pallas import tpu as pltpu
from jax.sharding import PartitionSpec as P

ROWS, SEQ = "rows", "seq"
NEG = -1e30
EPS = 1e-06


def joined(part, axis, combine):
    gathered = jax.tree.map(lambda a: lax.all_gather(a, axis), part)

    def take(source):
        return jax.tree.map(lambda a: lax.dynamic_index_in_dim(a, source, 0, False), gathered)

    return lax.fori_loop(
        1, lax.axis_size(axis), lambda source, state: combine(state, take(source)), take(0)
    )


def normalize(inputs, gain):
    scale = lax.rsqrt(jnp.mean(inputs * inputs, axis=-1, keepdims=True) + EPS)
    normed = inputs * scale
    return (normed, scale, (normed * gain).astype(jnp.bfloat16))


def norm_back(upstream, normed, scale, gain):
    scaled = upstream * gain
    back = scale * (scaled - normed * jnp.mean(scaled * normed, axis=-1, keepdims=True))
    return (back, jnp.sum(upstream * normed, axis=0))


def combine_stats(first, second):
    max_first, sum_first = first
    max_second, sum_second = second
    row_max = jnp.maximum(max_first, max_second)
    return (
        row_max,
        sum_first * jnp.exp(max_first - row_max) + sum_second * jnp.exp(max_second - row_max),
    )


def local_stats(mix_cols, row_segs, own_segs):
    same_doc = (row_segs[:, None] == own_segs[None, :])[None]
    masked = jnp.where(same_doc, mix_cols, NEG)
    row_max = jnp.max(masked, axis=-1)
    row_sum = jnp.sum(jnp.where(same_doc, jnp.exp(masked - row_max[..., None]), 0.0), axis=-1)
    return (row_max, row_sum)


def make_probs(mix_cols, row_segs, own_segs, row_max, row_sum):
    same_doc = (row_segs[:, None] == own_segs[None, :])[None]
    masked = jnp.where(same_doc, mix_cols, NEG)
    raised = jnp.where(same_doc, jnp.exp(masked - row_max[..., None]), 0.0)
    return raised / row_sum[..., None]


def generic_body(tokens, segments, mix, w_value, w_out, w_in, w_back, gain_one, gain_two, out_grad):
    seq_count, col_count, model_width = tokens.shape
    head_count = mix.shape[0]
    head_dim = model_width // head_count
    f32 = jnp.float32
    bf16 = jnp.bfloat16
    gathered = (
        lax.all_gather(w_value, ROWS, axis=0, tiled=True),
        lax.all_gather(w_out, ROWS, axis=0, tiled=True),
        lax.all_gather(w_in, ROWS, axis=1, tiled=True),
        lax.all_gather(w_back, ROWS, axis=0, tiled=True),
        lax.all_gather(gain_one, ROWS, axis=0, tiled=True),
        lax.all_gather(gain_two, ROWS, axis=0, tiled=True),
    )
    wv_full, wo_full, wi_full, wb_full, gain_first, gain_second = gathered
    gain_first = gain_first.astype(f32)
    gain_second = gain_second.astype(f32)
    resid_in = tokens.astype(f32).reshape(seq_count * col_count, model_width)
    normed_one, scale_one, entry_one = normalize(resid_in, gain_first)
    values = jnp.dot(entry_one, wv_full, preferred_element_type=f32).astype(bf16)
    value_heads = values.reshape(seq_count, col_count, head_count, head_dim)
    row_segs = lax.all_gather(segments, SEQ, axis=1, tiled=True)
    mix_cols = mix.astype(f32)
    local_max, local_sum = lax.map(
        lambda fields: local_stats(mix_cols, fields[0], fields[1]), (row_segs, segments)
    )
    row_max, row_sum = joined((local_max, local_sum), SEQ, combine_stats)
    probs_low = lax.map(
        lambda fields: make_probs(mix_cols, fields[0], fields[1], fields[2], fields[3]).astype(
            bf16
        ),
        (row_segs, segments, row_max, row_sum),
    )
    products = jnp.einsum("shic,schd->ishd", probs_low, value_heads, preferred_element_type=f32)
    mixed = lax.psum_scatter(
        products.reshape(col_count * lax.axis_size(SEQ), seq_count, model_width),
        SEQ,
        scatter_dimension=0,
        tiled=True,
    )
    mixed = mixed.transpose(1, 0, 2).reshape(seq_count * col_count, model_width)
    mixed_low = mixed.astype(bf16)
    hidden_one = resid_in + jnp.dot(mixed_low, wo_full, preferred_element_type=f32)
    normed_two, scale_two, entry_two = normalize(hidden_one, gain_second)
    pre_act = jnp.dot(entry_two, wi_full, preferred_element_type=f32)
    activ, activ_back = jax.vjp(partial(jax.nn.gelu, approximate=True), pre_act)
    activ_low = activ.astype(bf16)
    branch = jnp.dot(activ_low, wb_full, preferred_element_type=f32)
    result = (hidden_one + branch).astype(bf16).reshape(tokens.shape)
    rms_residual = jnp.sqrt(jnp.mean(hidden_one * hidden_one, axis=-1)).reshape(
        seq_count, col_count
    )
    rms_sublayer = jnp.sqrt(jnp.mean(branch * branch, axis=-1)).reshape(seq_count, col_count)
    wv_back, wo_back, wi_back, wb_back = (
        lax.all_gather(w_value, ROWS, axis=0, tiled=True),
        lax.all_gather(w_out, ROWS, axis=0, tiled=True),
        lax.all_gather(w_in, ROWS, axis=1, tiled=True),
        lax.all_gather(w_back, ROWS, axis=0, tiled=True),
    )
    grad_out = out_grad.reshape(seq_count * col_count, model_width)
    grad_back = jnp.dot(activ_low.T, grad_out, preferred_element_type=f32)
    grad_activ = jnp.dot(grad_out, wb_back.T, preferred_element_type=f32)
    grad_pre = activ_back(grad_activ)[0].astype(bf16)
    grad_in = jnp.dot(entry_two.T, grad_pre, preferred_element_type=f32)
    grad_entry_two = jnp.dot(grad_pre, wi_back.T, preferred_element_type=f32)
    back_two, grad_gain_two = norm_back(grad_entry_two, normed_two, scale_two, gain_second)
    grad_hidden = grad_out.astype(f32) + back_two
    grad_hidden_low = grad_hidden.astype(bf16)
    grad_wo = jnp.dot(mixed_low.T, grad_hidden_low, preferred_element_type=f32)
    grad_mixed = jnp.dot(grad_hidden_low, wo_back.T, preferred_element_type=f32).astype(bf16)
    grad_rows = lax.all_gather(
        grad_mixed.reshape(seq_count, col_count, model_width), SEQ, axis=1, tiled=True
    )
    grad_heads = grad_rows.reshape(seq_count, -1, head_count, head_dim)

    def delta_part(fields):
        seg_row, seg_own, max_row, sum_row, grad_row, value_row = fields
        soft_probs = make_probs(mix_cols, seg_row, seg_own, max_row, sum_row)
        grad_probs = jnp.einsum("ihd,chd->hic", grad_row, value_row, preferred_element_type=f32)
        return jnp.sum(soft_probs * grad_probs, axis=-1)

    partial_delta = lax.map(
        delta_part, (row_segs, segments, row_max, row_sum, grad_heads, value_heads)
    )
    delta = lax.psum(partial_delta, SEQ)

    def seq_back(running, fields):
        seg_row, seg_own, max_row, sum_row, grad_row, value_row, delta_row = fields
        soft_probs = make_probs(mix_cols, seg_row, seg_own, max_row, sum_row)
        grad_probs = jnp.einsum("ihd,chd->hic", grad_row, value_row, preferred_element_type=f32)
        running = running + soft_probs * (grad_probs - delta_row[..., None])
        grad_value_row = jnp.einsum(
            "hic,ihd->chd", soft_probs.astype(bf16), grad_row, preferred_element_type=f32
        )
        return (running, grad_value_row)

    local_mix_grad, grad_values = lax.scan(
        seq_back,
        jnp.zeros(mix_cols.shape, f32),
        (row_segs, segments, row_max, row_sum, grad_heads, value_heads, delta),
    )
    mix_grad = lax.psum(local_mix_grad, ROWS)
    grad_values = grad_values.reshape(seq_count * col_count, model_width).astype(bf16)
    grad_wv = jnp.dot(entry_one.T, grad_values, preferred_element_type=f32)
    grad_entry_one = jnp.dot(grad_values, wv_back.T, preferred_element_type=f32)
    back_one, grad_gain_one = norm_back(grad_entry_one, normed_one, scale_one, gain_first)
    tokens_grad = (grad_hidden + back_one).reshape(tokens.shape)
    owned = (
        lax.psum_scatter(grad_wv, ROWS, scatter_dimension=0, tiled=True),
        lax.psum_scatter(grad_wo, ROWS, scatter_dimension=0, tiled=True),
        lax.psum_scatter(grad_in, ROWS, scatter_dimension=1, tiled=True),
        lax.psum_scatter(grad_back, ROWS, scatter_dimension=0, tiled=True),
        lax.psum_scatter(grad_gain_one, ROWS, scatter_dimension=0, tiled=True),
        lax.psum_scatter(grad_gain_two, ROWS, scatter_dimension=0, tiled=True),
    )
    summed = lax.psum((owned[0], owned[1], owned[2], owned[3], owned[4], owned[5]), SEQ)
    return (
        result,
        tokens_grad,
        mix_grad,
        summed[0],
        summed[1],
        summed[2],
        summed[3],
        summed[4],
        summed[5],
        rms_residual,
        rms_sublayer,
    )


F32 = jnp.float32
BF16 = jnp.bfloat16
MESH = pl.DeviceIdType.MESH
NT = (((1,), (1,)), ((), ()))
TN = (((0,), (0,)), ((), ()))
ANY = pl.BlockSpec(memory_space=pl.ANY)
RATE = 0.0925
VMEM_LIMIT = 60 * 2**20
ROW_LINK = {1: ("y", 1.0), 2: ("z", 1.0), 4: ("z", 2.0)}
SEQ_LINK = {1: ("core", 0.12), 2: ("x", 1.0), 3: ("x", 1.0)}


def tag(*parts):
    return "".join(map(str, parts))


class Copy:
    def __init__(self, make, remote):
        self.make, self.remote, self.done = make, remote, False

    def recv(self):
        if not self.done:
            self.done = True
            if self.remote:
                self.make().wait_recv()
            else:
                self.make().wait()


class Net:
    def __init__(self, send, recv, local):
        self.send, self.recv, self.local = send, recv, local
        self.remote, self.near = [], []

    def go(self, src, dst, dev):
        i = len(self.remote)
        make = lambda: pltpu.make_async_remote_copy(
            src_ref=src(), dst_ref=dst(), send_sem=self.send.at[i], recv_sem=self.recv.at[i],
            device_id=dev, device_id_type=MESH)
        make().start()
        self.remote.append(Copy(make, True))
        return self.remote[-1]

    def cp(self, src, dst):
        i = len(self.near)
        make = lambda: pltpu.make_async_copy(src(), dst(), self.local.at[i])
        make().start()
        self.near.append(Copy(make, False))
        return self.near[-1]

    def finish(self):
        for copy in self.near + self.remote:
            copy.recv()
        for copy in self.remote:
            copy.make().wait_send()


class Plan:
    def __init__(self, net, r, s, inside):
        self.net, self.r, self.s, self.inside = net, r, s, inside
        self.tasks, self.copies, self.loops = [], {}, {}

    def comm(self, name, axis, bit, mb, deps, prio, src, dst):
        link, factor = (ROW_LINK if axis == ROWS else SEQ_LINK)[bit]
        dev = {axis: (self.r if axis == ROWS else self.s) ^ bit}

        def emit():
            self.wait(deps)
            self.copies[name] = self.net.go(src, dst, dev)

        self.tasks.append((name, link, factor * 2 * mb / RATE, deps, prio, emit))
        return name

    def near(self, name, mb, deps, prio, src, dst):
        def emit():
            self.wait(deps)
            self.copies[name] = self.net.cp(src, dst)

        self.tasks.append((name, "hbm", mb / 2.0, deps, prio, emit))
        return name

    def work(self, name, us, deps, prio, run):
        def emit():
            self.wait(deps)
            run()

        self.tasks.append((name, "tc", us, deps, prio, emit))
        return name

    def loop(self, name, count, us, deps, prio, body, setup=lambda: None):
        if not self.inside:
            def run():
                held = setup()

                @pl.loop(0, count)
                def _(t):
                    body(t, held)

            return self.work(name, us * count, deps, prio, run)
        for t in range(count):
            step = tag(name, "_", t)
            self.loops[step] = (name, t, count, body, setup, deps)
            self.tasks.append((step, "tc", us, deps if t == 0 else [tag(name, "_", t - 1)], prio, None))
        return tag(name, "_", count - 1)

    def emit_loop(self, inner):
        name, _, count, body, setup, deps = self.loops[inner[0][0]]
        slots = [[] for _ in range(count)]
        now = 0
        for task in inner:
            if task[0] in self.loops:
                assert self.loops[task[0]][0] == name
                now = self.loops[task[0]][1]
            else:
                slots[now].append(task)
        self.wait(deps)
        held = setup()

        @pl.loop(0, count)
        def _(t):
            body(t, held)
            for k, tasks in enumerate(slots):
                if tasks:
                    @pl.when(t == k)
                    def _(tasks=tasks):
                        for task in tasks:
                            task[5]()

    def add(self, name, deps, to, other, us=0.12):
        def run():
            target, term = to(), other()
            target[...] = target[...] + term[...]

        return self.work(name, us, deps, -5, run)

    def wait(self, deps):
        for dep in deps:
            if dep in self.copies:
                self.copies[dep].recv()

    def solve(self):
        end, start, free, now = {}, {}, {}, 0.0
        left = list(self.tasks)
        while left:
            ready = [
                (max([free.get(t[1], 0.0)] + [end[d] for d in t[3]]), t[4], i)
                for i, t in enumerate(left) if all(d in end for d in t[3])
            ]
            first = min(ready)
            begin, _, pick = min(
                (b, p, i) for b, p, i in ready if b <= first[0] + 1e-9)
            name, link, cost, _, prio, _ = left.pop(pick)
            start[name] = (begin, link == "tc", prio)
            free[link] = begin + cost
            end[name] = begin + cost + (0.0 if link == "tc" else 2.0)
        self.start, self.end = start, end
        return sorted(self.tasks, key=lambda t: start[t[0]])

    def run(self):
        order = self.solve()
        early = [task for task in order if task[1] == "hbm" and not task[3]]
        for task in early:
            task[5]()
        greet(self.r, self.s)
        rest = [task for task in order if task not in early]
        names = [task[0] for task in rest]
        i = 0
        while i < len(rest):
            if names[i] in self.loops:
                name, _, count = self.loops[names[i]][:3]
                end = names.index(tag(name, "_", count - 1))
                self.emit_loop(rest[i:end + 1])
                i = end
            else:
                rest[i][5]()
            i += 1
        self.net.finish()


def greet(r, s):
    barrier = pltpu.get_barrier_semaphore()
    for bit in (1, 2, 4):
        pl.semaphore_signal(barrier, inc=1, device_id={ROWS: r ^ bit}, device_id_type=MESH)
    for bit in (1, 2, 3):
        pl.semaphore_signal(barrier, inc=1, device_id={SEQ: s ^ bit}, device_id_type=MESH)
    pl.semaphore_wait(barrier, 6)


def cut(ref, start, size):
    return ref.at[pl.ds(pl.multiple_of(start, 16), size)]


def add_gather(plan, name, src, dst, order, ways, prio, mb):
    r, s = plan.r, plan.s
    core, x = s % 2, s // 2
    n = src.shape[0] // ways
    off = {1: 0, 2: core, 4: 2 * core + x}[ways] * n
    far = (2 * core + 1 - x) * n
    part = lambda q, o: cut(src if q == 0 else dst.at[r ^ q], o, n)
    home = lambda q, o: cut(dst.at[r ^ q], o, n)
    got = {0: None}
    for stage, bit in enumerate(order):
        new = {}
        for q, dep in got.items():
            new[q ^ bit] = plan.comm(
                tag(name, q ^ bit), ROWS, bit, mb / ways, [dep] if dep else [], prio + 0.1 * stage,
                lambda q=q: part(q, off), lambda q=q: home(q, off))
        got.update(new)
    need = {q: [dep or tag(name, "0")] for q, dep in got.items()}
    for q, dep in got.items():
        if q == 0 or ways == 1:
            continue
        need[q].append(plan.comm(tag(name, "c", q), SEQ, 1, mb / ways, [dep], prio + 1,
                                 lambda q=q: part(q, off), lambda q=q: home(q, off)))
        if ways == 4:
            need[q].append(plan.comm(tag(name, "x", q), SEQ, 2, mb / ways, [dep], prio + 1,
                                     lambda q=q: part(q, off), lambda q=q: home(q, off)))
            need[q].append(plan.comm(tag(name, "f", q), SEQ, 1, mb / ways, [tag(name, "x", q)], prio + 1,
                                     lambda q=q: part(q, far), lambda q=q: home(q, far)))
    return need


def column(row):
    return jnp.broadcast_to(row, (128, 128)).T[:, :1]


def as_row(col):
    return jnp.broadcast_to(col, (128, 128)).T[:1]


def segment_layouts(seg, col, row):
    for q in range(2):
        for k in range(4):
            ids = seg[k, q:q + 1].astype(F32)
            row[q, :, k * 128:(k + 1) * 128] = ids
            col[q, k * 128:(k + 1) * 128] = column(ids)


def gain_row(gains, i):
    total = gains[0, i:i + 1].astype(F32)
    for k in range(1, 8):
        total = total + gains[k, i:i + 1].astype(F32)
    return total


def forward_kernel(tok, grd, seg, mix, wv, wo, wi, wb, gn,
                   x_o, g_o, seg_o, m_o, wv_o, wo_o, gn_o, val_o, mxd_o, iz_o, h_o, e2_o, res_o, rms_o, gi_o, gb_o,
                   send, recv, local,
                   x_v, g_v, seg_v, m_v, wv_v, wo_v, wi_v, wb_v, gn_v, val_v, mxd_v, h_v, e_v, et_v, gt_v,
                   br_v, e2_v, act_v, pg_v, gi_v, gb_v, rms_v, sc_v, sr_v):
    r, s = lax.axis_index(ROWS), lax.axis_index(SEQ)
    y, zb = r % 2, (r // 2) % 2
    net = Net(send, recv, local)
    plan = Plan(net, r, s, True)
    block = lambda k: pl.ds(pl.multiple_of((s ^ k) * 128, 128), 128)
    for k in (2, 3, 1):
        plan.comm(tag("seg", k), SEQ, k, 0.001, [], 0, lambda k=k: seg.at[s ^ k], lambda: seg_v.at[s])
        plan.comm(tag("tok", k), SEQ, k, 0.393, [], 5, lambda k=k: tok.at[pl.ds(2 * (s ^ k), 2)],
                  lambda: x_v.at[:, block(0)])
        plan.comm(tag("grd", k), SEQ, k, 0.393, [], 15, lambda k=k: grd.at[pl.ds(2 * (s ^ k), 2)],
                  lambda: g_v.at[:, block(0)])
    groups = 3
    mixes = []
    for g, urgent in enumerate((1.0, 4.01, 1.02)):
        heads = pl.ds(12 // groups * g, 12 // groups)
        quarter = lambda ref, a, b, heads=heads: ref.at[heads, pl.ds((2 * a + b) * 128, 128)]
        other = lambda a, b, quarter=quarter: (lambda: quarter(m_v.at[s ^ 2], a, b))
        size = 0.393 / groups
        plan.comm(tag("mixc", g), SEQ, 1, 4 * size, [], 3 + 0.01 * g, lambda heads=heads: mix.at[heads],
                  lambda heads=heads: m_v.at[s, heads])
        plan.comm(tag("mixx", g), SEQ, 2, size, [], urgent, lambda quarter=quarter: quarter(mix, y, zb),
                  lambda quarter=quarter: quarter(m_v.at[s], y, zb))
        names = ["mix0", tag("mixc", g), tag("mixx", g)]
        for name, axis, bit, dep, prio, a, b in (
                ("mixz", ROWS, 2, "mixx", 2, y, zb), ("mixy", ROWS, 1, "mixx", 2, y, zb),
                ("mixw", ROWS, 1, "mixz", 2, y, 1 - zb), ("mixp", SEQ, 1, "mixx", 3, y, zb),
                ("mixq", SEQ, 1, "mixz", 3, y, 1 - zb), ("mixr", SEQ, 1, "mixy", 3, 1 - y, zb),
                ("mixs", SEQ, 1, "mixw", 3, 1 - y, 1 - zb)):
            names.append(plan.comm(tag(name, g), axis, bit, size, [tag(dep, g)], prio + 0.01 * g, other(a, b), other(a, b)))
        mixes.append(names)
    flat = lambda got, *qs: [d for q in qs for d in got[q]]
    every = range(8)
    gn_d = add_gather(plan, "gn", gn, gn_v, [4, 2, 1], 1, 0, 0.024)
    wv_d = add_gather(plan, "wv", wv, wv_v, [4, 2, 1], 2, 1, 0.147)
    wo_d = add_gather(plan, "wo", wo, wo_v, [4, 2, 1], 2, 10, 0.147)
    wi_d = add_gather(plan, "wi", wi, wi_v, [4, 1, 2], 4, 20, 0.59)
    wb_d = add_gather(plan, "wb", wb, wb_v, [4, 2, 1], 2, 20.05, 0.59)
    for name, mb, src, dst in (
            ("tok0", 0.4, lambda: tok.at[pl.ds(2 * s, 2)], lambda: x_v.at[:, block(0)]),
            ("gn0", 0.02, lambda: gn, lambda: gn_v.at[r]), ("wv0", 0.15, lambda: wv, lambda: wv_v.at[r]),
            ("seg0", 0.01, lambda: seg.at[s], lambda: seg_v.at[s]), ("mix0", 1.5, lambda: mix, lambda: m_v.at[s]),
            ("wo0", 0.15, lambda: wo, lambda: wo_v.at[r]), ("wi0", 0.6, lambda: wi, lambda: wi_v.at[r]),
            ("wb0", 0.6, lambda: wb, lambda: wb_v.at[r]),
            ("grd0", 0.4, lambda: grd.at[pl.ds(2 * s, 2)], lambda: g_v.at[:, block(0)])):
        plan.near(name, mb, [], 0, src, dst)

    def put(name, mb, deps, src, dst):
        plan.near(name, mb, deps, 90, lambda: src, lambda: dst)

    for k in range(4):
        def values(k=k):
            x = x_v[:, block(k)].reshape(256, 768).astype(F32)
            scale = lax.rsqrt(jnp.mean(x * x, axis=-1, keepdims=True) + EPS)
            entry = (x * scale * gain_row(gn_v, 0)).astype(BF16)
            out = jnp.dot(entry, wv_v[...].reshape(768, 768), preferred_element_type=F32)
            val_v[:, block(k)] = out.astype(BF16).reshape(2, 128, 768)

        plan.work(tag("val", k), 1.2, [tag("tok", k)] + flat(wv_d, *every) + flat(gn_d, *every), 1, values)
    plan.work("segs", 1.0, [tag("seg", k) for k in range(4)], 0, lambda: segment_layouts(seg_v, sc_v, sr_v))
    for k in range(4):
        def turn(k=k):
            for q in range(2):
                at = pl.ds(pl.multiple_of(q * 512 + (s ^ k) * 128, 128), 128)
                gt_v[:, at] = g_v[q, block(k)].T

        plan.work(tag("gt", k), 0.6, [tag("grd", k)], 9, turn)
    lane = lax.broadcasted_iota(jnp.int32, (1, 128), 1)
    last = ["segs"] + [tag("val", k) for k in range(4)]
    for g in range(groups):
        def mixing(t, _, g=g):
            p = g * (6 // groups) + t
            lanes = pl.ds(pl.multiple_of(p * 128, 128), 128)
            raised = [exp_mix(m_v, 2 * p + hh).astype(BF16) for hh in range(2)]
            for q in range(2):
                same = sc_v[q] == sr_v[q]
                rhs = jnp.concatenate([val_v[q, :, lanes], jnp.ones((512, 128), BF16)], axis=1)
                both = [jnp.dot(jnp.where(same, e, jnp.zeros_like(e)), rhs, preferred_element_type=F32)
                        for e in raised]
                total = jnp.where(lane < 64, both[0][:, :128], both[1][:, :128])
                inverse = 1.0 / jnp.where(lane < 64, both[0][:, 128:], both[1][:, 128:])
                mxd_v[q, :, lanes] = (total * inverse).astype(BF16)
                br_v[q * 512:(q + 1) * 512, lanes] = inverse

        last = [plan.loop(tag("mf", g), 6 // groups, 1.7, last + mixes[g], 1, mixing)]
    mixed_by = last
    put("iz_out", 1.5, last, br_v, iz_o)
    for q in range(2):
        def project(k, _, q=q):
            inside = pl.ds(pl.multiple_of(k * 128, 128), 128)
            at = pl.ds(pl.multiple_of(q * 512 + k * 128, 128), 128)
            h = x_v[q, inside].astype(F32) + jnp.dot(
                mxd_v[q, inside], wo_v[...].reshape(768, 768), preferred_element_type=F32)
            square = jnp.mean(h * h, axis=-1, keepdims=True)
            h_v[at] = h
            entry = (h * lax.rsqrt(square + EPS) * gain_row(gn_v, 1)).astype(BF16)
            e_v[at] = entry
            et_v[:, at] = entry.T
            rms_v[k, q:q + 1] = as_row(jnp.sqrt(square))

        last = [plan.loop(tag("out", q), 4, 0.6, last + flat(wo_d, *every), 1, project)]
    put("h_out", 1.5, last, h_v, h_o)
    c0, c1 = 0.7978845608028654, 0.044715
    step = 256
    for i, (a, b) in enumerate(((0, 4), (1, 5), (2, 6), (3, 7))):
        def load(a=a, b=b):
            weights = jnp.concatenate([wi_v[r ^ a], wi_v[r ^ b]], axis=1)
            return weights, jnp.concatenate([wb_v[r ^ a], wb_v[r ^ b]], axis=0)

        def feed(t, held, i=i):
            weights, back = held
            at = pl.ds(pl.multiple_of(t * step, step), step)
            inner = pl.ds(pl.multiple_of((t % 2) * step, step), step)
            pre = jnp.dot(e_v[at], weights, preferred_element_type=F32)
            up = lax.dot_general(g_v[t // 2, inner], back, NT, preferred_element_type=F32)
            square = pre * pre
            th = jnp.tanh(pre * (c0 + (c0 * c1) * square))
            gate = 0.5 + 0.5 * th
            act = (pre * gate).astype(BF16)
            slope = gate + pre * (1.0 - th * th) * ((0.5 * c0) + (1.5 * c0 * c1) * square)
            pg = (up * slope).astype(BF16)
            act_v[at] = act
            pg_v[at] = pg
            branch = jnp.dot(act, back, preferred_element_type=F32)
            e2 = lax.dot_general(pg, weights, NT, preferred_element_type=F32)
            if i == 0:
                br_v[at] = branch
                e2_v[at] = e2
            else:
                br_v[at] += branch
                e2_v[at] += e2

        need = flat(wi_d, a, b) + flat(wb_d, a, b) + [tag("grd", k) for k in range(4)] + ["iz_out"]
        last = [plan.loop(tag("ff", i), 4, 1.9, last + need, 1, feed, load)]

        def weight_grads(t, _, i=i):
            slot = i % 2
            at = pl.ds(pl.multiple_of(t * 256, 256), 256)
            gi = jnp.dot(et_v[at], pg_v[...], preferred_element_type=F32).astype(BF16)
            gb = jnp.dot(gt_v[at], act_v[...], preferred_element_type=F32).astype(BF16)
            for q in range(2):
                gi_v[slot, q, at] = gi[:, q * 384:(q + 1) * 384]
                gb_v[slot, q, at] = gb[:, q * 384:(q + 1) * 384]

        free = [tag("g", n, "_out", i - 2, q) for n in "ib" for q in range(2)] if i >= 2 else []
        last = [plan.loop(tag("fg", i), 3, 1.3, last + free + [tag("gt", k) for k in range(4)], 1, weight_grads)]
        for q, owner in enumerate((a, b)):
            put(tag("gi_out", i, q), 0.3, last, gi_v.at[i % 2, q], gi_o.at[r ^ owner])
            put(tag("gb_out", i, q), 0.3, last, gb_v.at[i % 2, q], gb_o.at[r ^ owner])

    def finish():
        @pl.loop(0, 8)
        def _(t):
            at = pl.ds(pl.multiple_of(t * 128, 128), 128)
            q, k = t // 4, t % 4
            branch = br_v[at]
            e_v[at] = (h_v[at] + branch).astype(BF16)
            rms_v[k, pl.ds(2 + q, 1)] = as_row(jnp.sqrt(jnp.mean(branch * branch, axis=-1, keepdims=True)))

    last = [plan.work("fin", 2.0, last, 1, finish)]
    put("e2_out", 1.5, last, e2_v, e2_o)
    put("res_out", 0.8, last, e_v, res_o)
    put("rms_out", 0.1, last, rms_v, rms_o)
    toks, grds = [tag("tok", k) for k in range(4)], [tag("grd", k) for k in range(4)]
    put("x_out", 0.8, toks, x_v, x_o)
    put("g_out", 0.8, grds, g_v, g_o)
    put("seg_out", 0.1, ["segs"], seg_v, seg_o)
    put("m_out", 3.0, sum(mixes, []), m_v, m_o)
    put("wv_out", 0.6, flat(wv_d, *every), wv_v, wv_o)
    put("wo_out", 0.6, flat(wo_d, *every), wo_v, wo_o)
    put("gn_out", 0.1, flat(gn_d, *every), gn_v, gn_o)
    put("val_out", 0.8, [tag("val", k) for k in range(4)], val_v, val_o)
    put("mxd_out", 0.8, mixed_by, mxd_v, mxd_o)
    plan.run()


def forward_all(tok, grd, seg, mix, wv, wo, wi, wb, gn):
    sd = jax.ShapeDtypeStruct
    rows, flat, big = (2, 512, 768), (1024, 768), (8, 768, 384)
    mixes, square, gains = (4, 12, 512, 128), (8, 96, 768), (8, 16, 768)
    outs = [sd(rows, BF16), sd(rows, BF16), sd((4, 2, 128), jnp.int32), sd(mixes, BF16), sd(square, BF16),
            sd(square, BF16), sd(gains, BF16), sd(rows, BF16), sd(rows, BF16), sd(flat, F32), sd(flat, F32),
            sd(flat, F32), sd(flat, BF16), sd((4, 8, 128), F32), sd(big, BF16), sd(big, BF16)]
    dma = pltpu.SemaphoreType.DMA
    v = lambda *a: pltpu.VMEM(a, BF16)
    f = lambda *a: pltpu.VMEM(a, F32)
    turned = (768, 1024)
    scratch = [v(*rows), v(*rows), pltpu.VMEM((4, 2, 128), jnp.int32), v(*mixes), v(*square), v(*square), v(*big),
               v(8, 384, 768), v(*gains), v(*rows), v(*rows), f(*flat), v(*flat), v(*turned), v(*turned),
               f(*flat), f(*flat), v(*flat), v(*flat), v(2, 2, 768, 384), v(2, 2, 768, 384), f(4, 8, 128),
               f(2, 512, 1), f(2, 1, 512)]
    return pl.pallas_call(
        forward_kernel, out_shape=outs, in_specs=[ANY] * 9, out_specs=[ANY] * len(outs),
        scratch_shapes=[dma((128,)), dma((128,)), dma((48,))] + scratch,
        compiler_params=pltpu.CompilerParams(collective_id=0, has_side_effects=True, vmem_limit_bytes=VMEM_LIMIT),
    )(tok, grd, seg, mix, wv, wo, wi, wb, gn)


def exp_mix(m_ref, hh):
    return jnp.concatenate([jnp.exp(m_ref[k, hh].astype(F32)) for k in range(4)], axis=1)


class Reduce:
    def __init__(self, plan, name, src, made, local, bufs, out, order, first, prio, mb, pieces):
        self.plan, self.name, self.src, self.local, self.bufs = plan, name, src, local, bufs
        r, s = plan.r, plan.s
        self.core, self.x = s % 2, s // 2
        self.n = src.shape[1] // 2
        half = mb / 2
        own, near, across, rows, final = bufs
        last = {}
        for q in pieces:
            deps = made[q]
            if not local:
                plan.near(tag(name, "l", q), half, deps, prio, lambda q=q: self.half(src.at[r ^ q], self.core),
                          lambda q=q: own.at[q])
            plan.comm(tag(name, "c", q), SEQ, 1, half, deps, prio, lambda q=q: self.half(src.at[r ^ q], 1 - self.core),
                      lambda q=q: near.at[q])
            last[q] = plan.add(tag(name, "a", q), [tag(name, "c", q)] + (deps if local else [tag(name, "l", q)]),
                               lambda q=q: self.mine(q), lambda q=q: near.at[q])
        if first:
            half = half / 2
            for q in pieces:
                plan.comm(tag(name, "X", q), SEQ, 2, half, [last[q]], prio,
                          lambda q=q: self.quarter(self.mine(q), 1 - self.x), lambda q=q: across.at[q])
                last[q] = plan.add(tag(name, "A", q), [tag(name, "X", q), last[q]],
                                   lambda q=q: self.quarter(self.mine(q), self.x), lambda q=q: across.at[q])
        item = (lambda q: self.quarter(self.mine(q), self.x)) if first else self.mine
        keep, slot = list(range(8)), 0
        for stage, bit in enumerate(order):
            for q in [q for q in pieces if q in keep and q & bit]:
                plan.comm(tag(name, "r", q), ROWS, bit, half, [last[q]], prio + 0.1 * stage,
                          lambda q=q: item(q), lambda slot=slot: rows.at[slot])
                last[q ^ bit] = plan.add(tag(name, "b", q), [tag(name, "r", q), last[q ^ bit]],
                                         lambda q=q ^ bit: item(q), lambda slot=slot: rows.at[slot])
                slot += 1
            keep = [q for q in keep if not q & bit]
        if first:
            def widen():
                self.quarter(final, self.x)[...] = item(0)[...].astype(F32)

            plan.work(tag(name, "t"), 0.2, [last[0]], -5, widen)
            plan.comm(tag(name, "x"), SEQ, 2, 2 * half, [tag(name, "t")], prio + 0.5,
                      lambda: self.quarter(final, self.x), lambda: self.quarter(final, self.x))
            for name2, dep, which in (("m", "t", 0), ("o", "x", 1)):
                side = (lambda which=which: self.quarter(final, self.x if which == 0 else 1 - self.x))
                place = (lambda which=which: self.quarter(self.half(out, self.core),
                                                          self.x if which == 0 else 1 - self.x))
                plan.near(tag(name, name2), mb / 2, [tag(name, dep)], prio, side, place)
                plan.comm(tag(name, name2, "k"), SEQ, 1, mb / 2, [tag(name, dep)], prio, side, place)
        else:
            plan.comm(tag(name, "x"), SEQ, 2, half, [last[0]], prio + 0.5, lambda: item(0), lambda: across)

            def total():
                final[...] = item(0)[...].astype(F32) + across[...].astype(F32)

            plan.work(tag(name, "t"), 0.2, [tag(name, "x"), last[0]], -5, total)
            plan.near(tag(name, "o"), mb, [tag(name, "t")], prio, lambda: final, lambda: self.half(out, self.core))
            plan.comm(tag(name, "k"), SEQ, 1, mb, [tag(name, "t")], prio, lambda: final, lambda: self.half(out, self.core))

    def half(self, ref, which):
        return cut(ref, which * self.n, self.n)

    def quarter(self, ref, which):
        return cut(ref, which * (self.n // 2), self.n // 2)

    def mine(self, q):
        return self.half(self.src.at[self.plan.r ^ q], self.core) if self.local else self.bufs[0].at[q]


def backward_kernel(x_i, g_i, seg_i, m_i, wv_i, wo_i, gn_i, val_i, mxd_i, iz_i, h_i, e2_i, res_i, rms_i, gi, gb,
                    res_o, tgr_o, gi_o, gb_o, go_o, gv_o, gn_o, mg_o, rms_o, send, recv, local,
                    x_v, g_v, seg_v, m_v, wv_v, wo_v, gn_v, val_v, mxd_v, iz_v, h_v, q_v, hl_v, go_v, gv_v,
                    sc_v, sr_v, n0, n1, m1, m3, m4, t0, t1,
                    i0, i1, i2, i3, i4, b0, b1, b2, b3, b4, o0, o1, o2, o3, o4, v0, v1, v2, v3, v4):
    r, s = lax.axis_index(ROWS), lax.axis_index(SEQ)
    core, x = s % 2, s // 2
    net = Net(send, recv, local)
    plan = Plan(net, r, s, False)
    place = lambda k: pl.ds(pl.multiple_of((s ^ k) * 128, 128), 128)
    for name, mb, prio, src, dst in (
            ("h0", 1.6, 0, h_i.at[:512], h_v.at[:512]), ("e0", 1.6, 1, e2_i.at[:512], q_v.at[:512]),
            ("g0", 0.8, 1, g_i.at[0], g_v.at[0]), ("gn", 0.1, 0, gn_i, gn_v), ("wo", 1.2, 1, wo_i, wo_v),
            ("h1", 1.6, 2, h_i.at[512:], h_v.at[512:]), ("e1", 1.6, 2, e2_i.at[512:], q_v.at[512:]),
            ("g1", 0.8, 2, g_i.at[1], g_v.at[1]), ("seg", 0.1, 3, seg_i, seg_v), ("mxd", 1.6, 4, mxd_i, mxd_v),
            ("val", 1.6, 4, val_i, val_v), ("iz", 3.1, 4, iz_i, iz_v), ("m", 6.3, 5, m_i, m_v),
            ("x", 1.6, 6, x_i, x_v), ("wv", 1.2, 6, wv_i, wv_v)):
        plan.near(tag("in_", name), mb, [], prio, lambda src=src: src, lambda dst=dst: dst)
    for k in (2, 3, 1):
        plan.comm(tag("res", k), SEQ, k, 0.393, [], 15.001, lambda k=k: res_i.at[:, place(k)], lambda: res_o.at[pl.ds(2 * s, 2)])
        plan.comm(tag("rms", k), SEQ, k, 0.004, [], 3, lambda k=k: rms_i.at[s ^ k], lambda: rms_o.at[s])
    for name, src, buf, dst in (("res", res_i.at[:, place(0)], t0, res_o.at[pl.ds(2 * s, 2)]),
                                ("rms", rms_i.at[s], t1, rms_o.at[s])):
        plan.near(tag(name, "i"), 0.4, [], 9, lambda src=src: src, lambda buf=buf: buf)
        plan.near(tag(name, "o"), 0.4, [tag(name, "i")], 9, lambda buf=buf: buf, lambda dst=dst: dst)

    def clear():
        n0[...] = jnp.zeros_like(n0)

    plan.work("zero", 0.1, [], -2, clear)
    plan.work("segs", 1.0, ["in_seg"], -1, lambda: segment_layouts(seg_v, sc_v, sr_v))
    last = ["in_gn", "in_wo"]
    for part in range(2):
        def post(k, _, part=part):
            at = pl.ds(pl.multiple_of(part * 512 + k * 128, 128), 128)
            inside = pl.ds(pl.multiple_of(k * 128, 128), 128)
            h = h_v[at]
            scale = lax.rsqrt(jnp.mean(h * h, axis=-1, keepdims=True) + EPS)
            normed = h * scale
            up = q_v[at]
            n0[0, 1:2] += jnp.sum(up * normed, axis=0, keepdims=True)
            scaled = up * gain_row(gn_v, 1)
            back = scale * (scaled - normed * jnp.mean(scaled * normed, axis=-1, keepdims=True))
            grad = g_v[part, inside].astype(F32) + back
            q_v[at] = grad
            grad_low = grad.astype(BF16)
            hl_v[at] = grad_low
            g_v[part, inside] = lax.dot_general(
                grad_low, wo_v[...].reshape(768, 768), NT, preferred_element_type=F32).astype(BF16)

        last = [plan.loop(tag("post", part), 4, 0.75, last + ["zero"] + [tag("in_", n, part) for n in "heg"], -1, post)]

    lane = lax.broadcasted_iota(jnp.int32, (1, 128), 1)
    orders = MIX_ORDERS
    groups = len(orders)
    heads = 12 // groups
    for g, order in enumerate(orders):
        def mixing(t, _, g=g):
            p = g * (heads // 2) + t
            lanes = pl.ds(pl.multiple_of(p * 128, 128), 128)
            raised = [exp_mix(m_v, 2 * p + hh) for hh in range(2)]
            low = [e.astype(BF16) for e in raised]
            acc = [None, None]
            for q in range(2):
                same = sc_v[q] == sr_v[q]
                scaled = g_v[q, :, lanes].astype(F32) * iz_v[q * 512:(q + 1) * 512, lanes]
                inner = scaled * mxd_v[q, :, lanes].astype(F32)
                grads = []
                for hh in range(2):
                    mine = (lane < 64) if hh == 0 else (lane >= 64)
                    delta = jnp.sum(jnp.where(mine, inner, 0.0), axis=1, keepdims=True)
                    lhs = jnp.where(mine, scaled, 0.0).astype(BF16)
                    back = lax.dot_general(lhs, val_v[q, :, lanes], NT, preferred_element_type=F32)
                    term = jnp.where(same, back - delta, 0.0)
                    acc[hh] = term if q == 0 else acc[hh] + term
                    masked = jnp.where(same, low[hh], jnp.zeros_like(low[hh]))
                    grads.append(lax.dot_general(masked, scaled.astype(BF16), TN, preferred_element_type=F32))
                val_v[q, :, lanes] = jnp.where(lane < 64, grads[0], grads[1]).astype(BF16)
            for hh in range(2):
                out = (acc[hh] * raised[hh]).astype(BF16)
                for k in range(4):
                    m_v[k, 2 * p + hh] = out[:, k * 128:(k + 1) * 128]

        last = [plan.loop(tag("mb", g), heads // 2, 2.7, last + ["segs", "in_m", "in_val", "in_iz", "in_mxd"], -1, mixing)]
        mine = pl.ds(g * heads, heads)
        mb = 0.01638 * heads
        prio = MIX_URGENCY[g]
        done = {}
        block = lambda h, side, mine=mine: m_v.at[2 * (x ^ h) + (core if side == 0 else 1 - core), mine]
        for h in range(2):
            plan.comm(tag("mg", g, "c", h), SEQ, 1, 8 * mb, last, prio, lambda h=h, block=block: block(h, 1),
                      lambda h=h, mine=mine: m1.at[h, mine])
            made = plan.add(tag("mg", g, "a", h), [tag("mg", g, "c", h)] + last, lambda h=h, block=block: block(h, 0),
                            lambda h=h, mine=mine: m1.at[h, mine], 0.3)
            for q in range(8):
                done[h, q] = made
        rows = lambda q: pl.ds(pl.multiple_of((r ^ q) * 64, 64), 64)
        item = lambda h, q, mine=mine: m_v.at[2 * (x ^ h) + core, mine, rows(q)]
        keep, slot = [(h, q) for h in range(2) for q in range(8)], 0
        for bit in order:
            hit = (lambda h, q: h) if bit == 0 else (lambda h, q, bit=bit: q & bit)
            for h, q in [k for k in keep if hit(*k)]:
                to = (0, q) if bit == 0 else (h, q ^ bit)
                name = tag("mg", g, "r", h, q)
                plan.comm(name, ROWS if bit else SEQ, bit or 2, mb, [done[h, q]], prio,
                          lambda h=h, q=q, item=item: item(h, q), lambda slot=slot, mine=mine: m3.at[slot, mine])
                done[to] = plan.add(name + "d", [name, done[to]], lambda to=to, item=item: item(*to),
                                    lambda slot=slot, mine=mine: m3.at[slot, mine])
                slot += 1
            keep = [k for k in keep if not hit(*k)]

        def final(mine=mine, item=item):
            m4[mine, rows(0)] = item(0, 0)[...]

        got = {0: plan.work(tag("mg", g, "f"), 0.1, [done[0, 0]], -5, final)}
        for bit in [b for b in reversed(order) if b]:
            new = {}
            for q, dep in got.items():
                part = lambda q=q, mine=mine: m4.at[mine, rows(q)]
                new[q ^ bit] = plan.comm(tag("mg", g, "g", q ^ bit), ROWS, bit, mb, [dep], prio, part, part)
            got.update(new)
        plan.near(tag("mg", g, "o"), 0.4, list(got.values()), 0, lambda mine=mine: m4.at[mine], lambda mine=mine: mg_o.at[mine])
    def out_grad():
        @pl.loop(0, 2)
        def _(t):
            lanes = pl.ds(pl.multiple_of(t * 384, 128), 384)
            grad = lax.dot_general(mxd_v[...].reshape(1024, 768), hl_v[:, lanes], TN, preferred_element_type=F32)
            go_v[:, :, lanes] = grad.astype(BF16).reshape(8, 96, 384)

    last = [plan.work("go", 2.5, last, -1, out_grad)]
    go_made = last
    for k in (2, 3, 1, 0):
        def tokens(k=k):
            for q in range(2):
                at = pl.ds(pl.multiple_of(q * 512 + (s ^ k) * 128, 128), 128)
                up = lax.dot_general(val_v[q, place(k)], wv_v[...].reshape(768, 768), NT, preferred_element_type=F32)
                xs = x_v[q, place(k)].astype(F32)
                scale = lax.rsqrt(jnp.mean(xs * xs, axis=-1, keepdims=True) + EPS)
                normed = xs * scale
                gain = gain_row(gn_v, 0)
                hl_v[at] = (normed * gain).astype(BF16)
                n0[0, 0:1] += jnp.sum(up * normed, axis=0, keepdims=True)
                scaled = up * gain
                back = scale * (scaled - normed * jnp.mean(scaled * normed, axis=-1, keepdims=True))
                x_v[q, place(k)] = (q_v[at] + back).astype(BF16)

        last = [plan.work(tag("tok", k), 1.2, last + ["in_x", "in_wv"], -1, tokens)]
        if k:
            plan.comm(tag("tgr", k), SEQ, k, 0.393, last, 30, lambda k=k: x_v.at[:, place(k)],
                      lambda: tgr_o.at[pl.ds(2 * s, 2)])
        else:
            plan.near("tgro", 0.4, last, 9, lambda: x_v.at[:, place(0)], lambda: tgr_o.at[pl.ds(2 * s, 2)])
    tok_done = last

    def value_grad():
        @pl.loop(0, 2)
        def _(t):
            lanes = pl.ds(pl.multiple_of(t * 384, 128), 384)
            grad = lax.dot_general(hl_v[...], val_v[:, :, lanes].reshape(1024, 384), TN, preferred_element_type=F32)
            gv_v[:, :, lanes] = grad.astype(BF16).reshape(8, 96, 384)

    gv_made = [plan.work("gv", 2.5, last, -1, value_grad)]
    every = range(8)
    Reduce(plan, "gi", gi, {q: [] for q in every}, False, (i0, i1, i2, i3, i4), gi_o, [1, 2, 4], True, 15.005, 0.59, HIGH)
    Reduce(plan, "gb", gb, {q: [] for q in every}, False, (b0, b1, b2, b3, b4), gb_o, [1, 2, 4], False, 0.009, 0.59, FAR)
    Reduce(plan, "go", go_v, {q: go_made for q in every}, True, (o0, o1, o2, o3, o4), go_o, [1, 2, 4], False, 15.007, 0.147, ODD)
    Reduce(plan, "gv", gv_v, {q: gv_made for q in every}, True, (v0, v1, v2, v3, v4), gv_o, [1, 2, 4], False, 13.008, 0.147, HIGH)
    last = tok_done
    for i, (axis, bit) in enumerate(((SEQ, 1), (SEQ, 2), (ROWS, 1), (ROWS, 2), (ROWS, 4))):
        plan.comm(tag("gn", i), axis, bit, 0.024, last, 0, lambda i=i: n0.at[i], lambda i=i: n1.at[i])

        def add(i=i):
            n0[i + 1] = n0[i] + n1[i]

        last = [plan.work(tag("gna", i), 0.1, [tag("gn", i)] + last, -5, add)]
    plan.near("gno", 0.02, last, 0, lambda: n0.at[5], lambda: gn_o)
    plan.run()


MIX_ORDERS = ((1, 0, 2, 4), (0, 1, 2, 4), (0, 1, 2, 4))
MIX_URGENCY = (15.31, 15.011, 12.02)
ODD, HIGH, FAR = (3, 7, 1, 5, 2, 6, 4, 0), (6, 7, 2, 3, 4, 5, 0, 1), (7, 3, 5, 1, 6, 2, 4, 0)


def backward_all(*args):
    sd = jax.ShapeDtypeStruct
    outs = [sd((8, 128, 768), BF16), sd((8, 128, 768), BF16), sd((768, 384), F32), sd((768, 384), F32),
            sd((96, 768), F32), sd((96, 768), F32), sd((8, 768), F32), sd((12, 512, 128), BF16), sd((4, 8, 128), F32)]
    dma = pltpu.SemaphoreType.DMA
    v = lambda *a: pltpu.VMEM(a, BF16)
    f = lambda *a: pltpu.VMEM(a, F32)
    big, piece, small = (384, 384), (192, 384), (48, 768)
    rows, flat = (2, 512, 768), (1024, 768)
    scratch = [v(*rows), v(*rows), pltpu.VMEM((4, 2, 128), jnp.int32), v(4, 12, 512, 128), v(8, 96, 768), v(8, 96, 768),
               v(8, 16, 768), v(*rows), v(*rows), f(*flat), f(*flat), f(*flat), v(*flat), v(8, 96, 768),
               v(8, 96, 768), f(2, 512, 1), f(2, 1, 512), f(6, 8, 768), f(5, 8, 768),
               v(2, 12, 512, 128), v(15, 12, 64, 128), v(12, 512, 128), v(2, 128, 768), f(8, 128)]
    scratch += [v(8, *big), v(8, *big), v(8, *piece), v(7, *piece), f(*big)]
    scratch += [v(8, *big), v(8, *big), v(*big), v(7, *big), f(*big)]
    for _ in range(2):
        scratch += [v(16, 128), v(8, *small), v(*small), v(7, *small), f(*small)]
    return pl.pallas_call(
        backward_kernel, out_shape=outs, in_specs=[ANY] * len(args), out_specs=[ANY] * len(outs),
        scratch_shapes=[dma((200,)), dma((200,)), dma((64,))] + scratch,
        compiler_params=pltpu.CompilerParams(collective_id=1, has_side_effects=True, vmem_limit_bytes=67043328),
    )(*args)


def own_gains(r, first, second):
    row = lax.broadcasted_iota(jnp.int32, (16, 8, 96), 0)
    owner = lax.broadcasted_iota(jnp.int32, (16, 8, 96), 1)
    both = jnp.where(row == 0, first, jnp.where(row == 1, second, jnp.zeros_like(second)))
    return jnp.where(owner == r, both, jnp.zeros_like(both)).reshape(16, 768)


def final_kernel(res, tgr, mg, gv, go, gi, gb, rms, res_o, tgr_o, mg_o, gv_o, go_o, gi_o, gb_o, first_o, second_o):
    for src, dst in ((res, res_o), (gv, gv_o), (go, go_o), (gi, gi_o)):
        dst[...] = src[...]
    tgr_o[...] = tgr[...].astype(F32)
    mg_o[...] = mg[...].astype(F32)
    gb_o[...] = gb[...].T
    for k in range(4):
        first_o[2 * k:2 * k + 2] = rms[k, :2]
        second_o[2 * k:2 * k + 2] = rms[k, 2:4]


def final_types(*args):
    sd = jax.ShapeDtypeStruct
    plain = lambda *b: pl.BlockSpec(b, lambda i: (i,) + (0,) * (len(b) - 1))
    tok, mix, small, wide = plain(2, 128, 768), plain(3, 512, 128), plain(24, 768), plain(192, 384)
    side = pl.BlockSpec((768, 128), lambda i: (0, jnp.minimum(i, 2)))
    turned = pl.BlockSpec((128, 768), lambda i: (jnp.minimum(i, 2), 0))
    means = pl.BlockSpec((4, 8, 128), lambda i: (0, 0, 0))
    mean = pl.BlockSpec((8, 128), lambda i: (0, 0))
    return pl.pallas_call(
        final_kernel, grid=(4,), in_specs=[tok, tok, mix, small, small, wide, side, means],
        out_specs=[tok, tok, mix, small, small, wide, turned, mean, mean],
        out_shape=[sd((8, 128, 768), BF16), sd((8, 128, 768), F32), sd((12, 512, 128), F32), sd((96, 768), F32),
                   sd((96, 768), F32), sd((768, 384), F32), sd((384, 768), F32), sd((8, 128), F32), sd((8, 128), F32)],
        compiler_params=pltpu.CompilerParams(vmem_limit_bytes=VMEM_LIMIT))(*args)


def fast_body(tokens, segments, mix, w_value, w_out, w_in, w_back, gain_one, gain_two, out_grad):
    r, s = lax.axis_index(ROWS), lax.axis_index(SEQ)
    gains = own_gains(r, gain_one, gain_two)
    (x_rows, grad_rows, seg_all, mix_all, wv, wo, gains_all, values, mixed, inverse, hidden_one, grad_entry_two,
     result, rms, grad_in, grad_back) = forward_all(
        tokens, out_grad, segments.reshape(4, 2, 128), mix, w_value, w_out, w_in, w_back, gains)
    res, tgr, gi, gb, go, gv, gn, mg, rms = backward_all(
        x_rows, grad_rows, seg_all, mix_all, wv, wo, gains_all, values, mixed, inverse, hidden_one, grad_entry_two,
        result.reshape(2, 512, 768), rms, grad_in, grad_back)
    own = lax.dynamic_slice(gn, (0, r * 96), (2, 96))
    res, tgr, mg, gv, go, gi, gb, first, second = final_types(res, tgr, mg, gv, go, gi, gb, rms)
    return (res, tgr, mg, gv, go, gi, gb, own[0], own[1], first, second)


def solution(mesh):
    in_specs = (
        P(ROWS, SEQ, None),
        P(ROWS, SEQ),
        P(None, None, SEQ),
        P(ROWS, None),
        P(ROWS, None),
        P(None, ROWS),
        P(ROWS, None),
        P(ROWS),
        P(ROWS),
        P(ROWS, SEQ, None),
    )
    out_specs = (
        P(ROWS, SEQ, None),
        P(ROWS, SEQ, None),
        P(None, None, SEQ),
        P(ROWS, None),
        P(ROWS, None),
        P(None, ROWS),
        P(ROWS, None),
        P(ROWS),
        P(ROWS),
        P(ROWS, SEQ),
        P(ROWS, SEQ),
    )
    shape = dict(mesh.shape)
    body = fast_body if shape[ROWS] == 8 and shape[SEQ] == 4 else generic_body
    return jax.shard_map(body, mesh=mesh, in_specs=in_specs, out_specs=out_specs, check_vma=False)
```
